32 devices in a mesh: fsdp: 2 (over y), ctx: 4 (over x, core), tp: 4 (over z).
Axes of the slice: x: 2, y: 2, z: 4, core: 2. Of those that a mesh axis runs over, the one named last changes fastest.
Arguments:
- tokens: bfloat16 [4, 2048, 1024], P('fsdp', 'ctx'), may hold values from -6 to 6
- first_values: bfloat16 [4, 2048, 1024], P('fsdp', 'ctx', 'tp'), may hold values from -6 to 6
- norm1_gain: bfloat16 [1024], P('fsdp'), may hold values from 0.5 to 1.5
- norm2_gain: bfloat16 [1024], P('fsdp'), may hold values from 0.5 to 1.5
- w_query: bfloat16 [1024, 1024], P('fsdp', 'tp'), may hold values from -0.1875 to 0.1875
- w_key: bfloat16 [1024, 1024], P('fsdp', 'tp'), may hold values from -0.1875 to 0.1875
- w_value: bfloat16 [1024, 1024], P('fsdp', 'tp'), may hold values from -0.1875 to 0.1875
- w_out: bfloat16 [1024, 1024], P('tp', 'fsdp'), may hold values from -2 to 2
- w_gate: bfloat16 [1024, 2816], P('fsdp', 'tp'), may hold values from -0.1875 to 0.1875
- w_up: bfloat16 [1024, 2816], P('fsdp', 'tp'), may hold values from -0.1875 to 0.1875
- w_down: bfloat16 [2816, 1024], P('tp', 'fsdp'), may hold values from -0.109375 to 0.109375
- prefix: int32 [4], P('fsdp'), may hold values from 204 to 1024
- cotangent: bfloat16 [4, 2048, 1024], P('fsdp', 'ctx'), may hold values from -6 to 6
Outputs:
- block_out: bfloat16 [4, 2048, 1024], P('fsdp', 'ctx')
- token_grad: float32 [4, 2048, 1024], P('fsdp', 'ctx')
- first_values_grad: float32 [4, 2048, 1024], P('fsdp', 'ctx', 'tp')
- norm1_gain_grad: float32 [1024], P('fsdp')
- norm2_gain_grad: float32 [1024], P('fsdp')
- w_query_grad: float32 [1024, 1024], P('fsdp', 'tp')
- w_key_grad: float32 [1024, 1024], P('fsdp', 'tp')
- w_value_grad: float32 [1024, 1024], P('fsdp', 'tp')
- w_out_grad: float32 [1024, 1024], P('tp', 'fsdp')
- w_gate_grad: float32 [1024, 2816], P('fsdp', 'tp')
- w_up_grad: float32 [1024, 2816], P('fsdp', 'tp')
- w_down_grad: float32 [2816, 1024], P('tp', 'fsdp')
The draws below stay inside these ranges and needn't reach their ends.
All inputs are finite; a program needn't handle non-finite values.
Results may differ from the reference program's by a relative error of at most 0.023.
Values may be sent and summed in bfloat16 or wider, within the bound.
A program may use at most 128 MiB of HBM per device.

```python
import jax
import jax.numpy as jnp
from jax import lax

D = 1024
HEADS = 16
HEAD_DIM = 64
FF = 2816
LEN = 2048
SEQS = 4


def plant(values, key, smallest, top_value):
    shape = values.shape
    place = [jax.random.randint(jax.random.fold_in(key, axis), (), 0, shape[axis]) for axis in range(len(shape))]
    values = values.at[tuple(place)].set(smallest)
    longest = shape.index(max(shape))
    place[longest] = (place[longest] + 1) % shape[longest]
    return values.at[tuple(place)].set(top_value)


def block_levels(rng, extent, cuts, low, top_value):
    level, own = 1.0, jax.random.fold_in(rng, 6)
    for axis_at, blocks in cuts:
        draws = jnp.exp(jax.random.uniform(jax.random.fold_in(own, axis_at), (blocks,), jnp.float32, low / len(cuts), top_value / len(cuts)))
        level = level * jnp.repeat(draws, extent[axis_at] // blocks).reshape([-1 if axis == axis_at else 1 for axis in range(len(extent))])
    return level


def normal_values(key, extent, width, limit, split=(), held_as=jnp.bfloat16):
    gain = block_levels(key, extent, split, -0.22, 0.18) if split else 1.0
    drawn = jax.random.normal(key, extent, jnp.float32) * width * gain
    return jnp.minimum(jnp.maximum(drawn, -limit), limit).astype(held_as)


def setup_inputs(seed: int = 0) -> dict:
    keys = jax.random.split(jax.random.key(seed), 14)
    return {
        "tokens": normal_values(keys[0], (SEQS, LEN, D), 1.0, 6.0, ((0, 2), (1, 4))),
        "first_values": normal_values(keys[1], (SEQS, LEN, D), 1.0, 6.0, ((0, 2), (1, 4), (2, 4))),
        "norm1_gain": jnp.clip(1.0 + 0.1 * jax.random.normal(keys[2], (D,), jnp.float32), 0.5, 1.5).astype(jnp.bfloat16),
        "norm2_gain": jnp.clip(1.0 + 0.1 * jax.random.normal(keys[3], (D,), jnp.float32), 0.5, 1.5).astype(jnp.bfloat16),
        "w_query": normal_values(keys[4], (D, D), D ** -0.5, 0.1875, ((0, 2), (1, 4))),
        "w_key": normal_values(keys[5], (D, D), D ** -0.5, 0.1875, ((0, 2), (1, 4))),
        "w_value": normal_values(keys[6], (D, D), D ** -0.5, 0.1875, ((0, 2), (1, 4))),
        "w_out": normal_values(keys[7], (D, D), (max(D // 128, 2)) ** -0.5, 2.0, ((0, 4), (1, 2))),
        "w_gate": normal_values(keys[8], (D, FF), D ** -0.5, 0.1875, ((0, 2), (1, 4))),
        "w_up": normal_values(keys[9], (D, FF), D ** -0.5, 0.1875, ((0, 2), (1, 4))),
        "w_down": normal_values(keys[10], (FF, D), FF ** -0.5, 0.109375, ((0, 4), (1, 2))),
        "prefix": plant(jax.random.randint(keys[11], (SEQS,), LEN // 10, LEN // 2 + 1), jax.random.fold_in(keys[11], 1), LEN // 10, (LEN // 2 + 1) - 1).astype(jnp.int32),
        "cotangent": normal_values(keys[12], (SEQS, LEN, D), 1.0, 6.0, ((0, 2), (1, 4))),
    }


@jax.custom_vjp
def low(v):
    return lax.optimization_barrier(v.astype(jnp.bfloat16)).astype(jnp.float32)

@jax.custom_vjp
def low_back(v):
    return v

def low_keep(v):
    return (low(v), None)

def low_pass(kept, grad):
    return (grad,)

def back_keep(v):
    return (v, None)

def back_low(kept, grad):
    return (low(grad),)
low.defvjp(low_keep, low_pass)
low_back.defvjp(back_keep, back_low)
epsilon = 1e-06
rope_base = 10000.0
masked_score = -1e+30

def exact_dot(left_side, right_side):
    return jnp.dot(left_side, right_side, precision=lax.Precision.HIGHEST, preferred_element_type=jnp.float32)

def rms_scale(values, gain_vector):
    return values * lax.rsqrt(lax.optimization_barrier(jnp.mean(values * values, axis=-1, keepdims=True)) + epsilon) * gain_vector

def rope_tables(positions):
    half_dim = HEAD_DIM // 2
    frequency = rope_base ** (-jnp.arange(half_dim, dtype=jnp.float32) / half_dim)
    angles = positions.astype(jnp.float32)[:, None] * frequency[None, :]
    angles = jnp.concatenate([angles, angles], axis=1)
    return (jnp.cos(angles), jnp.sin(angles))

def rotate(values, cosine_table, sine_table):
    half_dim = values.shape[-1] // 2
    turned = jnp.concatenate([-values[..., half_dim:], values[..., :half_dim]], axis=-1)
    return values * cosine_table[:, None, :] + turned * sine_table[:, None, :]

def attend_rows(query_rows, key_rows, value_rows, block_start, limit_value):
    row_count = query_rows.shape[0]
    query_pos = block_start + jnp.arange(row_count, dtype=jnp.int32)
    key_pos = jnp.arange(key_rows.shape[0], dtype=jnp.int32)
    scores = jnp.einsum('qhd,khd->hqk', query_rows, key_rows, precision=lax.Precision.HIGHEST) * HEAD_DIM ** (-0.5)
    scores = low_back(scores)
    allowed = (key_pos[None, :] <= query_pos[:, None]) | (key_pos[None, :] < limit_value)
    scores = jnp.where(allowed[None], scores, masked_score)
    probs = jax.nn.softmax(scores, axis=-1)
    return jnp.einsum('hqk,khd->qhd', low(probs), value_rows, precision=lax.Precision.HIGHEST)

def attend_sequence(argument):
    query_seq, key_seq, value_seq, limit_value = argument
    block_rows = min(512, LEN)
    block_count = LEN // block_rows
    query_blocks = query_seq.reshape(block_count, block_rows, HEADS, HEAD_DIM)
    starts = jnp.arange(block_count, dtype=jnp.int32) * block_rows

    def one_block(pair_item):
        return attend_rows(pair_item[0], key_seq, value_seq, pair_item[1], limit_value)
    result = lax.map(jax.checkpoint(one_block), (query_blocks, starts))
    return result.reshape(LEN, HEADS, HEAD_DIM)

def block_forward(tokens, first_values, norm1_gain, norm2_gain, w_query, w_key, w_value, w_out, w_gate, w_up, w_down, prefix):
    seq_count = tokens.shape[0]
    cosine_table, sine_table = rope_tables(jnp.arange(LEN, dtype=jnp.int32))
    shape_four = (seq_count, LEN, HEADS, HEAD_DIM)
    normed_one = low(rms_scale(tokens, norm1_gain))
    queries = low(rotate(low_back(exact_dot(normed_one, w_query)).reshape(shape_four), cosine_table, sine_table))
    key_rows = low(rotate(low_back(exact_dot(normed_one, w_key)).reshape(shape_four), cosine_table, sine_table))
    values = low(0.5 * low_back(exact_dot(normed_one, w_value)) + 0.5 * first_values).reshape(shape_four)
    context = lax.map(attend_sequence, (queries, key_rows, values, prefix))
    context = low(low_back(context)).reshape(seq_count, LEN, D)
    hidden_state = tokens + low_back(exact_dot(context, w_out))
    normed_two = low(rms_scale(hidden_state, norm2_gain))
    gate_value = low_back(exact_dot(normed_two, w_gate))
    up_value = low_back(exact_dot(normed_two, w_up))
    inner_low = low(jax.nn.silu(gate_value) * up_value)
    return hidden_state + low_back(exact_dot(inner_low, w_down))

def reference(tokens, first_values, norm1_gain, norm2_gain, w_query, w_key, w_value, w_out, w_gate, w_up, w_down, prefix, cotangent):
    floats = tuple((argument.astype(jnp.float32) for argument in (tokens, first_values, norm1_gain, norm2_gain, w_query, w_key, w_value, w_out, w_gate, w_up, w_down)))

    def forward(*pieces):
        return block_forward(*pieces, prefix)
    block_out, pullback = jax.vjp(forward, *floats)
    grads = pullback(cotangent.astype(jnp.float32))
    return (block_out.astype(jnp.bfloat16), grads[0], grads[1], grads[2], grads[3], grads[4], grads[5], grads[6], grads[7], grads[8], grads[9], grads[10])
```

```python
import functools

import jax
import jax.numpy as jnp
from jax import lax
from jax.experimental import pallas as pl
from jax.experimental.pallas import tpu as pltpu
from jax.sharding import PartitionSpec as P

HEAD_DIM = 64
epsilon = 1e-06
rope_base = 10000.0
masked_score = -1e30
MESH = pl.DeviceIdType.MESH
bf16 = jnp.bfloat16
f32 = jnp.float32


def dot(a, b):
    return jnp.dot(a, b, preferred_element_type=f32)


def dot_nt(a, b):
    return lax.dot_general(a, b, (((1,), (1,)), ((), ())), preferred_element_type=f32)


def unit_norm(values):
    return values * lax.rsqrt(jnp.mean(values * values, axis=-1, keepdims=True) + epsilon)


def low_half(shape):
    return lax.rem(lax.broadcasted_iota(jnp.int32, shape, 1), HEAD_DIM) < HEAD_DIM // 2


def turned(values):
    pieces = []
    half = HEAD_DIM // 2
    for at in range(0, values.shape[1], 128):
        piece = values[:, at : at + 128]
        up = pltpu.roll(piece, 128 - half, 1)
        down = pltpu.roll(piece, half, 1)
        pieces.append(jnp.where(low_half(piece.shape), up, down))
    return jnp.concatenate(pieces, axis=1)


class Sum:
    def __init__(self, place, part, inward, across, result, sems):
        self.pair = place + 1 - 2 * lax.rem(place, 2)
        self.middle = 3 - place
        self.inner = (place == 1) | (place == 2)
        self.outer = (place == 0) | (place == 3)
        self.part, self.inward, self.across, self.result = part, inward, across, result
        self.send_one, self.recv_one, self.send_two, self.recv_two = sems

    def copy_in(self, i):
        return pltpu.make_async_remote_copy(
            src_ref=self.part.at[i], dst_ref=self.inward.at[i], send_sem=self.send_one.at[i],
            recv_sem=self.recv_one.at[i], device_id={"tp": self.pair}, device_id_type=MESH)

    def copy_across(self, i):
        return pltpu.make_async_remote_copy(
            src_ref=self.part.at[i], dst_ref=self.across.at[i], send_sem=self.send_two.at[i],
            recv_sem=self.recv_two.at[i], device_id={"tp": self.middle}, device_id_type=MESH)

    def copy_out(self, i):
        return pltpu.make_async_remote_copy(
            src_ref=self.result.at[i], dst_ref=self.result.at[i], send_sem=self.send_one.at[i],
            recv_sem=self.recv_one.at[i], device_id={"tp": self.pair}, device_id_type=MESH)

    def offer(self, i):
        @pl.when(self.outer)
        def _():
            self.copy_in(i).start()

    def take_in(self, i):
        self.copy_in(i).wait_recv()
        self.part[i] = (self.part[i].astype(f32) + self.inward[i].astype(f32)).astype(bf16)
        self.copy_across(i).start()

    def finish(self, i):
        self.copy_across(i).wait_recv()
        self.result[i] = (self.part[i].astype(f32) + self.across[i].astype(f32)).astype(bf16)
        self.copy_out(i).start()

    def step(self, i, done):
        @pl.when(self.inner)
        def _():
            self.take_in(i)

            @pl.when(i > 0)
            def _():
                self.finish(i - 1)
                done(i - 1)

    def close(self, count, done):
        @pl.when(self.inner)
        def _():
            self.finish(count - 1)
            done(count - 1)

            @pl.loop(0, count)
            def _(i):
                self.copy_across(i).wait_send()
                self.copy_out(i).wait_send()

        @pl.when(self.outer)
        def _():
            @pl.loop(0, count)
            def _(i):
                self.copy_out(i).wait_recv()
                done(i)

            @pl.loop(0, count)
            def _(i):
                self.copy_in(i).wait_send()


def greet(place, ring):
    barrier = pltpu.get_barrier_semaphore()
    peers = (
        {"tp": place + 1 - 2 * lax.rem(place, 2)},
        {"tp": 3 - place},
        {"ctx": ring + 1 - 2 * lax.rem(ring, 2)},
        {"ctx": lax.rem(ring + 2, 4)},
    )
    for peer in peers:
        pl.semaphore_signal(barrier, inc=1, device_id=peer, device_id_type=MESH)
    pl.semaphore_wait(barrier, len(peers))


def attend_kernel(
    tok, fv, g1, wq, wk, wv, wo, cosine, sine, prefix,
    sum_hbm, q_out, kv_hbm, ctx_out, lse_out,
    kv, qtm, vt, acct, maxes, totals, part, inward, across, result,
    kv_send, kv_recv, kv_save, send_one, recv_one, send_two, recv_two, save,
):
    place, ring = lax.axis_index("tp"), lax.axis_index("ctx")
    seqs, rows, width = q_out.shape
    heads = width // HEAD_DIM
    tile = 256
    per_seq = part.shape[0] // seqs
    chunk = part.shape[1]
    mate = {"ctx": ring + 1 - 2 * lax.rem(ring, 2)}
    peer = {"ctx": lax.rem(ring + 2, 4)}
    blocks = (ring, ring + 1 - 2 * lax.rem(ring, 2), lax.rem(ring + 2, 4), 3 - ring)
    greet(place, ring)

    def pass_block(s, source, target, device, slot):
        return pltpu.make_async_remote_copy(
            src_ref=kv.at[s, source], dst_ref=kv.at[s, target], send_sem=kv_send.at[s, slot],
            recv_sem=kv_recv.at[s, target], device_id=device, device_id_type=MESH)

    to_mate = lambda s: pass_block(s, 0, 1, mate, 0)
    to_peer = lambda s: pass_block(s, 0, 2, peer, 1)
    onward = lambda s: pass_block(s, 2, 3, mate, 2)

    for s in range(seqs):
        @pl.loop(0, rows // tile)
        def _(t):
            at = pl.ds(pl.multiple_of(t * tile, tile), tile)
            normed = (unit_norm(tok[s, at, :].astype(f32)) * g1[...].astype(f32)).astype(bf16)
            co, si = cosine[at, :], sine[at, :]
            q = dot(normed, wq[...])
            q = (q * co + turned(q) * si) * HEAD_DIM ** (-0.5)
            q_out[s, at, :] = q.astype(bf16)
            qt = jnp.transpose(q)
            owner = lax.broadcasted_iota(jnp.int32, qt.shape, 0) // HEAD_DIM
            for h in range(heads):
                qtm[s, h, :, at] = jnp.where(owner == h, qt, 0.0).astype(bf16)
            k = dot(normed, wk[...])
            kv[s, 0, 0, at, :] = (k * co + turned(k) * si).astype(bf16)
            v = dot(normed, wv[...])
            kv[s, 0, 1, at, :] = (0.5 * v + 0.5 * fv[s, at, :].astype(f32)).astype(bf16)

        to_peer(s).start()
        to_mate(s).start()

    def attend_block(s, j, block, steps=None):
        vt[...] = jnp.transpose(kv[s, j, 1])
        key_pos = block * rows + lax.broadcasted_iota(jnp.int32, (rows, 1), 0)
        query_pos = ring * rows + lax.broadcasted_iota(jnp.int32, (1, rows), 1)
        seen = key_pos < jnp.maximum(query_pos + 1, prefix[s])

        @pl.loop(0, heads)
        def _(h):
            of_head = pl.ds(pl.multiple_of(h * HEAD_DIM, HEAD_DIM), HEAD_DIM)
            scores = jnp.where(seen, dot(kv[s, j, 0], qtm[s, h]), masked_score)
            old = maxes[h]
            new = jnp.maximum(old, jnp.max(scores, axis=0, keepdims=True))
            weights = jnp.exp(scores - new)
            fade = jnp.exp(old - new)
            maxes[h] = new
            totals[h] = totals[h] * fade + jnp.sum(weights, axis=0, keepdims=True)
            acct[of_head, :] = acct[of_head, :] * fade + dot(vt[of_head, :], weights.astype(bf16))
            if steps is not None:
                @pl.when(lax.rem(h, 2) == 1)
                def _():
                    sums.step(steps + h // 2, done)

    def saving(i):
        return pltpu.make_async_copy(result.at[i], sum_hbm.at[i], save.at[i])

    done = lambda i: saving(i).start()
    sums = Sum(place, part, inward, across, result, (send_one, recv_one, send_two, recv_two))

    for s in range(seqs):
        maxes[...] = jnp.full_like(maxes, masked_score)
        totals[...] = jnp.zeros_like(totals)
        acct[...] = jnp.zeros_like(acct)
        attend_block(s, 0, blocks[0], None if s == 0 else (s - 1) * per_seq + 0)
        to_mate(s).wait_recv()
        attend_block(s, 1, blocks[1], None if s == 0 else (s - 1) * per_seq + 2)
        to_peer(s).wait_recv()
        onward(s).start()
        attend_block(s, 2, blocks[2], None if s == 0 else (s - 1) * per_seq + 4)
        onward(s).wait_recv()
        attend_block(s, 3, blocks[3], None if s == 0 else (s - 1) * per_seq + 6)
        pltpu.make_async_copy(kv.at[s], kv_hbm.at[s], kv_save.at[s]).start()
        for h in range(heads):
            lse_out[s, h : h + 1, :] = maxes[h] + jnp.log(totals[h])
            of_head = slice(h * HEAD_DIM, (h + 1) * HEAD_DIM)
            acct[of_head, :] = acct[of_head, :] / totals[h]
        ctx_out[s] = jnp.transpose(acct[...]).astype(bf16)

        @pl.loop(0, per_seq)
        def _(i):
            at = pl.ds(pl.multiple_of(i * chunk, chunk), chunk)
            part[s * per_seq + i] = dot(ctx_out[s, at, :], wo[...]).astype(bf16)
            sums.offer(s * per_seq + i)

    @pl.loop((seqs - 1) * per_seq, seqs * per_seq)
    def _(i):
        sums.step(i, done)

    sums.close(seqs * per_seq, done)
    for s in range(seqs):
        to_mate(s).wait_send()
        to_peer(s).wait_send()
        onward(s).wait_send()
        pltpu.make_async_copy(kv.at[s], kv_hbm.at[s], kv_save.at[s]).wait()

    @pl.loop(0, seqs * per_seq)
    def _(i):
        saving(i).wait()


def attend(tok, fv, g1, wq, wk, wv, wo, cosine, sine, prefix):
    seqs, rows, dim = tok.shape
    width = wq.shape[1]
    heads = width // HEAD_DIM
    chunk = 64
    count = seqs * rows // chunk
    vmem = pl.BlockSpec(memory_space=pltpu.VMEM)
    anyw = pl.BlockSpec(memory_space=pl.ANY)
    dma = pltpu.SemaphoreType.DMA
    lines = pltpu.VMEM((count, chunk, dim), bf16)
    return pl.pallas_call(
        attend_kernel,
        name="attend",
        out_shape=(
            jax.ShapeDtypeStruct((count, chunk, dim), bf16),
            jax.ShapeDtypeStruct((seqs, rows, width), bf16),
            jax.ShapeDtypeStruct((seqs, 4, 2, rows, width), bf16),
            jax.ShapeDtypeStruct((seqs, rows, width), bf16),
            jax.ShapeDtypeStruct((seqs, heads, rows), f32),
        ),
        in_specs=[vmem] * 9 + [pl.BlockSpec(memory_space=pltpu.SMEM)],
        out_specs=(anyw, vmem, anyw, vmem, vmem),
        scratch_shapes=[
            pltpu.VMEM((seqs, 4, 2, rows, width), bf16),
            pltpu.VMEM((seqs, heads, width, rows), bf16),
            pltpu.VMEM((width, rows), bf16),
            pltpu.VMEM((width, rows), f32),
            pltpu.VMEM((heads, 1, rows), f32),
            pltpu.VMEM((heads, 1, rows), f32),
            lines, lines, lines, lines,
            dma((seqs, 3)), dma((seqs, 4)), dma((seqs,)),
            dma((count,)), dma((count,)), dma((count,)), dma((count,)), dma((count,)),
        ],
        compiler_params=pltpu.CompilerParams(
            collective_id=0, has_side_effects=True, vmem_limit_bytes=60 * 1024 * 1024),
        cost_estimate=pl.CostEstimate(flops=8 * 10**9, bytes_accessed=10**7, transcendentals=10**7),
    )(tok, fv, g1, wq, wk, wv, wo, cosine, sine, prefix)


def forward_ffn(normed, w_gate, w_up):
    gate = dot(normed, w_gate)
    up = dot(normed, w_up)
    return gate, up, jax.nn.sigmoid(gate)


def feed_kernel(
    tok, attn, cot, g2, wg, wu, wd,
    mixed_hbm, late_hbm, dwg, dwu, dwd,
    normed_t, inner_t, inner_s, gg, ug, late, part, inward, across, result,
    send_one, recv_one, send_two, recv_two, save, late_save,
):
    place, ring = lax.axis_index("tp"), lax.axis_index("ctx")
    seqs, rows, dim = tok.shape
    chunk = part.shape[1]
    tile = 256
    tiles = seqs * rows // tile
    early = tiles // 2
    per_tile = tile // chunk
    per_seq_tiles = rows // tile
    count = part.shape[0]
    greet(place, ring)
    sums = Sum(place, part, inward, across, result, (send_one, recv_one, send_two, recv_two))

    def saving(i):
        return pltpu.make_async_copy(result.at[i], mixed_hbm.at[i], save.at[i])

    done = lambda i: saving(i).start()

    def saving_late(t):
        return pltpu.make_async_copy(late.at[t], late_hbm.at[t], late_save.at[t])

    @pl.loop(0, tiles)
    def _(t):
        s, at = t // per_seq_tiles, pl.ds(pl.multiple_of(lax.rem(t, per_seq_tiles) * tile, tile), tile)
        flat = pl.ds(pl.multiple_of(t * tile, tile), tile)
        lanes = pl.ds(pl.multiple_of(t * tile, tile), tile)
        step_base = (t - 1) * per_tile

        def step(k):
            @pl.when(t > 0)
            def _():
                sums.step(step_base + k, done)

        hidden = tok[s, at, :].astype(f32) + attn[s, at, :].astype(f32)
        normed_wide = unit_norm(hidden) * g2[...].astype(f32)
        normed = normed_wide.astype(bf16)
        normed_t[:, lanes] = jnp.transpose(normed)
        gate, up, sigmoid = forward_ffn(normed, wg[...], wu[...])
        swish = gate * sigmoid
        inner = (swish * up).astype(bf16)
        inner_s[...] = inner
        inner_t[:, lanes] = jnp.transpose(inner)
        inner_grad = dot_nt(cot[s, at, :], wd[...])
        gg[flat, :] = (inner_grad * up * sigmoid * (1.0 + gate * (1.0 - sigmoid))).astype(bf16)
        ug[flat, :] = (inner_grad * swish).astype(bf16)
        step(0)

        @pl.loop(0, per_tile)
        def _(k):
            own = pl.ds(pl.multiple_of(t * tile + k * chunk, chunk), chunk)
            i = jnp.where(t < early, 2 * per_tile * t, per_tile * (early + t)) + k
            part[i] = (dot_nt(gg[own, :], wg[...]) + dot_nt(ug[own, :], wu[...])).astype(bf16)
            sums.offer(i)

        step(1)

        @pl.when(t < early)
        def _():
            @pl.loop(0, per_tile)
            def _(k):
                i = 2 * per_tile * t + per_tile + k
                own = pl.ds(pl.multiple_of(k * chunk, chunk), chunk)
                part[i] = dot(inner_s[own, :], wd[...]).astype(bf16)
                sums.offer(i)

        @pl.when(t >= early)
        def _():
            @pl.loop(0, per_tile)
            def _(k):
                own = pl.ds(pl.multiple_of(k * chunk, chunk), chunk)
                late[t - early, own, :] = dot(inner_s[own, :], wd[...]).astype(bf16)

            saving_late(t - early).start()

        step(2)
        step(3)

    begun = (tiles - 1) * per_tile

    @pl.loop(0, count - begun)
    def _(k):
        @pl.when(k < 4)
        def _():
            own = pl.ds(pl.multiple_of(k * tile, tile), tile)
            dwg[own, :] = dot(normed_t[own, :], gg[...]).astype(bf16)

        @pl.when((k >= 4) & (k < 8))
        def _():
            own = pl.ds(pl.multiple_of((k - 4) * tile, tile), tile)
            dwu[own, :] = dot(normed_t[own, :], ug[...]).astype(bf16)

        @pl.when(k >= 8)
        def _():
            share = inner_t.shape[0] // 4
            own = pl.ds(pl.multiple_of((k - 8) * share, 16), share)
            total = jnp.zeros((share, dim), f32)
            for s in range(seqs):
                total = total + dot(inner_t[own, s * rows : (s + 1) * rows], cot[s])
            dwd[own, :] = total.astype(bf16)

        sums.step(begun + k, done)

    sums.close(count, done)

    for t in range(tiles - early):
        saving_late(t).wait()

    @pl.loop(0, count)
    def _(i):
        saving(i).wait()


def feed(tok, attn, cot, g2, wg, wu, wd):
    seqs, rows, dim = tok.shape
    units = wg.shape[1]
    chunk = 64
    tokens = seqs * rows
    count = tokens // chunk * 3 // 2
    vmem = pl.BlockSpec(memory_space=pltpu.VMEM)
    anyw = pl.BlockSpec(memory_space=pl.ANY)
    dma = pltpu.SemaphoreType.DMA
    lines = pltpu.VMEM((count, chunk, dim), bf16)
    tile = 256
    late = tokens // tile // 2
    return pl.pallas_call(
        feed_kernel,
        name="feed",
        out_shape=(
            jax.ShapeDtypeStruct((count, chunk, dim), bf16),
            jax.ShapeDtypeStruct((late, tile, dim), bf16),
            jax.ShapeDtypeStruct((dim, units), bf16),
            jax.ShapeDtypeStruct((dim, units), bf16),
            jax.ShapeDtypeStruct((units, dim), bf16),
        ),
        in_specs=[vmem] * 7,
        out_specs=(anyw, anyw, vmem, vmem, vmem),
        scratch_shapes=[
            pltpu.VMEM((dim, tokens), bf16),
            pltpu.VMEM((units, tokens), bf16),
            pltpu.VMEM((tile, units), bf16),
            pltpu.VMEM((tokens, units), bf16),
            pltpu.VMEM((tokens, units), bf16),
            pltpu.VMEM((late, tile, dim), bf16),
            lines, lines, lines, lines,
            dma((count,)), dma((count,)), dma((count,)), dma((count,)), dma((count,)), dma((late,)),
        ],
        compiler_params=pltpu.CompilerParams(
            collective_id=1, has_side_effects=True, vmem_limit_bytes=60 * 1024 * 1024),
        cost_estimate=pl.CostEstimate(flops=14 * 10**9, bytes_accessed=10**7, transcendentals=10**6),
    )(tok, attn, cot, g2, wg, wu, wd)


def back_kernel(
    tok, attn, cot, mixed, late, g1, g2, wq, wk, wv, wo, q, kv, ctx, lse, cosine, sine, prefix,
    block_hbm, token_hbm, fv_grad, dwq, dwk, dwv, dwo, gains,
    hid, branch, qtm, qm, otm, om, kt, delta, dqt, dk, dv, give, take, proj, normed_t,
    block, part, inward, across, result,
    kv_send, kv_recv, send_one, recv_one, send_two, recv_two, save,
):
    place, ring = lax.axis_index("tp"), lax.axis_index("ctx")
    seqs, rows, dim = tok.shape
    width = wq.shape[1]
    heads = width // HEAD_DIM
    count, chunk = part.shape[0], part.shape[1]
    per_seq = rows // chunk
    mate = {"ctx": ring + 1 - 2 * lax.rem(ring, 2)}
    peer = {"ctx": lax.rem(ring + 2, 4)}
    blocks = (ring, ring + 1 - 2 * lax.rem(ring, 2), lax.rem(ring + 2, 4), 3 - ring)
    greet(place, ring)
    sums = Sum(place, part, inward, across, result, (send_one, recv_one, send_two, recv_two))
    gain_one, gain_two = g1[...].astype(f32), g2[...].astype(f32)
    gains[...] = jnp.zeros_like(gains)

    late_per = late.shape[1] // chunk

    @pl.loop(0, per_seq)
    def _(i):
        own = pl.ds(pl.multiple_of(lax.rem(i, late_per) * chunk, chunk), chunk)
        part[i] = late[i // late_per, own, :]
        sums.offer(i)

    def hidden_at(s, at):
        return tok[s, at, :].astype(f32) + attn[s, at, :].astype(f32)

    def saving_block(i):
        s, own = i // per_seq, pl.ds(pl.multiple_of(lax.rem(i, per_seq) * chunk, chunk), chunk)
        return pltpu.make_async_copy(block.at[i], block_hbm.at[s, own], save.at[i])

    def saving_token(i):
        s, own = i // per_seq, pl.ds(pl.multiple_of(lax.rem(i, per_seq) * chunk, chunk), chunk)
        return pltpu.make_async_copy(hid.at[s, own], token_hbm.at[s, own], save.at[seqs * per_seq + i])

    def done(i):
        @pl.when(i < per_seq)
        def _():
            own = pl.ds(pl.multiple_of(i * chunk, chunk), chunk)
            block[per_seq + i] = (hidden_at(1, own) + result[i].astype(f32)).astype(bf16)
            saving_block(per_seq + i).start()

        @pl.when(i >= per_seq)
        def _():
            n = i - per_seq
            s, own = n // per_seq, pl.ds(pl.multiple_of(lax.rem(n, per_seq) * chunk, chunk), chunk)
            values, upstream = tok[s, own, :].astype(f32), result[i].astype(f32)
            factor = lax.rsqrt(jnp.mean(values * values, axis=-1, keepdims=True) + epsilon)
            scaled = upstream * gain_one
            gains[0:1, :] += jnp.sum(upstream * values * factor, axis=0, keepdims=True)
            hid[s, own, :] += factor * scaled - values * factor**3 * jnp.mean(
                scaled * values, axis=-1, keepdims=True)
            saving_token(n).start()

    def move(s, source, target, device):
        return pltpu.make_async_remote_copy(
            src_ref=give.at[s, source], dst_ref=take.at[s, target], send_sem=kv_send.at[s, source],
            recv_sem=kv_recv.at[s, target], device_id=device, device_id_type=MESH)

    far_to_mate = lambda s: move(s, 2, 0, mate)
    peer_back = lambda s: move(s, 1, 1, peer)
    near_to_mate = lambda s: move(s, 0, 2, mate)
    tile = 256

    for s in range(seqs):
        @pl.loop(0, rows // tile)
        def _(t):
            at = pl.ds(pl.multiple_of(t * tile, tile), tile)
            values = hidden_at(s, at)
            picks = []
            for k in range(tile // chunk):
                n = (s * (rows // tile) + t)
                early = seqs * rows // tile // 2
                per_tile = tile // chunk
                picks.append(mixed[jnp.where(n < early, 2 * per_tile * n, per_tile * (early + n)) + k])
            upstream = jnp.concatenate(picks, axis=0).astype(f32)
            factor = lax.rsqrt(jnp.mean(values * values, axis=-1, keepdims=True) + epsilon)
            scaled = upstream * gain_two
            gains[1:2, :] += jnp.sum(upstream * values * factor, axis=0, keepdims=True)
            hid_now = cot[s, at, :].astype(f32) + factor * scaled - values * factor**3 * jnp.mean(
                scaled * values, axis=-1, keepdims=True)
            hid[s, at, :] = hid_now
            low = hid_now.astype(bf16)
            branch[s, at, :] = low
            grad = dot_nt(low, wo[...])
            lane_owner = lax.broadcasted_iota(jnp.int32, grad.shape, 1) // HEAD_DIM
            q_now = q[s, at, :]
            grad_t = dot_nt(wo[...], low)
            row_owner = lax.broadcasted_iota(jnp.int32, grad_t.shape, 0) // HEAD_DIM
            q_t = jnp.transpose(q_now.astype(f32))
            ctx_t = jnp.transpose(ctx[s, at, :].astype(f32))
            product = grad_t.astype(bf16).astype(f32) * ctx_t
            for h in range(heads):
                om[h, at, :] = jnp.where(lane_owner == h, grad, 0.0).astype(bf16)
                qm[h, at, :] = jnp.where(lane_owner == h, q_now.astype(f32), 0.0).astype(bf16)
                otm[h, :, at] = jnp.where(row_owner == h, grad_t, 0.0).astype(bf16)
                qtm[h, :, at] = jnp.where(row_owner == h, q_t, 0.0).astype(bf16)
                delta[h, :, at] = jnp.sum(
                    product[h * HEAD_DIM : (h + 1) * HEAD_DIM], axis=0, keepdims=True)
            normed = (unit_norm(tok[s, at, :].astype(f32)) * gain_one).astype(bf16)
            flat = pl.ds(pl.multiple_of(s * rows + t * tile, tile), tile)
            normed_t[:, flat] = jnp.transpose(normed)

        dqt[...] = jnp.zeros_like(dqt)

        def back_block(j, block_at, steps):
            kt[...] = jnp.transpose(kv[s, j, 0])
            key_pos = block_at * rows + lax.broadcasted_iota(jnp.int32, (rows, 1), 0)
            query_pos = ring * rows + lax.broadcasted_iota(jnp.int32, (1, rows), 1)
            seen = key_pos < jnp.maximum(query_pos + 1, prefix[s])
            dk[...] = jnp.zeros_like(dk)
            dv[...] = jnp.zeros_like(dv)

            @pl.loop(0, heads)
            def _(h):
                of_head = pl.ds(pl.multiple_of(h * HEAD_DIM, HEAD_DIM), HEAD_DIM)
                scores = dot(kv[s, j, 0], qtm[h])
                probs = jnp.where(seen, jnp.exp(scores - lse[s, pl.ds(h, 1), :]), 0.0)
                dprobs = dot(kv[s, j, 1], otm[h])
                dv[...] += dot(probs.astype(bf16), om[h])
                dscores = (probs * (dprobs - delta[h])).astype(bf16)
                dk[...] += dot(dscores, qm[h])
                dqt[of_head, :] += dot(kt[of_head, :], dscores)

                @pl.when(lax.rem(h, 2) == 1)
                def _():
                    sums.step(steps + h // 2, done)

        base = s * per_seq
        back_block(3, blocks[3], base)
        give[s, 2, 0] = dk[...].astype(bf16)
        give[s, 2, 1] = dv[...].astype(bf16)
        far_to_mate(s).start()
        back_block(2, blocks[2], base + 2)
        far_to_mate(s).wait_recv()
        give[s, 1, 0] = (dk[...] + take[s, 0, 0].astype(f32)).astype(bf16)
        give[s, 1, 1] = (dv[...] + take[s, 0, 1].astype(f32)).astype(bf16)
        peer_back(s).start()
        back_block(1, blocks[1], base + 4)
        give[s, 0, 0] = dk[...].astype(bf16)
        give[s, 0, 1] = dv[...].astype(bf16)
        near_to_mate(s).start()
        back_block(0, blocks[0], base + 6)
        near_to_mate(s).wait_recv()
        peer_back(s).wait_recv()

        @pl.loop(0, rows // tile)
        def _(t):
            at = pl.ds(pl.multiple_of(t * tile, tile), tile)
            flat = pl.ds(pl.multiple_of(s * rows + t * tile, tile), tile)
            co, si = cosine[at, :], sine[at, :]
            grad_v = 0.5 * (dv[at, :] + take[s, 2, 1, at, :].astype(f32) + take[s, 1, 1, at, :].astype(f32))
            fv_grad[s, at, :] = grad_v
            grad_k = dk[at, :] + take[s, 2, 0, at, :].astype(f32) + take[s, 1, 0, at, :].astype(f32)
            grad_q = jnp.transpose(dqt[:, at]) * HEAD_DIM ** (-0.5)
            proj[0, flat, :] = (grad_q * co - turned(grad_q) * si).astype(bf16)
            proj[1, flat, :] = (grad_k * co - turned(grad_k) * si).astype(bf16)
            proj[2, flat, :] = grad_v.astype(bf16)

        @pl.loop(0, per_seq)
        def _(k):
            own = pl.ds(pl.multiple_of(s * rows + k * chunk, chunk), chunk)
            i = per_seq * (s + 1) + k
            part[i] = (
                dot_nt(proj[0, own, :], wq[...]) + dot_nt(proj[1, own, :], wk[...])
                + dot_nt(proj[2, own, :], wv[...])).astype(bf16)
            sums.offer(i)

    @pl.loop(0, 4)
    def _(k):
        own = pl.ds(pl.multiple_of(k * tile, tile), tile)
        dwq[own, :] = dot(normed_t[own, :], proj[0]).astype(bf16)
        dwk[own, :] = dot(normed_t[own, :], proj[1]).astype(bf16)
        dwv[own, :] = dot(normed_t[own, :], proj[2]).astype(bf16)
        sums.step(2 * per_seq + k, done)

    total = jnp.zeros(dwo.shape, f32)
    for s in range(seqs):
        total = total + dot(jnp.transpose(ctx[s]), branch[s])
    dwo[...] = total.astype(bf16)

    @pl.loop(0, per_seq)
    def _(i):
        own = pl.ds(pl.multiple_of(i * chunk, chunk), chunk)
        per_tile = tile // chunk
        at = 2 * per_tile * (i // per_tile) + per_tile + lax.rem(i, per_tile)
        block[i] = (hidden_at(0, own) + mixed[at].astype(f32)).astype(bf16)
        saving_block(i).start()

    @pl.loop(2 * per_seq + 4, count)
    def _(i):
        sums.step(i, done)

    sums.close(count, done)
    for s in range(seqs):
        far_to_mate(s).wait_send()
        peer_back(s).wait_send()
        near_to_mate(s).wait_send()

    @pl.loop(0, seqs * per_seq)
    def _(i):
        saving_block(i).wait()
        saving_token(i).wait()


def back(tok, attn, cot, mixed, late, g1, g2, wq, wk, wv, wo, q, kv, ctx, lse, cosine, sine, prefix):
    seqs, rows, dim = tok.shape
    width = wq.shape[1]
    heads = width // HEAD_DIM
    count, chunk, _ = mixed.shape
    tokens = seqs * rows
    vmem = pl.BlockSpec(memory_space=pltpu.VMEM)
    anyw = pl.BlockSpec(memory_space=pl.ANY)
    dma = pltpu.SemaphoreType.DMA
    lines = pltpu.VMEM((count, chunk, dim), bf16)
    wide = pltpu.VMEM((heads, rows, width), bf16)
    tall = pltpu.VMEM((heads, width, rows), bf16)
    return pl.pallas_call(
        back_kernel,
        name="back",
        out_shape=(
            jax.ShapeDtypeStruct((seqs, rows, dim), bf16),
            jax.ShapeDtypeStruct((seqs, rows, dim), f32),
            jax.ShapeDtypeStruct((seqs, rows, width), f32),
            jax.ShapeDtypeStruct((dim, width), bf16),
            jax.ShapeDtypeStruct((dim, width), bf16),
            jax.ShapeDtypeStruct((dim, width), bf16),
            jax.ShapeDtypeStruct((width, dim), bf16),
            jax.ShapeDtypeStruct((2, dim), f32),
        ),
        in_specs=[vmem] * 17 + [pl.BlockSpec(memory_space=pltpu.SMEM)],
        out_specs=(anyw, anyw) + (vmem,) * 6,
        scratch_shapes=[
            pltpu.VMEM((seqs, rows, dim), f32),
            pltpu.VMEM((seqs, rows, dim), bf16),
            tall, wide, tall, wide,
            pltpu.VMEM((width, rows), bf16),
            pltpu.VMEM((heads, 1, rows), f32),
            pltpu.VMEM((width, rows), f32),
            pltpu.VMEM((rows, width), f32),
            pltpu.VMEM((rows, width), f32),
            pltpu.VMEM((seqs, 3, 2, rows, width), bf16),
            pltpu.VMEM((seqs, 3, 2, rows, width), bf16),
            pltpu.VMEM((3, tokens, width), bf16),
            pltpu.VMEM((dim, tokens), bf16),
            pltpu.VMEM((tokens // chunk, chunk, dim), bf16),
            lines, lines, lines, lines,
            dma((seqs, 3)), dma((seqs, 3)),
            dma((count,)), dma((count,)), dma((count,)), dma((count,)), dma((2 * tokens // chunk,)),
        ],
        compiler_params=pltpu.CompilerParams(
            collective_id=2, has_side_effects=True, vmem_limit_bytes=62 * 1024 * 1024),
        cost_estimate=pl.CostEstimate(flops=30 * 10**9, bytes_accessed=10**7, transcendentals=10**7),
    )(tok, attn, cot, mixed, late, g1, g2, wq, wk, wv, wo, q, kv, ctx, lse, cosine, sine, prefix)


def passed_along(block, axis, distance):
    devices = range(lax.axis_size(axis))
    route = [((i - distance) % len(devices), i) for i in devices]
    return lax.ppermute(block, axis, route)


def rms_scale(values, gain_vector):
    return (
        values
        * lax.rsqrt(jnp.mean(values * values, axis=-1, keepdims=True) + epsilon)
        * gain_vector
    )


def rms_back(values, gain_vector, upstream):
    factor = lax.rsqrt(jnp.mean(values * values, axis=-1, keepdims=True) + epsilon)
    scaled = upstream * gain_vector
    input_grad = factor * scaled - values * factor**3 * jnp.mean(
        scaled * values, axis=-1, keepdims=True
    )
    gain_grad = jnp.sum(upstream * values * factor, axis=(0, 1))
    return (input_grad, gain_grad)


def rope_tables(positions):
    half_dim = HEAD_DIM // 2
    frequency = rope_base ** (-jnp.arange(half_dim, dtype=jnp.float32) / half_dim)
    angles = positions.astype(jnp.float32)[:, None] * frequency[None, :]
    angles = jnp.concatenate([angles, angles], axis=1)
    return (jnp.cos(angles), jnp.sin(angles))


def rotate(values, cosine_table, sine_table):
    half_dim = values.shape[-1] // 2
    turned = jnp.concatenate([-values[..., half_dim:], values[..., :half_dim]], axis=-1)
    return values * cosine_table[:, None, :] + turned * sine_table[:, None, :]


def rotate_back(values, cosine_table, sine_table):
    half_dim = values.shape[-1] // 2
    scaled = values * sine_table[:, None, :]
    turned = jnp.concatenate([scaled[..., half_dim:], -scaled[..., :half_dim]], axis=-1)
    return values * cosine_table[:, None, :] + turned


def contract(left_side, right_side):
    return jnp.einsum("sra,srb->ab", left_side, right_side, preferred_element_type=jnp.float32)


def score_block(query_low, key_low, query_pos, key_pos, limits):
    scores = jnp.einsum(
        "sqhd,skhd->shqk", query_low, key_low, preferred_element_type=jnp.float32
    ) * HEAD_DIM ** (-0.5)
    allowed = (key_pos[None, None, :] <= query_pos[None, :, None]) | (
        key_pos[None, None, :] < limits[:, None, None]
    )
    return (scores, allowed[:, None])


def shards(
    tokens,
    first_values,
    norm1_gain,
    norm2_gain,
    w_query,
    w_key,
    w_value,
    w_out,
    w_gate,
    w_up,
    w_down,
    prefix,
    cotangent,
):
    gathered = (
        lax.all_gather(norm1_gain, "fsdp", axis=0, tiled=True),
        lax.all_gather(norm2_gain, "fsdp", axis=0, tiled=True),
        lax.all_gather(w_query, "fsdp", axis=0, tiled=True),
        lax.all_gather(w_key, "fsdp", axis=0, tiled=True),
        lax.all_gather(w_value, "fsdp", axis=0, tiled=True),
        lax.all_gather(w_out, "fsdp", axis=1, tiled=True),
        lax.all_gather(w_gate, "fsdp", axis=0, tiled=True),
        lax.all_gather(w_up, "fsdp", axis=0, tiled=True),
        lax.all_gather(w_down, "fsdp", axis=1, tiled=True),
    )
    (
        gain_one,
        gain_two,
        full_query,
        full_key,
        full_value,
        full_out,
        full_gate,
        full_up,
        full_down,
    ) = gathered
    seq_count, local_rows = (tokens.shape[0], tokens.shape[1])
    cycle_size = lax.axis_size("ctx")
    my_place = lax.axis_index("ctx")
    local_width = full_query.shape[1]
    head_count = local_width // HEAD_DIM
    shape_four = (seq_count, local_rows, head_count, HEAD_DIM)
    score_scale = HEAD_DIM ** (-0.5)
    positions = my_place * local_rows + jnp.arange(local_rows, dtype=jnp.int32)
    cosine_table, sine_table = rope_tables(positions)
    wide_cos = jnp.tile(cosine_table, (1, head_count))
    half = HEAD_DIM // 2
    signs = jnp.where(jnp.arange(local_width) % HEAD_DIM < half, -1.0, 1.0).astype(f32)
    wide_sin = jnp.tile(sine_table, (1, head_count)) * signs
    attn_sum, query_scaled, pairs, context_low, log_total = attend(
        tokens, first_values, gain_one[None, :], full_query, full_key, full_value, full_out,
        wide_cos, wide_sin, prefix)
    mixed, late, gate_weight_grad, up_weight_grad, down_weight_grad = feed(
        tokens, attn_sum.reshape(tokens.shape), cotangent, gain_two[None, :], full_gate, full_up, full_down)
    (block_out, token_grad, half_value_grad, query_weight_grad, key_weight_grad, value_weight_grad,
     out_weight_grad, gains) = back(
        tokens, attn_sum.reshape(tokens.shape), cotangent, mixed, late, gain_one[None, :], gain_two[None, :],
        full_query, full_key, full_value, full_out, query_scaled, pairs, context_low, log_total,
        wide_cos, wide_sin, prefix)
    gain_one_grad, gain_two_grad = gains[0], gains[1]
    shard_sums = (
        lax.psum_scatter(
            gain_one_grad.astype(jnp.bfloat16), "fsdp", scatter_dimension=0, tiled=True
        ).astype(jnp.float32),
        lax.psum_scatter(
            gain_two_grad.astype(jnp.bfloat16), "fsdp", scatter_dimension=0, tiled=True
        ).astype(jnp.float32),
        lax.psum_scatter(
            query_weight_grad.astype(jnp.bfloat16), "fsdp", scatter_dimension=0, tiled=True
        ).astype(jnp.float32),
        lax.psum_scatter(
            key_weight_grad.astype(jnp.bfloat16), "fsdp", scatter_dimension=0, tiled=True
        ).astype(jnp.float32),
        lax.psum_scatter(
            value_weight_grad.astype(jnp.bfloat16), "fsdp", scatter_dimension=0, tiled=True
        ).astype(jnp.float32),
        lax.psum_scatter(
            out_weight_grad.astype(jnp.bfloat16), "fsdp", scatter_dimension=1, tiled=True
        ).astype(jnp.float32),
        lax.psum_scatter(
            gate_weight_grad.astype(jnp.bfloat16), "fsdp", scatter_dimension=0, tiled=True
        ).astype(jnp.float32),
        lax.psum_scatter(
            up_weight_grad.astype(jnp.bfloat16), "fsdp", scatter_dimension=0, tiled=True
        ).astype(jnp.float32),
        lax.psum_scatter(
            down_weight_grad.astype(jnp.bfloat16), "fsdp", scatter_dimension=1, tiled=True
        ).astype(jnp.float32),
    )
    sum_one, sum_two, sum_query, sum_key, sum_value, sum_out, sum_gate, sum_up, sum_down = (
        shard_sums
    )
    totals = (
        lax.psum(sum_one.astype(jnp.bfloat16), "ctx").astype(jnp.float32),
        lax.psum(sum_two.astype(jnp.bfloat16), "ctx").astype(jnp.float32),
        lax.psum(sum_query.astype(jnp.bfloat16), "ctx").astype(jnp.float32),
        lax.psum(sum_key.astype(jnp.bfloat16), "ctx").astype(jnp.float32),
        lax.psum(sum_value.astype(jnp.bfloat16), "ctx").astype(jnp.float32),
        lax.psum(sum_out.astype(jnp.bfloat16), "ctx").astype(jnp.float32),
        lax.psum(sum_gate.astype(jnp.bfloat16), "ctx").astype(jnp.float32),
        lax.psum(sum_up.astype(jnp.bfloat16), "ctx").astype(jnp.float32),
        lax.psum(sum_down.astype(jnp.bfloat16), "ctx").astype(jnp.float32),
    )
    return (
        block_out,
        token_grad,
        half_value_grad,
        totals[0],
        totals[1],
        totals[2],
        totals[3],
        totals[4],
        totals[5],
        totals[6],
        totals[7],
        totals[8],
    )


def solution(mesh):
    return jax.shard_map(
        shards,
        mesh=mesh,
        in_specs=(
            P("fsdp", "ctx", None),
            P("fsdp", "ctx", "tp"),
            P("fsdp"),
            P("fsdp"),
            P("fsdp", "tp"),
            P("fsdp", "tp"),
            P("fsdp", "tp"),
            P("tp", "fsdp"),
            P("fsdp", "tp"),
            P("fsdp", "tp"),
            P("tp", "fsdp"),
            P("fsdp"),
            P("fsdp", "ctx", None),
        ),
        out_specs=(
            P("fsdp", "ctx", None),
            P("fsdp", "ctx", None),
            P("fsdp", "ctx", "tp"),
            P("fsdp"),
            P("fsdp"),
            P("fsdp", "tp"),
            P("fsdp", "tp"),
            P("fsdp", "tp"),
            P("tp", "fsdp"),
            P("fsdp", "tp"),
            P("fsdp", "tp"),
            P("tp", "fsdp"),
        ),
        check_vma=False,
    )
```

```python
import functools

import jax
import jax.numpy as jnp
from jax import lax
from jax.experimental import pallas as pl
from jax.experimental.pallas import tpu as pltpu
from jax.sharding import PartitionSpec as P

HEAD_DIM = 64
epsilon = 1e-06
rope_base = 10000.0
masked_score = -1e30
MESH = pl.DeviceIdType.MESH
bf16 = jnp.bfloat16
f32 = jnp.float32


def dot(a, b):
    return jnp.dot(a, b, preferred_element_type=f32)


def dot_nt(a, b):
    return lax.dot_general(a, b, (((1,), (1,)), ((), ())), preferred_element_type=f32)


def unit_norm(values):
    return values * lax.rsqrt(jnp.mean(values * values, axis=-1, keepdims=True) + epsilon)


def low_half(shape):
    return lax.rem(lax.broadcasted_iota(jnp.int32, shape, 1), HEAD_DIM) < HEAD_DIM // 2


def turned(values):
    pieces = []
    half = HEAD_DIM // 2
    for at in range(0, values.shape[1], 128):
        piece = values[:, at : at + 128]
        up = pltpu.roll(piece, 128 - half, 1)
        down = pltpu.roll(piece, half, 1)
        pieces.append(jnp.where(low_half(piece.shape), up, down))
    return jnp.concatenate(pieces, axis=1)


class Sum:
    def __init__(self, place, part, inward, across, result, sems):
        self.pair = place + 1 - 2 * lax.rem(place, 2)
        self.middle = 3 - place
        self.inner = (place == 1) | (place == 2)
        self.outer = (place == 0) | (place == 3)
        self.part, self.inward, self.across, self.result = part, inward, across, result
        self.send_one, self.recv_one, self.send_two, self.recv_two = sems

    def copy_in(self, i):
        return pltpu.make_async_remote_copy(
            src_ref=self.part.at[i], dst_ref=self.inward.at[i], send_sem=self.send_one.at[i],
            recv_sem=self.recv_one.at[i], device_id={"tp": self.pair}, device_id_type=MESH)

    def copy_across(self, i):
        return pltpu.make_async_remote_copy(
            src_ref=self.part.at[i], dst_ref=self.across.at[i], send_sem=self.send_two.at[i],
            recv_sem=self.recv_two.at[i], device_id={"tp": self.middle}, device_id_type=MESH)

    def copy_out(self, i):
        return pltpu.make_async_remote_copy(
            src_ref=self.result.at[i], dst_ref=self.result.at[i], send_sem=self.send_one.at[i],
            recv_sem=self.recv_one.at[i], device_id={"tp": self.pair}, device_id_type=MESH)

    def offer(self, i):
        @pl.when(self.outer)
        def _():
            self.copy_in(i).start()

    def take_in(self, i):
        self.copy_in(i).wait_recv()
        self.part[i] = (self.part[i].astype(f32) + self.inward[i].astype(f32)).astype(bf16)
        self.copy_across(i).start()

    def finish(self, i):
        self.copy_across(i).wait_recv()
        self.result[i] = (self.part[i].astype(f32) + self.across[i].astype(f32)).astype(bf16)
        self.copy_out(i).start()

    def step(self, i, done):
        @pl.when(self.inner)
        def _():
            self.take_in(i)

            @pl.when(i > 0)
            def _():
                self.finish(i - 1)
                done(i - 1)

    def close(self, count, done):
        @pl.when(self.inner)
        def _():
            self.finish(count - 1)
            done(count - 1)

            @pl.loop(0, count)
            def _(i):
                self.copy_across(i).wait_send()
                self.copy_out(i).wait_send()

        @pl.when(self.outer)
        def _():
            @pl.loop(0, count)
            def _(i):
                self.copy_out(i).wait_recv()
                done(i)

            @pl.loop(0, count)
            def _(i):
                self.copy_in(i).wait_send()


def near(place):
    return place + 1 - 2 * lax.rem(place, 2)


def greet(peers):
    barrier = pltpu.get_barrier_semaphore()
    for peer in peers:
        pl.semaphore_signal(barrier, inc=1, device_id=peer, device_id_type=MESH)
    pl.semaphore_wait(barrier, len(peers))


def line_peers(place):
    return [{"tp": near(place)}, {"tp": 3 - place}]


def ring_peers(ring):
    return [{"ctx": near(ring)}, {"ctx": lax.rem(ring + 2, 4)}]


def remote(source, target, send, recv, device):
    return pltpu.make_async_remote_copy(
        src_ref=source, dst_ref=target, send_sem=send, recv_sem=recv,
        device_id=device, device_id_type=MESH)


def rows_at(start, size):
    return pl.ds(pl.multiple_of(start, size), size)


class Fold:
    def __init__(self, side, ring, grad, refs, sems, saved):
        self.side, self.half = side, lax.rem(ring, 2)
        self.grad = grad
        self.one, self.two, self.three, self.final = refs
        self.send, self.recv, self.save = sems
        self.mate, self.peer, self.other = (
            {"ctx": near(ring)}, {"ctx": lax.rem(ring + 2, 4)}, {"fsdp": 1 - side})
        self.saved = saved

    def copy(self, n):
        source, target, device = (
            (self.grad.at[1 - self.half], self.one, self.mate),
            (self.grad.at[self.half, 1 - self.side], self.two, self.other),
            (self.grad.at[self.half, self.side], self.three, self.peer),
            (self.final.at[self.half], self.final.at[self.half], self.mate),
        )[n]
        return remote(source, target, self.send.at[n], self.recv.at[n], device)

    def first(self):
        self.copy(0).start()

    def second(self):
        self.copy(0).wait_recv()
        for side in range(2):
            self.grad[self.half, side] = (
                self.grad[self.half, side].astype(f32) + self.one[side].astype(f32)).astype(bf16)
        self.copy(1).start()

    def third(self):
        self.copy(1).wait_recv()
        self.grad[self.half, self.side] = (
            self.grad[self.half, self.side].astype(f32) + self.two[...].astype(f32)).astype(bf16)
        self.copy(2).start()

    def fourth(self):
        self.copy(2).wait_recv()
        self.final[self.half] = (
            self.grad[self.half, self.side].astype(f32) + self.three[...].astype(f32)).astype(bf16)
        self.copy(3).start()

    def saving(self):
        return pltpu.make_async_copy(self.final, self.saved, self.save)

    def last(self):
        self.copy(3).wait_recv()
        self.saving().start()

    def settle(self):
        for n in range(4):
            self.copy(n).wait_send()
        self.saving().wait()


class Whole:
    def __init__(self, grad, sems, saved):
        self.copy = lambda: pltpu.make_async_copy(grad, saved, sems[2])

    def first(self):
        self.copy().start()

    def second(self):
        pass

    third = fourth = last = second

    def settle(self):
        self.copy().wait()


def fold_shapes(shapes, split):
    scratch = []
    for r, c in shapes:
        scratch.append(pltpu.VMEM((2, 2, r, c), bf16))
        if split:
            scratch += [pltpu.VMEM((2, r, c), bf16), pltpu.VMEM((r, c), bf16), pltpu.VMEM((r, c), bf16),
                        pltpu.VMEM((2, r, c), bf16)]
    n = len(shapes)
    dma = pltpu.SemaphoreType.DMA
    scratch += [dma((n, 4)), dma((n, 4)), dma((n,))]
    outs = [jax.ShapeDtypeStruct((2, r, c) if split else (2, 2, r, c), bf16) for r, c in shapes]
    return scratch, outs


def make_folds(split, side, ring, scratch, saved):
    send, recv, save = scratch[-3:]
    folds, grads = [], []
    per = 5 if split else 1
    for n, target in enumerate(saved):
        mine = scratch[n * per : (n + 1) * per]
        sems = (send.at[n], recv.at[n], save.at[n])
        grads.append(mine[0])
        folds.append(
            Fold(side, ring, mine[0], mine[1:], sems, target) if split else Whole(mine[0], sems, target))
    return folds, grads


def gain_row(gains, which):
    return jnp.concatenate([gains[0, which : which + 1, :], gains[1, which : which + 1, :]], axis=1)


def attend_kernel(split, *refs):
    place, ring, side = lax.axis_index("tp"), lax.axis_index("ctx"), lax.axis_index("fsdp")
    (tok, fv, g1, g2, wq_in, wk_in, wv_in, wo_in), refs = refs[:8], refs[8:]
    if split:
        (wg_in, wu_in, wd_in), refs = refs[:3], refs[3:]
    (cosine, sine, prefix, sum_hbm, q_out, kv_hbm, ctx_out, lse_out, gains), refs = refs[:9], refs[9:]
    if split:
        (wq_hbm, wk_hbm, wv_hbm, wo_hbm, wg_out, wu_out, wd_out), refs = refs[:7], refs[7:]
        (wq, wk, wv, wo, w_send, w_recv, w_save, g_sems), refs = refs[:8], refs[8:]
    else:
        wq, wk, wv, wo = wq_in, wk_in, wv_in, wo_in
    (normed_s, kv, qtm, vt, acct, maxes, totals, part, inward, across, result,
     kv_send, kv_recv, kv_save, send_one, recv_one, send_two, recv_two, save) = refs
    seqs, rows, width = q_out.shape
    heads = width // HEAD_DIM
    tile = 256
    per_seq = part.shape[0] // seqs
    chunk = part.shape[1]
    mate, peer = ring_peers(ring)
    half = lax.rem(ring, 2)
    blocks = (ring, near(ring), lax.rem(ring + 2, 4), 3 - ring)
    greet(line_peers(place) + ring_peers(ring) + ([{"fsdp": 1 - side}] if split else []))

    if split:
        other = {"fsdp": 1 - side}
        gains[side, 0:1, :] = g1[...].astype(f32)
        gains[side, 1:2, :] = g2[...].astype(f32)
        move_gains = remote(gains.at[side], gains.at[side], g_sems.at[0], g_sems.at[1], other)
        move_gains.start()

        def spot(full, owner, part_at, size):
            if full.shape[0] == 2:
                return full.at[owner, rows_at(part_at * size, size)]
            return full.at[rows_at((2 * owner + part_at) * size, size)]

        def outside(full, owner, part_at, size):
            return full.at[rows_at(part_at * size, size)]

        table = (
            (wk_in, wk, spot), (wv_in, wv, spot), (wq_in, wq, spot), (wo_in, wo, spot),
            (wg_in, wg_out, outside), (wu_in, wu_out, outside), (wd_in, wd_out, outside))

        def cross(n):
            own, full, where = table[n]
            size = own.shape[0] // 2
            return remote(own.at[rows_at(half * size, size)], where(full, side, half, size),
                          w_send.at[n, 0], w_recv.at[n, 0], other)

        def onto_mate(n):
            own, full, where = table[n]
            here = where(full, 1 - side, half, own.shape[0] // 2)
            return remote(here, here, w_send.at[n, 1], w_recv.at[n, 1], mate)

        def hand_on(n):
            cross(n).wait_recv()
            onto_mate(n).start()

        saves = tuple(
            pltpu.make_async_copy(full, target, w_save.at[n])
            for n, (full, target) in enumerate(((wk, wk_hbm), (wv, wv_hbm), (wq, wq_hbm), (wo, wo_hbm))))
        for n in range(7):
            cross(n).start()
        for own, full, _ in table[:3]:
            full[rows_at(side * own.shape[0], own.shape[0]), :] = own[...]
        wo[side] = wo_in[...]
        remote(gains.at[side], gains.at[side], g_sems.at[0], g_sems.at[1], other).wait()
    else:
        for n, gain in enumerate((g1, g2)):
            size = gain.shape[1] // 2
            for piece in range(2):
                gains[piece, n : n + 1, :] = gain[:, piece * size : (piece + 1) * size].astype(f32)

    def pass_block(s, source, target, device, slot):
        return remote(kv.at[s, source], kv.at[s, target], kv_send.at[s, slot], kv_recv.at[s, target], device)

    to_mate = lambda s: pass_block(s, 0, 1, mate, 0)
    to_peer = lambda s: pass_block(s, 0, 2, peer, 1)
    onward = lambda s: pass_block(s, 2, 3, mate, 2)
    gain_one = gain_row(gains, 0)

    for s in range(seqs):
        @pl.loop(0, rows // tile)
        def _(t):
            at = rows_at(t * tile, tile)
            normed_s[s, at, :] = (unit_norm(tok[s, at, :].astype(f32)) * gain_one).astype(bf16)

    if split:
        hand_on(0)
        hand_on(1)
        onto_mate(0).wait_recv()
        onto_mate(1).wait_recv()

    for s in range(seqs):
        @pl.loop(0, rows // tile)
        def _(t):
            at = rows_at(t * tile, tile)
            normed = normed_s[s, at, :]
            co, si = cosine[at, :], sine[at, :]
            k = dot(normed, wk[...])
            kv[s, 0, 0, at, :] = (k * co + turned(k) * si).astype(bf16)
            v = dot(normed, wv[...])
            kv[s, 0, 1, at, :] = (0.5 * v + 0.5 * fv[s, at, :].astype(f32)).astype(bf16)

        to_peer(s).start()
        to_mate(s).start()

    if split:
        hand_on(2)
        hand_on(3)
        onto_mate(2).wait_recv()

    for s in range(seqs):
        @pl.loop(0, rows // tile)
        def _(t):
            at = rows_at(t * tile, tile)
            q = dot(normed_s[s, at, :], wq[...])
            q = (q * cosine[at, :] + turned(q) * sine[at, :]) * HEAD_DIM ** (-0.5)
            q_out[s, at, :] = q.astype(bf16)
            qt = jnp.transpose(q)
            owner = lax.broadcasted_iota(jnp.int32, qt.shape, 0) // HEAD_DIM
            for h in range(heads):
                qtm[s, h, :, at] = jnp.where(owner == h, qt, 0.0).astype(bf16)

    def saving(i):
        return pltpu.make_async_copy(result.at[i], sum_hbm.at[i], save.at[i])

    done = lambda i: saving(i).start()
    sums = Sum(place, part, inward, across, result, (send_one, recv_one, send_two, recv_two))

    def attend_block(s, j, block, steps):
        vt[...] = jnp.transpose(kv[s, j, 1])
        key_pos = block * rows + lax.broadcasted_iota(jnp.int32, (rows, 1), 0)
        query_pos = ring * rows + lax.broadcasted_iota(jnp.int32, (1, rows), 1)
        seen = key_pos < jnp.maximum(query_pos + 1, prefix[s])

        @pl.loop(0, heads)
        def _(h):
            of_head = rows_at(h * HEAD_DIM, HEAD_DIM)
            scores = jnp.where(seen, dot(kv[s, j, 0], qtm[s, h]), masked_score)
            old = maxes[h]
            new = jnp.maximum(old, jnp.max(scores, axis=0, keepdims=True))
            weights = jnp.exp(scores - new)
            fade = jnp.exp(old - new)
            maxes[h] = new
            totals[h] = totals[h] * fade + jnp.sum(weights, axis=0, keepdims=True)
            acct[of_head, :] = acct[of_head, :] * fade + dot(vt[of_head, :], weights.astype(bf16))
            if steps is not None:
                @pl.when(lax.rem(h, 2) == 1)
                def _():
                    sums.step(steps + h // 2, done)

    for s in range(seqs):
        maxes[...] = jnp.full_like(maxes, masked_score)
        totals[...] = jnp.zeros_like(totals)
        acct[...] = jnp.zeros_like(acct)
        begun = lambda j: None if s == 0 else (s - 1) * per_seq + 2 * j
        attend_block(s, 0, blocks[0], begun(0))
        to_mate(s).wait_recv()
        attend_block(s, 1, blocks[1], begun(1))
        to_peer(s).wait_recv()
        onward(s).start()
        attend_block(s, 2, blocks[2], begun(2))
        onward(s).wait_recv()
        attend_block(s, 3, blocks[3], begun(3))
        pltpu.make_async_copy(kv.at[s], kv_hbm.at[s], kv_save.at[s]).start()
        for h in range(heads):
            lse_out[s, h : h + 1, :] = maxes[h] + jnp.log(totals[h])
            of_head = slice(h * HEAD_DIM, (h + 1) * HEAD_DIM)
            acct[of_head, :] = acct[of_head, :] / totals[h]
        ctx_out[s] = jnp.transpose(acct[...]).astype(bf16)
        if split and s == 0:
            onto_mate(3).wait_recv()
            for copy in saves:
                copy.start()

        @pl.loop(0, per_seq)
        def _(i):
            at = rows_at(i * chunk, chunk)
            n = s * per_seq + i
            size = wo.shape[2]
            for piece in range(2):
                part[n, :, piece * size : (piece + 1) * size] = dot(ctx_out[s, at, :], wo[piece]).astype(bf16)
            sums.offer(n)

        if split and s == 0:
            hand_on(4)
            hand_on(5)
        if split and s == seqs - 1:
            hand_on(6)

    @pl.loop((seqs - 1) * per_seq, seqs * per_seq)
    def _(i):
        sums.step(i, done)

    sums.close(seqs * per_seq, done)
    for s in range(seqs):
        to_mate(s).wait_send()
        to_peer(s).wait_send()
        onward(s).wait_send()
        pltpu.make_async_copy(kv.at[s], kv_hbm.at[s], kv_save.at[s]).wait()

    @pl.loop(0, seqs * per_seq)
    def _(i):
        saving(i).wait()

    if split:
        for n in range(4, 7):
            onto_mate(n).wait_recv()
        for n in range(7):
            cross(n).wait_send()
            onto_mate(n).wait_send()
        for copy in saves:
            copy.wait()


def limits(ident, megabytes=60):
    return pltpu.CompilerParams(
        collective_id=ident, has_side_effects=True, vmem_limit_bytes=megabytes * 1024 * 1024)


def attend(split, tok, fv, gains, square, wide, cosine, sine, prefix):
    seqs, rows, dim = tok.shape
    width = square[0].shape[1]
    heads = width // HEAD_DIM
    chunk = 64
    count = seqs * rows // chunk
    vmem = pl.BlockSpec(memory_space=pltpu.VMEM)
    anyw = pl.BlockSpec(memory_space=pl.ANY)
    dma = pltpu.SemaphoreType.DMA
    lines = pltpu.VMEM((count, chunk, dim), bf16)
    shape = jax.ShapeDtypeStruct
    full = [(dim, width)] * 3 + [(2, width, dim // 2)]
    outs = [
        shape((count, chunk, dim), bf16), shape((seqs, rows, width), bf16),
        shape((seqs, 4, 2, rows, width), bf16), shape((seqs, rows, width), bf16),
        shape((seqs, heads, rows), f32), shape((2, 8, dim // 2), f32)]
    out_specs = [anyw, vmem, anyw, vmem, vmem, vmem]
    scratch = []
    if split:
        outs += [shape(size, bf16) for size in full] + [shape(w.shape, bf16) for w in wide]
        out_specs += [anyw] * 7
        scratch = [pltpu.VMEM(size, bf16) for size in full] + [dma((7, 2)), dma((7, 2)), dma((4,)), dma((2,))]
    scratch += [
        pltpu.VMEM((seqs, rows, dim), bf16),
        pltpu.VMEM((seqs, 4, 2, rows, width), bf16),
        pltpu.VMEM((seqs, heads, width, rows), bf16),
        pltpu.VMEM((width, rows), bf16),
        pltpu.VMEM((width, rows), f32),
        pltpu.VMEM((heads, 1, rows), f32),
        pltpu.VMEM((heads, 1, rows), f32),
        lines, lines, lines, lines,
        dma((seqs, 3)), dma((seqs, 4)), dma((seqs,)),
        dma((count,)), dma((count,)), dma((count,)), dma((count,)), dma((count,)),
    ]
    return pl.pallas_call(
        functools.partial(attend_kernel, split),
        name="attend",
        out_shape=outs,
        in_specs=[vmem] * 8 + ([anyw] * 3 if split else []) + [vmem] * 2 + [pl.BlockSpec(memory_space=pltpu.SMEM)],
        out_specs=out_specs,
        scratch_shapes=scratch,
        compiler_params=limits(0),
        cost_estimate=pl.CostEstimate(flops=8 * 10**9, bytes_accessed=10**7, transcendentals=10**7),
    )(tok, fv, *gains, *square, *(wide if split else ()), cosine, sine, prefix)


def feed_kernel(split, *refs):
    place, ring, side = lax.axis_index("tp"), lax.axis_index("ctx"), lax.axis_index("fsdp")
    (tok, attn, cot, gains), refs = refs[:4], refs[4:]
    weights, refs = refs[: 6 if split else 3], refs[6 if split else 3 :]
    (mixed_hbm, late_hbm), saved, refs = refs[:2], refs[2:5], refs[5:]
    (wg, wu, wd, w_load, normed_t, inner_t, inner_s, gg, ug, late, part, inward, across, result,
     send_one, recv_one, send_two, recv_two, save, late_save), refs = refs[:20], refs[20:]
    (fold_d, fold_g, fold_u), (dwd, dwg, dwu) = make_folds(split, side, ring, refs, saved)
    seqs, rows, dim = tok.shape
    chunk = part.shape[1]
    tile = 256
    tiles = seqs * rows // tile
    early = tiles // 2
    per_tile = tile // chunk
    per_seq_tiles = rows // tile
    count = part.shape[0]
    loads = []
    for n, full in enumerate((wg, wu, wd)):
        if split:
            size = weights[n].shape[0]
            for m, owner in ((0, side), (1, 1 - side)):
                target = full.at[owner] if full.shape[0] == 2 else full.at[rows_at(owner * size, size)]
                loads.append(pltpu.make_async_copy(weights[n + 3 * m], target, w_load.at[n, m]))
        else:
            loads.append(pltpu.make_async_copy(weights[n], full, w_load.at[n, 0]))
    for load in loads:
        load.start()
    greet(line_peers(place) + (ring_peers(ring) + [{"fsdp": 1 - side}] if split else []))
    sums = Sum(place, part, inward, across, result, (send_one, recv_one, send_two, recv_two))
    gain_two = gain_row(gains, 1)
    middle = dim // 2

    def saving(i):
        return pltpu.make_async_copy(result.at[i], mixed_hbm.at[i], save.at[i])

    done = lambda i: saving(i).start()

    def saving_late(t):
        return pltpu.make_async_copy(late.at[t], late_hbm.at[t], late_save.at[t])

    for load in loads:
        load.wait()

    @pl.loop(0, tiles)
    def _(t):
        s, at = t // per_seq_tiles, rows_at(lax.rem(t, per_seq_tiles) * tile, tile)
        flat = rows_at(t * tile, tile)
        step_base = (t - 1) * per_tile

        def step(k):
            @pl.when(t > 0)
            def _():
                sums.step(step_base + k, done)

        hidden = tok[s, at, :].astype(f32) + attn[s, at, :].astype(f32)
        normed = (unit_norm(hidden) * gain_two).astype(bf16)
        normed_t[:, flat] = jnp.transpose(normed)
        gate = dot(normed, wg[...])
        up = dot(normed, wu[...])
        sigmoid = jax.nn.sigmoid(gate)
        swish = gate * sigmoid
        inner = (swish * up).astype(bf16)
        inner_s[...] = inner
        inner_t[:, flat] = jnp.transpose(inner)
        upstream = cot[s, at, :]
        inner_grad = dot_nt(upstream[:, :middle], wd[0]) + dot_nt(upstream[:, middle:], wd[1])
        gg[flat, :] = (inner_grad * up * sigmoid * (1.0 + gate * (1.0 - sigmoid))).astype(bf16)
        ug[flat, :] = (inner_grad * swish).astype(bf16)
        step(0)

        @pl.loop(0, per_tile)
        def _(k):
            own = rows_at(t * tile + k * chunk, chunk)
            i = jnp.where(t < early, 2 * per_tile * t, per_tile * (early + t)) + k
            part[i] = (dot_nt(gg[own, :], wg[...]) + dot_nt(ug[own, :], wu[...])).astype(bf16)
            sums.offer(i)

        step(1)

        @pl.when(t < early)
        def _():
            @pl.loop(0, per_tile)
            def _(k):
                i = 2 * per_tile * t + per_tile + k
                own = rows_at(k * chunk, chunk)
                for piece in range(2):
                    part[i, :, piece * middle : (piece + 1) * middle] = dot(inner_s[own, :], wd[piece]).astype(bf16)
                sums.offer(i)

        @pl.when(t >= early)
        def _():
            @pl.loop(0, per_tile)
            def _(k):
                own = rows_at(k * chunk, chunk)
                for piece in range(2):
                    late[t - early, own, piece * middle : (piece + 1) * middle] = dot(
                        inner_s[own, :], wd[piece]).astype(bf16)

            saving_late(t - early).start()

        step(2)
        step(3)

    begun = (tiles - 1) * per_tile
    deep, share = dwd.shape[2], dwg.shape[2]

    def wide_grad(target, right, first_step):
        @pl.loop(0, 4)
        def _(k):
            h, y = k // 2, lax.rem(k, 2)
            target[h, y] = dot(normed_t[rows_at((2 * y + h) * share, share), :], right[...]).astype(bf16)

            @pl.when(y == 1)
            def _():
                sums.step(first_step + h, done)

    for h in range(2):
        for y in range(2):
            total = jnp.zeros((deep, middle), f32)
            for s in range(seqs):
                total = total + dot(
                    inner_t[h * deep : (h + 1) * deep, s * rows : (s + 1) * rows],
                    cot[s, :, y * middle : (y + 1) * middle])
            dwd[h, y] = total.astype(bf16)
        sums.step(begun + h, done)
    fold_d.first()
    wide_grad(dwg, gg, begun + 2)
    fold_g.first()
    fold_d.second()
    wide_grad(dwu, ug, begun + 4)
    fold_u.first()
    fold_g.second()
    sums.step(begun + 6, done)
    fold_u.second()
    sums.step(begun + 7, done)
    fold_d.third()
    sums.step(begun + 8, done)
    fold_g.third()
    sums.step(begun + 9, done)
    fold_d.fourth()
    sums.step(begun + 10, done)
    fold_u.third()
    sums.step(begun + 11, done)
    fold_g.fourth()

    @pl.loop(begun + 12, count)
    def _(i):
        sums.step(i, done)

    sums.close(count, done)
    fold_u.fourth()
    folds = (fold_d, fold_g, fold_u)
    for fold in folds:
        fold.last()
    for fold in folds:
        fold.settle()
    for t in range(tiles - early):
        saving_late(t).wait()

    @pl.loop(0, count)
    def _(i):
        saving(i).wait()


def feed(split, tok, attn, cot, gains, weights, units):
    seqs, rows, dim = tok.shape
    chunk = 64
    tokens = seqs * rows
    count = tokens // chunk * 3 // 2
    vmem = pl.BlockSpec(memory_space=pltpu.VMEM)
    anyw = pl.BlockSpec(memory_space=pl.ANY)
    dma = pltpu.SemaphoreType.DMA
    lines = pltpu.VMEM((count, chunk, dim), bf16)
    tile = 256
    late = tokens // tile // 2
    shape = jax.ShapeDtypeStruct
    fold_scratch, fold_outs = fold_shapes(
        [(units // 2, dim // 2), (dim // 4, units), (dim // 4, units)], split)
    return pl.pallas_call(
        functools.partial(feed_kernel, split),
        name="feed",
        out_shape=[shape((count, chunk, dim), bf16), shape((late, tile, dim), bf16)] + fold_outs,
        in_specs=[vmem] * 4 + [anyw] * len(weights),
        out_specs=[anyw] * 5,
        scratch_shapes=[
            pltpu.VMEM((dim, units), bf16),
            pltpu.VMEM((dim, units), bf16),
            pltpu.VMEM((2, units, dim // 2), bf16),
            dma((3, 2)),
            pltpu.VMEM((dim, tokens), bf16),
            pltpu.VMEM((units, tokens), bf16),
            pltpu.VMEM((tile, units), bf16),
            pltpu.VMEM((tokens, units), bf16),
            pltpu.VMEM((tokens, units), bf16),
            pltpu.VMEM((late, tile, dim), bf16),
            lines, lines, lines, lines,
            dma((count,)), dma((count,)), dma((count,)), dma((count,)), dma((count,)), dma((late,)),
        ] + fold_scratch,
        compiler_params=limits(1),
        cost_estimate=pl.CostEstimate(flops=14 * 10**9, bytes_accessed=10**7, transcendentals=10**6),
    )(tok, attn, cot, gains, *weights)


def back_kernel(split, *refs):
    place, ring, side = lax.axis_index("tp"), lax.axis_index("ctx"), lax.axis_index("fsdp")
    (tok, attn, cot, mixed, late, gain_in, wq, wk, wv, wo, q, kv, ctx, lse, cosine, sine, prefix,
     block_hbm, token_hbm, fv_hbm, gain_out), saved, refs = refs[:21], refs[21:25], refs[25:]
    (hid, branch, qtm, qm, otm, om, kt, delta, dqt, dk, dv, give, take, proj, normed_t,
     part, inward, across, result, gain_part, gain_all,
     kv_send, kv_recv, send_one, recv_one, send_two, recv_two, save, fv_save, gain_send, gain_recv), refs = (
        refs[:31], refs[31:])
    (fold_o, fold_k, fold_v, fold_q), (dwo, dwk, dwv, dwq) = make_folds(split, side, ring, refs, saved)
    seqs, rows, dim = tok.shape
    width = wq.shape[1]
    heads = width // HEAD_DIM
    count, chunk = part.shape[0], part.shape[1]
    per_seq = rows // chunk
    tile = 256
    per_tile = tile // chunk
    middle = dim // 2
    mate, peer = ring_peers(ring)
    blocks = (ring, near(ring), lax.rem(ring + 2, 4), 3 - ring)
    others = [(dy, dc) for dy in range(2) for dc in range(4) if dy or dc]
    group = [{"fsdp": lax.rem(side + dy, 2), "ctx": lax.rem(ring + dc, 4)} for dy, dc in others]
    greet(line_peers(place) + (group if split else ring_peers(ring)))
    sums = Sum(place, part, inward, across, result, (send_one, recv_one, send_two, recv_two))
    gain_one, gain_two = gain_row(gain_in, 0), gain_row(gain_in, 1)
    gain_part[...] = jnp.zeros_like(gain_part)
    late_per = late.shape[1] // chunk

    @pl.loop(0, per_seq)
    def _(i):
        part[i] = late[i // late_per, rows_at(lax.rem(i, late_per) * chunk, chunk), :]
        sums.offer(i)

    def hidden_at(s, at):
        return tok[s, at, :].astype(f32) + attn[s, at, :].astype(f32)

    def chunk_of(n):
        return n // per_seq, rows_at(lax.rem(n, per_seq) * chunk, chunk)

    def saving_block(n):
        s, own = chunk_of(n)
        source = inward.at[n] if s == 0 else across.at[n - per_seq]
        return pltpu.make_async_copy(source, block_hbm.at[s, own], save.at[n])

    def saving_first(n):
        return pltpu.make_async_copy(inward.at[n], block_hbm.at[0, rows_at(n * chunk, chunk)], save.at[n])

    def saving_second(n):
        return pltpu.make_async_copy(
            across.at[n], block_hbm.at[1, rows_at(n * chunk, chunk)], save.at[per_seq + n])

    def saving_token(n):
        s, own = chunk_of(n)
        return pltpu.make_async_copy(across.at[per_seq + n], token_hbm.at[s, own], save.at[seqs * per_seq + n])

    def add_gain(which, value):
        for piece in range(2):
            gain_part[piece, which : which + 1, :] += value[:, piece * middle : (piece + 1) * middle]

    def done(i):
        @pl.when(i < per_seq)
        def _():
            across[i] = (hidden_at(1, rows_at(i * chunk, chunk)) + result[i].astype(f32)).astype(bf16)
            saving_second(i).start()

        @pl.when(i >= per_seq)
        def _():
            n = i - per_seq
            s, own = chunk_of(n)
            values, upstream = tok[s, own, :].astype(f32), result[i].astype(f32)
            factor = lax.rsqrt(jnp.mean(values * values, axis=-1, keepdims=True) + epsilon)
            scaled = upstream * gain_one
            add_gain(0, jnp.sum(upstream * values * factor, axis=0, keepdims=True))
            across[i] = (hid[s, own, :] + factor * scaled - values * factor**3 * jnp.mean(
                scaled * values, axis=-1, keepdims=True)).astype(bf16)
            saving_token(n).start()

    def move(s, source, target, device):
        return remote(give.at[source], take.at[s, target], kv_send.at[source], kv_recv.at[s, target], device)

    far_to_mate = lambda s: move(s, 2, 0, mate)
    peer_back = lambda s: move(s, 1, 1, peer)
    near_to_mate = lambda s: move(s, 0, 2, mate)

    for s in range(seqs):
        @pl.loop(0, rows // tile)
        def _(t):
            at = rows_at(t * tile, tile)
            values = hidden_at(s, at)
            n = s * (rows // tile) + t
            early = seqs * rows // tile // 2
            first = jnp.where(n < early, 2 * per_tile * n, per_tile * (early + n))
            upstream = jnp.concatenate([mixed[first + k] for k in range(per_tile)], axis=0).astype(f32)
            factor = lax.rsqrt(jnp.mean(values * values, axis=-1, keepdims=True) + epsilon)
            scaled = upstream * gain_two
            add_gain(1, jnp.sum(upstream * values * factor, axis=0, keepdims=True))
            hid_now = cot[s, at, :].astype(f32) + factor * scaled - values * factor**3 * jnp.mean(
                scaled * values, axis=-1, keepdims=True)
            hid[s, at, :] = hid_now
            low = hid_now.astype(bf16)
            branch[s, at, :] = low
            left, right = low[:, :middle], low[:, middle:]
            grad = dot_nt(left, wo[0]) + dot_nt(right, wo[1])
            lane_owner = lax.broadcasted_iota(jnp.int32, grad.shape, 1) // HEAD_DIM
            q_now = q[s, at, :].astype(f32)
            grad_t = dot_nt(wo[0], left) + dot_nt(wo[1], right)
            row_owner = lax.broadcasted_iota(jnp.int32, grad_t.shape, 0) // HEAD_DIM
            q_t = jnp.transpose(q_now)
            ctx_t = jnp.transpose(ctx[s, at, :].astype(f32))
            product = grad_t.astype(bf16).astype(f32) * ctx_t
            for h in range(heads):
                om[h, at, :] = jnp.where(lane_owner == h, grad, 0.0).astype(bf16)
                qm[h, at, :] = jnp.where(lane_owner == h, q_now, 0.0).astype(bf16)
                otm[h, :, at] = jnp.where(row_owner == h, grad_t, 0.0).astype(bf16)
                qtm[h, :, at] = jnp.where(row_owner == h, q_t, 0.0).astype(bf16)
                delta[h, :, at] = jnp.sum(
                    product[h * HEAD_DIM : (h + 1) * HEAD_DIM], axis=0, keepdims=True)
            normed = (unit_norm(tok[s, at, :].astype(f32)) * gain_one).astype(bf16)
            normed_t[:, rows_at(s * rows + t * tile, tile)] = jnp.transpose(normed)

        if s == seqs - 1:
            deep = dwo.shape[2]
            total = jnp.zeros((width, dim), f32)
            for r in range(seqs):
                total = total + dot(jnp.transpose(ctx[r]), branch[r])
            for h in range(2):
                for y in range(2):
                    dwo[h, y] = total[h * deep : (h + 1) * deep, y * middle : (y + 1) * middle].astype(bf16)
            fold_o.first()

        dqt[...] = jnp.zeros_like(dqt)

        def back_block(j, block_at, steps):
            kt[...] = jnp.transpose(kv[s, j, 0])
            key_pos = block_at * rows + lax.broadcasted_iota(jnp.int32, (rows, 1), 0)
            query_pos = ring * rows + lax.broadcasted_iota(jnp.int32, (1, rows), 1)
            seen = key_pos < jnp.maximum(query_pos + 1, prefix[s])
            dk[...] = jnp.zeros_like(dk)
            dv[...] = jnp.zeros_like(dv)

            @pl.loop(0, heads)
            def _(h):
                of_head = rows_at(h * HEAD_DIM, HEAD_DIM)
                scores = dot(kv[s, j, 0], qtm[h])
                probs = jnp.where(seen, jnp.exp(scores - lse[s, pl.ds(h, 1), :]), 0.0)
                dprobs = dot(kv[s, j, 1], otm[h])
                dv[...] += dot(probs.astype(bf16), om[h])
                dscores = (probs * (dprobs - delta[h])).astype(bf16)
                dk[...] += dot(dscores, qm[h])
                dqt[of_head, :] += dot(kt[of_head, :], dscores)

                @pl.when(lax.rem(h, 2) == 1)
                def _():
                    sums.step(steps + h // 2, done)

        base = s * per_seq
        last = s == seqs - 1
        back_block(3, blocks[3], base)
        if last:
            fold_o.second()
        if s > 0:
            far_to_mate(s - 1).wait_send()
        give[2, 0] = dk[...].astype(bf16)
        give[2, 1] = dv[...].astype(bf16)
        far_to_mate(s).start()
        back_block(2, blocks[2], base + 2)
        far_to_mate(s).wait_recv()
        if s > 0:
            peer_back(s - 1).wait_send()
        give[1, 0] = (dk[...] + take[s, 0, 0].astype(f32)).astype(bf16)
        give[1, 1] = (dv[...] + take[s, 0, 1].astype(f32)).astype(bf16)
        peer_back(s).start()
        back_block(1, blocks[1], base + 4)
        if last:
            fold_o.third()
        if s > 0:
            near_to_mate(s - 1).wait_send()
        give[0, 0] = dk[...].astype(bf16)
        give[0, 1] = dv[...].astype(bf16)
        near_to_mate(s).start()
        back_block(0, blocks[0], base + 6)
        near_to_mate(s).wait_recv()
        peer_back(s).wait_recv()

        @pl.loop(0, rows // tile)
        def _(t):
            at = rows_at(t * tile, tile)
            flat = rows_at(s * rows + t * tile, tile)
            co, si = cosine[at, :], sine[at, :]
            grad_v = 0.5 * (dv[at, :] + take[s, 2, 1, at, :].astype(f32) + take[s, 1, 1, at, :].astype(f32))
            grad_k = dk[at, :] + take[s, 2, 0, at, :].astype(f32) + take[s, 1, 0, at, :].astype(f32)
            grad_q = jnp.transpose(dqt[:, at]) * HEAD_DIM ** (-0.5)
            proj[0, flat, :] = (grad_q * co - turned(grad_q) * si).astype(bf16)
            proj[1, flat, :] = (grad_k * co - turned(grad_k) * si).astype(bf16)
            proj[2, flat, :] = grad_v.astype(bf16)

        @pl.loop(0, per_seq)
        def _(k):
            own = rows_at(s * rows + k * chunk, chunk)
            i = per_seq * (s + 1) + k
            part[i] = (
                dot_nt(proj[0, own, :], wq[...]) + dot_nt(proj[1, own, :], wk[...])
                + dot_nt(proj[2, own, :], wv[...])).astype(bf16)
            sums.offer(i)

    fv_copy = pltpu.make_async_copy(proj.at[2], fv_hbm, fv_save)
    fv_copy.start()
    share = dwq.shape[2]

    def square_grad(target, which):
        @pl.loop(0, 4)
        def _(k):
            h, y = k // 2, lax.rem(k, 2)
            target[h, y] = dot(normed_t[rows_at((2 * y + h) * share, share), :], proj[which]).astype(bf16)

    at_step = 2 * per_seq
    square_grad(dwk, 1)
    fold_k.first()
    sums.step(at_step, done)
    square_grad(dwv, 2)
    fold_v.first()
    fold_k.second()
    sums.step(at_step + 1, done)
    square_grad(dwq, 0)
    fold_q.first()
    fold_v.second()
    sums.step(at_step + 2, done)
    fold_q.second()
    fold_o.fourth()
    sums.step(at_step + 3, done)

    @pl.loop(0, per_seq)
    def _(i):
        own = rows_at(i * chunk, chunk)
        at = 2 * per_tile * (i // per_tile) + per_tile + lax.rem(i, per_tile)
        inward[i] = (hidden_at(0, own) + mixed[at].astype(f32)).astype(bf16)
        saving_first(i).start()

    fold_k.third()
    sums.step(at_step + 4, done)
    fold_v.third()
    sums.step(at_step + 5, done)
    fold_q.third()
    fold_k.fourth()
    sums.step(at_step + 6, done)
    fold_v.fourth()
    sums.step(at_step + 7, done)
    fold_q.fourth()

    @pl.loop(at_step + 8, count)
    def _(i):
        sums.step(i, done)

    sums.close(count, done)
    if split:
        me = 4 * side + ring
        gain_all[me] = gain_part[side]

        def share_gain(n):
            dy, dc = others[n]
            y = lax.rem(side + dy, 2)
            return remote(gain_part.at[y], gain_all.at[me], gain_send.at[n], gain_recv.at[n], group[n])

        for n in range(7):
            share_gain(n).start()
    folds = (fold_o, fold_k, fold_v, fold_q)
    for fold in folds:
        fold.last()
    if split:
        for n in range(7):
            share_gain(n).wait()
        total = gain_all[0]
        for n in range(1, 8):
            total = total + gain_all[n]
        gain_out[...] = total
    else:
        gain_out[...] = gain_part[...]
    for fold in folds:
        fold.settle()
    for copy in (far_to_mate, peer_back, near_to_mate):
        copy(seqs - 1).wait_send()
    fv_copy.wait()

    @pl.loop(0, per_seq)
    def _(i):
        saving_first(i).wait()
        saving_second(i).wait()

    @pl.loop(0, seqs * per_seq)
    def _(i):
        saving_token(i).wait()


def back(split, tok, attn, cot, mixed, late, gains, square, q, kv, ctx, lse, cosine, sine, prefix):
    seqs, rows, dim = tok.shape
    width = q.shape[2]
    heads = width // HEAD_DIM
    count, chunk, _ = mixed.shape
    tokens = seqs * rows
    vmem = pl.BlockSpec(memory_space=pltpu.VMEM)
    anyw = pl.BlockSpec(memory_space=pl.ANY)
    dma = pltpu.SemaphoreType.DMA
    lines = pltpu.VMEM((count, chunk, dim), bf16)
    wide = pltpu.VMEM((heads, rows, width), bf16)
    tall = pltpu.VMEM((heads, width, rows), bf16)
    shape = jax.ShapeDtypeStruct
    fold_scratch, fold_outs = fold_shapes([(width // 2, dim // 2)] + [(dim // 4, width)] * 3, split)
    return pl.pallas_call(
        functools.partial(back_kernel, split),
        name="back",
        out_shape=[
            shape((seqs, rows, dim), bf16), shape((seqs, rows, dim), bf16), shape((tokens, width), bf16),
            shape((8, dim // 2) if split else (2, 8, dim // 2), f32)] + fold_outs,
        in_specs=[vmem] * 16 + [pl.BlockSpec(memory_space=pltpu.SMEM)],
        out_specs=[anyw, anyw, anyw, vmem] + [anyw] * 4,
        scratch_shapes=[
            pltpu.VMEM((seqs, rows, dim), f32),
            pltpu.VMEM((seqs, rows, dim), bf16),
            tall, wide, tall, wide,
            pltpu.VMEM((width, rows), bf16),
            pltpu.VMEM((heads, 1, rows), f32),
            pltpu.VMEM((width, rows), f32),
            pltpu.VMEM((rows, width), f32),
            pltpu.VMEM((rows, width), f32),
            pltpu.VMEM((3, 2, rows, width), bf16),
            pltpu.VMEM((seqs, 3, 2, rows, width), bf16),
            pltpu.VMEM((3, tokens, width), bf16),
            pltpu.VMEM((dim, tokens), bf16),
            lines, lines, lines, lines,
            pltpu.VMEM((2, 8, dim // 2), f32),
            pltpu.VMEM((8, 8, dim // 2), f32),
            dma((3,)), dma((seqs, 3)),
            dma((count,)), dma((count,)), dma((count,)), dma((count,)), dma((2 * tokens // chunk,)),
            dma(()), dma((7,)), dma((7,)),
        ] + fold_scratch,
        compiler_params=limits(2, 62),
        cost_estimate=pl.CostEstimate(flops=30 * 10**9, bytes_accessed=10**7, transcendentals=10**7),
    )(tok, attn, cot, mixed, late, gains, *square, q, kv, ctx, lse, cosine, sine, prefix)


def rope_tables(positions, lanes):
    half_dim = HEAD_DIM // 2
    lane = jnp.arange(lanes, dtype=jnp.int32) % HEAD_DIM
    frequency = rope_base ** (-(lane % half_dim).astype(f32) / half_dim)
    angles = positions.astype(f32)[:, None] * frequency[None, :]
    return jnp.cos(angles), jnp.sin(angles) * jnp.where(lane < half_dim, -1.0, 1.0)


def halves(weight):
    rows, columns = weight.shape
    return jnp.swapaxes(weight.reshape(rows, 2, columns // 2), 0, 1)


def shards(
    tokens, first_values, norm1_gain, norm2_gain, w_query, w_key, w_value, w_out, w_gate, w_up, w_down,
    prefix, cotangent,
):
    split = lax.axis_size("fsdp") == 2
    seqs, rows, dim = tokens.shape
    width, units = w_query.shape[1], w_gate.shape[1]
    positions = lax.axis_index("ctx") * rows + jnp.arange(rows, dtype=jnp.int32)
    cosine, sine = rope_tables(positions, width)
    gather = functools.partial(lax.all_gather, axis_name="fsdp", tiled=True)
    if split:
        gains = (norm1_gain[None, :], norm2_gain[None, :])
        square = (w_query, w_key, w_value, w_out)
        wide = (w_gate, w_up, w_down)
    else:
        gains = (gather(norm1_gain)[None, :], gather(norm2_gain)[None, :])
        square = (gather(w_query), gather(w_key), gather(w_value), halves(gather(w_out, axis=1)))
        wide = (gather(w_gate), gather(w_up), halves(gather(w_down, axis=1)))
    attn_sum, query, pairs, context, log_total, gain_rows, *gathered = attend(
        split, tokens, first_values, gains, square, wide, cosine, sine, prefix)
    if split:
        square = tuple(gathered[:4])
        wide = wide + tuple(gathered[4:])
    attn_sum = attn_sum.reshape(tokens.shape)
    mixed, late, down_grad, gate_grad, up_grad = feed(
        split, tokens, attn_sum, cotangent, gain_rows, wide, units)
    block_out, token_grad, half_value_grad, gain_grads, out_grad, key_grad, value_grad, query_grad = back(
        split, tokens, attn_sum, cotangent, mixed, late, gain_rows, square, query, pairs, context,
        log_total, cosine, sine, prefix)
    if split:
        over_rows = lambda grad: grad.reshape(-1, grad.shape[-1]).astype(f32)
        over_columns = over_rows
        gain_one_grad, gain_two_grad = gain_grads[0], gain_grads[1]
    else:
        total = lambda grad, axis: lax.psum(
            lax.psum_scatter(grad, "fsdp", scatter_dimension=axis, tiled=True), "ctx").astype(f32)
        over_rows = lambda grad: total(jnp.swapaxes(grad, 0, 1).reshape(-1, grad.shape[-1]), 0)
        over_columns = lambda grad: total(
            jnp.transpose(grad, (0, 2, 1, 3)).reshape(2 * grad.shape[2], -1), 1)
        gain_one_grad, gain_two_grad = (total(gain_grads[:, n].reshape(-1), 0) for n in range(2))
    return (
        block_out,
        token_grad.astype(f32),
        half_value_grad.reshape(seqs, rows, width).astype(f32),
        gain_one_grad,
        gain_two_grad,
        over_rows(query_grad),
        over_rows(key_grad),
        over_rows(value_grad),
        over_columns(out_grad),
        over_rows(gate_grad),
        over_rows(up_grad),
        over_columns(down_grad),
    )


def solution(mesh):
    return jax.shard_map(
        shards,
        mesh=mesh,
        in_specs=(
            P("fsdp", "ctx", None),
            P("fsdp", "ctx", "tp"),
            P("fsdp"),
            P("fsdp"),
            P("fsdp", "tp"),
            P("fsdp", "tp"),
            P("fsdp", "tp"),
            P("tp", "fsdp"),
            P("fsdp", "tp"),
            P("fsdp", "tp"),
            P("tp", "fsdp"),
            P("fsdp"),
            P("fsdp", "ctx", None),
        ),
        out_specs=(
            P("fsdp", "ctx", None),
            P("fsdp", "ctx", None),
            P("fsdp", "ctx", "tp"),
            P("fsdp"),
            P("fsdp"),
            P("fsdp", "tp"),
            P("fsdp", "tp"),
            P("fsdp", "tp"),
            P("tp", "fsdp"),
            P("fsdp", "tp"),
            P("fsdp", "tp"),
            P("tp", "fsdp"),
        ),
        check_vma=False,
    )
```

```python
import functools

import jax
import jax.numpy as jnp
import numpy as np
from jax import lax
from jax.experimental import pallas as pl
from jax.experimental.pallas import tpu as pltpu
from jax.sharding import PartitionSpec as P

HEAD_DIM = 64
epsilon = 1e-06
rope_base = 10000.0
masked_score = -1e30
MESH = pl.DeviceIdType.MESH
bf16 = jnp.bfloat16
f32 = jnp.float32


def dot(a, b):
    return jnp.dot(a, b, preferred_element_type=f32)


def dot_nt(a, b):
    return lax.dot_general(a, b, (((1,), (1,)), ((), ())), preferred_element_type=f32)


def unit_norm(values):
    return values * lax.rsqrt(jnp.mean(values * values, axis=-1, keepdims=True) + epsilon)


def low_half(shape):
    return lax.rem(lax.broadcasted_iota(jnp.int32, shape, 1), HEAD_DIM) < HEAD_DIM // 2


class Sum:
    def __init__(self, place, part, inward, across, sems, done):
        self.pair = near(place)
        self.middle = 3 - place
        self.inner = (place == 1) | (place == 2)
        self.outer = (place == 0) | (place == 3)
        self.part, self.inward, self.across, self.done = part, inward, across, done
        self.send_one, self.recv_one, self.send_two, self.recv_two = sems

    def copy_in(self, i):
        return remote(
            self.part.at[i], self.inward.at[i], self.send_one.at[i], self.recv_one.at[i], {"tp": self.pair})

    def copy_across(self, i):
        return remote(
            self.part.at[i], self.across.at[i], self.send_two.at[i], self.recv_two.at[i], {"tp": self.middle})

    def copy_out(self, i):
        return remote(
            self.part.at[i], self.inward.at[i], self.send_one.at[i], self.recv_one.at[i], {"tp": self.pair})

    def fill(self, first, piece, values):
        chunk, size = self.part.shape[1], values.shape[1]
        for k in range(values.shape[0] // chunk):
            self.part[first + k, :, piece * size : (piece + 1) * size] = values[
                k * chunk : (k + 1) * chunk].astype(bf16)

    def offer(self, first, count):
        @pl.when(self.outer)
        def _():
            @pl.loop(0, count)
            def _(k):
                self.copy_in(first + k).start()

    def take_in(self, i):
        self.copy_in(i).wait_recv()
        self.part[i] = (self.part[i].astype(f32) + self.inward[i].astype(f32)).astype(bf16)
        self.copy_across(i).start()

    def finish(self, i):
        self.copy_across(i).wait()
        self.part[i] = (self.part[i].astype(f32) + self.across[i].astype(f32)).astype(bf16)
        self.copy_out(i).start()
        self.done(i)

    def steps(self, first, count):
        @pl.when(self.inner)
        def _():
            @pl.loop(first, first + count)
            def _(i):
                self.take_in(i)

                @pl.when(i > 0)
                def _():
                    self.finish(i - 1)

    def settled(self, first, count):
        @pl.when(self.outer)
        def _():
            @pl.loop(first, first + count)
            def _(i):
                self.copy_out(i).wait_recv()
                self.copy_in(i).wait_send()
                self.part[i] = self.inward[i]
                self.done(i)

    def close(self, count):
        @pl.when(self.inner)
        def _():
            self.finish(count - 1)

            @pl.loop(0, count)
            def _(i):
                self.copy_out(i).wait_send()


def near(place):
    return place + 1 - 2 * lax.rem(place, 2)


def greet(peers):
    barrier = pltpu.get_barrier_semaphore()
    for peer in peers:
        pl.semaphore_signal(barrier, inc=1, device_id=peer, device_id_type=MESH)
    pl.semaphore_wait(barrier, len(peers))


def line_peers(place):
    return [{"tp": near(place)}, {"tp": 3 - place}]


def ring_peers(ring):
    return [{"ctx": near(ring)}, {"ctx": lax.rem(ring + 2, 4)}]


def remote(source, target, send, recv, device):
    return pltpu.make_async_remote_copy(
        src_ref=source, dst_ref=target, send_sem=send, recv_sem=recv,
        device_id=device, device_id_type=MESH)


def rows_at(start, size):
    return pl.ds(pl.multiple_of(start, size), size)


class Fold:
    def __init__(self, side, ring, grad, refs, sems, saved, ahead=None):
        self.ahead = ahead
        self.side, self.half = side, lax.rem(ring, 2)
        self.grad = grad
        self.one, self.two, self.three, self.final, self.wide = refs
        self.send, self.recv, self.save = sems
        self.mate, self.peer, self.other = (
            {"ctx": near(ring)}, {"ctx": lax.rem(ring + 2, 4)}, {"fsdp": 1 - side})
        self.saved = saved

    def copy(self, n):
        source, target, device = (
            (self.grad.at[1 - self.half], self.one, self.mate),
            (self.grad.at[self.half, 1 - self.side], self.two, self.other),
            (self.grad.at[self.half, self.side], self.three, self.peer),
            (self.final.at[self.half], self.final.at[self.half], self.mate),
        )[n]
        return remote(source, target, self.send.at[n], self.recv.at[n], device)

    def first(self):
        self.copy(0).start()

    def second(self):
        self.copy(0).wait_recv()
        for side in range(2):
            self.grad[self.half, side] = (
                self.grad[self.half, side].astype(f32) + self.one[side].astype(f32)).astype(bf16)
        self.copy(1).start()

    def third(self):
        self.copy(1).wait_recv()
        self.grad[self.half, self.side] = (
            self.grad[self.half, self.side].astype(f32) + self.two[...].astype(f32)).astype(bf16)
        self.copy(2).start()

    def fourth(self):
        self.copy(2).wait_recv()
        self.final[self.half] = (
            self.grad[self.half, self.side].astype(f32) + self.three[...].astype(f32)).astype(bf16)
        self.copy(3).start()

    def saving(self):
        return pltpu.make_async_copy(self.wide, self.saved, self.save)

    def last(self):
        self.copy(3).wait_recv()
        if self.ahead is not None:
            self.ahead.saving().wait()
        self.wide[...] = self.final[...].astype(f32)
        self.saving().start()

    def settle(self, saving=True):
        for n in range(4):
            self.copy(n).wait_send()
        if saving:
            self.saving().wait()


class Whole:
    def __init__(self, grad, sems, saved):
        self.copy = lambda: pltpu.make_async_copy(grad, saved, sems[2])

    def first(self):
        self.copy().start()

    def second(self):
        pass

    third = fourth = last = second

    def settle(self, saving=True):
        self.copy().wait()


def fold_shapes(shapes, split, shared=False):
    scratch = []
    for n, (r, c) in enumerate(shapes):
        scratch.append(pltpu.VMEM((2, 2, r, c), bf16))
        if split:
            scratch += [pltpu.VMEM((2, r, c), bf16), pltpu.VMEM((r, c), bf16), pltpu.VMEM((r, c), bf16),
                        pltpu.VMEM((2, r, c), bf16)]
            if n == 0 or not shared:
                scratch.append(pltpu.VMEM((2, r, c), f32))
    n = len(shapes)
    dma = pltpu.SemaphoreType.DMA
    scratch += [dma((n, 4)), dma((n, 4)), dma((n,))]
    outs = [
        jax.ShapeDtypeStruct((2, r, c), f32) if split else jax.ShapeDtypeStruct((2, 2, r, c), bf16)
        for r, c in shapes]
    return scratch, outs


def make_folds(split, side, ring, scratch, saved, shared=False):
    send, recv, save = scratch[-3:]
    folds, grads = [], []
    at = 0
    for n, target in enumerate(saved):
        sems = (send.at[n], recv.at[n], save.at[n])
        grads.append(scratch[at])
        if not split:
            folds.append(Whole(scratch[at], sems, target))
            at += 1
            continue
        own_wide = n == 0 or not shared
        refs = list(scratch[at + 1 : at + 5]) + [scratch[at + 5] if own_wide else scratch[5]]
        folds.append(Fold(side, ring, scratch[at], refs, sems, target, None if own_wide else folds[-1]))
        at += 6 if own_wide else 5
    return folds, grads


def turn(values, cosine, sine, sign=1.0):
    pieces = []
    half = HEAD_DIM // 2
    sine = sine * sign
    for at in range(0, values.shape[1], 128):
        piece = values[:, at : at + 128]
        swapped = jnp.where(
            low_half(piece.shape), pltpu.roll(piece, 128 - half, 1), pltpu.roll(piece, half, 1))
        pieces.append(piece * cosine + swapped * sine)
    return jnp.concatenate(pieces, axis=1)


def spread(target, values_t, start, rows):
    owner = lax.broadcasted_iota(jnp.int32, values_t.shape, 0) // HEAD_DIM
    for h in range(values_t.shape[0] // HEAD_DIM):
        target[h // 2, :, rows_at(h % 2 * rows + start, values_t.shape[1])] = jnp.where(
            owner == h, values_t, 0.0).astype(bf16)


def gain_row(gains, which):
    return jnp.concatenate([gains[0, which : which + 1, :], gains[1, which : which + 1, :]], axis=1)


def front_kernel(split, *refs):
    place, ring, side = lax.axis_index("tp"), lax.axis_index("ctx"), lax.axis_index("fsdp")
    (tok, fv, cot_hbm, gain_in, wq_in, wk_in, wv_in, wo_in, wg_in, wu_in, wd_in), refs = refs[:11], refs[11:]
    (frequency, prefix, sum_hbm, late_hbm, q_out, kv_hbm, ctx_out, lse_out, gains, cosine, sine), refs = (
        refs[:11], refs[11:])
    saved, refs = refs[:3], refs[3:]
    if split:
        (wq_hbm, wk_hbm, wv_hbm, wo_hbm), refs = refs[:4], refs[4:]
        (wq, wk, wv, wo, w_send, w_recv, w_save, g_sems), refs = refs[:8], refs[8:]
    else:
        wq, wk, wv, wo = wq_in, wk_in, wv_in, wo_in
    (normed_s, kv, qtm, vt, acct, maxes, totals, part, inward, across,
     kv_send, kv_recv, kv_save, send_one, recv_one, send_two, recv_two, save,
     wg, wu, wd, loads, cot, inner_t, gg_t, ug_t, late, late_save), refs = refs[:28], refs[28:]
    (fold_d, fold_g, fold_u), grads = make_folds(split, side, ring, refs, saved, True)
    seqs, rows, width = q_out.shape
    heads = width // HEAD_DIM
    tile = 256
    chunk, dim = part.shape[1:]
    per_seq = rows // chunk
    per_tile = tile // chunk
    middle = dim // 2
    units = wg_in.shape[-2]
    mate, peer = ring_peers(ring)
    half = lax.rem(ring, 2)
    blocks = (ring, near(ring), lax.rem(ring + 2, 4), 3 - ring)
    for full in (wg, wu, wd):
        for piece in range(2):
            full[piece, units:] = jnp.zeros((full.shape[1] - units, full.shape[2]), bf16)
    own_loads = [pltpu.make_async_copy(cot_hbm, cot, loads.at[6])]
    for n, (source, full) in enumerate(((wg_in, wg), (wu_in, wu), (wd_in, wd))):
        if split:
            own_loads.append(pltpu.make_async_copy(source, full.at[side, 0:units], loads.at[n]))
        else:
            for piece in range(2):
                own_loads.append(pltpu.make_async_copy(
                    source.at[piece], full.at[piece, 0:units], loads.at[2 * n + piece]))
    greet(line_peers(place) + ring_peers(ring) + ([{"fsdp": 1 - side}] if split else []))

    if split:
        other = {"fsdp": 1 - side}
        gains[side, 0:2, :] = gain_in[...]
        move_gains = remote(gains.at[side], gains.at[side], g_sems.at[0], g_sems.at[1], other)
        move_gains.start()

        def spot(full, owner, part_at, size):
            if full.shape[0] == 2:
                return full.at[owner, rows_at(part_at * size, size)]
            return full.at[rows_at((2 * owner + part_at) * size, size)]

        table = (
            (wk_in, wk, spot), (wv_in, wv, spot), (wq_in, wq, spot), (wo_in, wo, spot),
            (wg_in, wg, spot), (wu_in, wu, spot), (wd_in, wd, spot))

        def cross(n):
            own, full, where = table[n]
            size = own.shape[0] // 2
            return remote(own.at[rows_at(half * size, size)], where(full, side, half, size),
                          w_send.at[n, 0], w_recv.at[n, 0], other)

        def onto_mate(n):
            own, full, where = table[n]
            here = where(full, 1 - side, half, own.shape[0] // 2)
            return remote(here, here, w_send.at[n, 1], w_recv.at[n, 1], mate)

        def hand_on(n):
            cross(n).wait_recv()
            onto_mate(n).start()

        saves = tuple(
            pltpu.make_async_copy(full, target, w_save.at[n])
            for n, (full, target) in enumerate(((wk, wk_hbm), (wv, wv_hbm), (wq, wq_hbm), (wo, wo_hbm))))
        for n in range(2):
            cross(n).start()
        for own, full, _ in table[:3]:
            full[rows_at(side * own.shape[0], own.shape[0]), :] = own[...]
        wo[side] = wo_in[...]
        remote(gains.at[side], gains.at[side], g_sems.at[0], g_sems.at[1], other).wait()
    else:
        size = gains.shape[2]
        for piece in range(2):
            gains[piece, 0:2, :] = gain_in[:, piece * size : (piece + 1) * size]

    for load in own_loads:
        load.start()

    def pass_block(s, source, target, device, slot):
        return remote(kv.at[s, source], kv.at[s, target], kv_send.at[s, slot], kv_recv.at[s, target], device)

    to_mate = lambda s: pass_block(s, 0, 1, mate, 0)
    to_peer = lambda s: pass_block(s, 0, 2, peer, 1)
    onward = lambda s: pass_block(s, 2, 3, mate, 2)
    gain_one = gain_row(gains, 0)
    position = (ring * rows + lax.broadcasted_iota(jnp.int32, cosine.shape, 0)).astype(f32)
    angles = position * frequency[0:1, :]
    cosine[...] = jnp.cos(angles)
    sine[...] = jnp.sin(angles) * jnp.where(low_half(cosine.shape), -1.0, 1.0)

    for s in range(seqs):
        @pl.loop(0, rows // tile)
        def _(t):
            at = rows_at(t * tile, tile)
            normed_s[s, at, :] = (unit_norm(tok[s, at, :].astype(f32)) * gain_one).astype(bf16)

    if split:
        hand_on(0)
        hand_on(1)
        for n in range(2, 4):
            cross(n).start()
        onto_mate(0).wait_recv()
        onto_mate(1).wait_recv()

    for s in range(seqs):
        @pl.loop(0, rows // tile)
        def _(t):
            at = rows_at(t * tile, tile)
            normed = normed_s[s, at, :]
            k = dot(normed, wk[...])
            kv[s, 0, 0, at, :] = turn(k, cosine[at, :], sine[at, :]).astype(bf16)
            v = dot(normed, wv[...])
            kv[s, 0, 1, at, :] = (0.5 * v + 0.5 * fv[s, at, :].astype(f32)).astype(bf16)

        to_peer(s).start()
        to_mate(s).start()

    if split:
        hand_on(2)
        hand_on(3)
        for n in range(4, 7):
            cross(n).start()
        onto_mate(2).wait_recv()

    for s in range(seqs):
        @pl.loop(0, rows // tile)
        def _(t):
            at = rows_at(t * tile, tile)
            q = dot(normed_s[s, at, :], wq[...])
            q = turn(q, cosine[at, :], sine[at, :]) * HEAD_DIM ** (-0.5)
            q_out[s, at, :] = q.astype(bf16)
            spread(qtm.at[s], jnp.transpose(q), t * tile, rows)

    def saving(i):
        return pltpu.make_async_copy(part.at[i], sum_hbm.at[i], save.at[i])

    sums = Sum(
        place, part, inward, across, (send_one, recv_one, send_two, recv_two), lambda i: saving(i).start())

    def attend_block(s, j, block, steps):
        vt[...] = jnp.transpose(kv[s, j, 1])
        key_pos = block * rows + lax.broadcasted_iota(jnp.int32, (rows, 1), 0)
        query_pos = ring * rows + lax.rem(lax.broadcasted_iota(jnp.int32, (1, 2 * rows), 1), rows)
        seen = key_pos < jnp.maximum(query_pos + 1, prefix[s])

        @pl.loop(0, heads // 2)
        def _(h):
            scores = jnp.where(seen, dot(kv[s, j, 0], qtm[s, h]), masked_score)
            old = maxes[h]
            new = jnp.maximum(old, jnp.max(scores, axis=0, keepdims=True))
            weights = jnp.exp(scores - new)
            fade = jnp.exp(old - new)
            maxes[h] = new
            totals[h] = totals[h] * fade + jnp.sum(weights, axis=0, keepdims=True)
            low = weights.astype(bf16)
            for n in range(2):
                of_head = rows_at((2 * h + n) * HEAD_DIM, HEAD_DIM)
                lanes = slice(n * rows, (n + 1) * rows)
                acct[of_head, :] = acct[of_head, :] * fade[:, lanes] + dot(vt[of_head, :], low[:, lanes])
            if steps is not None:
                sums.steps(steps + h, 1)

    for s in range(seqs):
        maxes[...] = jnp.full_like(maxes, masked_score)
        totals[...] = jnp.zeros_like(totals)
        acct[...] = jnp.zeros_like(acct)
        begun = lambda j: None if s == 0 else (s - 1) * per_seq + 2 * j
        attend_block(s, 0, blocks[0], begun(0))
        to_mate(s).wait_recv()
        attend_block(s, 1, blocks[1], begun(1))
        to_peer(s).wait_recv()
        onward(s).start()
        attend_block(s, 2, blocks[2], begun(2))
        onward(s).wait_recv()
        attend_block(s, 3, blocks[3], begun(3))
        pltpu.make_async_copy(kv.at[s], kv_hbm.at[s], kv_save.at[s]).start()
        for h in range(heads):
            if h % 2 == 0:
                lse_out[s, h // 2 : h // 2 + 1, :] = maxes[h // 2] + jnp.log(totals[h // 2])
            of_head = slice(h * HEAD_DIM, (h + 1) * HEAD_DIM)
            acct[of_head, :] = acct[of_head, :] / totals[h // 2][:, h % 2 * rows : (h % 2 + 1) * rows]
        ctx_out[s] = jnp.transpose(acct[...]).astype(bf16)
        if split and s == 0:
            onto_mate(3).wait_recv()
            for copy in saves:
                copy.start()

        @pl.loop(0, rows // tile)
        def _(t):
            context = ctx_out[s, rows_at(t * tile, tile), :]
            n = s * per_seq + t * (tile // chunk)
            sums.fill(n, 0, dot(context, wo[0]))
            sums.fill(n, 1, dot(context, wo[1]))
            sums.offer(n, tile // chunk)

        if split and s == 0:
            hand_on(4)
            hand_on(5)
        if split and s == seqs - 1:
            hand_on(6)

    if split:
        for n in range(4, 7):
            onto_mate(n).wait_recv()
    for load in own_loads:
        load.wait()
    lines = seqs * per_seq
    early = 2 * lines
    count = part.shape[0]
    per_seq_tiles = rows // tile
    tiles = seqs * per_seq_tiles
    gain_two = gain_row(gains, 1)
    sums.steps(per_seq, 1)

    def across_both(left, full):
        return dot_nt(left[:, :middle], full[0]) + dot_nt(left[:, middle:], full[1])

    def saving_late(t):
        mine = pl.ds((t - 1) * per_tile, per_tile)
        return pltpu.make_async_copy(late.at[mine], late_hbm.at[mine], late_save.at[t - 1])

    @pl.loop(0, tiles)
    def _(t):
        s, at = t // per_seq_tiles, rows_at(lax.rem(t, per_seq_tiles) * tile, tile)
        flat = rows_at(t * tile, tile)
        mine = t * per_tile
        final = t == tiles - 1

        @pl.when(final)
        def _():
            sums.steps(lines - 1, 2)

        sums.settled(mine, per_tile)
        begun = per_seq + 1 + 2 * t + jnp.where(final, 2, 0)
        attended = jnp.concatenate([part[mine + k] for k in range(per_tile)], axis=0)
        hidden = tok[s, at, :].astype(f32) + attended.astype(f32)
        normed = (unit_norm(hidden) * gain_two).astype(bf16)
        normed_s[s, at, :] = normed
        gate = across_both(normed, wg)
        up = across_both(normed, wu)
        sigmoid = jax.nn.sigmoid(gate)
        swish = gate * sigmoid
        inner = (swish * up).astype(bf16)
        inner_t[:, flat] = jnp.transpose(inner)
        inner_grad = across_both(cot[s, at, :], wd)
        gate_grad = (inner_grad * up * sigmoid * (1.0 + gate * (1.0 - sigmoid))).astype(bf16)
        up_grad = (inner_grad * swish).astype(bf16)
        sums.steps(begun, 1)
        for piece in range(2):
            sums.fill(lines + mine, piece, dot(gate_grad, wg[piece]) + dot(up_grad, wu[piece]))
        sums.offer(lines + mine, per_tile)
        feeds = [dot(inner, wd[piece]) for piece in range(2)]

        @pl.when(t == 0)
        def _():
            for piece in range(2):
                sums.fill(early, piece, feeds[piece])

        @pl.when(t > 0)
        def _():
            for piece in range(2):
                for k in range(per_tile):
                    late[mine - per_tile + k, :, piece * middle : (piece + 1) * middle] = feeds[piece][
                        k * chunk : (k + 1) * chunk].astype(bf16)
            saving_late(t).start()

        gg_t[:, flat] = jnp.transpose(gate_grad)
        ug_t[:, flat] = jnp.transpose(up_grad)
        sums.steps(begun + 1, 1)

    sums.offer(early, count - early)
    deep = units // 2

    def weight_grad(n, left_t, right):
        for h in range(2):
            for y in range(2):
                total = jnp.zeros((deep, middle), f32)
                for s in range(seqs):
                    total = total + dot(
                        left_t[h * deep : (h + 1) * deep, s * rows : (s + 1) * rows],
                        right[s, :, y * middle : (y + 1) * middle])
                grads[n][h, y] = total.astype(bf16)

    begun = lines + 3
    weight_grad(0, inner_t, cot)
    fold_d.first()
    sums.steps(begun, 1)
    weight_grad(1, gg_t, normed_s)
    fold_g.first()
    fold_d.second()
    sums.steps(begun + 1, 1)
    weight_grad(2, ug_t, normed_s)
    fold_u.first()
    fold_g.second()
    sums.steps(begun + 2, 1)
    fold_u.second()
    sums.steps(begun + 3, 2)
    fold_d.third()
    sums.steps(begun + 5, 3)
    fold_g.third()
    fold_d.fourth()
    sums.steps(begun + 8, 3)
    fold_u.third()
    fold_g.fourth()
    fold_d.last()
    sums.steps(begun + 11, 3)
    fold_u.fourth()
    fold_g.last()
    sums.steps(begun + 14, count - begun - 14)
    fold_u.last()
    sums.settled(lines, count - lines)
    sums.close(count)
    for fold in (fold_d, fold_g):
        fold.settle(False)
    fold_u.settle()
    for t in range(1, tiles):
        saving_late(t).wait()
    for s in range(seqs):
        to_mate(s).wait_send()
        to_peer(s).wait_send()
        onward(s).wait_send()
        pltpu.make_async_copy(kv.at[s], kv_hbm.at[s], kv_save.at[s]).wait()

    @pl.loop(0, count)
    def _(i):
        saving(i).wait()

    if split:
        for n in range(7):
            cross(n).wait_send()
            onto_mate(n).wait_send()
        for copy in saves:
            copy.wait()


def limits(ident, megabytes=60):
    return pltpu.CompilerParams(
        collective_id=ident, has_side_effects=True, vmem_limit_bytes=megabytes * 1024 * 1024)


def front(split, tok, fv, cot, gains, square, wide, frequency, prefix):
    seqs, rows, dim = tok.shape
    width, units = square[0].shape[1], wide[0].shape[-2]
    heads = width // HEAD_DIM
    chunk, tile = 64, 256
    tokens = seqs * rows
    count = 2 * tokens // chunk + tile // chunk
    after = (tokens - tile) // chunk
    padded = -(-units // 256) * 256
    vmem = pl.BlockSpec(memory_space=pltpu.VMEM)
    anyw = pl.BlockSpec(memory_space=pl.ANY)
    dma = pltpu.SemaphoreType.DMA
    lines = pltpu.VMEM((count, chunk, dim), bf16)
    shape = jax.ShapeDtypeStruct
    full = [(dim, width)] * 3 + [(2, width, dim // 2)]
    fold_scratch, fold_outs = fold_shapes([(units // 2, dim // 2)] * 3, split, True)
    outs = [
        shape((count, chunk, dim), bf16), shape((after, chunk, dim), bf16), shape((seqs, rows, width), bf16),
        shape((seqs, 4, 2, rows, width), bf16), shape((seqs, rows, width), bf16),
        shape((seqs, heads // 2, 2 * rows), f32), shape((2, 8, dim // 2), f32),
        shape((rows, 128), f32), shape((rows, 128), f32)] + fold_outs
    out_specs = [anyw, anyw, vmem, anyw, vmem, vmem, vmem, vmem, vmem] + [anyw] * 3
    scratch = []
    if split:
        outs += [shape(size, bf16) for size in full]
        out_specs += [anyw] * 4
        scratch = [pltpu.VMEM(size, bf16) for size in full] + [dma((7, 2)), dma((7, 2)), dma((4,)), dma((2,))]
    scratch += [
        pltpu.VMEM((seqs, rows, dim), bf16),
        pltpu.VMEM((seqs, 4, 2, rows, width), bf16),
        pltpu.VMEM((seqs, heads // 2, width, 2 * rows), bf16),
        pltpu.VMEM((width, rows), bf16),
        pltpu.VMEM((width, rows), f32),
        pltpu.VMEM((heads // 2, 1, 2 * rows), f32),
        pltpu.VMEM((heads // 2, 1, 2 * rows), f32),
        lines, lines, lines,
        dma((seqs, 3)), dma((seqs, 4)), dma((seqs,)),
        dma((count,)), dma((count,)), dma((count,)), dma((count,)), dma((count,)),
        pltpu.VMEM((2, padded, dim // 2), bf16),
        pltpu.VMEM((2, padded, dim // 2), bf16),
        pltpu.VMEM((2, padded, dim // 2), bf16),
        dma((7,)),
        pltpu.VMEM((seqs, rows, dim), bf16),
        pltpu.VMEM((padded, tokens), bf16),
        pltpu.VMEM((padded, tokens), bf16),
        pltpu.VMEM((padded, tokens), bf16),
        pltpu.VMEM((after, chunk, dim), bf16),
        dma((tokens // tile,)),
    ] + fold_scratch
    return pl.pallas_call(
        functools.partial(front_kernel, split),
        name="front",
        out_shape=outs,
        in_specs=[vmem] * 2 + [anyw] + [vmem] * 5 + [anyw] * 3 + [vmem, pl.BlockSpec(memory_space=pltpu.SMEM)],
        out_specs=out_specs,
        scratch_shapes=scratch,
        compiler_params=limits(0, 63),
        cost_estimate=pl.CostEstimate(flops=22 * 10**9, bytes_accessed=2 * 10**7, transcendentals=10**7),
    )(tok, fv, cot, gains, *square, *wide, frequency, prefix)


def back_kernel(split, *refs):
    place, ring, side = lax.axis_index("tp"), lax.axis_index("ctx"), lax.axis_index("fsdp")
    loaded, refs = refs[:11], refs[11:]
    (gain_in, lse, cosine, sine, prefix, block_hbm, token_hbm, fv_out, gain_out), saved, refs = (
        refs[:9], refs[9:13], refs[13:])
    (tok, cot, wq, wk, wv, wo, q, kv, ctx, attn, mixed, early), refs = refs[:12], refs[12:]
    (hid, branch, qtm, qm, otm, om, kt, delta, dqt, dk, dv, give, take, proj, normed_t,
     part, inward, across, gain_part, gain_all,
     kv_send, kv_recv, send_one, recv_one, send_two, recv_two, save, gain_send, gain_recv, loads), refs = (
        refs[:30], refs[30:])
    (fold_o, fold_k, fold_v, fold_q), (dwo, dwk, dwv, dwq) = make_folds(split, side, ring, refs, saved)
    late_hbm, sum_hbm, tok_hbm, cot_hbm, wq_hbm, wk_hbm, wv_hbm, wo_hbm, q_hbm, kv_hbm, ctx_hbm = loaded
    seqs, rows, dim = tok.shape
    width = wq.shape[1]
    heads = width // HEAD_DIM
    chunk = part.shape[1]
    per_seq = rows // chunk
    tile = 256
    per_tile = tile // chunk
    middle = dim // 2
    lines = seqs * per_seq
    count = 2 * lines - per_tile
    head_start, rest = per_seq, per_seq - per_tile
    rest_start = head_start + per_seq
    own_start = (head_start, rest_start + rest)
    mate, peer = ring_peers(ring)
    blocks = (ring, near(ring), lax.rem(ring + 2, 4), 3 - ring)
    others = [(dy, dc) for dy in range(2) for dc in range(4) if dy or dc]
    group = [{"fsdp": lax.rem(side + dy, 2), "ctx": lax.rem(ring + dc, 4)} for dy, dc in others]

    copies = {}

    def load(name, source, target):
        copies[name] = pltpu.make_async_copy(source, target, loads.at[len(copies)])
        copies[name].start()

    def ready(*names):
        for name in names:
            copies[name].wait()

    load("late", late_hbm.at[0:head_start], part.at[0:head_start])
    for s in range(seqs):
        mine = slice(s * per_seq, (s + 1) * per_seq)
        load(f"tok{s}", tok_hbm.at[s], tok.at[s])
        load(f"attn{s}", sum_hbm.at[mine], attn.at[mine])
        load(f"cot{s}", cot_hbm.at[s], cot.at[s])
        load(f"mixed{s}", sum_hbm.at[lines + s * per_seq : lines + (s + 1) * per_seq], mixed.at[mine])
        if s == 0:
            load("wo", wo_hbm, wo)
        load(f"q{s}", q_hbm.at[s], q.at[s])
        load(f"ctx{s}", ctx_hbm.at[s], ctx.at[s])
        load(f"kv{s}", kv_hbm.at[s], kv.at[s])
    load("rest", late_hbm.at[head_start : head_start + rest], part.at[rest_start : rest_start + rest])
    load("early", sum_hbm.at[2 * lines : 2 * lines + per_tile], early)
    load("wq", wq_hbm, wq)
    load("wk", wk_hbm, wk)
    load("wv", wv_hbm, wv)
    greet(line_peers(place) + (group if split else ring_peers(ring)))
    gain_one, gain_two = gain_row(gain_in, 0), gain_row(gain_in, 1)
    gain_part[...] = jnp.zeros_like(gain_part)

    def chunk_at(n):
        return n // per_seq, rows_at(lax.rem(n, per_seq) * chunk, chunk)

    def saving_block(i, n):
        s, own = chunk_at(n)
        return pltpu.make_async_copy(across.at[i], block_hbm.at[s, own], save.at[i])

    def saving_early(n):
        return pltpu.make_async_copy(early.at[n], block_hbm.at[0, n * chunk : (n + 1) * chunk], save.at[count + n])

    def saving_token(i, n):
        s, own = chunk_at(n)
        return pltpu.make_async_copy(hid.at[s, own], token_hbm.at[s, own], save.at[i])

    def add_gain(which, value):
        for piece in range(2):
            gain_part[piece, which : which + 1, :] += value[:, piece * middle : (piece + 1) * middle]

    is_block = lambda i: (i < head_start) | ((i >= rest_start) & (i < own_start[1]))
    block_of = lambda i: per_tile + jnp.where(i < head_start, i, i - per_seq)
    token_of = lambda i: jnp.where(i < rest_start, i - head_start, i - own_start[1] + per_seq)

    def done(i):
        @pl.when(is_block(i))
        def _():
            n = block_of(i)
            s, own = chunk_at(n)
            across[i] = (
                tok[s, own, :].astype(f32) + attn[n].astype(f32) + part[i].astype(f32)).astype(bf16)
            saving_block(i, n).start()

        @pl.when(jnp.logical_not(is_block(i)))
        def _():
            n = token_of(i)
            s, own = chunk_at(n)
            values, upstream = tok[s, own, :].astype(f32), part[i].astype(f32)
            factor = lax.rsqrt(jnp.mean(values * values, axis=-1, keepdims=True) + epsilon)
            scaled = upstream * gain_one
            add_gain(0, jnp.sum(upstream * values * factor, axis=0, keepdims=True))
            hid[s, own, :] += factor * scaled - values * factor**3 * jnp.mean(
                scaled * values, axis=-1, keepdims=True)
            saving_token(i, n).start()

    sums = Sum(place, part, inward, across, (send_one, recv_one, send_two, recv_two), done)

    def move(s, source, target, device):
        return remote(give.at[source], take.at[s, target], kv_send.at[source], kv_recv.at[s, target], device)

    far_to_mate = lambda s: move(s, 2, 0, mate)
    peer_back = lambda s: move(s, 1, 1, peer)
    near_to_mate = lambda s: move(s, 0, 2, mate)
    ready("late")
    sums.offer(0, head_start)

    def hidden_stage(s):
        ready(f"tok{s}", f"attn{s}", f"cot{s}", f"mixed{s}", f"q{s}", f"ctx{s}")

        @pl.loop(0, rows // tile)
        def _(t):
            at = rows_at(t * tile, tile)
            first = s * per_seq + t * per_tile
            join = lambda ref: jnp.concatenate([ref[first + k] for k in range(per_tile)], axis=0).astype(f32)
            token = tok[s, at, :].astype(f32)
            values = token + join(attn)
            upstream = join(mixed)
            factor = lax.rsqrt(jnp.mean(values * values, axis=-1, keepdims=True) + epsilon)
            scaled = upstream * gain_two
            add_gain(1, jnp.sum(upstream * values * factor, axis=0, keepdims=True))
            hid_now = cot[s, at, :].astype(f32) + factor * scaled - values * factor**3 * jnp.mean(
                scaled * values, axis=-1, keepdims=True)
            hid[s, at, :] = hid_now
            low = hid_now.astype(bf16)
            branch[s, at, :] = low
            left, right = low[:, :middle], low[:, middle:]
            grad = dot_nt(left, wo[0]) + dot_nt(right, wo[1])
            lane_owner = lax.broadcasted_iota(jnp.int32, grad.shape, 1) // HEAD_DIM
            q_now = q[s, at, :].astype(f32)
            grad_t = jnp.transpose(grad)
            q_t = jnp.transpose(q_now)
            product = jnp.transpose(grad.astype(bf16).astype(f32) * ctx[s, at, :].astype(f32))
            for h in range(heads):
                low_rows = rows_at(h % 2 * rows + t * tile, tile)
                om[h // 2, low_rows, :] = jnp.where(lane_owner == h, grad, 0.0).astype(bf16)
                qm[h // 2, low_rows, :] = jnp.where(lane_owner == h, q_now, 0.0).astype(bf16)
                delta[h // 2, :, low_rows] = jnp.sum(
                    product[h * HEAD_DIM : (h + 1) * HEAD_DIM], axis=0, keepdims=True)
            spread(otm, grad_t, t * tile, rows)
            spread(qtm, q_t, t * tile, rows)
            normed = (unit_norm(token) * gain_one).astype(bf16)
            normed_t[:, rows_at(s * rows + t * tile, tile)] = jnp.transpose(normed)

    def back_block(s, j):
        kt[...] = jnp.transpose(kv[s, j, 0])
        key_pos = blocks[j] * rows + lax.broadcasted_iota(jnp.int32, (rows, 1), 0)
        query_pos = ring * rows + lax.rem(lax.broadcasted_iota(jnp.int32, (1, 2 * rows), 1), rows)
        seen = key_pos < jnp.maximum(query_pos + 1, prefix[s])
        dk[...] = jnp.zeros_like(dk)
        dv[...] = jnp.zeros_like(dv)

        @pl.loop(0, heads // 2)
        def _(h):
            scores = dot(kv[s, j, 0], qtm[h])
            probs = jnp.where(seen, jnp.exp(scores - lse[s, pl.ds(h, 1), :]), 0.0)
            dprobs = dot(kv[s, j, 1], otm[h])
            dv[...] += dot(probs.astype(bf16), om[h])
            dscores = (probs * (dprobs - delta[h])).astype(bf16)
            dk[...] += dot(dscores, qm[h])
            for n in range(2):
                of_head = rows_at((2 * h + n) * HEAD_DIM, HEAD_DIM)
                dqt[of_head, :] += dot(kt[of_head, :], dscores[:, n * rows : (n + 1) * rows])

    def finalize(s):
        near_to_mate(s).wait_recv()
        peer_back(s).wait_recv()
        if s == 0:
            ready("wq", "wk", "wv", "rest")

        @pl.loop(0, rows // tile)
        def _(t):
            at = rows_at(t * tile, tile)
            flat = rows_at(s * rows + t * tile, tile)
            co, si = cosine[at, :], sine[at, :]
            grad_v = 0.5 * (dv[at, :] + take[s, 2, 1, at, :].astype(f32) + take[s, 1, 1, at, :].astype(f32))
            grad_k = dk[at, :] + take[s, 2, 0, at, :].astype(f32) + take[s, 1, 0, at, :].astype(f32)
            grad_q = jnp.transpose(dqt[:, at]) * HEAD_DIM ** (-0.5)
            proj[0, flat, :] = turn(grad_q, co, si, -1.0).astype(bf16)
            proj[1, flat, :] = turn(grad_k, co, si, -1.0).astype(bf16)
            proj[2, flat, :] = grad_v.astype(bf16)
            fv_out[s, at, :] = grad_v
            i = own_start[s] + t * per_tile
            for piece in range(2):
                cut = slice(piece * middle, (piece + 1) * middle)
                sums.fill(i, piece, dot_nt(proj[0, flat, :], wq[cut, :]) + dot_nt(
                    proj[1, flat, :], wk[cut, :]) + dot_nt(proj[2, flat, :], wv[cut, :]))
            sums.offer(i, per_tile)

        if s == 0:
            sums.offer(rest_start, rest)

    ready("wo")
    hidden_stage(0)
    sums.steps(0, 1)
    begun = 1
    for s in range(seqs):
        last = s == seqs - 1
        ready(f"kv{s}")
        dqt[...] = jnp.zeros_like(dqt)
        back_block(s, 3)
        if s > 0:
            far_to_mate(s - 1).wait_send()
        give[2, 0] = dk[...].astype(bf16)
        give[2, 1] = dv[...].astype(bf16)
        far_to_mate(s).start()
        sums.steps(begun, 1)
        if last:
            fold_o.second()
        back_block(s, 2)
        far_to_mate(s).wait_recv()
        if s > 0:
            peer_back(s - 1).wait_send()
        give[1, 0] = (dk[...] + take[s, 0, 0].astype(f32)).astype(bf16)
        give[1, 1] = (dv[...] + take[s, 0, 1].astype(f32)).astype(bf16)
        peer_back(s).start()
        sums.steps(begun + 1, 1)
        back_block(s, 1)
        if s > 0:
            near_to_mate(s - 1).wait_send()
        give[0, 0] = dk[...].astype(bf16)
        give[0, 1] = dv[...].astype(bf16)
        near_to_mate(s).start()
        sums.steps(begun + 2, 1)
        if last:
            fold_o.third()
        back_block(s, 0)
        sums.steps(begun + 3, 1)
        if not last:
            hidden_stage(s + 1)
            sums.steps(begun + 4, 2)
        finalize(s)
        sums.steps(begun + (6 if not last else 4), 1)
        begun += 7 if not last else 5
        if s == seqs - 2:
            deep = dwo.shape[2]
            total = jnp.zeros((width, dim), f32)
            for r in range(seqs):
                total = total + dot(jnp.transpose(ctx[r]), branch[r])
            for h in range(2):
                for y in range(2):
                    dwo[h, y] = total[h * deep : (h + 1) * deep, y * middle : (y + 1) * middle].astype(bf16)
            fold_o.first()
            sums.steps(begun, 1)
            begun += 1

    share = dwq.shape[2]

    def square_grad(target, which):
        @pl.loop(0, 4)
        def _(k):
            h, y = k // 2, lax.rem(k, 2)
            target[h, y] = dot(normed_t[rows_at((2 * y + h) * share, share), :], proj[which]).astype(bf16)

    ready("early")
    for n in range(per_tile):
        own = slice(n * chunk, (n + 1) * chunk)
        early[n] = (tok[0, own, :].astype(f32) + attn[n].astype(f32) + early[n].astype(f32)).astype(bf16)
        saving_early(n).start()
    square_grad(dwk, 1)
    fold_k.first()
    sums.steps(begun, 1)
    square_grad(dwv, 2)
    fold_v.first()
    fold_k.second()
    sums.steps(begun + 1, 1)
    square_grad(dwq, 0)
    fold_q.first()
    fold_v.second()
    sums.steps(begun + 2, 1)
    fold_q.second()
    fold_o.fourth()
    sums.steps(begun + 3, 2)
    fold_k.third()
    sums.steps(begun + 5, 1)
    fold_v.third()
    sums.steps(begun + 6, 1)
    fold_q.third()
    fold_k.fourth()
    sums.steps(begun + 7, 1)
    fold_v.fourth()
    sums.steps(begun + 8, 1)
    fold_q.fourth()
    for fold in (fold_o, fold_k, fold_v):
        fold.last()
    sums.steps(begun + 9, count - begun - 9)
    fold_q.last()
    sums.settled(0, count)
    sums.close(count)
    if split:
        me = 4 * side + ring
        gain_all[me] = gain_part[side]

        def share_gain(n):
            dy, dc = others[n]
            y = lax.rem(side + dy, 2)
            return remote(gain_part.at[y], gain_all.at[me], gain_send.at[n], gain_recv.at[n], group[n])

        for n in range(7):
            share_gain(n).start()
        for n in range(7):
            share_gain(n).wait()
        total = gain_all[0]
        for n in range(1, 8):
            total = total + gain_all[n]
        gain_out[...] = total
    else:
        gain_out[...] = gain_part[...]
    for fold in (fold_o, fold_k, fold_v, fold_q):
        fold.settle()
    for copy in (far_to_mate, peer_back, near_to_mate):
        copy(seqs - 1).wait_send()

    for n in range(per_tile):
        saving_early(n).wait()

    @pl.loop(0, count)
    def _(i):
        @pl.when(is_block(i))
        def _():
            saving_block(i, block_of(i)).wait()

        @pl.when(jnp.logical_not(is_block(i)))
        def _():
            saving_token(i, token_of(i)).wait()


def back(split, tok, cot, sums, late, gains, square, q, kv, ctx, lse, cosine, sine, prefix):
    seqs, rows, dim = tok.shape
    width = q.shape[2]
    heads = width // HEAD_DIM
    _, chunk, _ = sums.shape
    tokens = seqs * rows
    early = 256 // chunk
    count = 2 * tokens // chunk - early
    vmem = pl.BlockSpec(memory_space=pltpu.VMEM)
    anyw = pl.BlockSpec(memory_space=pl.ANY)
    dma = pltpu.SemaphoreType.DMA
    lines = pltpu.VMEM((count, chunk, dim), bf16)
    half_lines = pltpu.VMEM((tokens // chunk, chunk, dim), bf16)
    wide = pltpu.VMEM((heads // 2, 2 * rows, width), bf16)
    tall = pltpu.VMEM((heads // 2, width, 2 * rows), bf16)
    shape = jax.ShapeDtypeStruct
    fold_scratch, fold_outs = fold_shapes([(width // 2, dim // 2)] + [(dim // 4, width)] * 3, split)
    loaded = (tok, cot) + tuple(square) + (q, kv, ctx)
    return pl.pallas_call(
        functools.partial(back_kernel, split),
        name="back",
        out_shape=[
            shape((seqs, rows, dim), bf16), shape((seqs, rows, dim), f32), shape((seqs, rows, width), f32),
            shape((8, dim // 2) if split else (2, 8, dim // 2), f32)] + fold_outs,
        in_specs=[anyw] * 11 + [vmem] * 4 + [pl.BlockSpec(memory_space=pltpu.SMEM)],
        out_specs=[anyw, anyw, vmem, vmem] + [anyw] * 4,
        scratch_shapes=[pltpu.VMEM(x.shape, bf16) for x in loaded] + [
            half_lines, half_lines, pltpu.VMEM((early, chunk, dim), bf16),
            pltpu.VMEM((seqs, rows, dim), f32),
            pltpu.VMEM((seqs, rows, dim), bf16),
            tall, wide, tall, wide,
            pltpu.VMEM((width, rows), bf16),
            pltpu.VMEM((heads // 2, 1, 2 * rows), f32),
            pltpu.VMEM((width, rows), f32),
            pltpu.VMEM((rows, width), f32),
            pltpu.VMEM((rows, width), f32),
            pltpu.VMEM((3, 2, rows, width), bf16),
            pltpu.VMEM((seqs, 3, 2, rows, width), bf16),
            pltpu.VMEM((3, tokens, width), bf16),
            pltpu.VMEM((dim, tokens), bf16),
            lines, lines, lines,
            pltpu.VMEM((2, 8, dim // 2), f32),
            pltpu.VMEM((8, 8, dim // 2), f32),
            dma((3,)), dma((seqs, 3)),
            dma((count,)), dma((count,)), dma((count,)), dma((count,)), dma((count + early,)),
            dma((7,)), dma((7,)), dma((8 * seqs + 8,)),
        ] + fold_scratch,
        compiler_params=limits(2, 62),
        cost_estimate=pl.CostEstimate(flops=30 * 10**9, bytes_accessed=10**7, transcendentals=10**7),
    )(late, sums, *loaded, gains, lse, cosine, sine, prefix)


def frequencies():
    half = HEAD_DIM // 2
    lane = np.arange(128) % half
    return np.broadcast_to((rope_base ** (-lane / half)).astype(np.float32), (8, 128))


def halves(weight):
    rows, columns = weight.shape
    return jnp.swapaxes(weight.reshape(rows, 2, columns // 2), 0, 1)


def shards(
    tokens, first_values, norm1_gain, norm2_gain, w_query, w_key, w_value, w_out, w_gate, w_up, w_down,
    prefix, cotangent,
):
    split = lax.axis_size("fsdp") == 2
    seqs, rows, dim = tokens.shape
    width, units = w_query.shape[1], w_gate.shape[1]
    gather = functools.partial(lax.all_gather, axis_name="fsdp", tiled=True)
    if split:
        gains = (norm1_gain, norm2_gain)
        square = (w_query, w_key, w_value, w_out)
        wide = (w_gate.T, w_up.T, w_down)
    else:
        gains = (gather(norm1_gain), gather(norm2_gain))
        square = (gather(w_query), gather(w_key), gather(w_value), halves(gather(w_out, axis=1)))
        wide = (halves(gather(w_gate).T), halves(gather(w_up).T), halves(gather(w_down, axis=1)))
    (sums, late, query, pairs, context, log_total, gain_rows, cosine, sine, down_grad, gate_grad, up_grad,
     *gathered) = front(
        split, tokens, first_values, cotangent, jnp.stack(gains).astype(f32), square, wide, frequencies(), prefix)
    if split:
        square = tuple(gathered)
    block_out, token_grad, half_value_grad, gain_grads, out_grad, key_grad, value_grad, query_grad = back(
        split, tokens, cotangent, sums, late, gain_rows, square, query, pairs, context,
        log_total, cosine, sine, prefix)
    if split:
        over_rows = lambda grad: grad.reshape(-1, grad.shape[-1])
        over_columns = over_rows
        over_turned = lambda grad: over_rows(grad).T
        gain_one_grad, gain_two_grad = gain_grads[0], gain_grads[1]
    else:
        total = lambda grad, axis: lax.psum(
            lax.psum_scatter(grad, "fsdp", scatter_dimension=axis, tiled=True), "ctx").astype(f32)
        over_rows = lambda grad: total(jnp.swapaxes(grad, 0, 1).reshape(-1, grad.shape[-1]), 0)
        over_columns = lambda grad: total(
            jnp.transpose(grad, (0, 2, 1, 3)).reshape(2 * grad.shape[2], -1), 1)
        over_turned = lambda grad: over_columns(grad).T
        gain_one_grad, gain_two_grad = (total(gain_grads[:, n].reshape(-1), 0) for n in range(2))
    return (
        block_out,
        token_grad,
        half_value_grad,
        gain_one_grad,
        gain_two_grad,
        over_rows(query_grad),
        over_rows(key_grad),
        over_rows(value_grad),
        over_columns(out_grad),
        over_turned(gate_grad),
        over_turned(up_grad),
        over_columns(down_grad),
    )


def solution(mesh):
    return jax.shard_map(
        shards,
        mesh=mesh,
        in_specs=(
            P("fsdp", "ctx", None),
            P("fsdp", "ctx", "tp"),
            P("fsdp"),
            P("fsdp"),
            P("fsdp", "tp"),
            P("fsdp", "tp"),
            P("fsdp", "tp"),
            P("tp", "fsdp"),
            P("fsdp", "tp"),
            P("fsdp", "tp"),
            P("tp", "fsdp"),
            P("fsdp"),
            P("fsdp", "ctx", None),
        ),
        out_specs=(
            P("fsdp", "ctx", None),
            P("fsdp", "ctx", None),
            P("fsdp", "ctx", "tp"),
            P("fsdp"),
            P("fsdp"),
            P("fsdp", "tp"),
            P("fsdp", "tp"),
            P("fsdp", "tp"),
            P("tp", "fsdp"),
            P("fsdp", "tp"),
            P("fsdp", "tp"),
            P("tp", "fsdp"),
        ),
        check_vma=False,
    )
```

```python
import functools

import jax
import jax.numpy as jnp
import numpy as np
from jax import lax
from jax.experimental import pallas as pl
from jax.experimental.pallas import tpu as pltpu
from jax.sharding import PartitionSpec as P

HEAD_DIM = 64
epsilon = 1e-06
rope_base = 10000.0
masked_score = -1e30
MESH = pl.DeviceIdType.MESH
bf16 = jnp.bfloat16
f32 = jnp.float32


def dot(a, b):
    return jnp.dot(a, b, preferred_element_type=f32)


def dot_nt(a, b):
    return lax.dot_general(a, b, (((1,), (1,)), ((), ())), preferred_element_type=f32)


def unit_norm(values):
    return values * lax.rsqrt(jnp.mean(values * values, axis=-1, keepdims=True) + epsilon)


def low_half(shape):
    return lax.rem(lax.broadcasted_iota(jnp.int32, shape, 1), HEAD_DIM) < HEAD_DIM // 2


class Sum:
    def __init__(self, place, part, inward, across, sems, done):
        self.pair = near(place)
        self.middle = 3 - place
        self.inner = (place == 1) | (place == 2)
        self.outer = (place == 0) | (place == 3)
        self.part, self.inward, self.across, self.done = part, inward, across, done
        self.send_one, self.recv_one, self.send_two, self.recv_two = sems

    def copy_in(self, i):
        return remote(
            self.part.at[i], self.inward.at[i], self.send_one.at[i], self.recv_one.at[i], {"tp": self.pair})

    def copy_across(self, i):
        return remote(
            self.part.at[i], self.across.at[i], self.send_two.at[i], self.recv_two.at[i], {"tp": self.middle})

    def copy_out(self, i):
        return remote(
            self.part.at[i], self.inward.at[i], self.send_one.at[i], self.recv_one.at[i], {"tp": self.pair})

    def fill(self, first, piece, values):
        chunk, size = self.part.shape[1], values.shape[1]
        for k in range(values.shape[0] // chunk):
            self.part[first + k, :, piece * size : (piece + 1) * size] = values[
                k * chunk : (k + 1) * chunk].astype(bf16)

    def offer(self, first, count):
        @pl.when(self.outer)
        def _():
            @pl.loop(0, count)
            def _(k):
                self.copy_in(first + k).start()

    def take_in(self, i):
        self.copy_in(i).wait_recv()
        self.part[i] = (self.part[i].astype(f32) + self.inward[i].astype(f32)).astype(bf16)
        self.copy_across(i).start()

    def finish(self, i):
        self.copy_across(i).wait()
        self.part[i] = (self.part[i].astype(f32) + self.across[i].astype(f32)).astype(bf16)
        self.copy_out(i).start()
        self.done(i)

    def steps(self, first, count):
        @pl.when(self.inner)
        def _():
            @pl.loop(first, first + count)
            def _(i):
                self.take_in(i)

                @pl.when(i > 0)
                def _():
                    self.finish(i - 1)

    def settled(self, first, count):
        @pl.when(self.outer)
        def _():
            @pl.loop(first, first + count)
            def _(i):
                self.copy_out(i).wait_recv()
                self.copy_in(i).wait_send()
                self.part[i] = self.inward[i]
                self.done(i)

    def close(self, count):
        @pl.when(self.inner)
        def _():
            self.finish(count - 1)

            @pl.loop(0, count)
            def _(i):
                self.copy_out(i).wait_send()


def near(place):
    return place + 1 - 2 * lax.rem(place, 2)


def greet(peers):
    barrier = pltpu.get_barrier_semaphore()
    for peer in peers:
        pl.semaphore_signal(barrier, inc=1, device_id=peer, device_id_type=MESH)
    pl.semaphore_wait(barrier, len(peers))


def block_place(ring, j):
    return jnp.where(
        j == 0, ring, jnp.where(j == 1, near(ring), jnp.where(j == 2, lax.rem(ring + 2, 4), 3 - ring)))


def line_peers(place):
    return [{"tp": near(place)}, {"tp": 3 - place}]


def ring_peers(ring):
    return [{"ctx": near(ring)}, {"ctx": lax.rem(ring + 2, 4)}]


def remote(source, target, send, recv, device):
    return pltpu.make_async_remote_copy(
        src_ref=source, dst_ref=target, send_sem=send, recv_sem=recv,
        device_id=device, device_id_type=MESH)


class Passing:
    def __init__(self, place, spot, sems, own=None):
        self.place, self.spot, self.own = place, spot, own
        self.send, self.recv = sems

    def move(self, piece, item, way, source=None):
        here = self.spot(piece, item)
        return remote(
            here if source is None else source, here, self.send.at[item, way, piece], self.recv.at[item, piece],
            {"tp": self.place + 1 - 2 * way})

    def begin(self, item):
        source = None if self.own is None else self.own(item)

        @pl.when(self.place < 3)
        def _():
            self.move(self.place, item, 0, source).start()

        @pl.when(self.place > 0)
        def _():
            self.move(self.place, item, 1, source).start()

    def step(self, item, distance):
        @pl.when(self.place >= distance)
        def _():
            piece = self.place - distance
            self.move(piece, item, 0).wait_recv()

            @pl.when(self.place < 3)
            def _():
                self.move(piece, item, 0).start()

        @pl.when(self.place + distance <= 3)
        def _():
            piece = self.place + distance
            self.move(piece, item, 1).wait_recv()

            @pl.when(self.place > 0)
            def _():
                self.move(piece, item, 1).start()

    def settle(self, items):
        for item in range(items):
            @pl.loop(0, 4)
            def _(piece, item=item):
                @pl.when((self.place < 3) & (piece <= self.place))
                def _():
                    self.move(piece, item, 0).wait_send()

                @pl.when((self.place > 0) & (piece >= self.place))
                def _():
                    self.move(piece, item, 1).wait_send()


def rows_at(start, size):
    return pl.ds(pl.multiple_of(start, size), size)


class Fold:
    def __init__(self, side, ring, grad, refs, sems, saved, ahead=None):
        self.ahead = ahead
        self.side, self.half = side, lax.rem(ring, 2)
        self.grad = grad
        self.one, self.two, self.three, self.final, self.wide = refs
        self.send, self.recv, self.save = sems
        self.mate, self.peer, self.other = (
            {"ctx": near(ring)}, {"ctx": lax.rem(ring + 2, 4)}, {"fsdp": 1 - side})
        self.saved = saved

    def copy(self, n):
        source, target, device = (
            (self.grad.at[1 - self.half], self.one, self.mate),
            (self.grad.at[self.half, 1 - self.side], self.two, self.other),
            (self.grad.at[self.half, self.side], self.three, self.peer),
            (self.final.at[self.half], self.final.at[self.half], self.mate),
        )[n]
        return remote(source, target, self.send.at[n], self.recv.at[n], device)

    def first(self):
        self.copy(0).start()

    def second(self):
        self.copy(0).wait_recv()
        for side in range(2):
            self.grad[self.half, side] = (
                self.grad[self.half, side].astype(f32) + self.one[side].astype(f32)).astype(bf16)
        self.copy(1).start()

    def third(self):
        self.copy(1).wait_recv()
        self.grad[self.half, self.side] = (
            self.grad[self.half, self.side].astype(f32) + self.two[...].astype(f32)).astype(bf16)
        self.copy(2).start()

    def fourth(self):
        self.copy(2).wait_recv()
        self.final[self.half] = (
            self.grad[self.half, self.side].astype(f32) + self.three[...].astype(f32)).astype(bf16)
        self.copy(3).start()

    def saving(self):
        return pltpu.make_async_copy(self.wide, self.saved, self.save)

    def last(self):
        self.copy(3).wait_recv()
        if self.ahead is not None:
            self.ahead.saving().wait()
        self.wide[...] = self.final[...].astype(f32)
        self.saving().start()

    def settle(self, saving=True):
        for n in range(4):
            self.copy(n).wait_send()
        if saving:
            self.saving().wait()


class Whole:
    def __init__(self, grad, sems, saved):
        self.copy = lambda: pltpu.make_async_copy(grad, saved, sems[2])

    def first(self):
        self.copy().start()

    def second(self):
        pass

    third = fourth = last = second

    def settle(self, saving=True):
        self.copy().wait()


def fold_shapes(shapes, split, shared=False):
    scratch = []
    for n, (r, c) in enumerate(shapes):
        scratch.append(pltpu.VMEM((2, 2, r, c), bf16))
        if split:
            scratch += [pltpu.VMEM((2, r, c), bf16), pltpu.VMEM((r, c), bf16), pltpu.VMEM((r, c), bf16),
                        pltpu.VMEM((2, r, c), bf16)]
            if n == 0 or not shared:
                scratch.append(pltpu.VMEM((2, r, c), f32))
    n = len(shapes)
    dma = pltpu.SemaphoreType.DMA
    scratch += [dma((n, 4)), dma((n, 4)), dma((n,))]
    outs = [
        jax.ShapeDtypeStruct((2, r, c), f32) if split else jax.ShapeDtypeStruct((2, 2, r, c), bf16)
        for r, c in shapes]
    return scratch, outs


def make_folds(split, side, ring, scratch, saved, shared=False):
    send, recv, save = scratch[-3:]
    folds, grads = [], []
    at = 0
    for n, target in enumerate(saved):
        sems = (send.at[n], recv.at[n], save.at[n])
        grads.append(scratch[at])
        if not split:
            folds.append(Whole(scratch[at], sems, target))
            at += 1
            continue
        own_wide = n == 0 or not shared
        refs = list(scratch[at + 1 : at + 5]) + [scratch[at + 5] if own_wide else scratch[5]]
        folds.append(Fold(side, ring, scratch[at], refs, sems, target, None if own_wide else folds[-1]))
        at += 6 if own_wide else 5
    return folds, grads


def turn(values, cosine, sine, sign=1.0):
    pieces = []
    half = HEAD_DIM // 2
    sine = sine * sign
    for at in range(0, values.shape[1], 128):
        piece = values[:, at : at + 128]
        swapped = jnp.where(
            low_half(piece.shape), pltpu.roll(piece, 128 - half, 1), pltpu.roll(piece, half, 1))
        pieces.append(piece * cosine + swapped * sine)
    return jnp.concatenate(pieces, axis=1)


def spread(target, values_t, start, rows):
    owner = lax.broadcasted_iota(jnp.int32, values_t.shape, 0) // HEAD_DIM
    for h in range(values_t.shape[0] // HEAD_DIM):
        target[h // 2, :, rows_at(h % 2 * rows + start, values_t.shape[1])] = jnp.where(
            owner == h, values_t, 0.0).astype(bf16)


def gain_row(gains, which):
    return jnp.concatenate([gains[0, which : which + 1, :], gains[1, which : which + 1, :]], axis=1)


def front_kernel(split, *refs):
    place, ring, side = lax.axis_index("tp"), lax.axis_index("ctx"), lax.axis_index("fsdp")
    (tok, fv, cot_hbm, gain_in, wq_in, wk_in, wv_in, wo_in, wg_in, wu_in, wd_in), refs = refs[:11], refs[11:]
    (frequency, prefix, sum_hbm, late_hbm, q_out, kv_hbm, attn_hbm, ctx_hbm, lse_out, gains, cosine, sine), refs = (
        refs[:12], refs[12:])
    saved, refs = refs[:3], refs[3:]
    if split:
        (wq_hbm, wk_hbm, wv_hbm, wo_hbm), refs = refs[:4], refs[4:]
        (wq, wk, wv, w_send, w_recv, w_save, g_sems, o_send, o_recv), refs = refs[:9], refs[9:]
    else:
        wq, wk, wv = wq_in, wk_in, wv_in
    (normed_s, kv, qtm, vt, acct, maxes, totals, part, inward, across,
     kv_send, kv_recv, kv_save, send_one, recv_one, send_two, recv_two, save,
     wg, wu, wd, loads, cot, inner_t, gg_t, ug_t, late, late_save, wo_all, ctx_all, attn,
     p_send, p_recv, c_send, c_recv, c_save, a_save), refs = refs[:37], refs[37:]
    (fold_d, fold_g, fold_u), grads = make_folds(split, side, ring, refs, saved, True)
    seqs, rows, width = q_out.shape
    heads = width // HEAD_DIM
    tile = 256
    chunk, dim = part.shape[1:]
    per_seq = rows // chunk
    per_tile = tile // chunk
    middle = dim // 2
    units = wg_in.shape[-2]
    mate, peer = ring_peers(ring)
    half = lax.rem(ring, 2)
    for full in (wg, wu, wd):
        for piece in range(2):
            full[piece, units:] = jnp.zeros((full.shape[1] - units, full.shape[2]), bf16)
    own_loads = [pltpu.make_async_copy(cot_hbm, cot, loads.at[6])]
    for n, (source, full) in enumerate(((wg_in, wg), (wu_in, wu), (wd_in, wd))):
        if split:
            own_loads.append(pltpu.make_async_copy(source, full.at[side, 0:units], loads.at[n]))
        else:
            for piece in range(2):
                own_loads.append(pltpu.make_async_copy(
                    source.at[piece], full.at[piece, 0:units], loads.at[2 * n + piece]))
    greet(line_peers(place) + ring_peers(ring) + ([{"fsdp": 1 - side}] if split else []))

    if split:
        other = {"fsdp": 1 - side}
        gains[side, 0:2, :] = gain_in[...]
        move_gains = remote(gains.at[side], gains.at[side], g_sems.at[0], g_sems.at[1], other)
        move_gains.start()

        def spot(full, owner, part_at, size):
            if full is wo_all:
                return full.at[place, owner, rows_at(part_at * size, size)]
            if full.shape[0] == 2:
                return full.at[owner, rows_at(part_at * size, size)]
            return full.at[rows_at((2 * owner + part_at) * size, size)]

        table = (
            (wk_in, wk, spot), (wv_in, wv, spot), (wq_in, wq, spot), (wo_in, wo_all, spot),
            (wg_in, wg, spot), (wu_in, wu, spot), (wd_in, wd, spot))

        def cross(n):
            own, full, where = table[n]
            size = own.shape[0] // 2
            return remote(own.at[rows_at(half * size, size)], where(full, side, half, size),
                          w_send.at[n, 0], w_recv.at[n, 0], other)

        def onto_mate(n):
            own, full, where = table[n]
            here = where(full, 1 - side, half, own.shape[0] // 2)
            return remote(here, here, w_send.at[n, 1], w_recv.at[n, 1], mate)

        def hand_on(n):
            cross(n).wait_recv()
            onto_mate(n).start()

        saves = tuple(
            pltpu.make_async_copy(full, target, w_save.at[n])
            for n, (full, target) in enumerate(((wk, wk_hbm), (wv, wv_hbm), (wq, wq_hbm), (wo_all.at[place], wo_hbm))))
        for n in (0, 1, 3):
            cross(n).start()
        for own, full, _ in table[:3]:
            full[rows_at(side * own.shape[0], own.shape[0]), :] = own[...]
        wo_all[place, side] = wo_in[...]
        part_o = wo_in.shape[0] // 2
        item_side = lambda item: side if item == 0 else 1 - side
        pass_o = Passing(
            place, lambda piece, item: wo_all.at[piece, item_side(item), rows_at(half * part_o, part_o)],
            (p_send, p_recv),
            lambda item: wo_in.at[rows_at(half * part_o, part_o)] if item == 0 else None)
        pass_o.begin(0)

        def share_o(n):
            here = wo_all.at[lax.rem(place + n + 1, 4), :, rows_at(half * part_o, part_o)]
            return remote(here, here, o_send.at[n], o_recv.at[n], mate)
        remote(gains.at[side], gains.at[side], g_sems.at[0], g_sems.at[1], other).wait()
    else:
        size = gains.shape[2]
        for piece in range(2):
            gains[piece, 0:2, :] = gain_in[:, piece * size : (piece + 1) * size]
        wo_all[place] = wo_in[...]
        pass_o = Passing(place, lambda piece, item: wo_all.at[piece, item], (p_send, p_recv))
        pass_o.begin(0)
        pass_o.begin(1)

    for load in own_loads:
        load.start()

    def pass_block(s, source, target, device, slot):
        return remote(kv.at[s, source], kv.at[s, target], kv_send.at[s, slot], kv_recv.at[s, target], device)

    to_mate = lambda s: pass_block(s, 0, 1, mate, 0)
    to_peer = lambda s: pass_block(s, 0, 2, peer, 1)
    onward = lambda s: pass_block(s, 2, 3, mate, 2)
    gain_one = gain_row(gains, 0)
    position = (ring * rows + lax.broadcasted_iota(jnp.int32, cosine.shape, 0)).astype(f32)
    angles = position * frequency[0:1, :]
    cosine[...] = jnp.cos(angles)
    sine[...] = jnp.sin(angles) * jnp.where(low_half(cosine.shape), -1.0, 1.0)

    per_seq_tiles = rows // tile
    tiles = seqs * per_seq_tiles

    def tile_at(t):
        return t // per_seq_tiles, rows_at(lax.rem(t, per_seq_tiles) * tile, tile)

    @pl.loop(0, tiles)
    def _(t):
        s, at = tile_at(t)
        normed_s[s, at, :] = (unit_norm(tok[s, at, :].astype(f32)) * gain_one).astype(bf16)

    if split:
        hand_on(0)
        hand_on(1)
        cross(2).start()
        pass_o.step(0, 1)
        onto_mate(0).wait_recv()
        onto_mate(1).wait_recv()

    @pl.loop(0, tiles)
    def _(t):
        s, at = tile_at(t)
        normed = normed_s[s, at, :]
        k = dot(normed, wk[...])
        kv[s, 0, 0, at, :] = turn(k, cosine[at, :], sine[at, :]).astype(bf16)
        v = dot(normed, wv[...])
        kv[s, 0, 1, at, :] = (0.5 * v + 0.5 * fv[s, at, :].astype(f32)).astype(bf16)

        @pl.when(lax.rem(t, per_seq_tiles) == per_seq_tiles - 1)
        def _():
            to_peer(s).start()
            to_mate(s).start()

    if split:
        hand_on(3)
        pass_o.step(0, 2)
        pass_o.begin(1)
        hand_on(2)
        for n in range(4, 7):
            cross(n).start()
        onto_mate(2).wait_recv()

    @pl.loop(0, tiles)
    def _(t):
        s, at = tile_at(t)
        q = dot(normed_s[s, at, :], wq[...])
        q = turn(q, cosine[at, :], sine[at, :]) * HEAD_DIM ** (-0.5)
        q_out[s, at, :] = q.astype(bf16)
        spread(qtm.at[s], jnp.transpose(q), lax.rem(t, per_seq_tiles) * tile, rows)

    if not split:
        pass_o.step(0, 1)
        pass_o.step(0, 2)
    pass_o.step(0, 3)
    pass_o.step(1, 1)

    def saving(i):
        return pltpu.make_async_copy(part.at[i], sum_hbm.at[i], save.at[i])

    sums = Sum(
        place, part, inward, across, (send_one, recv_one, send_two, recv_two), lambda i: saving(i).start())
    passing = Passing(place, lambda piece, item: ctx_all.at[piece, item], (c_send, c_recv))

    def saving_context(s):
        mine = pl.ds(s * per_seq_tiles, per_seq_tiles)
        return pltpu.make_async_copy(ctx_all.at[place, mine], ctx_hbm.at[mine], c_save.at[s])

    def saving_kv(s):
        return pltpu.make_async_copy(kv.at[s], kv_hbm.at[s], kv_save.at[s])

    @pl.loop(0, seqs)
    def _(s):
        maxes[...] = jnp.full_like(maxes, masked_score)
        totals[...] = jnp.zeros_like(totals)
        acct[...] = jnp.zeros_like(acct)

        @pl.loop(0, 4)
        def _(j):
            @pl.when(j == 1)
            def _():
                to_mate(s).wait_recv()

            @pl.when(j == 2)
            def _():
                to_peer(s).wait_recv()
                onward(s).start()

            @pl.when(j == 3)
            def _():
                onward(s).wait_recv()

            vt[...] = jnp.transpose(kv[s, j, 1])
            key_pos = block_place(ring, j) * rows + lax.broadcasted_iota(jnp.int32, (rows, 1), 0)
            query_pos = ring * rows + lax.rem(lax.broadcasted_iota(jnp.int32, (1, 2 * rows), 1), rows)
            seen = key_pos < jnp.maximum(query_pos + 1, prefix[s])

            @pl.loop(0, heads // 2)
            def _(h):
                scores = jnp.where(seen, dot(kv[s, j, 0], qtm[s, h]), masked_score)
                old = maxes[h]
                new = jnp.maximum(old, jnp.max(scores, axis=0, keepdims=True))
                weights = jnp.exp(scores - new)
                fade = jnp.exp(old - new)
                maxes[h] = new
                totals[h] = totals[h] * fade + jnp.sum(weights, axis=0, keepdims=True)
                low = weights.astype(bf16)
                for n in range(2):
                    of_head = rows_at((2 * h + n) * HEAD_DIM, HEAD_DIM)
                    lanes = slice(n * rows, (n + 1) * rows)
                    acct[of_head, :] = acct[of_head, :] * fade[:, lanes] + dot(vt[of_head, :], low[:, lanes])
                at_step = j * (heads // 2) + h

                @pl.when((s > 0) & (at_step < 3 * per_seq_tiles))
                def _():
                    passing.step(
                        (s - 1) * per_seq_tiles + lax.rem(at_step, per_seq_tiles), 1 + at_step // per_seq_tiles)

        for h in range(heads):
            if h % 2 == 0:
                lse_out[s, h // 2 : h // 2 + 1, :] = maxes[h // 2] + jnp.log(totals[h // 2])
            of_head = slice(h * HEAD_DIM, (h + 1) * HEAD_DIM)
            acct[of_head, :] = acct[of_head, :] / totals[h // 2][:, h % 2 * rows : (h % 2 + 1) * rows]
        for t in range(per_seq_tiles):
            ctx_all[place, s * per_seq_tiles + t] = jnp.transpose(acct[:, t * tile : (t + 1) * tile]).astype(bf16)
        for t in range(per_seq_tiles):
            passing.begin(s * per_seq_tiles + t)
        saving_context(s).start()
        saving_kv(s).start()

        @pl.when(s == 0)
        def _():
            pass_o.step(1, 2)
            if split:
                onto_mate(3).wait_recv()
                for copy in saves:
                    copy.start()
                hand_on(4)
                hand_on(5)

    if split:
        hand_on(6)
    pass_o.step(1, 3)
    if split:
        for n in range(3):
            share_o(n).start()
        for n in range(3):
            share_o(n).wait_recv()
    if split:
        for n in range(4, 7):
            onto_mate(n).wait_recv()
    for load in own_loads:
        load.wait()
    lines = seqs * per_seq
    early = lines
    count = part.shape[0]
    gain_two = gain_row(gains, 1)

    def saving_attn(t):
        mine = pl.ds(t * per_tile, per_tile)
        return pltpu.make_async_copy(attn.at[mine], attn_hbm.at[mine], a_save.at[t])

    def across_both(left, full):
        return dot_nt(left[:, :middle], full[0]) + dot_nt(left[:, middle:], full[1])

    def saving_late(t):
        mine = pl.ds((t - 1) * per_tile, per_tile)
        return pltpu.make_async_copy(late.at[mine], late_hbm.at[mine], late_save.at[t - 1])

    @pl.loop(0, tiles)
    def _(t):
        s, at = tile_at(t)
        flat = rows_at(t * tile, tile)
        mine = t * per_tile

        def tick(n):
            at_step = 3 * t + n

            @pl.when(t < per_seq_tiles)
            def _():
                passing.step(
                    (seqs - 1) * per_seq_tiles + lax.rem(at_step, per_seq_tiles), 1 + at_step // per_seq_tiles)

            @pl.when((t >= per_seq_tiles) & (n > 0))
            def _():
                sums.steps(2 * (t - per_seq_tiles) + n - 1, 1)

        context = jnp.concatenate([ctx_all[p, t] for p in range(4)], axis=1)
        attended = [
            dot(context, jnp.concatenate([wo_all[p, piece] for p in range(4)], axis=0)) for piece in range(2)]
        for piece in range(2):
            for k in range(per_tile):
                attn[mine + k, :, piece * middle : (piece + 1) * middle] = attended[piece][
                    k * chunk : (k + 1) * chunk].astype(bf16)
        saving_attn(t).start()
        hidden = tok[s, at, :].astype(f32) + jnp.concatenate(attended, axis=1)
        normed = (unit_norm(hidden) * gain_two).astype(bf16)
        normed_s[s, at, :] = normed
        gate = across_both(normed, wg)
        up = across_both(normed, wu)
        sigmoid = jax.nn.sigmoid(gate)
        swish = gate * sigmoid
        inner = (swish * up).astype(bf16)
        inner_t[:, flat] = jnp.transpose(inner)
        inner_grad = across_both(cot[s, at, :], wd)
        gate_grad = (inner_grad * up * sigmoid * (1.0 + gate * (1.0 - sigmoid))).astype(bf16)
        up_grad = (inner_grad * swish).astype(bf16)
        tick(0)
        for piece in range(2):
            sums.fill(mine, piece, dot(gate_grad, wg[piece]) + dot(up_grad, wu[piece]))
        sums.offer(mine, per_tile)
        tick(1)
        feeds = [dot(inner, wd[piece]) for piece in range(2)]

        @pl.when(t == 0)
        def _():
            for piece in range(2):
                sums.fill(early, piece, feeds[piece])

        @pl.when(t > 0)
        def _():
            for piece in range(2):
                for k in range(per_tile):
                    late[mine - per_tile + k, :, piece * middle : (piece + 1) * middle] = feeds[piece][
                        k * chunk : (k + 1) * chunk].astype(bf16)
            saving_late(t).start()

        gg_t[:, flat] = jnp.transpose(gate_grad)
        ug_t[:, flat] = jnp.transpose(up_grad)
        tick(2)

    sums.offer(early, count - early)
    deep = units // 2

    def weight_grad(n, left_t, right):
        for h in range(2):
            for y in range(2):
                total = jnp.zeros((deep, middle), f32)
                for s in range(seqs):
                    total = total + dot(
                        left_t[h * deep : (h + 1) * deep, s * rows : (s + 1) * rows],
                        right[s, :, y * middle : (y + 1) * middle])
                grads[n][h, y] = total.astype(bf16)

    begun = 2 * (tiles - per_seq_tiles)
    weight_grad(0, inner_t, cot)
    fold_d.first()
    sums.steps(begun, 1)
    weight_grad(1, gg_t, normed_s)
    fold_g.first()
    fold_d.second()
    sums.steps(begun + 1, 1)
    weight_grad(2, ug_t, normed_s)
    fold_u.first()
    fold_g.second()
    sums.steps(begun + 2, 1)
    fold_u.second()
    sums.steps(begun + 3, 2)
    fold_d.third()
    sums.steps(begun + 5, 3)
    fold_g.third()
    fold_d.fourth()
    sums.steps(begun + 8, 3)
    fold_u.third()
    fold_g.fourth()
    fold_d.last()
    sums.steps(begun + 11, 3)
    fold_u.fourth()
    fold_g.last()
    sums.steps(begun + 14, count - begun - 14)
    fold_u.last()
    sums.settled(0, count)
    sums.close(count)
    for fold in (fold_d, fold_g):
        fold.settle(False)
    fold_u.settle()
    for t in range(1, tiles):
        saving_late(t).wait()
    for s in range(seqs):
        to_mate(s).wait_send()
        to_peer(s).wait_send()
        onward(s).wait_send()
        saving_kv(s).wait()
        saving_context(s).wait()
    for t in range(tiles):
        saving_attn(t).wait()
    pass_o.settle(2)
    passing.settle(tiles)

    @pl.loop(0, count)
    def _(i):
        saving(i).wait()

    if split:
        for n in range(7):
            cross(n).wait_send()
            onto_mate(n).wait_send()
        for n in range(3):
            share_o(n).wait_send()
        for copy in saves:
            copy.wait()


def limits(ident, megabytes=60):
    return pltpu.CompilerParams(
        collective_id=ident, has_side_effects=True, vmem_limit_bytes=megabytes * 1024 * 1024)


def front(split, tok, fv, cot, gains, square, wide, frequency, prefix):
    seqs, rows, dim = tok.shape
    width, units = square[0].shape[1], wide[0].shape[-2]
    heads = width // HEAD_DIM
    chunk, tile = 64, 256
    tokens = seqs * rows
    count = tokens // chunk + tile // chunk
    after = (tokens - tile) // chunk
    padded = -(-units // 256) * 256
    vmem = pl.BlockSpec(memory_space=pltpu.VMEM)
    anyw = pl.BlockSpec(memory_space=pl.ANY)
    dma = pltpu.SemaphoreType.DMA
    lines = pltpu.VMEM((count, chunk, dim), bf16)
    shape = jax.ShapeDtypeStruct
    full = [(dim, width)] * 3 + [(2, width, dim // 2)]
    fold_scratch, fold_outs = fold_shapes([(units // 2, dim // 2)] * 3, split, True)
    outs = [
        shape((count, chunk, dim), bf16), shape((after, chunk, dim), bf16), shape((seqs, rows, width), bf16),
        shape((seqs, 4, 2, rows, width), bf16), shape((tokens // chunk, chunk, dim), bf16),
        shape((tokens // tile, tile, width), bf16),
        shape((seqs, heads // 2, 2 * rows), f32), shape((2, 8, dim // 2), f32),
        shape((rows, 128), f32), shape((rows, 128), f32)] + fold_outs
    out_specs = [anyw, anyw, vmem, anyw, anyw, anyw, vmem, vmem, vmem, vmem] + [anyw] * 3
    scratch = []
    if split:
        outs += [shape(size, bf16) for size in full]
        out_specs += [anyw] * 4
        scratch = [pltpu.VMEM(size, bf16) for size in full[:3]] + [
            dma((7, 2)), dma((7, 2)), dma((4,)), dma((2,)), dma((3,)), dma((3,))]
    scratch += [
        pltpu.VMEM((seqs, rows, dim), bf16),
        pltpu.VMEM((seqs, 4, 2, rows, width), bf16),
        pltpu.VMEM((seqs, heads // 2, width, 2 * rows), bf16),
        pltpu.VMEM((width, rows), bf16),
        pltpu.VMEM((width, rows), f32),
        pltpu.VMEM((heads // 2, 1, 2 * rows), f32),
        pltpu.VMEM((heads // 2, 1, 2 * rows), f32),
        lines, lines, lines,
        dma((seqs, 3)), dma((seqs, 4)), dma((seqs,)),
        dma((count,)), dma((count,)), dma((count,)), dma((count,)), dma((count,)),
        pltpu.VMEM((2, padded, dim // 2), bf16),
        pltpu.VMEM((2, padded, dim // 2), bf16),
        pltpu.VMEM((2, padded, dim // 2), bf16),
        dma((7,)),
        pltpu.VMEM((seqs, rows, dim), bf16),
        pltpu.VMEM((padded, tokens), bf16),
        pltpu.VMEM((padded, tokens), bf16),
        pltpu.VMEM((padded, tokens), bf16),
        pltpu.VMEM((after, chunk, dim), bf16),
        dma((tokens // tile,)),
        pltpu.VMEM((4, 2, width, dim // 2), bf16),
        pltpu.VMEM((4, tokens // tile, tile, width), bf16),
        pltpu.VMEM((tokens // chunk, chunk, dim), bf16),
        dma((2, 2, 4)), dma((2, 4)), dma((tokens // tile, 2, 4)), dma((tokens // tile, 4)),
        dma((seqs,)), dma((tokens // tile,)),
    ] + fold_scratch
    return pl.pallas_call(
        functools.partial(front_kernel, split),
        name="front",
        out_shape=outs,
        in_specs=[vmem] * 2 + [anyw] + [vmem] * 5 + [anyw] * 3 + [vmem, pl.BlockSpec(memory_space=pltpu.SMEM)],
        out_specs=out_specs,
        scratch_shapes=scratch,
        compiler_params=limits(0, 63),
        cost_estimate=pl.CostEstimate(flops=22 * 10**9, bytes_accessed=2 * 10**7, transcendentals=10**7),
    )(tok, fv, cot, gains, *square, *wide, frequency, prefix)


def back_kernel(split, *refs):
    place, ring, side = lax.axis_index("tp"), lax.axis_index("ctx"), lax.axis_index("fsdp")
    loaded, refs = refs[:12], refs[12:]
    (gain_in, lse, cosine, sine, prefix, block_hbm, token_hbm, fv_out, gain_out), saved, refs = (
        refs[:9], refs[9:13], refs[13:])
    (tok, cot, wq, wk, wv, wo, q, kv, ctx, attn, mixed, early), refs = refs[:12], refs[12:]
    (hid, branch, qtm, qm, otm, om, kt, delta, dqt, dk, dv, give, take, proj, normed_t,
     part, inward, across, gain_part, gain_all,
     kv_send, kv_recv, send_one, recv_one, send_two, recv_two, save, gain_send, gain_recv, loads), refs = (
        refs[:30], refs[30:])
    (fold_o, fold_k, fold_v, fold_q), (dwo, dwk, dwv, dwq) = make_folds(split, side, ring, refs, saved)
    late_hbm, sum_hbm, attn_hbm, tok_hbm, cot_hbm, wq_hbm, wk_hbm, wv_hbm, wo_hbm, q_hbm, kv_hbm, ctx_hbm = loaded
    seqs, rows, dim = tok.shape
    width = wq.shape[1]
    heads = width // HEAD_DIM
    chunk = part.shape[1]
    per_seq = rows // chunk
    tile = 256
    per_tile = tile // chunk
    middle = dim // 2
    lines = seqs * per_seq
    count = 2 * lines - per_tile
    head_start, rest = per_seq, per_seq - per_tile
    rest_start = head_start + per_seq
    own_start = (head_start, rest_start + rest)
    mate, peer = ring_peers(ring)
    others = [(dy, dc) for dy in range(2) for dc in range(4) if dy or dc]
    group = [{"fsdp": lax.rem(side + dy, 2), "ctx": lax.rem(ring + dc, 4)} for dy, dc in others]

    copies = {}

    def load(name, source, target):
        copies[name] = pltpu.make_async_copy(source, target, loads.at[len(copies)])
        copies[name].start()

    def ready(*names):
        for name in names:
            copies[name].wait()

    load("late", late_hbm.at[0:head_start], part.at[0:head_start])
    for s in range(seqs):
        mine = slice(s * per_seq, (s + 1) * per_seq)
        load(f"tok{s}", tok_hbm.at[s], tok.at[s])
        load(f"attn{s}", attn_hbm.at[mine], attn.at[mine])
        load(f"cot{s}", cot_hbm.at[s], cot.at[s])
        load(f"mixed{s}", sum_hbm.at[mine], mixed.at[mine])
        if s == 0:
            load("wo", wo_hbm, wo)
        load(f"q{s}", q_hbm.at[s], q.at[s])
        load(f"ctx{s}", ctx_hbm.at[s], ctx.at[s])
        load(f"kv{s}", kv_hbm.at[s], kv.at[s])
    load("rest", late_hbm.at[head_start : head_start + rest], part.at[rest_start : rest_start + rest])
    load("early", sum_hbm.at[lines : lines + per_tile], early)
    load("wq", wq_hbm, wq)
    load("wk", wk_hbm, wk)
    load("wv", wv_hbm, wv)
    greet(line_peers(place) + (group if split else ring_peers(ring)))
    gain_one, gain_two = gain_row(gain_in, 0), gain_row(gain_in, 1)
    gain_part[...] = jnp.zeros_like(gain_part)

    def chunk_at(n):
        return n // per_seq, rows_at(lax.rem(n, per_seq) * chunk, chunk)

    def saving_block(i, n):
        s, own = chunk_at(n)
        return pltpu.make_async_copy(across.at[i], block_hbm.at[s, own], save.at[i])

    def saving_early(n):
        return pltpu.make_async_copy(early.at[n], block_hbm.at[0, n * chunk : (n + 1) * chunk], save.at[count + n])

    def saving_token(i, n):
        s, own = chunk_at(n)
        return pltpu.make_async_copy(hid.at[s, own], token_hbm.at[s, own], save.at[i])

    def add_gain(which, value):
        for piece in range(2):
            gain_part[piece, which : which + 1, :] += value[:, piece * middle : (piece + 1) * middle]

    is_block = lambda i: (i < head_start) | ((i >= rest_start) & (i < own_start[1]))
    block_of = lambda i: per_tile + jnp.where(i < head_start, i, i - per_seq)
    token_of = lambda i: jnp.where(i < rest_start, i - head_start, i - own_start[1] + per_seq)

    def done(i):
        @pl.when(is_block(i))
        def _():
            n = block_of(i)
            s, own = chunk_at(n)
            across[i] = (
                tok[s, own, :].astype(f32) + attn[n].astype(f32) + part[i].astype(f32)).astype(bf16)
            saving_block(i, n).start()

        @pl.when(jnp.logical_not(is_block(i)))
        def _():
            n = token_of(i)
            s, own = chunk_at(n)
            values, upstream = tok[s, own, :].astype(f32), part[i].astype(f32)
            factor = lax.rsqrt(jnp.mean(values * values, axis=-1, keepdims=True) + epsilon)
            scaled = upstream * gain_one
            add_gain(0, jnp.sum(upstream * values * factor, axis=0, keepdims=True))
            hid[s, own, :] += factor * scaled - values * factor**3 * jnp.mean(
                scaled * values, axis=-1, keepdims=True)
            saving_token(i, n).start()

    sums = Sum(place, part, inward, across, (send_one, recv_one, send_two, recv_two), done)

    def move(s, source, target, device):
        return remote(give.at[source], take.at[s, target], kv_send.at[source], kv_recv.at[s, target], device)

    far_to_mate = lambda s: move(s, 2, 0, mate)
    peer_back = lambda s: move(s, 1, 1, peer)
    near_to_mate = lambda s: move(s, 0, 2, mate)
    ready("late")
    sums.offer(0, head_start)

    def hidden_stage(s):
        @pl.loop(0, rows // tile)
        def _(t):
            at = rows_at(t * tile, tile)
            first = s * per_seq + t * per_tile
            join = lambda ref: jnp.concatenate([ref[first + k] for k in range(per_tile)], axis=0).astype(f32)
            token = tok[s, at, :].astype(f32)
            values = token + join(attn)
            upstream = join(mixed)
            factor = lax.rsqrt(jnp.mean(values * values, axis=-1, keepdims=True) + epsilon)
            scaled = upstream * gain_two
            add_gain(1, jnp.sum(upstream * values * factor, axis=0, keepdims=True))
            hid_now = cot[s, at, :].astype(f32) + factor * scaled - values * factor**3 * jnp.mean(
                scaled * values, axis=-1, keepdims=True)
            hid[s, at, :] = hid_now
            low = hid_now.astype(bf16)
            branch[s, at, :] = low
            left, right = low[:, :middle], low[:, middle:]
            grad = dot_nt(left, wo[0]) + dot_nt(right, wo[1])
            lane_owner = lax.broadcasted_iota(jnp.int32, grad.shape, 1) // HEAD_DIM
            q_now = q[s, at, :].astype(f32)
            grad_t = jnp.transpose(grad)
            q_t = jnp.transpose(q_now)
            product = jnp.transpose(grad.astype(bf16).astype(f32) * ctx[s, at, :].astype(f32))
            for h in range(heads):
                low_rows = rows_at(h % 2 * rows + t * tile, tile)
                om[h // 2, low_rows, :] = jnp.where(lane_owner == h, grad, 0.0).astype(bf16)
                qm[h // 2, low_rows, :] = jnp.where(lane_owner == h, q_now, 0.0).astype(bf16)
                delta[h // 2, :, low_rows] = jnp.sum(
                    product[h * HEAD_DIM : (h + 1) * HEAD_DIM], axis=0, keepdims=True)
            spread(otm, grad_t, t * tile, rows)
            spread(qtm, q_t, t * tile, rows)
            normed = (unit_norm(token) * gain_one).astype(bf16)
            normed_t[:, rows_at(s * rows + t * tile, tile)] = jnp.transpose(normed)

    def back_block(s, j):
        kt[...] = jnp.transpose(kv[s, j, 0])
        key_pos = block_place(ring, j) * rows + lax.broadcasted_iota(jnp.int32, (rows, 1), 0)
        query_pos = ring * rows + lax.rem(lax.broadcasted_iota(jnp.int32, (1, 2 * rows), 1), rows)
        seen = key_pos < jnp.maximum(query_pos + 1, prefix[s])
        dk[...] = jnp.zeros_like(dk)
        dv[...] = jnp.zeros_like(dv)

        @pl.loop(0, heads // 2)
        def _(h):
            scores = dot(kv[s, j, 0], qtm[h])
            probs = jnp.where(seen, jnp.exp(scores - lse[s, pl.ds(h, 1), :]), 0.0)
            dprobs = dot(kv[s, j, 1], otm[h])
            dv[...] += dot(probs.astype(bf16), om[h])
            dscores = (probs * (dprobs - delta[h])).astype(bf16)
            dk[...] += dot(dscores, qm[h])
            for n in range(2):
                of_head = rows_at((2 * h + n) * HEAD_DIM, HEAD_DIM)
                dqt[of_head, :] += dot(kt[of_head, :], dscores[:, n * rows : (n + 1) * rows])

    def finalize(s):
        near_to_mate(s).wait_recv()
        peer_back(s).wait_recv()
        @pl.loop(0, rows // tile)
        def _(t):
            at = rows_at(t * tile, tile)
            flat = rows_at(s * rows + t * tile, tile)
            co, si = cosine[at, :], sine[at, :]
            grad_v = 0.5 * (dv[at, :] + take[s, 2, 1, at, :].astype(f32) + take[s, 1, 1, at, :].astype(f32))
            grad_k = dk[at, :] + take[s, 2, 0, at, :].astype(f32) + take[s, 1, 0, at, :].astype(f32)
            grad_q = jnp.transpose(dqt[:, at]) * HEAD_DIM ** (-0.5)
            proj[0, flat, :] = turn(grad_q, co, si, -1.0).astype(bf16)
            proj[1, flat, :] = turn(grad_k, co, si, -1.0).astype(bf16)
            proj[2, flat, :] = grad_v.astype(bf16)
            fv_out[s, at, :] = grad_v
            i = jnp.where(s == 0, own_start[0], own_start[1]) + t * per_tile
            for piece in range(2):
                cut = slice(piece * middle, (piece + 1) * middle)
                sums.fill(i, piece, dot_nt(proj[0, flat, :], wq[cut, :]) + dot_nt(
                    proj[1, flat, :], wk[cut, :]) + dot_nt(proj[2, flat, :], wv[cut, :]))
            sums.offer(i, per_tile)

        @pl.when(s == 0)
        def _():
            sums.offer(rest_start, rest)

    ready("wo")

    def at_phase(phase, wanted, names):
        @pl.when(phase == wanted)
        def _():
            ready(*names)

    @pl.loop(0, seqs + 1)
    def _(phase):
        s = jnp.maximum(phase - 1, 0)
        follows = phase > 1

        @pl.when(phase > 0)
        def _():
            for wanted in range(seqs):
                at_phase(phase, wanted + 1, [f"kv{wanted}"])
            dqt[...] = jnp.zeros_like(dqt)

            @pl.loop(0, 4)
            def _(n):
                back_block(s, 3 - n)

                @pl.when(n == 0)
                def _():
                    @pl.when(follows)
                    def _():
                        far_to_mate(s - 1).wait_send()
                        fold_o.second()

                    give[2, 0] = dk[...].astype(bf16)
                    give[2, 1] = dv[...].astype(bf16)
                    far_to_mate(s).start()

                @pl.when(n == 1)
                def _():
                    far_to_mate(s).wait_recv()

                    @pl.when(follows)
                    def _():
                        peer_back(s - 1).wait_send()

                    give[1, 0] = (dk[...] + take[s, 0, 0].astype(f32)).astype(bf16)
                    give[1, 1] = (dv[...] + take[s, 0, 1].astype(f32)).astype(bf16)
                    peer_back(s).start()

                @pl.when(n == 2)
                def _():
                    @pl.when(follows)
                    def _():
                        near_to_mate(s - 1).wait_send()
                        fold_o.third()

                    give[0, 0] = dk[...].astype(bf16)
                    give[0, 1] = dv[...].astype(bf16)
                    near_to_mate(s).start()

                first = jnp.where(phase == 1, 1 + n, jnp.where(n == 0, 8, 7 + 2 * n))
                sums.steps(first, jnp.where((phase == 1) | (n == 0), 1, 2))

        @pl.when(phase < seqs)
        def _():
            for wanted in range(seqs):
                at_phase(phase, wanted, [
                    f"{name}{wanted}" for name in ("tok", "attn", "cot", "mixed", "q", "ctx")])
            hidden_stage(phase)
            sums.steps(jnp.where(phase == 0, 0, 5), 1 + phase)

        @pl.when(phase > 0)
        def _():
            at_phase(phase, 1, ["wq", "wk", "wv", "rest"])
            finalize(s)
            sums.steps(jnp.where(phase == 1, 7, 15), 1)

        @pl.when(phase == seqs - 1)
        def _():
            deep = dwo.shape[2]
            total = jnp.zeros((width, dim), f32)
            for r in range(seqs):
                total = total + dot(jnp.transpose(ctx[r]), branch[r])
            for h in range(2):
                for y in range(2):
                    dwo[h, y] = total[h * deep : (h + 1) * deep, y * middle : (y + 1) * middle].astype(bf16)
            fold_o.first()

    begun = 16
    share = dwq.shape[2]

    def square_grad(target, which):
        @pl.loop(0, 4)
        def _(k):
            h, y = k // 2, lax.rem(k, 2)
            target[h, y] = dot(normed_t[rows_at((2 * y + h) * share, share), :], proj[which]).astype(bf16)

    ready("early")
    for n in range(per_tile):
        own = slice(n * chunk, (n + 1) * chunk)
        early[n] = (tok[0, own, :].astype(f32) + attn[n].astype(f32) + early[n].astype(f32)).astype(bf16)
        saving_early(n).start()
    square_grad(dwk, 1)
    fold_k.first()
    sums.steps(begun, 1)
    square_grad(dwv, 2)
    fold_v.first()
    fold_k.second()
    sums.steps(begun + 1, 1)
    square_grad(dwq, 0)
    fold_q.first()
    fold_v.second()
    sums.steps(begun + 2, 1)
    fold_q.second()
    fold_o.fourth()
    sums.steps(begun + 3, 2)
    fold_k.third()
    sums.steps(begun + 5, 1)
    fold_v.third()
    sums.steps(begun + 6, 1)
    fold_q.third()
    fold_k.fourth()
    sums.steps(begun + 7, 1)
    fold_v.fourth()
    sums.steps(begun + 8, 1)
    fold_q.fourth()
    for fold in (fold_o, fold_k, fold_v):
        fold.last()
    sums.steps(begun + 9, count - begun - 9)
    fold_q.last()
    sums.settled(0, count)
    sums.close(count)
    if split:
        me = 4 * side + ring
        gain_all[me] = gain_part[side]

        def share_gain(n):
            dy, dc = others[n]
            y = lax.rem(side + dy, 2)
            return remote(gain_part.at[y], gain_all.at[me], gain_send.at[n], gain_recv.at[n], group[n])

        for n in range(7):
            share_gain(n).start()
        for n in range(7):
            share_gain(n).wait()
        total = gain_all[0]
        for n in range(1, 8):
            total = total + gain_all[n]
        gain_out[...] = total
    else:
        gain_out[...] = gain_part[...]
    for fold in (fold_o, fold_k, fold_v, fold_q):
        fold.settle()
    for copy in (far_to_mate, peer_back, near_to_mate):
        copy(seqs - 1).wait_send()

    for n in range(per_tile):
        saving_early(n).wait()

    @pl.loop(0, count)
    def _(i):
        @pl.when(is_block(i))
        def _():
            saving_block(i, block_of(i)).wait()

        @pl.when(jnp.logical_not(is_block(i)))
        def _():
            saving_token(i, token_of(i)).wait()


def back(split, tok, cot, sums, attn, late, gains, square, q, kv, ctx, lse, cosine, sine, prefix):
    seqs, rows, dim = tok.shape
    width = q.shape[2]
    heads = width // HEAD_DIM
    _, chunk, _ = sums.shape
    tokens = seqs * rows
    early = 256 // chunk
    count = 2 * tokens // chunk - early
    vmem = pl.BlockSpec(memory_space=pltpu.VMEM)
    anyw = pl.BlockSpec(memory_space=pl.ANY)
    dma = pltpu.SemaphoreType.DMA
    lines = pltpu.VMEM((count, chunk, dim), bf16)
    half_lines = pltpu.VMEM((tokens // chunk, chunk, dim), bf16)
    wide = pltpu.VMEM((heads // 2, 2 * rows, width), bf16)
    tall = pltpu.VMEM((heads // 2, width, 2 * rows), bf16)
    shape = jax.ShapeDtypeStruct
    fold_scratch, fold_outs = fold_shapes([(width // 2, dim // 2)] + [(dim // 4, width)] * 3, split)
    loaded = (tok, cot) + tuple(square) + (q, kv, ctx)
    return pl.pallas_call(
        functools.partial(back_kernel, split),
        name="back",
        out_shape=[
            shape((seqs, rows, dim), bf16), shape((seqs, rows, dim), f32), shape((seqs, rows, width), f32),
            shape((8, dim // 2) if split else (2, 8, dim // 2), f32)] + fold_outs,
        in_specs=[anyw] * 12 + [vmem] * 4 + [pl.BlockSpec(memory_space=pltpu.SMEM)],
        out_specs=[anyw, anyw, vmem, vmem] + [anyw] * 4,
        scratch_shapes=[pltpu.VMEM(x.shape, bf16) for x in loaded] + [
            half_lines, half_lines, pltpu.VMEM((early, chunk, dim), bf16),
            pltpu.VMEM((seqs, rows, dim), f32),
            pltpu.VMEM((seqs, rows, dim), bf16),
            tall, wide, tall, wide,
            pltpu.VMEM((width, rows), bf16),
            pltpu.VMEM((heads // 2, 1, 2 * rows), f32),
            pltpu.VMEM((width, rows), f32),
            pltpu.VMEM((rows, width), f32),
            pltpu.VMEM((rows, width), f32),
            pltpu.VMEM((3, 2, rows, width), bf16),
            pltpu.VMEM((seqs, 3, 2, rows, width), bf16),
            pltpu.VMEM((3, tokens, width), bf16),
            pltpu.VMEM((dim, tokens), bf16),
            lines, lines, lines,
            pltpu.VMEM((2, 8, dim // 2), f32),
            pltpu.VMEM((8, 8, dim // 2), f32),
            dma((3,)), dma((seqs, 3)),
            dma((count,)), dma((count,)), dma((count,)), dma((count,)), dma((count + early,)),
            dma((7,)), dma((7,)), dma((8 * seqs + 8,)),
        ] + fold_scratch,
        compiler_params=limits(2, 62),
        cost_estimate=pl.CostEstimate(flops=30 * 10**9, bytes_accessed=10**7, transcendentals=10**7),
    )(late, sums, attn, *loaded, gains, lse, cosine, sine, prefix)


def frequencies():
    half = HEAD_DIM // 2
    lane = np.arange(128) % half
    return np.broadcast_to((rope_base ** (-lane / half)).astype(np.float32), (8, 128))


def halves(weight):
    rows, columns = weight.shape
    return jnp.swapaxes(weight.reshape(rows, 2, columns // 2), 0, 1)


def shards(
    tokens, first_values, norm1_gain, norm2_gain, w_query, w_key, w_value, w_out, w_gate, w_up, w_down,
    prefix, cotangent,
):
    split = lax.axis_size("fsdp") == 2
    seqs, rows, dim = tokens.shape
    width, units = w_query.shape[1], w_gate.shape[1]
    gather = functools.partial(lax.all_gather, axis_name="fsdp", tiled=True)
    if split:
        gains = (norm1_gain, norm2_gain)
        square = (w_query, w_key, w_value, w_out)
        wide = (w_gate.T, w_up.T, w_down)
    else:
        gains = (gather(norm1_gain), gather(norm2_gain))
        square = (gather(w_query), gather(w_key), gather(w_value), halves(gather(w_out, axis=1)))
        wide = (halves(gather(w_gate).T), halves(gather(w_up).T), halves(gather(w_down, axis=1)))
    (sums, late, query, pairs, attn, context, log_total, gain_rows, cosine, sine, down_grad, gate_grad, up_grad,
     *gathered) = front(
        split, tokens, first_values, cotangent, jnp.stack(gains).astype(f32), square, wide, frequencies(), prefix)
    if split:
        square = tuple(gathered)
    block_out, token_grad, half_value_grad, gain_grads, out_grad, key_grad, value_grad, query_grad = back(
        split, tokens, cotangent, sums, attn, late, gain_rows, square, query, pairs, context.reshape(query.shape),
        log_total, cosine, sine, prefix)
    if split:
        over_rows = lambda grad: grad.reshape(-1, grad.shape[-1])
        over_columns = over_rows
        over_turned = lambda grad: over_rows(grad).T
        gain_one_grad, gain_two_grad = gain_grads[0], gain_grads[1]
    else:
        total = lambda grad, axis: lax.psum(
            lax.psum_scatter(grad, "fsdp", scatter_dimension=axis, tiled=True), "ctx").astype(f32)
        over_rows = lambda grad: total(jnp.swapaxes(grad, 0, 1).reshape(-1, grad.shape[-1]), 0)
        over_columns = lambda grad: total(
            jnp.transpose(grad, (0, 2, 1, 3)).reshape(2 * grad.shape[2], -1), 1)
        over_turned = lambda grad: over_columns(grad).T
        gain_one_grad, gain_two_grad = (total(gain_grads[:, n].reshape(-1), 0) for n in range(2))
    return (
        block_out,
        token_grad,
        half_value_grad,
        gain_one_grad,
        gain_two_grad,
        over_rows(query_grad),
        over_rows(key_grad),
        over_rows(value_grad),
        over_columns(out_grad),
        over_turned(gate_grad),
        over_turned(up_grad),
        over_columns(down_grad),
    )


def solution(mesh):
    return jax.shard_map(
        shards,
        mesh=mesh,
        in_specs=(
            P("fsdp", "ctx", None),
            P("fsdp", "ctx", "tp"),
            P("fsdp"),
            P("fsdp"),
            P("fsdp", "tp"),
            P("fsdp", "tp"),
            P("fsdp", "tp"),
            P("tp", "fsdp"),
            P("fsdp", "tp"),
            P("fsdp", "tp"),
            P("tp", "fsdp"),
            P("fsdp"),
            P("fsdp", "ctx", None),
        ),
        out_specs=(
            P("fsdp", "ctx", None),
            P("fsdp", "ctx", None),
            P("fsdp", "ctx", "tp"),
            P("fsdp"),
            P("fsdp"),
            P("fsdp", "tp"),
            P("fsdp", "tp"),
            P("fsdp", "tp"),
            P("tp", "fsdp"),
            P("fsdp", "tp"),
            P("fsdp", "tp"),
            P("tp", "fsdp"),
        ),
        check_vma=False,
    )
```

```python
import functools

import jax
import jax.numpy as jnp
from jax import lax
from jax.experimental import pallas as pl
from jax.experimental.pallas import tpu as pltpu
from jax.sharding import PartitionSpec as P

HEAD_DIM = 64
epsilon = 1e-06
rope_base = 10000.0
masked_score = -1e30
MESH = pl.DeviceIdType.MESH
bf16 = jnp.bfloat16
f32 = jnp.float32


def dot(a, b):
    return jnp.dot(a, b, preferred_element_type=f32)


def dot_nt(a, b):
    return lax.dot_general(a, b, (((1,), (1,)), ((), ())), preferred_element_type=f32)


def unit_norm(values):
    return values * lax.rsqrt(jnp.mean(values * values, axis=-1, keepdims=True) + epsilon)


def low_half(shape):
    return lax.rem(lax.broadcasted_iota(jnp.int32, shape, 1), HEAD_DIM) < HEAD_DIM // 2


class Sum:
    def __init__(self, place, part, inward, across, sems, done):
        self.pair = near(place)
        self.middle = 3 - place
        self.inner = (place == 1) | (place == 2)
        self.outer = (place == 0) | (place == 3)
        self.part, self.inward, self.across, self.done = part, inward, across, done
        self.send_one, self.recv_one, self.send_two, self.recv_two = sems

    def copy_in(self, i):
        return remote(
            self.part.at[i], self.inward.at[i], self.send_one.at[i], self.recv_one.at[i], {"tp": self.pair})

    def copy_across(self, i):
        return remote(
            self.part.at[i], self.across.at[i], self.send_two.at[i], self.recv_two.at[i], {"tp": self.middle})

    def copy_out(self, i):
        return remote(
            self.part.at[i], self.inward.at[i], self.send_one.at[i], self.recv_one.at[i], {"tp": self.pair})

    def fill(self, first, piece, values):
        chunk, size = self.part.shape[1], values.shape[1]
        for k in range(values.shape[0] // chunk):
            self.part[first + k, :, piece * size : (piece + 1) * size] = values[
                k * chunk : (k + 1) * chunk].astype(bf16)

    def offer(self, first, count):
        @pl.when(self.outer)
        def _():
            @pl.loop(0, count)
            def _(k):
                self.copy_in(first + k).start()

    def take_in(self, i):
        self.copy_in(i).wait_recv()
        self.part[i] = (self.part[i].astype(f32) + self.inward[i].astype(f32)).astype(bf16)
        self.copy_across(i).start()

    def finish(self, i):
        self.copy_across(i).wait()
        self.part[i] = (self.part[i].astype(f32) + self.across[i].astype(f32)).astype(bf16)
        self.copy_out(i).start()
        self.done(i)

    def steps(self, first, count):
        @pl.when(self.inner)
        def _():
            @pl.loop(first, first + count)
            def _(i):
                self.take_in(i)

                @pl.when(i > 0)
                def _():
                    self.finish(i - 1)

    def settled(self, first, count):
        @pl.when(self.outer)
        def _():
            @pl.loop(first, first + count)
            def _(i):
                self.copy_out(i).wait_recv()
                self.copy_in(i).wait_send()
                self.part[i] = self.inward[i]
                self.done(i)

    def close(self, count):
        @pl.when(self.inner)
        def _():
            self.finish(count - 1)

            @pl.loop(0, count)
            def _(i):
                self.copy_out(i).wait_send()


def near(place):
    return place + 1 - 2 * lax.rem(place, 2)


def greet(peers):
    barrier = pltpu.get_barrier_semaphore()
    for peer in peers:
        pl.semaphore_signal(barrier, inc=1, device_id=peer, device_id_type=MESH)
    pl.semaphore_wait(barrier, len(peers))


def block_place(ring, j):
    return jnp.where(
        j == 0, ring, jnp.where(j == 1, near(ring), jnp.where(j == 2, lax.rem(ring + 2, 4), 3 - ring)))


def line_peers(place):
    return [{"tp": near(place)}, {"tp": 3 - place}]


def ring_peers(ring):
    return [{"ctx": near(ring)}, {"ctx": lax.rem(ring + 2, 4)}]


def remote(source, target, send, recv, device):
    return pltpu.make_async_remote_copy(
        src_ref=source, dst_ref=target, send_sem=send, recv_sem=recv,
        device_id=device, device_id_type=MESH)


class Passing:
    def __init__(self, place, spot, sems, own=None):
        self.place, self.spot, self.own = place, spot, own
        self.send, self.recv = sems

    def move(self, piece, item, way, source=None):
        here = self.spot(piece, item)
        return remote(
            here if source is None else source, here, self.send.at[item, way, piece], self.recv.at[item, piece],
            {"tp": self.place + 1 - 2 * way})

    def begin(self, item):
        source = None if self.own is None else self.own(item)

        @pl.when(self.place < 3)
        def _():
            self.move(self.place, item, 0, source).start()

        @pl.when(self.place > 0)
        def _():
            self.move(self.place, item, 1, source).start()

    def step(self, item, distance):
        @pl.when(self.place >= distance)
        def _():
            piece = self.place - distance
            self.move(piece, item, 0).wait_recv()

            @pl.when(self.place < 3)
            def _():
                self.move(piece, item, 0).start()

        @pl.when(self.place + distance <= 3)
        def _():
            piece = self.place + distance
            self.move(piece, item, 1).wait_recv()

            @pl.when(self.place > 0)
            def _():
                self.move(piece, item, 1).start()

    def settle(self, items):
        for item in range(items):
            @pl.loop(0, 4)
            def _(piece, item=item):
                @pl.when((self.place < 3) & (piece <= self.place))
                def _():
                    self.move(piece, item, 0).wait_send()

                @pl.when((self.place > 0) & (piece >= self.place))
                def _():
                    self.move(piece, item, 1).wait_send()


def rows_at(start, size):
    return pl.ds(pl.multiple_of(start, size), size)


class Fold:
    def __init__(self, side, ring, refs, sems, saved):
        self.side, self.half = side, lax.rem(ring, 2)
        self.grad, self.one, self.two, self.three, self.final = refs
        self.send, self.recv, self.save = sems
        self.mate, self.peer, self.other = (
            {"ctx": near(ring)}, {"ctx": lax.rem(ring + 2, 4)}, {"fsdp": 1 - side})
        self.saved = saved
        self.began = set()

    def mine(self):
        return self.grad if self.one is None else self.grad.at[self.half, self.side]

    def copy(self, n):
        source, target, device = (
            lambda: (self.grad.at[1 - self.half], self.one, self.mate),
            lambda: (self.grad.at[self.half, 1 - self.side], self.two, self.other),
            lambda: (self.mine(), self.three, self.peer),
            lambda: (self.final.at[self.half], self.final.at[self.half], self.mate),
        )[n]()
        return remote(source, target, self.send.at[n], self.recv.at[n], device)

    def begin(self, n):
        self.began.add(n)
        self.copy(n).start()

    def first(self):
        self.begin(0)

    def second(self):
        self.copy(0).wait_recv()
        for side in range(2):
            self.grad[self.half, side] = (
                self.grad[self.half, side].astype(f32) + self.one[side].astype(f32)).astype(bf16)
        self.begin(1)

    def join(self):
        self.copy(1).wait_recv()
        mine = self.mine()
        mine[...] = (mine[...].astype(f32) + self.two[...].astype(f32)).astype(bf16)

    def quarter(self):
        self.join()
        self.saving().start()

    def resume(self):
        self.begin(2)

    def third(self):
        self.join()
        self.resume()

    def fourth(self):
        self.copy(2).wait_recv()
        self.final[self.half] = (self.mine()[...].astype(f32) + self.three[...].astype(f32)).astype(bf16)
        self.begin(3)

    def saving(self):
        return pltpu.make_async_copy(self.mine() if self.final is None else self.final, self.saved, self.save)

    def last(self):
        self.copy(3).wait_recv()
        self.saving().start()

    def settle(self):
        for n in sorted(self.began):
            self.copy(n).wait_send()
        self.saving().wait()


class Whole:
    def __init__(self, grad, sems, saved):
        self.copy = lambda: pltpu.make_async_copy(grad, saved, sems[2])

    def first(self):
        self.copy().start()

    def second(self):
        pass

    third = fourth = last = quarter = second

    def settle(self):
        self.copy().wait()


def fold_shapes(shapes, split, kinds):
    scratch = []
    for r, c in shapes:
        sizes = ((2, 2, r, c), (2, r, c), (r, c), (r, c), (2, r, c))
        if not split:
            kinds = (0,)
        elif 0 not in kinds:
            scratch.append(pltpu.VMEM((r, c), bf16))
        scratch += [pltpu.VMEM(sizes[kind], bf16) for kind in kinds]
    n = len(shapes)
    dma = pltpu.SemaphoreType.DMA
    scratch += [dma((n, 4)), dma((n, 4)), dma((n,))]
    ends = (2, 2) if not split else (2,) if 4 in kinds else ()
    return scratch, [jax.ShapeDtypeStruct(ends + (r, c), bf16) for r, c in shapes]


def make_folds(split, side, ring, scratch, saved, kinds):
    send, recv, save = scratch[-3:]
    folds, grads = [], []
    per = 1 if not split else len(kinds) + (0 not in kinds)
    for n, target in enumerate(saved):
        own = list(scratch[n * per : (n + 1) * per])
        sems = (send.at[n], recv.at[n], save.at[n])
        grads.append(own[0])
        if split:
            held = dict(zip(kinds if 0 in kinds else (0,) + kinds, own))
            folds.append(Fold(side, ring, [held.get(kind) for kind in range(5)], sems, target))
        else:
            folds.append(Whole(own[0], sems, target))
    return folds, grads


def turn(values, cosine, sine, sign=1.0):
    pieces = []
    half = HEAD_DIM // 2
    sine = sine * sign
    for at in range(0, values.shape[1], 128):
        piece = values[:, at : at + 128]
        swapped = jnp.where(
            low_half(piece.shape), pltpu.roll(piece, 128 - half, 1), pltpu.roll(piece, half, 1))
        pieces.append(piece * cosine + swapped * sine)
    return jnp.concatenate(pieces, axis=1)


def spread(target, values_t, start, rows):
    owner = lax.broadcasted_iota(jnp.int32, values_t.shape, 0) // HEAD_DIM
    for h in range(values_t.shape[0] // HEAD_DIM):
        target[h // 2, :, rows_at(h % 2 * rows + start, values_t.shape[1])] = jnp.where(
            owner == h, values_t, 0.0).astype(bf16)


def flat_row(folded):
    return jnp.concatenate([folded[n : n + 1, :].astype(f32) for n in range(folded.shape[0])], axis=1)


def gain_row(gains, which):
    return jnp.concatenate([gains[0, which : which + 1, :], gains[1, which : which + 1, :]], axis=1)


def front_kernel(split, *refs):
    place, ring, side = lax.axis_index("tp"), lax.axis_index("ctx"), lax.axis_index("fsdp")
    (tok, fv, cot_hbm, g1, g2, wq_in, wk_in, wv_in, wo_in, wg_in, wu_in, wd_in), refs = refs[:12], refs[12:]
    (prefix, sum_hbm, late_hbm, q_out, kv_hbm, attn_hbm, ctx_hbm, lse_out, gains, cosine, sine), refs = (
        refs[:11], refs[11:])
    saved, refs = refs[:3], refs[3:]
    if split:
        (wq_hbm, wk_hbm, wv_hbm, wo_hbm), refs = refs[:4], refs[4:]
        (wq, wk, wv, w_send, w_recv, w_save, g_sems, o_send, o_recv), refs = refs[:9], refs[9:]
    else:
        wq, wk, wv = wq_in, wk_in, wv_in
    (normed_s, kv, qtm, vt, acct, maxes, totals, part, inward, across,
     kv_send, kv_recv, kv_save, send_one, recv_one, send_two, recv_two, save,
     wg, wu, wd, loads, cot, inner_t, gg_t, ug_t, late, late_save, wo_all, ctx_all, attn,
     p_send, p_recv, c_send, c_recv, c_save, a_save), refs = refs[:37], refs[37:]
    (fold_d, fold_g, fold_u), grads = make_folds(split, side, ring, refs, saved, (0, 1, 2))
    seqs, rows, width = q_out.shape
    heads = width // HEAD_DIM
    tile = 256
    chunk, dim = part.shape[1:]
    per_seq = rows // chunk
    per_tile = tile // chunk
    middle = dim // 2
    units = wg_in.shape[-2]
    mate, peer = ring_peers(ring)
    half = lax.rem(ring, 2)
    for full in (wg, wu, wd):
        for piece in range(2):
            full[piece, units:] = jnp.zeros((full.shape[1] - units, full.shape[2]), bf16)
    own_loads = [pltpu.make_async_copy(cot_hbm, cot, loads.at[6])]
    for n, (source, full) in enumerate(((wg_in, wg), (wu_in, wu), (wd_in, wd))):
        if split:
            own_loads.append(pltpu.make_async_copy(source, full.at[side, 0:units], loads.at[n]))
        else:
            for piece in range(2):
                own_loads.append(pltpu.make_async_copy(
                    source.at[piece], full.at[piece, 0:units], loads.at[2 * n + piece]))
    greet(line_peers(place) + ring_peers(ring) + ([{"fsdp": 1 - side}] if split else []))

    if split:
        other = {"fsdp": 1 - side}
        for n, gain in enumerate((g1, g2)):
            gains[side, n : n + 1, :] = flat_row(gain)
        move_gains = remote(gains.at[side], gains.at[side], g_sems.at[0], g_sems.at[1], other)
        move_gains.start()

        def spot(full, owner, part_at, size):
            if full is wo_all:
                return full.at[place, owner, rows_at(part_at * size, size)]
            if full.shape[0] == 2:
                return full.at[owner, rows_at(part_at * size, size)]
            return full.at[rows_at((2 * owner + part_at) * size, size)]

        table = (
            (wk_in, wk, spot), (wv_in, wv, spot), (wq_in, wq, spot), (wo_in, wo_all, spot),
            (wg_in, wg, spot), (wu_in, wu, spot), (wd_in, wd, spot))

        def cross(n):
            own, full, where = table[n]
            size = own.shape[0] // 2
            return remote(own.at[rows_at(half * size, size)], where(full, side, half, size),
                          w_send.at[n, 0], w_recv.at[n, 0], other)

        def onto_mate(n):
            own, full, where = table[n]
            here = where(full, 1 - side, half, own.shape[0] // 2)
            return remote(here, here, w_send.at[n, 1], w_recv.at[n, 1], mate)

        def hand_on(n):
            cross(n).wait_recv()
            onto_mate(n).start()

        saves = tuple(
            pltpu.make_async_copy(full, target, w_save.at[n])
            for n, (full, target) in enumerate(((wk, wk_hbm), (wv, wv_hbm), (wq, wq_hbm), (wo_all.at[place], wo_hbm))))
        for n in range(3):
            cross(n).start()
        for own, full, _ in table[:3]:
            full[rows_at(side * own.shape[0], own.shape[0]), :] = own[...]
        wo_all[place, side] = wo_in[...]
        part_o = wo_in.shape[0] // 2
        item_side = lambda item: side if item == 0 else 1 - side
        pass_o = Passing(
            place, lambda piece, item: wo_all.at[piece, item_side(item), rows_at(half * part_o, part_o)],
            (p_send, p_recv),
            lambda item: wo_in.at[rows_at(half * part_o, part_o)] if item == 0 else None)
        pass_o.begin(0)

        def share_o(n):
            here = wo_all.at[lax.rem(place + n + 1, 4), :, rows_at(half * part_o, part_o)]
            return remote(here, here, o_send.at[n], o_recv.at[n], mate)
        remote(gains.at[side], gains.at[side], g_sems.at[0], g_sems.at[1], other).wait()
    else:
        size = gains.shape[2]
        for piece in range(2):
            for n, gain in enumerate((g1, g2)):
                gains[piece, n : n + 1, :] = flat_row(gain)[:, piece * size : (piece + 1) * size]
        wo_all[place] = wo_in[...]
        pass_o = Passing(place, lambda piece, item: wo_all.at[piece, item], (p_send, p_recv))
        pass_o.begin(0)
        pass_o.begin(1)

    for load in own_loads:
        load.start()

    def pass_block(s, which, source, target, device, slot):
        return remote(
            kv.at[s, source, which], kv.at[s, target, which], kv_send.at[s, which, slot],
            kv_recv.at[s, which, target], device)

    to_mate = lambda s, which: pass_block(s, which, 0, 1, mate, 0)
    to_peer = lambda s, which: pass_block(s, which, 0, 2, peer, 1)
    onward = lambda s, which: pass_block(s, which, 2, 3, mate, 2)
    gain_one = gain_row(gains, 0)
    fine = 16
    coarse_at = (ring * rows + fine * lax.broadcasted_iota(jnp.int32, (rows // fine, 128), 0)).astype(f32)
    fine_at = lax.broadcasted_iota(jnp.int32, (fine, 128), 0).astype(f32)
    step = lax.rem(lax.broadcasted_iota(jnp.int32, (1, 128), 1), HEAD_DIM // 2)
    frequency = jnp.ones((1, 128), f32)
    for bit in range(5):
        ratio = rope_base ** (-(2**bit) / (HEAD_DIM // 2))
        frequency = frequency * jnp.where(lax.rem(step // 2**bit, 2) == 1, ratio, 1.0)
    turns = [at * frequency for at in (coarse_at, fine_at)]
    (cos_a, sin_a), (cos_b, sin_b) = ((jnp.cos(x), jnp.sin(x)) for x in turns)
    cos_a, sin_a = cos_a[:, None, :], sin_a[:, None, :]
    cos_b, sin_b = cos_b[None], sin_b[None]
    cosine[...] = (cos_a * cos_b - sin_a * sin_b).reshape(rows, 128)
    sine[...] = (sin_a * cos_b + cos_a * sin_b).reshape(rows, 128) * jnp.where(
        low_half((rows, 128)), -1.0, 1.0)

    per_seq_tiles = rows // tile
    tiles = seqs * per_seq_tiles

    def tile_at(t):
        return t // per_seq_tiles, rows_at(lax.rem(t, per_seq_tiles) * tile, tile)

    @pl.loop(0, tiles)
    def _(t):
        s, at = tile_at(t)
        normed_s[s, at, :] = (unit_norm(tok[s, at, :].astype(f32)) * gain_one).astype(bf16)

    def keys(s):
        @pl.loop(0, per_seq_tiles)
        def _(t):
            at = rows_at(t * tile, tile)
            k = dot(normed_s[s, at, :], wk[...])
            kv[s, 0, 0, at, :] = turn(k, cosine[at, :], sine[at, :]).astype(bf16)

        to_peer(s, 0).start()
        to_mate(s, 0).start()

    def values(s):
        @pl.loop(0, per_seq_tiles)
        def _(t):
            at = rows_at(t * tile, tile)
            v = dot(normed_s[s, at, :], wv[...])
            kv[s, 0, 1, at, :] = (0.5 * v + 0.5 * fv[s, at, :].astype(f32)).astype(bf16)

        to_peer(s, 1).start()
        to_mate(s, 1).start()

    if split:
        hand_on(0)
        onto_mate(0).wait_recv()
    keys(0)
    if split:
        hand_on(1)
        cross(3).start()
        onto_mate(1).wait_recv()
    values(0)
    if split:
        hand_on(2)
    for s in range(1, seqs):
        keys(s)
        values(s)
    if split:
        onto_mate(2).wait_recv()

    @pl.loop(0, tiles)
    def _(t):
        s, at = tile_at(t)
        q = dot(normed_s[s, at, :], wq[...])
        q = turn(q, cosine[at, :], sine[at, :]) * HEAD_DIM ** (-0.5)
        q_out[s, at, :] = q.astype(bf16)
        spread(qtm.at[s], jnp.transpose(q), lax.rem(t, per_seq_tiles) * tile, rows)

    pass_o.step(0, 1)
    if split:
        hand_on(3)
        pass_o.begin(1)
        for n in range(4, 7):
            cross(n).start()

    def saving(i):
        return pltpu.make_async_copy(part.at[i], sum_hbm.at[i], save.at[i])

    sums = Sum(
        place, part, inward, across, (send_one, recv_one, send_two, recv_two), lambda i: saving(i).start())
    passing = Passing(place, lambda piece, item: ctx_all.at[piece, item], (c_send, c_recv))

    def saving_context(s):
        mine = pl.ds(s * per_seq_tiles, per_seq_tiles)
        return pltpu.make_async_copy(ctx_all.at[place, mine], ctx_hbm.at[mine], c_save.at[s])

    def saving_kv(s):
        return pltpu.make_async_copy(kv.at[s], kv_hbm.at[s], kv_save.at[s])

    @pl.loop(0, seqs)
    def _(s):
        maxes[...] = jnp.full_like(maxes, masked_score)
        totals[...] = jnp.zeros_like(totals)
        acct[...] = jnp.zeros_like(acct)

        @pl.loop(0, 4)
        def _(j):
            @pl.when(j == 1)
            def _():
                for which in range(2):
                    to_mate(s, which).wait_recv()

                @pl.when(s > 0)
                def _():
                    pass_o.step(1, 2)

            @pl.when(j == 2)
            def _():
                for which in range(2):
                    to_peer(s, which).wait_recv()
                    onward(s, which).start()

                @pl.when(s == 0)
                def _():
                    pass_o.step(0, 2)
                    pass_o.step(1, 1)

            @pl.when(j == 3)
            def _():
                for which in range(2):
                    onward(s, which).wait_recv()

                @pl.when(s > 0)
                def _():
                    pass_o.step(0, 3)
                    pass_o.step(1, 3)
                    if split:
                        for n in range(3):
                            share_o(n).start()
                        hand_on(6)

            vt[...] = jnp.transpose(kv[s, j, 1])
            key_pos = block_place(ring, j) * rows + lax.broadcasted_iota(jnp.int32, (rows, 1), 0)
            query_pos = ring * rows + lax.rem(lax.broadcasted_iota(jnp.int32, (1, 2 * rows), 1), rows)
            seen = key_pos < jnp.maximum(query_pos + 1, prefix[s])

            @pl.loop(0, heads // 2)
            def _(h):
                scores = jnp.where(seen, dot(kv[s, j, 0], qtm[s, h]), masked_score)
                old = maxes[h]
                new = jnp.maximum(old, jnp.max(scores, axis=0, keepdims=True))
                weights = jnp.exp(scores - new)
                fade = jnp.exp(old - new)
                maxes[h] = new
                totals[h] = totals[h] * fade + jnp.sum(weights, axis=0, keepdims=True)
                low = weights.astype(bf16)
                for n in range(2):
                    of_head = rows_at((2 * h + n) * HEAD_DIM, HEAD_DIM)
                    lanes = slice(n * rows, (n + 1) * rows)
                    acct[of_head, :] = acct[of_head, :] * fade[:, lanes] + dot(vt[of_head, :], low[:, lanes])
                at_step = j * (heads // 2) + h

                n = jnp.where(at_step == 7, 3, at_step // 2 - 1)

                @pl.when((s > 0) & (at_step > 1) & ((at_step == 7) | (lax.rem(at_step, 2) == 0)))
                def _():
                    passing.step((s - 1) * per_seq_tiles + lax.rem(n, per_seq_tiles), 1 + n // per_seq_tiles)

        for h in range(heads):
            if h % 2 == 0:
                lse_out[s, h // 2 : h // 2 + 1, :] = maxes[h // 2] + jnp.log(totals[h // 2])
            of_head = slice(h * HEAD_DIM, (h + 1) * HEAD_DIM)
            acct[of_head, :] = acct[of_head, :] / totals[h // 2][:, h % 2 * rows : (h % 2 + 1) * rows]
        for t in range(per_seq_tiles):
            ctx_all[place, s * per_seq_tiles + t] = jnp.transpose(acct[:, t * tile : (t + 1) * tile]).astype(bf16)
            passing.begin(s * per_seq_tiles + t)
        saving_context(s).start()
        saving_kv(s).start()

        @pl.when(s == 0)
        def _():
            if split:
                onto_mate(3).wait_recv()
                for copy in saves:
                    copy.start()
                hand_on(4)
                hand_on(5)

    if split:
        for n in range(3):
            share_o(n).wait_recv()
    if split:
        for n in range(4, 7):
            onto_mate(n).wait_recv()
    for load in own_loads:
        load.wait()
    lines = seqs * per_seq
    early = lines
    count = part.shape[0]
    gain_two = gain_row(gains, 1)

    def saving_attn(t):
        mine = pl.ds(t * per_tile, per_tile)
        return pltpu.make_async_copy(attn.at[mine], attn_hbm.at[mine], a_save.at[t])

    def across_both(left, full):
        return dot_nt(left[:, :middle], full[0]) + dot_nt(left[:, middle:], full[1])

    def saving_late(t):
        mine = pl.ds((t - 1) * per_tile, per_tile)
        return pltpu.make_async_copy(late.at[mine], late_hbm.at[mine], late_save.at[t - 1])

    stepped = [0]

    def act(*plan):
        for what in plan:
            if what == "sum":
                sums.steps(stepped[0], 1)
                stepped[0] += 1
            else:
                passing.step(*what)

    plans = {
        (0, 0): [(0, 3)], (0, 1): [(1, 3)], (0, 2): [(2, 1)], (0, 3): [],
        (1, 0): [], (1, 1): [(3, 1)], (1, 2): [], (1, 3): ["sum"],
        (2, 0): [(2, 2), "sum", (3, 2), "sum", (2, 3)], (2, 1): ["sum"], (2, 2): [], (2, 3): ["sum"],
        (3, 0): [(3, 3)], (3, 1): ["sum"], (3, 2): ["sum"], (3, 3): ["sum"],
    }
    for t in range(tiles):
        s, at = t // per_seq_tiles, slice(t % per_seq_tiles * tile, (t % per_seq_tiles + 1) * tile)
        flat = slice(t * tile, (t + 1) * tile)
        mine = t * per_tile
        act(*plans[t, 0])
        context = jnp.concatenate([ctx_all[p, t] for p in range(4)], axis=1)
        attended = [
            dot(context, jnp.concatenate([wo_all[p, piece] for p in range(4)], axis=0)) for piece in range(2)]
        for piece in range(2):
            for k in range(per_tile):
                attn[mine + k, :, piece * middle : (piece + 1) * middle] = attended[piece][
                    k * chunk : (k + 1) * chunk].astype(bf16)
        saving_attn(t).start()
        hidden = tok[s, at, :].astype(f32) + jnp.concatenate(attended, axis=1)
        normed = (unit_norm(hidden) * gain_two).astype(bf16)
        normed_s[s, at, :] = normed
        gate = across_both(normed, wg)
        up = across_both(normed, wu)
        sigmoid = jax.nn.sigmoid(gate)
        swish = gate * sigmoid
        inner = (swish * up).astype(bf16)
        inner_t[:, flat] = jnp.transpose(inner)
        inner_grad = across_both(cot[s, at, :], wd)
        gate_grad = (inner_grad * up * sigmoid * (1.0 + gate * (1.0 - sigmoid))).astype(bf16)
        up_grad = (inner_grad * swish).astype(bf16)
        act(*plans[t, 1])
        for piece in range(2):
            sums.fill(mine, piece, dot(gate_grad, wg[piece]) + dot(up_grad, wu[piece]))
        sums.offer(mine, per_tile)
        act(*plans[t, 2])
        feeds = [dot(inner, wd[piece]) for piece in range(2)]

        if t == 0:
            for piece in range(2):
                sums.fill(early, piece, feeds[piece])
        else:
            for piece in range(2):
                for k in range(per_tile):
                    late[mine - per_tile + k, :, piece * middle : (piece + 1) * middle] = feeds[piece][
                        k * chunk : (k + 1) * chunk].astype(bf16)
            saving_late(t).start()

        gg_t[:, flat] = jnp.transpose(gate_grad)
        ug_t[:, flat] = jnp.transpose(up_grad)
        act(*plans[t, 3])

    sums.offer(early, count - early)
    deep = units // 2

    def weight_grad(n, left_t, right):
        for h in range(2):
            for y in range(2):
                total = jnp.zeros((deep, middle), f32)
                for s in range(seqs):
                    total = total + dot(
                        left_t[h * deep : (h + 1) * deep, s * rows : (s + 1) * rows],
                        right[s, :, y * middle : (y + 1) * middle])
                grads[n][h, y] = total.astype(bf16)

    begun = stepped[0]
    weight_grad(0, inner_t, cot)
    fold_d.first()
    sums.steps(begun, 1)
    weight_grad(1, gg_t, normed_s)
    fold_g.first()
    fold_d.second()
    sums.steps(begun + 1, 1)
    weight_grad(2, ug_t, normed_s)
    fold_u.first()
    fold_g.second()
    sums.steps(begun + 2, 1)
    fold_u.second()
    sums.steps(begun + 3, 3)
    fold_d.quarter()
    sums.steps(begun + 6, 3)
    fold_g.quarter()
    sums.steps(begun + 9, count - begun - 9)
    fold_u.quarter()
    sums.settled(0, count)
    sums.close(count)
    for fold in (fold_d, fold_g, fold_u):
        fold.settle()
    for t in range(1, tiles):
        saving_late(t).wait()
    for s in range(seqs):
        for which in range(2):
            to_mate(s, which).wait_send()
            to_peer(s, which).wait_send()
            onward(s, which).wait_send()
        saving_kv(s).wait()
        saving_context(s).wait()
    for t in range(tiles):
        saving_attn(t).wait()
    pass_o.settle(2)
    passing.settle(tiles)

    @pl.loop(0, count)
    def _(i):
        saving(i).wait()

    if split:
        for n in range(7):
            cross(n).wait_send()
            onto_mate(n).wait_send()
        for n in range(3):
            share_o(n).wait_send()
        for copy in saves:
            copy.wait()


def limits(ident, megabytes=60):
    return pltpu.CompilerParams(
        collective_id=ident, has_side_effects=True, vmem_limit_bytes=megabytes * 1024 * 1024)


def front(split, tok, fv, cot, gains, square, wide, prefix):
    seqs, rows, dim = tok.shape
    width, units = square[0].shape[1], wide[0].shape[-2]
    heads = width // HEAD_DIM
    chunk, tile = 64, 256
    tokens = seqs * rows
    count = tokens // chunk + tile // chunk
    after = (tokens - tile) // chunk
    padded = -(-units // 256) * 256
    vmem = pl.BlockSpec(memory_space=pltpu.VMEM)
    anyw = pl.BlockSpec(memory_space=pl.ANY)
    dma = pltpu.SemaphoreType.DMA
    lines = pltpu.VMEM((count, chunk, dim), bf16)
    shape = jax.ShapeDtypeStruct
    full = [(dim, width)] * 3 + [(2, width, dim // 2)]
    fold_scratch, fold_outs = fold_shapes([(units // 2, dim // 2)] * 3, split, (0, 1, 2))
    outs = [
        shape((count, chunk, dim), bf16), shape((after, chunk, dim), bf16), shape((seqs, rows, width), bf16),
        shape((seqs, 4, 2, rows, width), bf16), shape((tokens // chunk, chunk, dim), bf16),
        shape((tokens // tile, tile, width), bf16),
        shape((seqs, heads // 2, 2 * rows), f32), shape((2, 8, dim // 2), f32),
        shape((rows, 128), f32), shape((rows, 128), f32)] + fold_outs
    out_specs = [anyw, anyw, vmem, anyw, anyw, anyw, vmem, vmem, vmem, vmem] + [anyw] * 3
    scratch = []
    if split:
        outs += [shape(size, bf16) for size in full]
        out_specs += [anyw] * 4
        scratch = [pltpu.VMEM(size, bf16) for size in full[:3]] + [
            dma((7, 2)), dma((7, 2)), dma((4,)), dma((2,)), dma((3,)), dma((3,))]
    scratch += [
        pltpu.VMEM((seqs, rows, dim), bf16),
        pltpu.VMEM((seqs, 4, 2, rows, width), bf16),
        pltpu.VMEM((seqs, heads // 2, width, 2 * rows), bf16),
        pltpu.VMEM((width, rows), bf16),
        pltpu.VMEM((width, rows), f32),
        pltpu.VMEM((heads // 2, 1, 2 * rows), f32),
        pltpu.VMEM((heads // 2, 1, 2 * rows), f32),
        lines, lines, lines,
        dma((seqs, 2, 3)), dma((seqs, 2, 4)), dma((seqs,)),
        dma((count,)), dma((count,)), dma((count,)), dma((count,)), dma((count,)),
        pltpu.VMEM((2, padded, dim // 2), bf16),
        pltpu.VMEM((2, padded, dim // 2), bf16),
        pltpu.VMEM((2, padded, dim // 2), bf16),
        dma((7,)),
        pltpu.VMEM((seqs, rows, dim), bf16),
        pltpu.VMEM((padded, tokens), bf16),
        pltpu.VMEM((padded, tokens), bf16),
        pltpu.VMEM((padded, tokens), bf16),
        pltpu.VMEM((after, chunk, dim), bf16),
        dma((tokens // tile,)),
        pltpu.VMEM((4, 2, width, dim // 2), bf16),
        pltpu.VMEM((4, tokens // tile, tile, width), bf16),
        pltpu.VMEM((tokens // chunk, chunk, dim), bf16),
        dma((2, 2, 4)), dma((2, 4)), dma((tokens // tile, 2, 4)), dma((tokens // tile, 4)),
        dma((seqs,)), dma((tokens // tile,)),
    ] + fold_scratch
    return pl.pallas_call(
        functools.partial(front_kernel, split),
        name="front",
        out_shape=outs,
        in_specs=[vmem] * 2 + [anyw] + [vmem] * 6 + [anyw] * 3 + [pl.BlockSpec(memory_space=pltpu.SMEM)],
        out_specs=out_specs,
        scratch_shapes=scratch,
        compiler_params=limits(0, 63),
        cost_estimate=pl.CostEstimate(flops=22 * 10**9, bytes_accessed=2 * 10**7, transcendentals=10**7),
    )(tok, fv, cot, *gains, *square, *wide, prefix)


def back_kernel(split, *refs):
    place, ring, side = lax.axis_index("tp"), lax.axis_index("ctx"), lax.axis_index("fsdp")
    quarters, refs = (refs[:3], refs[3:]) if split else ((), refs)
    loaded, refs = refs[:12], refs[12:]
    (gain_in, lse, cosine, sine, prefix, block_hbm, token_hbm, fv_hbm, gain_out), saved, refs = (
        refs[:9], refs[9:13], refs[13:])
    ends_saved, refs = (refs[:3], refs[3:]) if split else ((), refs)
    (tok, cot, wq, wk, wv, wo, q, kv, ctx, attn, mixed, early), refs = refs[:12], refs[12:]
    (hid, dwo_sum, qtm, qm, otm, om, kt, delta, dqt, dk, dv, give, take, proj, normed_t,
     part, inward, across, gain_part, gain_all,
     kv_send, kv_recv, send_one, recv_one, send_two, recv_two, save, gain_send, gain_recv, loads, fv_save), refs = (
        refs[:31], refs[31:])
    ends_scratch, refs = (refs[:12], refs[12:]) if split else ((), refs)
    (fold_o, fold_k, fold_v, fold_q), (dwo, dwk, dwv, dwq) = make_folds(split, side, ring, refs, saved, (0, 1, 2, 3, 4))
    ends, ends_mine = make_folds(split, side, ring, ends_scratch, ends_saved, (3, 4)) if split else ((), ())
    late_hbm, sum_hbm, attn_hbm, tok_hbm, cot_hbm, wq_hbm, wk_hbm, wv_hbm, wo_hbm, q_hbm, kv_hbm, ctx_hbm = loaded
    seqs, rows, dim = tok.shape
    width = wq.shape[1]
    heads = width // HEAD_DIM
    chunk = part.shape[1]
    per_seq = rows // chunk
    tile = 256
    per_tile = tile // chunk
    middle = dim // 2
    lines = seqs * per_seq
    count = 2 * lines - per_tile
    head_start = per_seq + 2
    rest = 2 * per_seq - per_tile - head_start
    rest_start = head_start + per_seq
    own_start = (head_start, rest_start + rest)
    mate, peer = ring_peers(ring)
    others = [(dy, dc) for dy in range(2) for dc in range(4) if dy or dc]
    group = [{"fsdp": lax.rem(side + dy, 2), "ctx": lax.rem(ring + dc, 4)} for dy, dc in others]

    copies = {}

    def load(name, source, target, start=True):
        copies[name] = pltpu.make_async_copy(source, target, loads.at[len(copies)])
        if start:
            copies[name].start()

    def ready(*names):
        for name in names:
            copies[name].wait()

    load("late", late_hbm.at[0:head_start], part.at[0:head_start])
    later = []
    for s in range(seqs):
        mine = slice(s * per_seq, (s + 1) * per_seq)
        for name, source, target in (
            ("tok", tok_hbm.at[s], tok.at[s]), ("attn", attn_hbm.at[mine], attn.at[mine]),
            ("cot", cot_hbm.at[s], cot), ("mixed", sum_hbm.at[mine], mixed),
            ("q", q_hbm.at[s], q.at[s]), ("ctx", ctx_hbm.at[s], ctx.at[s]), ("kv", kv_hbm.at[s], kv),
        ):
            now = s == 0 and name != "kv"
            load(f"{name}{s}", source, target, now)
            if not now and (s == 0 or name not in ("cot", "mixed", "kv")):
                later.append(f"{name}{s}")
        if s == 0:
            load("wo", wo_hbm, wo)
    for name, source, target in (
        [(f"quarter{n}", quarter, ends_mine[n]) for n, quarter in enumerate(quarters)] + [
            ("rest", late_hbm.at[head_start : head_start + rest], part.at[rest_start : rest_start + rest]),
            ("early", sum_hbm.at[lines : lines + per_tile], early),
            ("wq", wq_hbm, wq), ("wk", wk_hbm, wk), ("wv", wv_hbm, wv)]
    ):
        load(name, source, target, False)
        later.append(name)
    greet(line_peers(place) + (group if split else ring_peers(ring)))
    gain_one, gain_two = gain_row(gain_in, 0), gain_row(gain_in, 1)
    gain_part[...] = jnp.zeros_like(gain_part)

    def chunk_at(n):
        return n // per_seq, rows_at(lax.rem(n, per_seq) * chunk, chunk)

    def saving_block(i, n):
        s, own = chunk_at(n)
        return pltpu.make_async_copy(across.at[i], block_hbm.at[s, own], save.at[i])

    def saving_early(n):
        return pltpu.make_async_copy(early.at[n], block_hbm.at[0, n * chunk : (n + 1) * chunk], save.at[count + n])

    def saving_token(i, n):
        s, own = chunk_at(n)
        return pltpu.make_async_copy(hid.at[s, own], token_hbm.at[s, own], save.at[i])

    def add_gain(which, value):
        for piece in range(2):
            gain_part[piece, which : which + 1, :] += value[:, piece * middle : (piece + 1) * middle]

    is_block = lambda i: (i < head_start) | ((i >= rest_start) & (i < own_start[1]))
    block_of = lambda i: per_tile + jnp.where(i < head_start, i, i - per_seq)
    token_of = lambda i: jnp.where(i < rest_start, i - head_start, i - own_start[1] + per_seq)

    def done(i):
        @pl.when(is_block(i))
        def _():
            n = block_of(i)
            s, own = chunk_at(n)
            across[i] = (
                tok[s, own, :].astype(f32) + attn[n].astype(f32) + part[i].astype(f32)).astype(bf16)
            saving_block(i, n).start()

        @pl.when(jnp.logical_not(is_block(i)))
        def _():
            n = token_of(i)
            s, own = chunk_at(n)
            values, upstream = tok[s, own, :].astype(f32), part[i].astype(f32)
            factor = lax.rsqrt(jnp.mean(values * values, axis=-1, keepdims=True) + epsilon)
            scaled = upstream * gain_one
            add_gain(0, jnp.sum(upstream * values * factor, axis=0, keepdims=True))
            hid[s, own, :] += factor * scaled - values * factor**3 * jnp.mean(
                scaled * values, axis=-1, keepdims=True)
            saving_token(i, n).start()

    sums = Sum(place, part, inward, across, (send_one, recv_one, send_two, recv_two), done)

    def move(s, source, target, device):
        return remote(give.at[source], take.at[s, target], kv_send.at[source], kv_recv.at[s, target], device)

    far_to_mate = lambda s: move(s, 2, 0, mate)
    peer_back = lambda s: move(s, 1, 1, peer)
    near_to_mate = lambda s: move(s, 0, 2, mate)
    ready("late")
    sums.offer(0, head_start)
    for name in later:
        copies[name].start()

    def hidden_stage(s):
        @pl.loop(0, rows // tile)
        def _(t):
            at = rows_at(t * tile, tile)
            first = s * per_seq + t * per_tile
            join = lambda ref: jnp.concatenate([ref[first + k] for k in range(per_tile)], axis=0).astype(f32)
            token = tok[s, at, :].astype(f32)
            values = token + join(attn)
            upstream = jnp.concatenate(
                [mixed[t * per_tile + k] for k in range(per_tile)], axis=0).astype(f32)
            factor = lax.rsqrt(jnp.mean(values * values, axis=-1, keepdims=True) + epsilon)
            scaled = upstream * gain_two
            add_gain(1, jnp.sum(upstream * values * factor, axis=0, keepdims=True))
            hid_now = cot[at, :].astype(f32) + factor * scaled - values * factor**3 * jnp.mean(
                scaled * values, axis=-1, keepdims=True)
            hid[s, at, :] = hid_now
            low = hid_now.astype(bf16)
            dwo_sum[...] += dot(jnp.transpose(ctx[s, at, :]), low)
            left, right = low[:, :middle], low[:, middle:]
            grad = dot_nt(left, wo[0]) + dot_nt(right, wo[1])
            lane_owner = lax.broadcasted_iota(jnp.int32, grad.shape, 1) // HEAD_DIM
            q_now = q[s, at, :].astype(f32)
            grad_t = jnp.transpose(grad)
            q_t = jnp.transpose(q_now)
            product = jnp.transpose(grad.astype(bf16).astype(f32) * ctx[s, at, :].astype(f32))
            for h in range(heads):
                low_rows = rows_at(h % 2 * rows + t * tile, tile)
                om[h // 2, low_rows, :] = jnp.where(lane_owner == h, grad, 0.0).astype(bf16)
                qm[h // 2, low_rows, :] = jnp.where(lane_owner == h, q_now, 0.0).astype(bf16)
                delta[h // 2, :, low_rows] = jnp.sum(
                    product[h * HEAD_DIM : (h + 1) * HEAD_DIM], axis=0, keepdims=True)
            spread(otm, grad_t, t * tile, rows)
            spread(qtm, q_t, t * tile, rows)
            normed = (unit_norm(token) * gain_one).astype(bf16)
            normed_t[:, rows_at(s * rows + t * tile, tile)] = jnp.transpose(normed)

    def back_block(s, j, tick):
        kt[...] = jnp.transpose(kv[j, 0])
        key_pos = block_place(ring, j) * rows + lax.broadcasted_iota(jnp.int32, (rows, 1), 0)
        query_pos = ring * rows + lax.rem(lax.broadcasted_iota(jnp.int32, (1, 2 * rows), 1), rows)
        seen = key_pos < jnp.maximum(query_pos + 1, prefix[s])
        dk[...] = jnp.zeros_like(dk)
        dv[...] = jnp.zeros_like(dv)

        @pl.loop(0, heads // 2)
        def _(h):
            scores = dot(kv[j, 0], qtm[h])
            probs = jnp.where(seen, jnp.exp(scores - lse[s, pl.ds(h, 1), :]), 0.0)
            dprobs = dot(kv[j, 1], otm[h])
            dv[...] += dot(probs.astype(bf16), om[h])
            dscores = (probs * (dprobs - delta[h])).astype(bf16)
            dk[...] += dot(dscores, qm[h])
            for n in range(2):
                of_head = rows_at((2 * h + n) * HEAD_DIM, HEAD_DIM)
                dqt[of_head, :] += dot(kt[of_head, :], dscores[:, n * rows : (n + 1) * rows])
            tick(h)

    def finalize(s):
        near_to_mate(s).wait_recv()
        peer_back(s).wait_recv()
        @pl.loop(0, rows // tile)
        def _(t):
            at = rows_at(t * tile, tile)
            flat = rows_at(s * rows + t * tile, tile)
            co, si = cosine[at, :], sine[at, :]
            grad_v = 0.5 * (dv[at, :] + take[s, 2, 1, at, :].astype(f32) + take[s, 1, 1, at, :].astype(f32))
            grad_k = dk[at, :] + take[s, 2, 0, at, :].astype(f32) + take[s, 1, 0, at, :].astype(f32)
            grad_q = jnp.transpose(dqt[:, at]) * HEAD_DIM ** (-0.5)
            proj[0, flat, :] = turn(grad_q, co, si, -1.0).astype(bf16)
            proj[1, flat, :] = turn(grad_k, co, si, -1.0).astype(bf16)
            proj[2, flat, :] = grad_v.astype(bf16)
            i = jnp.where(s == 0, own_start[0], own_start[1]) + t * per_tile
            for piece in range(2):
                cut = slice(piece * middle, (piece + 1) * middle)
                sums.fill(i, piece, dot_nt(proj[0, flat, :], wq[cut, :]) + dot_nt(
                    proj[1, flat, :], wk[cut, :]) + dot_nt(proj[2, flat, :], wv[cut, :]))
            sums.offer(i, per_tile)

        @pl.when(s == 0)
        def _():
            sums.offer(rest_start, rest)

    ready("wo")
    dwo_sum[...] = jnp.zeros_like(dwo_sum)
    if split:
        ready("quarter0")
        ends[0].resume()

    def start_at(phase, *names):
        for wanted in range(1, seqs):
            @pl.when(phase == wanted - 1)
            def _():
                for name in names:
                    copies[f"{name}{wanted}"].start()

    def at_phase(phase, wanted, names):
        @pl.when(phase == wanted)
        def _():
            ready(*names)

    plan = [(1, m, line) for line, m in enumerate((0, 2, 3, 5, 7))] + [
        (2, m, 9 + line) for line, m in enumerate((1, 3, 4, 6))]

    @pl.loop(0, seqs + 1)
    def _(phase):
        s = jnp.maximum(phase - 1, 0)
        follows = phase > 1

        @pl.when(phase > 0)
        def _():
            for wanted in range(seqs):
                at_phase(phase, wanted + 1, [f"kv{wanted}"])
            dqt[...] = jnp.zeros_like(dqt)

            @pl.loop(0, 4)
            def _(n):
                def tick(h):
                    chosen = -1
                    for at_phase, at_step, line in plan:
                        chosen = jnp.where((phase == at_phase) & (2 * n + h == at_step), line, chosen)

                    @pl.when(chosen >= 0)
                    def _():
                        sums.steps(chosen, 1)

                back_block(s, 3 - n, tick)

                @pl.when(n == 0)
                def _():
                    @pl.when(follows)
                    def _():
                        far_to_mate(s - 1).wait_send()
                        fold_o.second()

                    give[2, 0] = dk[...].astype(bf16)
                    give[2, 1] = dv[...].astype(bf16)
                    far_to_mate(s).start()

                @pl.when(n == 1)
                def _():
                    far_to_mate(s).wait_recv()

                    @pl.when(follows)
                    def _():
                        peer_back(s - 1).wait_send()

                    give[1, 0] = (dk[...] + take[s, 0, 0].astype(f32)).astype(bf16)
                    give[1, 1] = (dv[...] + take[s, 0, 1].astype(f32)).astype(bf16)
                    peer_back(s).start()

                @pl.when(n == 2)
                def _():
                    @pl.when(follows)
                    def _():
                        near_to_mate(s - 1).wait_send()
                        fold_o.third()

                    give[0, 0] = dk[...].astype(bf16)
                    give[0, 1] = dv[...].astype(bf16)
                    near_to_mate(s).start()

            start_at(phase - 1, "kv")

        @pl.when(phase < seqs)
        def _():
            for wanted in range(seqs):
                at_phase(phase, wanted, [
                    f"{name}{wanted}" for name in ("tok", "attn", "cot", "mixed", "q", "ctx")])
            hidden_stage(phase)
            start_at(phase, "cot", "mixed")

            @pl.when(phase == 1)
            def _():
                sums.steps(5, 1)

        @pl.when(phase > 0)
        def _():
            at_phase(phase, 1, ["wq", "wk", "wv", "rest"])
            sums.steps(jnp.where(phase == 1, 6, 13), jnp.where(phase == 1, 1, 2))
            finalize(s)
            sums.steps(jnp.where(phase == 1, 7, 15), 1)

        @pl.when(phase == seqs - 1)
        def _():
            deep = dwo.shape[2]
            for h in range(2):
                for y in range(2):
                    dwo[h, y] = dwo_sum[h * deep : (h + 1) * deep, y * middle : (y + 1) * middle].astype(bf16)
            fold_o.first()
            if split:
                ends[0].fourth()
                ready("quarter1")
                ends[1].resume()
            sums.steps(8, 1)

    begun = 16
    fv_copy = pltpu.make_async_copy(proj.at[2], fv_hbm, fv_save)
    fv_copy.start()
    if split:
        ends[1].fourth()
        ready("quarter2")
        ends[2].resume()
        ends[0].last()
    share = dwq.shape[2]

    def square_grad(target, which):
        @pl.loop(0, 4)
        def _(k):
            h, y = k // 2, lax.rem(k, 2)
            target[h, y] = dot(normed_t[rows_at((2 * y + h) * share, share), :], proj[which]).astype(bf16)

    ready("early")
    for n in range(per_tile):
        own = slice(n * chunk, (n + 1) * chunk)
        early[n] = (tok[0, own, :].astype(f32) + attn[n].astype(f32) + early[n].astype(f32)).astype(bf16)
        saving_early(n).start()
    square_grad(dwk, 1)
    fold_k.first()
    sums.steps(begun, 1)
    square_grad(dwv, 2)
    fold_v.first()
    fold_k.second()
    sums.steps(begun + 1, 1)
    square_grad(dwq, 0)
    fold_q.first()
    fold_v.second()
    sums.steps(begun + 2, 1)
    fold_q.second()
    fold_o.fourth()
    sums.steps(begun + 3, 2)
    fold_k.third()
    sums.steps(begun + 5, 1)
    fold_v.third()
    sums.steps(begun + 6, 1)
    fold_q.third()
    fold_k.fourth()
    sums.steps(begun + 7, 1)
    fold_v.fourth()
    sums.steps(begun + 8, 1)
    fold_q.fourth()
    for fold in (fold_o, fold_k, fold_v) + tuple(ends[1:2]):
        fold.last()
    if split:
        ends[2].fourth()
    sums.steps(begun + 9, count - begun - 9)
    for fold in (fold_q,) + tuple(ends[2:]):
        fold.last()
    sums.settled(0, count)
    sums.close(count)
    if split:
        me = 4 * side + ring
        gain_all[me] = gain_part[side]

        def share_gain(n):
            dy, dc = others[n]
            y = lax.rem(side + dy, 2)
            return remote(gain_part.at[y], gain_all.at[me], gain_send.at[n], gain_recv.at[n], group[n])

        for n in range(7):
            share_gain(n).start()
        for n in range(7):
            share_gain(n).wait()
        total = gain_all[0]
        for n in range(1, 8):
            total = total + gain_all[n]
        gain_out[...] = total
    else:
        gain_out[...] = gain_part[...]
    for fold in (fold_o, fold_k, fold_v, fold_q) + tuple(ends):
        fold.settle()
    fv_copy.wait()
    for copy in (far_to_mate, peer_back, near_to_mate):
        copy(seqs - 1).wait_send()

    for n in range(per_tile):
        saving_early(n).wait()

    @pl.loop(0, count)
    def _(i):
        @pl.when(is_block(i))
        def _():
            saving_block(i, block_of(i)).wait()

        @pl.when(jnp.logical_not(is_block(i)))
        def _():
            saving_token(i, token_of(i)).wait()


def back(split, quarters, tok, cot, sums, attn, late, gains, square, q, kv, ctx, lse, cosine, sine, prefix):
    seqs, rows, dim = tok.shape
    width = q.shape[2]
    heads = width // HEAD_DIM
    _, chunk, _ = sums.shape
    tokens = seqs * rows
    early = 256 // chunk
    count = 2 * tokens // chunk - early
    vmem = pl.BlockSpec(memory_space=pltpu.VMEM)
    anyw = pl.BlockSpec(memory_space=pl.ANY)
    dma = pltpu.SemaphoreType.DMA
    lines = pltpu.VMEM((count, chunk, dim), bf16)
    half_lines = pltpu.VMEM((tokens // chunk, chunk, dim), bf16)
    wide = pltpu.VMEM((heads // 2, 2 * rows, width), bf16)
    tall = pltpu.VMEM((heads // 2, width, 2 * rows), bf16)
    shape = jax.ShapeDtypeStruct
    fold_scratch, fold_outs = fold_shapes(
        [(width // 2, dim // 2)] + [(dim // 4, width)] * 3, split, (0, 1, 2, 3, 4))
    ends_scratch, ends_outs = fold_shapes([x.shape for x in quarters], True, (3, 4)) if split else ([], [])
    loaded = (tok, cot) + tuple(square) + (q, kv, ctx)
    held = [tok.shape, cot.shape[1:]] + [x.shape for x in square] + [q.shape, kv.shape[1:], ctx.shape]
    return pl.pallas_call(
        functools.partial(back_kernel, split),
        name="back",
        out_shape=[
            shape((seqs, rows, dim), bf16), shape((seqs, rows, dim), f32), shape((tokens, width), bf16),
            shape((8, dim // 2) if split else (2, 8, dim // 2), f32)] + fold_outs + ends_outs,
        in_specs=[anyw] * (len(quarters) + 12) + [vmem] * 4 + [pl.BlockSpec(memory_space=pltpu.SMEM)],
        out_specs=[anyw, anyw, anyw, vmem] + [anyw] * (4 + len(quarters)),
        scratch_shapes=[pltpu.VMEM(x, bf16) for x in held] + [
            half_lines, pltpu.VMEM((rows // chunk, chunk, dim), bf16), pltpu.VMEM((early, chunk, dim), bf16),
            pltpu.VMEM((seqs, rows, dim), f32),
            pltpu.VMEM((width, dim), f32),
            tall, wide, tall, wide,
            pltpu.VMEM((width, rows), bf16),
            pltpu.VMEM((heads // 2, 1, 2 * rows), f32),
            pltpu.VMEM((width, rows), f32),
            pltpu.VMEM((rows, width), f32),
            pltpu.VMEM((rows, width), f32),
            pltpu.VMEM((3, 2, rows, width), bf16),
            pltpu.VMEM((seqs, 3, 2, rows, width), bf16),
            pltpu.VMEM((3, tokens, width), bf16),
            pltpu.VMEM((dim, tokens), bf16),
            lines, lines, lines,
            pltpu.VMEM((2, 8, dim // 2), f32),
            pltpu.VMEM((8, 8, dim // 2), f32),
            dma((3,)), dma((seqs, 3)),
            dma((count,)), dma((count,)), dma((count,)), dma((count,)), dma((count + early,)),
            dma((7,)), dma((7,)), dma((8 * seqs + 11,)), dma(()),
        ] + ends_scratch + fold_scratch,
        compiler_params=limits(2, 62),
        cost_estimate=pl.CostEstimate(flops=30 * 10**9, bytes_accessed=10**7, transcendentals=10**7),
    )(*quarters, late, sums, attn, *loaded, gains, lse, cosine, sine, prefix)


def finish_kernel(parts, *refs):
    n = len(parts)
    sources, gain_in, refs = refs[:n], refs[n], refs[n + 1 :]
    targets, gain_one, gain_two, refs = refs[:n], refs[n], refs[n + 1], refs[n + 2 :]
    held, wide, (loads, saves) = refs[:n], refs[n : 2 * n], refs[2 * n :]
    loading, saving = [], []
    for k, count in enumerate(parts):
        size = sources[k].shape[0] // count
        for piece in range(count):
            at = slice(piece * size, (piece + 1) * size)
            place = len(loading)
            loading.append(pltpu.make_async_copy(sources[k].at[at], held[k].at[at], loads.at[place]))
            plain = sources[k].dtype == targets[k].dtype
            saving.append((k, at, plain, pltpu.make_async_copy(
                (held if plain else wide)[k].at[at], targets[k].at[at], saves.at[place])))
    for load in loading:
        load.start()
    gain_one[...] = gain_in[0:1, :]
    gain_two[...] = gain_in[1:2, :]
    for load, (k, at, plain, save) in zip(loading, saving):
        load.wait()
        if not plain:
            wide[k][at] = held[k][at].astype(f32)
        save.start()
    for *_, save in saving:
        save.wait()


def finish(arrays, types, gain_rows):
    parts = [2 if x.size > 300000 else 1 for x in arrays]
    vmem = pl.BlockSpec(memory_space=pltpu.VMEM)
    anyw = pl.BlockSpec(memory_space=pl.ANY)
    dma = pltpu.SemaphoreType.DMA
    shape = jax.ShapeDtypeStruct
    row = shape((1, gain_rows.shape[1]), f32)
    return pl.pallas_call(
        functools.partial(finish_kernel, parts),
        name="finish",
        out_shape=[shape(x.shape, t) for x, t in zip(arrays, types)] + [row, row],
        in_specs=[anyw] * len(arrays) + [vmem],
        out_specs=[anyw] * len(arrays) + [vmem, vmem],
        scratch_shapes=[pltpu.VMEM(x.shape, x.dtype) for x in arrays] + [
            pltpu.VMEM((8, 128) if x.dtype == t else x.shape, f32) for x, t in zip(arrays, types)] + [
            dma((sum(parts),)), dma((sum(parts),))],
        compiler_params=pltpu.CompilerParams(vmem_limit_bytes=60 * 1024 * 1024),
        cost_estimate=pl.CostEstimate(flops=10**6, bytes_accessed=25 * 10**6, transcendentals=0),
    )(*arrays, gain_rows)


def halves(weight):
    rows, columns = weight.shape
    return jnp.swapaxes(weight.reshape(rows, 2, columns // 2), 0, 1)


def shards(
    tokens, first_values, norm1_gain, norm2_gain, w_query, w_key, w_value, w_out, w_gate, w_up, w_down,
    prefix, cotangent,
):
    split = lax.axis_size("fsdp") == 2
    seqs, rows, dim = tokens.shape
    width, units = w_query.shape[1], w_gate.shape[1]
    gather = functools.partial(lax.all_gather, axis_name="fsdp", tiled=True)
    if split:
        gains = (norm1_gain, norm2_gain)
        square = (w_query, w_key, w_value, w_out)
        wide = (w_gate.T, w_up.T, w_down)
    else:
        gains = (gather(norm1_gain), gather(norm2_gain))
        square = (gather(w_query), gather(w_key), gather(w_value), halves(gather(w_out, axis=1)))
        wide = (halves(gather(w_gate).T), halves(gather(w_up).T), halves(gather(w_down, axis=1)))
    (sums, late, query, pairs, attn, context, log_total, gain_rows, cosine, sine, down_grad, gate_grad, up_grad,
     *gathered) = front(
        split, tokens, first_values, cotangent, [gain.reshape(-1, 128) for gain in gains], square, wide, prefix)
    if split:
        square = tuple(gathered)
    wide_grads = (down_grad, gate_grad, up_grad)
    block_out, token_grad, half_value_grad, gain_grads, out_grad, key_grad, value_grad, query_grad, *ends = back(
        split, wide_grads if split else (), tokens, cotangent, sums, attn, late, gain_rows, square, query, pairs,
        context.reshape(query.shape), log_total, cosine, sine, prefix)
    half_value_grad = half_value_grad.reshape(seqs, rows, width)
    if split:
        arrays = (token_grad, block_out, half_value_grad, query_grad, key_grad, value_grad, out_grad, *ends)
        (token_grad, block_out, half_value_grad, query_grad, key_grad, value_grad, out_grad, down_grad, gate_grad,
         up_grad, gain_one_grad, gain_two_grad) = finish(arrays, (f32, bf16) + (f32,) * 8, gain_grads)
        over_rows = lambda grad: grad.reshape(-1, grad.shape[-1])
        over_columns = over_rows
        over_turned = lambda grad: over_rows(grad).T
        gain_one_grad, gain_two_grad = gain_one_grad[0], gain_two_grad[0]
    else:
        half_value_grad = half_value_grad.astype(f32)
        total = lambda grad, axis: lax.psum(
            lax.psum_scatter(grad, "fsdp", scatter_dimension=axis, tiled=True), "ctx").astype(f32)
        over_rows = lambda grad: total(jnp.swapaxes(grad, 0, 1).reshape(-1, grad.shape[-1]), 0)
        over_columns = lambda grad: total(
            jnp.transpose(grad, (0, 2, 1, 3)).reshape(2 * grad.shape[2], -1), 1)
        over_turned = lambda grad: over_columns(grad).T
        gain_one_grad, gain_two_grad = (total(gain_grads[:, n].reshape(-1), 0) for n in range(2))
    return (
        block_out,
        token_grad,
        half_value_grad,
        gain_one_grad,
        gain_two_grad,
        over_rows(query_grad),
        over_rows(key_grad),
        over_rows(value_grad),
        over_columns(out_grad),
        over_turned(gate_grad),
        over_turned(up_grad),
        over_columns(down_grad),
    )


def solution(mesh):
    return jax.shard_map(
        shards,
        mesh=mesh,
        in_specs=(
            P("fsdp", "ctx", None),
            P("fsdp", "ctx", "tp"),
            P("fsdp"),
            P("fsdp"),
            P("fsdp", "tp"),
            P("fsdp", "tp"),
            P("fsdp", "tp"),
            P("tp", "fsdp"),
            P("fsdp", "tp"),
            P("fsdp", "tp"),
            P("tp", "fsdp"),
            P("fsdp"),
            P("fsdp", "ctx", None),
        ),
        out_specs=(
            P("fsdp", "ctx", None),
            P("fsdp", "ctx", None),
            P("fsdp", "ctx", "tp"),
            P("fsdp"),
            P("fsdp"),
            P("fsdp", "tp"),
            P("fsdp", "tp"),
            P("fsdp", "tp"),
            P("tp", "fsdp"),
            P("fsdp", "tp"),
            P("fsdp", "tp"),
            P("tp", "fsdp"),
        ),
        check_vma=False,
    )
```

```python
import functools

import jax
import jax.numpy as jnp
from jax import lax
from jax.experimental import pallas as pl
from jax.experimental.pallas import tpu as pltpu
from jax.sharding import PartitionSpec as P

HEAD_DIM = 64
epsilon = 1e-06
rope_base = 10000.0
masked_score = -1e30
MESH = pl.DeviceIdType.MESH
bf16 = jnp.bfloat16
f32 = jnp.float32


def dot(a, b):
    return jnp.dot(a, b, preferred_element_type=f32)


def dot_nt(a, b):
    return lax.dot_general(a, b, (((1,), (1,)), ((), ())), preferred_element_type=f32)


def unit_norm(values):
    return values * lax.rsqrt(jnp.mean(values * values, axis=-1, keepdims=True) + epsilon)


def low_half(shape):
    return lax.rem(lax.broadcasted_iota(jnp.int32, shape, 1), HEAD_DIM) < HEAD_DIM // 2


class Sum:
    lag = 2

    def __init__(self, place, part, inward, across, sems, done):
        self.pair = near(place)
        self.middle = 3 - place
        self.inner = (place == 1) | (place == 2)
        self.outer = (place == 0) | (place == 3)
        self.part, self.inward, self.across, self.done = part, inward, across, done
        self.send_one, self.recv_one, self.send_two, self.recv_two = sems

    def copy_in(self, i):
        return remote(
            self.part.at[i], self.inward.at[i], self.send_one.at[i], self.recv_one.at[i], {"tp": self.pair})

    def copy_across(self, i):
        return remote(
            self.part.at[i], self.across.at[i], self.send_two.at[i], self.recv_two.at[i], {"tp": self.middle})

    def copy_out(self, i):
        return remote(
            self.part.at[i], self.inward.at[i], self.send_one.at[i], self.recv_one.at[i], {"tp": self.pair})

    def fill(self, first, piece, values):
        chunk, size = self.part.shape[1], values.shape[1]
        for k in range(values.shape[0] // chunk):
            self.part[first + k, :, piece * size : (piece + 1) * size] = values[
                k * chunk : (k + 1) * chunk].astype(bf16)

    def offer(self, first, count):
        @pl.when(self.outer)
        def _():
            @pl.loop(0, count)
            def _(k):
                self.copy_in(first + k).start()

    def take_in(self, i):
        self.copy_in(i).wait_recv()
        self.part[i] = (self.part[i].astype(f32) + self.inward[i].astype(f32)).astype(bf16)
        self.copy_across(i).start()

    def finish(self, i):
        self.copy_across(i).wait()
        self.part[i] = (self.part[i].astype(f32) + self.across[i].astype(f32)).astype(bf16)
        self.copy_out(i).start()
        self.done(i)

    def steps(self, first, count):
        @pl.when(self.inner)
        def _():
            @pl.loop(first, first + count)
            def _(i):
                self.take_in(i)

                @pl.when(i >= self.lag)
                def _():
                    self.finish(i - self.lag)

    def settled(self, first, count):
        @pl.when(self.outer)
        def _():
            @pl.loop(first, first + count)
            def _(i):
                self.copy_out(i).wait_recv()
                self.copy_in(i).wait_send()
                self.part[i] = self.inward[i]
                self.done(i)

    def close(self, count):
        @pl.when(self.inner)
        def _():
            for n in range(self.lag):
                self.finish(count - self.lag + n)

            @pl.loop(0, count)
            def _(i):
                self.copy_out(i).wait_send()


def near(place):
    return place + 1 - 2 * lax.rem(place, 2)


def greet(peers):
    barrier = pltpu.get_barrier_semaphore()
    for peer in peers:
        pl.semaphore_signal(barrier, inc=1, device_id=peer, device_id_type=MESH)
    pl.semaphore_wait(barrier, len(peers))


def block_place(ring, j):
    return jnp.where(
        j == 0, ring, jnp.where(j == 1, near(ring), jnp.where(j == 2, lax.rem(ring + 2, 4), 3 - ring)))


def line_peers(place):
    return [{"tp": near(place)}, {"tp": 3 - place}]


def ring_peers(ring):
    return [{"ctx": near(ring)}, {"ctx": lax.rem(ring + 2, 4)}]


def remote(source, target, send, recv, device):
    return pltpu.make_async_remote_copy(
        src_ref=source, dst_ref=target, send_sem=send, recv_sem=recv,
        device_id=device, device_id_type=MESH)


class Passing:
    def __init__(self, place, spot, sems, own=None):
        self.place, self.spot, self.own = place, spot, own
        self.send, self.recv = sems

    def move(self, piece, item, way, source=None):
        here = self.spot(piece, item)
        return remote(
            here if source is None else source, here, self.send.at[item, way, piece], self.recv.at[item, piece],
            {"tp": self.place + 1 - 2 * way})

    def begin(self, item):
        source = None if self.own is None else self.own(item)

        @pl.when(self.place < 3)
        def _():
            self.move(self.place, item, 0, source).start()

        @pl.when(self.place > 0)
        def _():
            self.move(self.place, item, 1, source).start()

    def step(self, item, distance):
        @pl.when(self.place >= distance)
        def _():
            piece = self.place - distance
            self.move(piece, item, 0).wait_recv()

            @pl.when(self.place < 3)
            def _():
                self.move(piece, item, 0).start()

        @pl.when(self.place + distance <= 3)
        def _():
            piece = self.place + distance
            self.move(piece, item, 1).wait_recv()

            @pl.when(self.place > 0)
            def _():
                self.move(piece, item, 1).start()

    def settle(self, items):
        for item in range(items):
            @pl.loop(0, 4)
            def _(piece, item=item):
                @pl.when((self.place < 3) & (piece <= self.place))
                def _():
                    self.move(piece, item, 0).wait_send()

                @pl.when((self.place > 0) & (piece >= self.place))
                def _():
                    self.move(piece, item, 1).wait_send()


def rows_at(start, size):
    return pl.ds(pl.multiple_of(start, size), size)


class Fold:
    def __init__(self, side, ring, refs, sems, saved):
        self.side, self.half = side, lax.rem(ring, 2)
        self.grad, self.one, self.two, self.three, self.final = refs
        self.send, self.recv, self.save = sems
        self.mate, self.peer, self.other = (
            {"ctx": near(ring)}, {"ctx": lax.rem(ring + 2, 4)}, {"fsdp": 1 - side})
        self.saved = saved
        self.began = set()

    def mine(self):
        return self.grad if self.one is None else self.grad.at[self.half, self.side]

    def copy(self, n):
        source, target, device = (
            lambda: (self.grad.at[1 - self.half], self.one, self.mate),
            lambda: (self.grad.at[self.half, 1 - self.side], self.two, self.other),
            lambda: (self.mine(), self.three, self.peer),
            lambda: (self.final.at[self.half], self.final.at[self.half], self.mate),
        )[n]()
        return remote(source, target, self.send.at[n], self.recv.at[n], device)

    def begin(self, n):
        self.began.add(n)
        self.copy(n).start()

    def first(self):
        self.begin(0)

    def second(self):
        self.copy(0).wait_recv()
        for side in range(2):
            self.grad[self.half, side] = (
                self.grad[self.half, side].astype(f32) + self.one[side].astype(f32)).astype(bf16)
        self.begin(1)

    def join(self):
        self.copy(1).wait_recv()
        mine = self.mine()
        mine[...] = (mine[...].astype(f32) + self.two[...].astype(f32)).astype(bf16)

    def quarter(self):
        self.join()
        self.saving().start()

    def resume(self):
        self.begin(2)

    def third(self):
        self.join()
        self.resume()

    def fourth(self):
        self.copy(2).wait_recv()
        self.final[self.half] = (self.mine()[...].astype(f32) + self.three[...].astype(f32)).astype(bf16)
        self.begin(3)

    def saving(self):
        return pltpu.make_async_copy(self.mine() if self.final is None else self.final, self.saved, self.save)

    def last(self):
        self.copy(3).wait_recv()
        self.saving().start()

    def settle(self):
        for n in sorted(self.began):
            self.copy(n).wait_send()
        self.saving().wait()


class Whole:
    def __init__(self, grad, sems, saved):
        self.copy = lambda: pltpu.make_async_copy(grad, saved, sems[2])

    def first(self):
        self.copy().start()

    def second(self):
        pass

    third = fourth = last = quarter = second

    def settle(self):
        self.copy().wait()


def fold_shapes(shapes, split, kinds):
    scratch = []
    for r, c in shapes:
        sizes = ((2, 2, r, c), (2, r, c), (r, c), (r, c), (2, r, c))
        if not split:
            kinds = (0,)
        elif 0 not in kinds:
            scratch.append(pltpu.VMEM((r, c), bf16))
        scratch += [pltpu.VMEM(sizes[kind], bf16) for kind in kinds]
    n = len(shapes)
    dma = pltpu.SemaphoreType.DMA
    scratch += [dma((n, 4)), dma((n, 4)), dma((n,))]
    ends = (2, 2) if not split else (2,) if 4 in kinds else ()
    return scratch, [jax.ShapeDtypeStruct(ends + (r, c), bf16) for r, c in shapes]


def make_folds(split, side, ring, scratch, saved, kinds):
    send, recv, save = scratch[-3:]
    folds, grads = [], []
    per = 1 if not split else len(kinds) + (0 not in kinds)
    for n, target in enumerate(saved):
        own = list(scratch[n * per : (n + 1) * per])
        sems = (send.at[n], recv.at[n], save.at[n])
        grads.append(own[0])
        if split:
            held = dict(zip(kinds if 0 in kinds else (0,) + kinds, own))
            folds.append(Fold(side, ring, [held.get(kind) for kind in range(5)], sems, target))
        else:
            folds.append(Whole(own[0], sems, target))
    return folds, grads


def turn(values, cosine, sine, sign=1.0):
    pieces = []
    half = HEAD_DIM // 2
    sine = sine * sign
    for at in range(0, values.shape[1], 128):
        piece = values[:, at : at + 128]
        swapped = jnp.where(
            low_half(piece.shape), pltpu.roll(piece, 128 - half, 1), pltpu.roll(piece, half, 1))
        pieces.append(piece * cosine + swapped * sine)
    return jnp.concatenate(pieces, axis=1)


def spread(target, values_t, start, rows):
    owner = lax.broadcasted_iota(jnp.int32, values_t.shape, 0) // HEAD_DIM
    for h in range(values_t.shape[0] // HEAD_DIM):
        target[h // 2, :, rows_at(h % 2 * rows + start, values_t.shape[1])] = jnp.where(
            owner == h, values_t, 0.0).astype(bf16)


def flat_row(folded):
    return jnp.concatenate([folded[n : n + 1, :].astype(f32) for n in range(folded.shape[0])], axis=1)


def gain_row(gains, which):
    return jnp.concatenate([gains[0, which : which + 1, :], gains[1, which : which + 1, :]], axis=1)


def front_kernel(split, *refs):
    place, ring, side = lax.axis_index("tp"), lax.axis_index("ctx"), lax.axis_index("fsdp")
    (tok, fv, cot_hbm, g1, g2, wq_in, wk_in, wv_in, wo_in, wg_in, wu_in, wd_in), refs = refs[:12], refs[12:]
    (prefix, sum_hbm, late_hbm, q_out, kv_hbm, attn_hbm, ctx_hbm, lse_out, gains, cosine, sine), refs = (
        refs[:11], refs[11:])
    saved, refs = refs[:3], refs[3:]
    if split:
        (wq_hbm, wk_hbm, wv_hbm, wo_hbm), refs = refs[:4], refs[4:]
        (wq, wk, wv, w_send, w_recv, w_save, g_sems, o_send, o_recv), refs = refs[:9], refs[9:]
    else:
        wq, wk, wv = wq_in, wk_in, wv_in
    (normed_s, kv, qtm, vt, acct, maxes, totals, part, inward, across,
     kv_send, kv_recv, kv_save, send_one, recv_one, send_two, recv_two, save,
     wg, wu, wd, loads, cot, inner_t, gg_t, ug_t, late, late_save, wo_all, ctx_all, attn,
     p_send, p_recv, c_send, c_recv, c_save, a_save), refs = refs[:37], refs[37:]
    (fold_d, fold_g, fold_u), grads = make_folds(split, side, ring, refs, saved, (0, 1, 2))
    seqs, rows, width = q_out.shape
    heads = width // HEAD_DIM
    tile = 256
    chunk, dim = part.shape[1:]
    per_seq = rows // chunk
    per_tile = tile // chunk
    middle = dim // 2
    units = wg_in.shape[-2]
    mate, peer = ring_peers(ring)
    half = lax.rem(ring, 2)
    for full in (wg, wu, wd):
        for piece in range(2):
            full[piece, units:] = jnp.zeros((full.shape[1] - units, full.shape[2]), bf16)
    own_loads = [pltpu.make_async_copy(cot_hbm, cot, loads.at[6])]
    for n, (source, full) in enumerate(((wg_in, wg), (wu_in, wu), (wd_in, wd))):
        if split:
            own_loads.append(pltpu.make_async_copy(source, full.at[side, 0:units], loads.at[n]))
        else:
            for piece in range(2):
                own_loads.append(pltpu.make_async_copy(
                    source.at[piece], full.at[piece, 0:units], loads.at[2 * n + piece]))
    greet(line_peers(place) + ring_peers(ring) + ([{"fsdp": 1 - side}] if split else []))

    if split:
        other = {"fsdp": 1 - side}
        for n, gain in enumerate((g1, g2)):
            gains[side, n : n + 1, :] = flat_row(gain)
        move_gains = remote(gains.at[side], gains.at[side], g_sems.at[0], g_sems.at[1], other)
        move_gains.start()

        def spot(full, owner, part_at, size):
            if full is wo_all:
                return full.at[place, owner, rows_at(part_at * size, size)]
            if full.shape[0] == 2:
                return full.at[owner, rows_at(part_at * size, size)]
            return full.at[rows_at((2 * owner + part_at) * size, size)]

        table = (
            (wk_in, wk, spot), (wv_in, wv, spot), (wq_in, wq, spot), (wo_in, wo_all, spot),
            (wg_in, wg, spot), (wu_in, wu, spot), (wd_in, wd, spot))

        def cross(n):
            own, full, where = table[n]
            size = own.shape[0] // 2
            return remote(own.at[rows_at(half * size, size)], where(full, side, half, size),
                          w_send.at[n, 0], w_recv.at[n, 0], other)

        def onto_mate(n):
            own, full, where = table[n]
            here = where(full, 1 - side, half, own.shape[0] // 2)
            return remote(here, here, w_send.at[n, 1], w_recv.at[n, 1], mate)

        def hand_on(n):
            cross(n).wait_recv()
            onto_mate(n).start()

        saves = tuple(
            pltpu.make_async_copy(full, target, w_save.at[n])
            for n, (full, target) in enumerate(((wk, wk_hbm), (wv, wv_hbm), (wq, wq_hbm), (wo_all.at[place], wo_hbm))))
        for n in range(3):
            cross(n).start()
        for own, full, _ in table[:3]:
            full[rows_at(side * own.shape[0], own.shape[0]), :] = own[...]
        wo_all[place, side] = wo_in[...]
        part_o = wo_in.shape[0] // 2
        item_side = lambda item: side if item == 0 else 1 - side
        pass_o = Passing(
            place, lambda piece, item: wo_all.at[piece, item_side(item), rows_at(half * part_o, part_o)],
            (p_send, p_recv),
            lambda item: wo_in.at[rows_at(half * part_o, part_o)] if item == 0 else None)
        pass_o.begin(0)

        def share_o(n):
            here = wo_all.at[lax.rem(place + n + 1, 4), :, rows_at(half * part_o, part_o)]
            return remote(here, here, o_send.at[n], o_recv.at[n], mate)
        remote(gains.at[side], gains.at[side], g_sems.at[0], g_sems.at[1], other).wait()
    else:
        size = gains.shape[2]
        for piece in range(2):
            for n, gain in enumerate((g1, g2)):
                gains[piece, n : n + 1, :] = flat_row(gain)[:, piece * size : (piece + 1) * size]
        wo_all[place] = wo_in[...]
        pass_o = Passing(place, lambda piece, item: wo_all.at[piece, item], (p_send, p_recv))
        pass_o.begin(0)
        pass_o.begin(1)

    for load in own_loads:
        load.start()

    def pass_block(s, which, source, target, device, slot):
        return remote(
            kv.at[s, source, which], kv.at[s, target, which], kv_send.at[s, which, slot],
            kv_recv.at[s, which, target], device)

    to_mate = lambda s, which: pass_block(s, which, 0, 1, mate, 0)
    to_peer = lambda s, which: pass_block(s, which, 0, 2, peer, 1)
    onward = lambda s, which: pass_block(s, which, 2, 3, mate, 2)
    gain_one = gain_row(gains, 0)
    fine = 16
    coarse_at = (ring * rows + fine * lax.broadcasted_iota(jnp.int32, (rows // fine, 128), 0)).astype(f32)
    fine_at = lax.broadcasted_iota(jnp.int32, (fine, 128), 0).astype(f32)
    step = lax.rem(lax.broadcasted_iota(jnp.int32, (1, 128), 1), HEAD_DIM // 2)
    frequency = jnp.ones((1, 128), f32)
    for bit in range(5):
        ratio = rope_base ** (-(2**bit) / (HEAD_DIM // 2))
        frequency = frequency * jnp.where(lax.rem(step // 2**bit, 2) == 1, ratio, 1.0)
    turns = [at * frequency for at in (coarse_at, fine_at)]
    (cos_a, sin_a), (cos_b, sin_b) = ((jnp.cos(x), jnp.sin(x)) for x in turns)
    cos_a, sin_a = cos_a[:, None, :], sin_a[:, None, :]
    cos_b, sin_b = cos_b[None], sin_b[None]
    cosine[...] = (cos_a * cos_b - sin_a * sin_b).reshape(rows, 128)
    sine[...] = (sin_a * cos_b + cos_a * sin_b).reshape(rows, 128) * jnp.where(
        low_half((rows, 128)), -1.0, 1.0)

    per_seq_tiles = rows // tile
    tiles = seqs * per_seq_tiles

    def tile_at(t):
        return t // per_seq_tiles, rows_at(lax.rem(t, per_seq_tiles) * tile, tile)

    @pl.loop(0, tiles)
    def _(t):
        s, at = tile_at(t)
        normed_s[s, at, :] = (unit_norm(tok[s, at, :].astype(f32)) * gain_one).astype(bf16)

    def keys(s):
        @pl.loop(0, per_seq_tiles)
        def _(t):
            at = rows_at(t * tile, tile)
            k = dot(normed_s[s, at, :], wk[...])
            kv[s, 0, 0, at, :] = turn(k, cosine[at, :], sine[at, :]).astype(bf16)

        to_peer(s, 0).start()
        to_mate(s, 0).start()

    def values(s):
        @pl.loop(0, per_seq_tiles)
        def _(t):
            at = rows_at(t * tile, tile)
            v = dot(normed_s[s, at, :], wv[...])
            kv[s, 0, 1, at, :] = (0.5 * v + 0.5 * fv[s, at, :].astype(f32)).astype(bf16)

        to_peer(s, 1).start()
        to_mate(s, 1).start()

    if split:
        hand_on(0)
        onto_mate(0).wait_recv()
    keys(0)
    if split:
        hand_on(1)
        cross(3).start()
        onto_mate(1).wait_recv()
    values(0)
    if split:
        hand_on(2)
    for s in range(1, seqs):
        keys(s)
        values(s)
    if split:
        onto_mate(2).wait_recv()

    @pl.loop(0, tiles)
    def _(t):
        s, at = tile_at(t)
        q = dot(normed_s[s, at, :], wq[...])
        q = turn(q, cosine[at, :], sine[at, :]) * HEAD_DIM ** (-0.5)
        q_out[s, at, :] = q.astype(bf16)
        spread(qtm.at[s], jnp.transpose(q), lax.rem(t, per_seq_tiles) * tile, rows)

    pass_o.step(0, 1)
    if split:
        hand_on(3)
        pass_o.begin(1)
        for n in range(4, 7):
            cross(n).start()

    def saving(i):
        return pltpu.make_async_copy(part.at[i], sum_hbm.at[i], save.at[i])

    sums = Sum(
        place, part, inward, across, (send_one, recv_one, send_two, recv_two), lambda i: saving(i).start())
    passing = Passing(place, lambda piece, item: ctx_all.at[piece, item], (c_send, c_recv))

    def saving_context(s):
        mine = pl.ds(s * per_seq_tiles, per_seq_tiles)
        return pltpu.make_async_copy(ctx_all.at[place, mine], ctx_hbm.at[mine], c_save.at[s])

    def saving_kv(s):
        return pltpu.make_async_copy(kv.at[s], kv_hbm.at[s], kv_save.at[s])

    @pl.loop(0, seqs)
    def _(s):
        maxes[...] = jnp.full_like(maxes, masked_score)
        totals[...] = jnp.zeros_like(totals)
        acct[...] = jnp.zeros_like(acct)

        @pl.loop(0, 4)
        def _(j):
            @pl.when(j == 1)
            def _():
                for which in range(2):
                    to_mate(s, which).wait_recv()

                @pl.when(s > 0)
                def _():
                    pass_o.step(1, 2)

            @pl.when(j == 2)
            def _():
                for which in range(2):
                    to_peer(s, which).wait_recv()
                    onward(s, which).start()

                @pl.when(s == 0)
                def _():
                    pass_o.step(0, 2)
                    pass_o.step(1, 1)

            @pl.when(j == 3)
            def _():
                for which in range(2):
                    onward(s, which).wait_recv()

                @pl.when(s > 0)
                def _():
                    pass_o.step(0, 3)
                    pass_o.step(1, 3)
                    if split:
                        for n in range(3):
                            share_o(n).start()
                        hand_on(6)

            vt[...] = jnp.transpose(kv[s, j, 1])
            key_pos = block_place(ring, j) * rows + lax.broadcasted_iota(jnp.int32, (rows, 1), 0)
            query_pos = ring * rows + lax.rem(lax.broadcasted_iota(jnp.int32, (1, 2 * rows), 1), rows)
            seen = key_pos < jnp.maximum(query_pos + 1, prefix[s])

            @pl.loop(0, heads // 2)
            def _(h):
                scores = jnp.where(seen, dot(kv[s, j, 0], qtm[s, h]), masked_score)
                old = maxes[h]
                new = jnp.maximum(old, jnp.max(scores, axis=0, keepdims=True))
                weights = jnp.exp(scores - new)
                fade = jnp.exp(old - new)
                maxes[h] = new
                totals[h] = totals[h] * fade + jnp.sum(weights, axis=0, keepdims=True)
                low = weights.astype(bf16)
                for n in range(2):
                    of_head = rows_at((2 * h + n) * HEAD_DIM, HEAD_DIM)
                    lanes = slice(n * rows, (n + 1) * rows)
                    acct[of_head, :] = acct[of_head, :] * fade[:, lanes] + dot(vt[of_head, :], low[:, lanes])
                at_step = j * (heads // 2) + h

                n = jnp.where(at_step == 7, 3, at_step // 2 - 1)

                @pl.when((s > 0) & (at_step > 1) & ((at_step == 7) | (lax.rem(at_step, 2) == 0)))
                def _():
                    passing.step((s - 1) * per_seq_tiles + lax.rem(n, per_seq_tiles), 1 + n // per_seq_tiles)

        for h in range(heads):
            if h % 2 == 0:
                lse_out[s, h // 2 : h // 2 + 1, :] = maxes[h // 2] + jnp.log(totals[h // 2])
            of_head = slice(h * HEAD_DIM, (h + 1) * HEAD_DIM)
            acct[of_head, :] = acct[of_head, :] / totals[h // 2][:, h % 2 * rows : (h % 2 + 1) * rows]
        for t in range(per_seq_tiles):
            ctx_all[place, s * per_seq_tiles + t] = jnp.transpose(acct[:, t * tile : (t + 1) * tile]).astype(bf16)
            passing.begin(s * per_seq_tiles + t)
        saving_context(s).start()
        saving_kv(s).start()

        @pl.when(s == 0)
        def _():
            if split:
                onto_mate(3).wait_recv()
                for copy in saves:
                    copy.start()
                hand_on(4)
                hand_on(5)

    if split:
        for n in range(3):
            share_o(n).wait_recv()
    if split:
        for n in range(4, 7):
            onto_mate(n).wait_recv()
    for load in own_loads:
        load.wait()
    lines = seqs * per_seq
    early = lines
    count = part.shape[0]
    gain_two = gain_row(gains, 1)

    def saving_attn(t):
        mine = pl.ds(t * per_tile, per_tile)
        return pltpu.make_async_copy(attn.at[mine], attn_hbm.at[mine], a_save.at[t])

    def across_both(left, full):
        return dot_nt(left[:, :middle], full[0]) + dot_nt(left[:, middle:], full[1])

    def saving_late(t):
        mine = pl.ds((t - 1) * per_tile, per_tile)
        return pltpu.make_async_copy(late.at[mine], late_hbm.at[mine], late_save.at[t - 1])

    stepped = [0]

    def act(*plan):
        for what in plan:
            if what == "sum":
                sums.steps(stepped[0], 1)
                stepped[0] += 1
            else:
                passing.step(*what)

    plans = {
        (0, 0): [(0, 3)], (0, 1): [(1, 3)], (0, 2): [(2, 1)], (0, 3): [],
        (1, 0): [], (1, 1): [(3, 1)], (1, 2): [], (1, 3): ["sum"],
        (2, 0): [(2, 2), "sum", (3, 2), "sum", (2, 3)], (2, 1): ["sum"], (2, 2): [], (2, 3): ["sum"],
        (3, 0): [(3, 3)], (3, 1): ["sum"], (3, 2): ["sum"], (3, 3): ["sum"],
    }
    for t in range(tiles):
        s, at = t // per_seq_tiles, slice(t % per_seq_tiles * tile, (t % per_seq_tiles + 1) * tile)
        flat = slice(t * tile, (t + 1) * tile)
        mine = t * per_tile
        act(*plans[t, 0])
        context = jnp.concatenate([ctx_all[p, t] for p in range(4)], axis=1)
        attended = [
            dot(context, jnp.concatenate([wo_all[p, piece] for p in range(4)], axis=0)) for piece in range(2)]
        for piece in range(2):
            for k in range(per_tile):
                attn[mine + k, :, piece * middle : (piece + 1) * middle] = attended[piece][
                    k * chunk : (k + 1) * chunk].astype(bf16)
        saving_attn(t).start()
        hidden = tok[s, at, :].astype(f32) + jnp.concatenate(attended, axis=1)
        normed = (unit_norm(hidden) * gain_two).astype(bf16)
        normed_s[s, at, :] = normed
        gate = across_both(normed, wg)
        up = across_both(normed, wu)
        sigmoid = jax.nn.sigmoid(gate)
        swish = gate * sigmoid
        inner = (swish * up).astype(bf16)
        inner_t[:, flat] = jnp.transpose(inner)
        inner_grad = across_both(cot[s, at, :], wd)
        gate_grad = (inner_grad * up * sigmoid * (1.0 + gate * (1.0 - sigmoid))).astype(bf16)
        up_grad = (inner_grad * swish).astype(bf16)
        act(*plans[t, 1])
        for piece in range(2):
            sums.fill(mine, piece, dot(gate_grad, wg[piece]) + dot(up_grad, wu[piece]))
        sums.offer(mine, per_tile)
        act(*plans[t, 2])
        feeds = [dot(inner, wd[piece]) for piece in range(2)]

        if t == 0:
            for piece in range(2):
                sums.fill(early, piece, feeds[piece])
        else:
            for piece in range(2):
                for k in range(per_tile):
                    late[mine - per_tile + k, :, piece * middle : (piece + 1) * middle] = feeds[piece][
                        k * chunk : (k + 1) * chunk].astype(bf16)
            saving_late(t).start()

        gg_t[:, flat] = jnp.transpose(gate_grad)
        ug_t[:, flat] = jnp.transpose(up_grad)
        act(*plans[t, 3])

    sums.offer(early, count - early)
    deep = units // 2

    def weight_grad(n, left_t, right):
        for h in range(2):
            for y in range(2):
                total = jnp.zeros((deep, middle), f32)
                for s in range(seqs):
                    total = total + dot(
                        left_t[h * deep : (h + 1) * deep, s * rows : (s + 1) * rows],
                        right[s, :, y * middle : (y + 1) * middle])
                grads[n][h, y] = total.astype(bf16)

    begun = stepped[0]
    weight_grad(0, inner_t, cot)
    fold_d.first()
    sums.steps(begun, 1)
    weight_grad(1, gg_t, normed_s)
    fold_g.first()
    fold_d.second()
    sums.steps(begun + 1, 1)
    weight_grad(2, ug_t, normed_s)
    fold_u.first()
    fold_g.second()
    sums.steps(begun + 2, 1)
    fold_u.second()
    sums.steps(begun + 3, 3)
    fold_d.quarter()
    sums.steps(begun + 6, 3)
    fold_g.quarter()
    sums.steps(begun + 9, count - begun - 9)
    fold_u.quarter()
    sums.settled(0, count)
    sums.close(count)
    for fold in (fold_d, fold_g, fold_u):
        fold.settle()
    for t in range(1, tiles):
        saving_late(t).wait()
    for s in range(seqs):
        for which in range(2):
            to_mate(s, which).wait_send()
            to_peer(s, which).wait_send()
            onward(s, which).wait_send()
        saving_kv(s).wait()
        saving_context(s).wait()
    for t in range(tiles):
        saving_attn(t).wait()
    pass_o.settle(2)
    passing.settle(tiles)

    @pl.loop(0, count)
    def _(i):
        saving(i).wait()

    if split:
        for n in range(7):
            cross(n).wait_send()
            onto_mate(n).wait_send()
        for n in range(3):
            share_o(n).wait_send()
        for copy in saves:
            copy.wait()


def limits(ident, megabytes=60):
    return pltpu.CompilerParams(
        collective_id=ident, has_side_effects=True, vmem_limit_bytes=megabytes * 1024 * 1024)


def front(split, tok, fv, cot, gains, square, wide, prefix):
    seqs, rows, dim = tok.shape
    width, units = square[0].shape[1], wide[0].shape[-2]
    heads = width // HEAD_DIM
    chunk, tile = 64, 256
    tokens = seqs * rows
    count = tokens // chunk + tile // chunk
    after = (tokens - tile) // chunk
    padded = -(-units // 256) * 256
    vmem = pl.BlockSpec(memory_space=pltpu.VMEM)
    anyw = pl.BlockSpec(memory_space=pl.ANY)
    dma = pltpu.SemaphoreType.DMA
    lines = pltpu.VMEM((count, chunk, dim), bf16)
    shape = jax.ShapeDtypeStruct
    full = [(dim, width)] * 3 + [(2, width, dim // 2)]
    fold_scratch, fold_outs = fold_shapes([(units // 2, dim // 2)] * 3, split, (0, 1, 2))
    outs = [
        shape((count, chunk, dim), bf16), shape((after, chunk, dim), bf16), shape((seqs, rows, width), bf16),
        shape((seqs, 4, 2, rows, width), bf16), shape((tokens // chunk, chunk, dim), bf16),
        shape((tokens // tile, tile, width), bf16),
        shape((seqs, heads // 2, 2 * rows), f32), shape((2, 8, dim // 2), f32),
        shape((rows, 128), f32), shape((rows, 128), f32)] + fold_outs
    out_specs = [anyw, anyw, vmem, anyw, anyw, anyw, vmem, vmem, vmem, vmem] + [anyw] * 3
    scratch = []
    if split:
        outs += [shape(size, bf16) for size in full]
        out_specs += [anyw] * 4
        scratch = [pltpu.VMEM(size, bf16) for size in full[:3]] + [
            dma((7, 2)), dma((7, 2)), dma((4,)), dma((2,)), dma((3,)), dma((3,))]
    scratch += [
        pltpu.VMEM((seqs, rows, dim), bf16),
        pltpu.VMEM((seqs, 4, 2, rows, width), bf16),
        pltpu.VMEM((seqs, heads // 2, width, 2 * rows), bf16),
        pltpu.VMEM((width, rows), bf16),
        pltpu.VMEM((width, rows), f32),
        pltpu.VMEM((heads // 2, 1, 2 * rows), f32),
        pltpu.VMEM((heads // 2, 1, 2 * rows), f32),
        lines, lines, lines,
        dma((seqs, 2, 3)), dma((seqs, 2, 4)), dma((seqs,)),
        dma((count,)), dma((count,)), dma((count,)), dma((count,)), dma((count,)),
        pltpu.VMEM((2, padded, dim // 2), bf16),
        pltpu.VMEM((2, padded, dim // 2), bf16),
        pltpu.VMEM((2, padded, dim // 2), bf16),
        dma((7,)),
        pltpu.VMEM((seqs, rows, dim), bf16),
        pltpu.VMEM((padded, tokens), bf16),
        pltpu.VMEM((padded, tokens), bf16),
        pltpu.VMEM((padded, tokens), bf16),
        pltpu.VMEM((after, chunk, dim), bf16),
        dma((tokens // tile,)),
        pltpu.VMEM((4, 2, width, dim // 2), bf16),
        pltpu.VMEM((4, tokens // tile, tile, width), bf16),
        pltpu.VMEM((tokens // chunk, chunk, dim), bf16),
        dma((2, 2, 4)), dma((2, 4)), dma((tokens // tile, 2, 4)), dma((tokens // tile, 4)),
        dma((seqs,)), dma((tokens // tile,)),
    ] + fold_scratch
    return pl.pallas_call(
        functools.partial(front_kernel, split),
        name="front",
        out_shape=outs,
        in_specs=[vmem] * 2 + [anyw] + [vmem] * 6 + [anyw] * 3 + [pl.BlockSpec(memory_space=pltpu.SMEM)],
        out_specs=out_specs,
        scratch_shapes=scratch,
        compiler_params=limits(0, 63),
        cost_estimate=pl.CostEstimate(flops=22 * 10**9, bytes_accessed=2 * 10**7, transcendentals=10**7),
    )(tok, fv, cot, *gains, *square, *wide, prefix)


def back_kernel(split, *refs):
    place, ring, side = lax.axis_index("tp"), lax.axis_index("ctx"), lax.axis_index("fsdp")
    quarters, refs = (refs[:3], refs[3:]) if split else ((), refs)
    loaded, refs = refs[:12], refs[12:]
    (gain_in, lse, cosine, sine, prefix, block_hbm, token_hbm, fv_hbm, gain_out), saved, refs = (
        refs[:9], refs[9:13], refs[13:])
    ends_saved, refs = (refs[:3], refs[3:]) if split else ((), refs)
    (tok, cot, wq, wk, wv, wo, q, kv, ctx, attn, mixed, early), refs = refs[:12], refs[12:]
    (hid, dwo_sum, qtm, qm, otm, om, kt, delta, dqt, dk, dv, give, take, proj, normed_t,
     part, inward, across, gain_part, gain_all,
     kv_send, kv_recv, send_one, recv_one, send_two, recv_two, save, gain_send, gain_recv, loads, fv_save), refs = (
        refs[:31], refs[31:])
    ends_scratch, refs = (refs[:12], refs[12:]) if split else ((), refs)
    (fold_o, fold_k, fold_v, fold_q), (dwo, dwk, dwv, dwq) = make_folds(split, side, ring, refs, saved, (0, 1, 2, 3, 4))
    ends, ends_mine = make_folds(split, side, ring, ends_scratch, ends_saved, (3, 4)) if split else ((), ())
    late_hbm, sum_hbm, attn_hbm, tok_hbm, cot_hbm, wq_hbm, wk_hbm, wv_hbm, wo_hbm, q_hbm, kv_hbm, ctx_hbm = loaded
    seqs, rows, dim = tok.shape
    width = wq.shape[1]
    heads = width // HEAD_DIM
    chunk = part.shape[1]
    per_seq = rows // chunk
    tile = 256
    per_tile = tile // chunk
    middle = dim // 2
    lines = seqs * per_seq
    count = 2 * lines - per_tile
    head_start = per_seq + 3
    rest = 2 * per_seq - per_tile - head_start
    rest_start = head_start + per_seq
    own_start = (head_start, rest_start + rest)
    mate, peer = ring_peers(ring)
    others = [(dy, dc) for dy in range(2) for dc in range(4) if dy or dc]
    group = [{"fsdp": lax.rem(side + dy, 2), "ctx": lax.rem(ring + dc, 4)} for dy, dc in others]

    copies = {}

    def load(name, source, target, start=True):
        copies[name] = pltpu.make_async_copy(source, target, loads.at[len(copies)])
        if start:
            copies[name].start()

    def ready(*names):
        for name in names:
            copies[name].wait()

    load("late", late_hbm.at[0:head_start], part.at[0:head_start])
    later = []
    for s in range(seqs):
        mine = slice(s * per_seq, (s + 1) * per_seq)
        for name, source, target in (
            ("tok", tok_hbm.at[s], tok.at[s]), ("attn", attn_hbm.at[mine], attn.at[mine]),
            ("cot", cot_hbm.at[s], cot), ("mixed", sum_hbm.at[mine], mixed),
            ("q", q_hbm.at[s], q.at[s]), ("ctx", ctx_hbm.at[s], ctx.at[s]), ("kv", kv_hbm.at[s], kv),
        ):
            now = s == 0 and name != "kv"
            load(f"{name}{s}", source, target, now)
            if not now and (s == 0 or name not in ("cot", "mixed", "kv")):
                later.append(f"{name}{s}")
        if s == 0:
            load("wo", wo_hbm, wo)
    for name, source, target in (
        [(f"quarter{n}", quarter, ends_mine[n]) for n, quarter in enumerate(quarters)] + [
            ("rest", late_hbm.at[head_start : head_start + rest], part.at[rest_start : rest_start + rest]),
            ("early", sum_hbm.at[lines : lines + per_tile], early),
            ("wq", wq_hbm, wq), ("wk", wk_hbm, wk), ("wv", wv_hbm, wv)]
    ):
        load(name, source, target, False)
        later.append(name)
    greet(line_peers(place) + (group if split else ring_peers(ring)))
    gain_one, gain_two = gain_row(gain_in, 0), gain_row(gain_in, 1)
    gain_part[...] = jnp.zeros_like(gain_part)

    def chunk_at(n):
        return n // per_seq, rows_at(lax.rem(n, per_seq) * chunk, chunk)

    def saving_block(i, n):
        s, own = chunk_at(n)
        return pltpu.make_async_copy(across.at[i], block_hbm.at[s, own], save.at[i])

    def saving_early(n):
        return pltpu.make_async_copy(early.at[n], block_hbm.at[0, n * chunk : (n + 1) * chunk], save.at[count + n])

    def saving_token(i, n):
        s, own = chunk_at(n)
        return pltpu.make_async_copy(hid.at[s, own], token_hbm.at[s, own], save.at[i])

    def add_gain(which, value):
        for piece in range(2):
            gain_part[piece, which : which + 1, :] += value[:, piece * middle : (piece + 1) * middle]

    is_block = lambda i: (i < head_start) | ((i >= rest_start) & (i < own_start[1]))
    block_of = lambda i: per_tile + jnp.where(i < head_start, i, i - per_seq)
    token_of = lambda i: jnp.where(i < rest_start, i - head_start, i - own_start[1] + per_seq)

    def done(i):
        @pl.when(is_block(i))
        def _():
            n = block_of(i)
            s, own = chunk_at(n)
            across[i] = (
                tok[s, own, :].astype(f32) + attn[n].astype(f32) + part[i].astype(f32)).astype(bf16)
            saving_block(i, n).start()

        @pl.when(jnp.logical_not(is_block(i)))
        def _():
            n = token_of(i)
            s, own = chunk_at(n)
            values, upstream = tok[s, own, :].astype(f32), part[i].astype(f32)
            factor = lax.rsqrt(jnp.mean(values * values, axis=-1, keepdims=True) + epsilon)
            scaled = upstream * gain_one
            add_gain(0, jnp.sum(upstream * values * factor, axis=0, keepdims=True))
            hid[s, own, :] += factor * scaled - values * factor**3 * jnp.mean(
                scaled * values, axis=-1, keepdims=True)
            saving_token(i, n).start()

    sums = Sum(place, part, inward, across, (send_one, recv_one, send_two, recv_two), done)

    def move(s, source, target, device):
        return remote(give.at[source], take.at[s, target], kv_send.at[source], kv_recv.at[s, target], device)

    far_to_mate = lambda s: move(s, 2, 0, mate)
    peer_back = lambda s: move(s, 1, 1, peer)
    near_to_mate = lambda s: move(s, 0, 2, mate)
    ready("late")
    sums.offer(0, head_start)
    for name in later:
        copies[name].start()

    def hidden_stage(s):
        @pl.loop(0, rows // tile)
        def _(t):
            at = rows_at(t * tile, tile)
            first = s * per_seq + t * per_tile
            join = lambda ref: jnp.concatenate([ref[first + k] for k in range(per_tile)], axis=0).astype(f32)
            token = tok[s, at, :].astype(f32)
            values = token + join(attn)
            upstream = jnp.concatenate(
                [mixed[t * per_tile + k] for k in range(per_tile)], axis=0).astype(f32)
            factor = lax.rsqrt(jnp.mean(values * values, axis=-1, keepdims=True) + epsilon)
            scaled = upstream * gain_two
            add_gain(1, jnp.sum(upstream * values * factor, axis=0, keepdims=True))
            hid_now = cot[at, :].astype(f32) + factor * scaled - values * factor**3 * jnp.mean(
                scaled * values, axis=-1, keepdims=True)
            hid[s, at, :] = hid_now
            low = hid_now.astype(bf16)
            dwo_sum[...] += dot(jnp.transpose(ctx[s, at, :]), low)
            left, right = low[:, :middle], low[:, middle:]
            grad = dot_nt(left, wo[0]) + dot_nt(right, wo[1])
            lane_owner = lax.broadcasted_iota(jnp.int32, grad.shape, 1) // HEAD_DIM
            q_now = q[s, at, :].astype(f32)
            grad_t = jnp.transpose(grad)
            q_t = jnp.transpose(q_now)
            product = jnp.transpose(grad.astype(bf16).astype(f32) * ctx[s, at, :].astype(f32))
            for h in range(heads):
                low_rows = rows_at(h % 2 * rows + t * tile, tile)
                om[h // 2, low_rows, :] = jnp.where(lane_owner == h, grad, 0.0).astype(bf16)
                qm[h // 2, low_rows, :] = jnp.where(lane_owner == h, q_now, 0.0).astype(bf16)
                delta[h // 2, :, low_rows] = jnp.sum(
                    product[h * HEAD_DIM : (h + 1) * HEAD_DIM], axis=0, keepdims=True)
            spread(otm, grad_t, t * tile, rows)
            spread(qtm, q_t, t * tile, rows)
            normed = (unit_norm(token) * gain_one).astype(bf16)
            normed_t[:, rows_at(s * rows + t * tile, tile)] = jnp.transpose(normed)

    def back_block(s, j, tick):
        kt[...] = jnp.transpose(kv[j, 0])
        key_pos = block_place(ring, j) * rows + lax.broadcasted_iota(jnp.int32, (rows, 1), 0)
        query_pos = ring * rows + lax.rem(lax.broadcasted_iota(jnp.int32, (1, 2 * rows), 1), rows)
        seen = key_pos < jnp.maximum(query_pos + 1, prefix[s])
        dk[...] = jnp.zeros_like(dk)
        dv[...] = jnp.zeros_like(dv)

        @pl.loop(0, heads // 2)
        def _(h):
            scores = dot(kv[j, 0], qtm[h])
            probs = jnp.where(seen, jnp.exp(scores - lse[s, pl.ds(h, 1), :]), 0.0)
            dprobs = dot(kv[j, 1], otm[h])
            dv[...] += dot(probs.astype(bf16), om[h])
            dscores = (probs * (dprobs - delta[h])).astype(bf16)
            dk[...] += dot(dscores, qm[h])
            for n in range(2):
                of_head = rows_at((2 * h + n) * HEAD_DIM, HEAD_DIM)
                dqt[of_head, :] += dot(kt[of_head, :], dscores[:, n * rows : (n + 1) * rows])
            tick(h)

    def finalize(s):
        near_to_mate(s).wait_recv()
        peer_back(s).wait_recv()
        @pl.loop(0, rows // tile)
        def _(t):
            at = rows_at(t * tile, tile)
            flat = rows_at(s * rows + t * tile, tile)
            co, si = cosine[at, :], sine[at, :]
            grad_v = 0.5 * (dv[at, :] + take[s, 2, 1, at, :].astype(f32) + take[s, 1, 1, at, :].astype(f32))
            grad_k = dk[at, :] + take[s, 2, 0, at, :].astype(f32) + take[s, 1, 0, at, :].astype(f32)
            grad_q = jnp.transpose(dqt[:, at]) * HEAD_DIM ** (-0.5)
            proj[0, flat, :] = turn(grad_q, co, si, -1.0).astype(bf16)
            proj[1, flat, :] = turn(grad_k, co, si, -1.0).astype(bf16)
            proj[2, flat, :] = grad_v.astype(bf16)
            i = jnp.where(s == 0, own_start[0], own_start[1]) + t * per_tile
            for piece in range(2):
                cut = slice(piece * middle, (piece + 1) * middle)
                sums.fill(i, piece, dot_nt(proj[0, flat, :], wq[cut, :]) + dot_nt(
                    proj[1, flat, :], wk[cut, :]) + dot_nt(proj[2, flat, :], wv[cut, :]))
            sums.offer(i, per_tile)

        @pl.when(s == 0)
        def _():
            sums.offer(rest_start, rest)

    ready("wo")
    dwo_sum[...] = jnp.zeros_like(dwo_sum)
    if split:
        ready("quarter0")
        ends[0].resume()

    def start_at(phase, *names):
        for wanted in range(1, seqs):
            @pl.when(phase == wanted - 1)
            def _():
                for name in names:
                    copies[f"{name}{wanted}"].start()

    def at_phase(phase, wanted, names):
        @pl.when(phase == wanted)
        def _():
            ready(*names)

    plan = [(1, m, m) for m in range(7)] + [(2, m, 10 + line) for line, m in enumerate((0, 1, 3, 4, 6, 7))]

    @pl.loop(0, seqs + 1)
    def _(phase):
        s = jnp.maximum(phase - 1, 0)
        follows = phase > 1

        @pl.when(phase > 0)
        def _():
            for wanted in range(seqs):
                at_phase(phase, wanted + 1, [f"kv{wanted}"])
            for wanted in range(1, seqs):
                at_phase(phase, 1, [f"tok{wanted}", f"attn{wanted}"])
            dqt[...] = jnp.zeros_like(dqt)

            @pl.loop(0, 4)
            def _(n):
                def tick(h):
                    chosen = -1
                    for at_phase, at_step, line in plan:
                        chosen = jnp.where((phase == at_phase) & (2 * n + h == at_step), line, chosen)

                    @pl.when(chosen >= 0)
                    def _():
                        sums.steps(chosen, 1)

                back_block(s, 3 - n, tick)

                @pl.when(n == 0)
                def _():
                    @pl.when(follows)
                    def _():
                        far_to_mate(s - 1).wait_send()
                        fold_o.second()

                    give[2, 0] = dk[...].astype(bf16)
                    give[2, 1] = dv[...].astype(bf16)
                    far_to_mate(s).start()

                @pl.when(n == 1)
                def _():
                    far_to_mate(s).wait_recv()

                    @pl.when(follows)
                    def _():
                        peer_back(s - 1).wait_send()

                    give[1, 0] = (dk[...] + take[s, 0, 0].astype(f32)).astype(bf16)
                    give[1, 1] = (dv[...] + take[s, 0, 1].astype(f32)).astype(bf16)
                    peer_back(s).start()

                @pl.when(n == 2)
                def _():
                    @pl.when(follows)
                    def _():
                        near_to_mate(s - 1).wait_send()
                        fold_o.third()

                    give[0, 0] = dk[...].astype(bf16)
                    give[0, 1] = dv[...].astype(bf16)
                    near_to_mate(s).start()

            start_at(phase - 1, "kv")

        @pl.when(phase < seqs)
        def _():
            for wanted in range(seqs):
                names = ("tok", "attn") * (wanted == 0) + ("cot", "mixed", "q", "ctx")
                at_phase(phase, wanted, [f"{name}{wanted}" for name in names])
            hidden_stage(phase)
            start_at(phase, "cot", "mixed")

            @pl.when(phase == 1)
            def _():
                sums.steps(7, 1)

        @pl.when(phase > 0)
        def _():
            at_phase(phase, 1, ["wq", "wk", "wv", "rest"])
            sums.steps(jnp.where(phase == 1, 8, 16), 1)
            finalize(s)
            sums.steps(jnp.where(phase == 1, 9, 17), 1)

        @pl.when(phase == seqs - 1)
        def _():
            deep = dwo.shape[2]
            for h in range(2):
                for y in range(2):
                    dwo[h, y] = dwo_sum[h * deep : (h + 1) * deep, y * middle : (y + 1) * middle].astype(bf16)
            fold_o.first()
            if split:
                ends[0].fourth()
                ready("quarter1")
                ends[1].resume()

    begun = 18
    fv_copy = pltpu.make_async_copy(proj.at[2], fv_hbm, fv_save)
    fv_copy.start()
    if split:
        ends[1].fourth()
        ready("quarter2")
        ends[2].resume()
        ends[0].last()
    share = dwq.shape[2]

    def square_grad(target, which):
        @pl.loop(0, 4)
        def _(k):
            h, y = k // 2, lax.rem(k, 2)
            target[h, y] = dot(normed_t[rows_at((2 * y + h) * share, share), :], proj[which]).astype(bf16)

    ready("early")
    for n in range(per_tile):
        own = slice(n * chunk, (n + 1) * chunk)
        early[n] = (tok[0, own, :].astype(f32) + attn[n].astype(f32) + early[n].astype(f32)).astype(bf16)
        saving_early(n).start()
    square_grad(dwk, 1)
    fold_k.first()
    sums.steps(begun, 1)
    square_grad(dwv, 2)
    fold_v.first()
    fold_k.second()
    sums.steps(begun + 1, 1)
    square_grad(dwq, 0)
    fold_q.first()
    fold_v.second()
    sums.steps(begun + 2, 1)
    fold_q.second()
    fold_o.fourth()
    sums.steps(begun + 3, 1)
    fold_k.third()
    sums.steps(begun + 4, 1)
    fold_v.third()
    sums.steps(begun + 5, 1)
    fold_q.third()
    fold_k.fourth()
    sums.steps(begun + 6, 1)
    fold_v.fourth()
    sums.steps(begun + 7, 1)
    fold_q.fourth()
    for fold in (fold_o, fold_k, fold_v) + tuple(ends[1:2]):
        fold.last()
    if split:
        ends[2].fourth()
    sums.steps(begun + 8, count - begun - 8)
    for fold in (fold_q,) + tuple(ends[2:]):
        fold.last()
    sums.settled(0, count)
    sums.close(count)
    if split:
        me = 4 * side + ring
        gain_all[me] = gain_part[side]

        def share_gain(n):
            dy, dc = others[n]
            y = lax.rem(side + dy, 2)
            return remote(gain_part.at[y], gain_all.at[me], gain_send.at[n], gain_recv.at[n], group[n])

        for n in range(7):
            share_gain(n).start()
        for n in range(7):
            share_gain(n).wait()
        total = gain_all[0]
        for n in range(1, 8):
            total = total + gain_all[n]
        gain_out[...] = total
    else:
        gain_out[...] = gain_part[...]
    for fold in (fold_o, fold_k, fold_v, fold_q) + tuple(ends):
        fold.settle()
    fv_copy.wait()
    for copy in (far_to_mate, peer_back, near_to_mate):
        copy(seqs - 1).wait_send()

    for n in range(per_tile):
        saving_early(n).wait()

    @pl.loop(0, count)
    def _(i):
        @pl.when(is_block(i))
        def _():
            saving_block(i, block_of(i)).wait()

        @pl.when(jnp.logical_not(is_block(i)))
        def _():
            saving_token(i, token_of(i)).wait()


def back(split, quarters, tok, cot, sums, attn, late, gains, square, q, kv, ctx, lse, cosine, sine, prefix):
    seqs, rows, dim = tok.shape
    width = q.shape[2]
    heads = width // HEAD_DIM
    _, chunk, _ = sums.shape
    tokens = seqs * rows
    early = 256 // chunk
    count = 2 * tokens // chunk - early
    vmem = pl.BlockSpec(memory_space=pltpu.VMEM)
    anyw = pl.BlockSpec(memory_space=pl.ANY)
    dma = pltpu.SemaphoreType.DMA
    lines = pltpu.VMEM((count, chunk, dim), bf16)
    half_lines = pltpu.VMEM((tokens // chunk, chunk, dim), bf16)
    wide = pltpu.VMEM((heads // 2, 2 * rows, width), bf16)
    tall = pltpu.VMEM((heads // 2, width, 2 * rows), bf16)
    shape = jax.ShapeDtypeStruct
    fold_scratch, fold_outs = fold_shapes(
        [(width // 2, dim // 2)] + [(dim // 4, width)] * 3, split, (0, 1, 2, 3, 4))
    ends_scratch, ends_outs = fold_shapes([x.shape for x in quarters], True, (3, 4)) if split else ([], [])
    loaded = (tok, cot) + tuple(square) + (q, kv, ctx)
    held = [tok.shape, cot.shape[1:]] + [x.shape for x in square] + [q.shape, kv.shape[1:], ctx.shape]
    return pl.pallas_call(
        functools.partial(back_kernel, split),
        name="back",
        out_shape=[
            shape((seqs, rows, dim), bf16), shape((seqs, rows, dim), f32), shape((tokens, width), bf16),
            shape((8, dim // 2) if split else (2, 8, dim // 2), f32)] + fold_outs + ends_outs,
        in_specs=[anyw] * (len(quarters) + 12) + [vmem] * 4 + [pl.BlockSpec(memory_space=pltpu.SMEM)],
        out_specs=[anyw, anyw, anyw, vmem] + [anyw] * (4 + len(quarters)),
        scratch_shapes=[pltpu.VMEM(x, bf16) for x in held] + [
            half_lines, pltpu.VMEM((rows // chunk, chunk, dim), bf16), pltpu.VMEM((early, chunk, dim), bf16),
            pltpu.VMEM((seqs, rows, dim), f32),
            pltpu.VMEM((width, dim), f32),
            tall, wide, tall, wide,
            pltpu.VMEM((width, rows), bf16),
            pltpu.VMEM((heads // 2, 1, 2 * rows), f32),
            pltpu.VMEM((width, rows), f32),
            pltpu.VMEM((rows, width), f32),
            pltpu.VMEM((rows, width), f32),
            pltpu.VMEM((3, 2, rows, width), bf16),
            pltpu.VMEM((seqs, 3, 2, rows, width), bf16),
            pltpu.VMEM((3, tokens, width), bf16),
            pltpu.VMEM((dim, tokens), bf16),
            lines, lines, lines,
            pltpu.VMEM((2, 8, dim // 2), f32),
            pltpu.VMEM((8, 8, dim // 2), f32),
            dma((3,)), dma((seqs, 3)),
            dma((count,)), dma((count,)), dma((count,)), dma((count,)), dma((count + early,)),
            dma((7,)), dma((7,)), dma((8 * seqs + 11,)), dma(()),
        ] + ends_scratch + fold_scratch,
        compiler_params=limits(2, 62),
        cost_estimate=pl.CostEstimate(flops=30 * 10**9, bytes_accessed=10**7, transcendentals=10**7),
    )(*quarters, late, sums, attn, *loaded, gains, lse, cosine, sine, prefix)


def finish_kernel(parts, *refs):
    n = len(parts)
    sources, gain_in, refs = refs[:n], refs[n], refs[n + 1 :]
    targets, gain_one, gain_two, refs = refs[:n], refs[n], refs[n + 1], refs[n + 2 :]
    held, wide, (loads, saves) = refs[:n], refs[n : 2 * n], refs[2 * n :]
    loading, saving = [], []
    for k, count in enumerate(parts):
        size = sources[k].shape[0] // count
        for piece in range(count):
            at = slice(piece * size, (piece + 1) * size)
            place = len(loading)
            loading.append(pltpu.make_async_copy(sources[k].at[at], held[k].at[at], loads.at[place]))
            plain = sources[k].dtype == targets[k].dtype
            saving.append((k, at, plain, pltpu.make_async_copy(
                (held if plain else wide)[k].at[at], targets[k].at[at], saves.at[place])))
    for load in loading:
        load.start()
    gain_one[...] = gain_in[0:1, :]
    gain_two[...] = gain_in[1:2, :]
    for load, (k, at, plain, save) in zip(loading, saving):
        load.wait()
        if not plain:
            wide[k][at] = held[k][at].astype(f32)
        save.start()
    for *_, save in saving:
        save.wait()


def finish(arrays, types, gain_rows):
    parts = [2 if x.size > 300000 else 1 for x in arrays]
    vmem = pl.BlockSpec(memory_space=pltpu.VMEM)
    anyw = pl.BlockSpec(memory_space=pl.ANY)
    dma = pltpu.SemaphoreType.DMA
    shape = jax.ShapeDtypeStruct
    row = shape((1, gain_rows.shape[1]), f32)
    return pl.pallas_call(
        functools.partial(finish_kernel, parts),
        name="finish",
        out_shape=[shape(x.shape, t) for x, t in zip(arrays, types)] + [row, row],
        in_specs=[anyw] * len(arrays) + [vmem],
        out_specs=[anyw] * len(arrays) + [vmem, vmem],
        scratch_shapes=[pltpu.VMEM(x.shape, x.dtype) for x in arrays] + [
            pltpu.VMEM((8, 128) if x.dtype == t else x.shape, f32) for x, t in zip(arrays, types)] + [
            dma((sum(parts),)), dma((sum(parts),))],
        compiler_params=pltpu.CompilerParams(vmem_limit_bytes=60 * 1024 * 1024),
        cost_estimate=pl.CostEstimate(flops=10**6, bytes_accessed=25 * 10**6, transcendentals=0),
    )(*arrays, gain_rows)


def halves(weight):
    rows, columns = weight.shape
    return jnp.swapaxes(weight.reshape(rows, 2, columns // 2), 0, 1)


def shards(
    tokens, first_values, norm1_gain, norm2_gain, w_query, w_key, w_value, w_out, w_gate, w_up, w_down,
    prefix, cotangent,
):
    split = lax.axis_size("fsdp") == 2
    seqs, rows, dim = tokens.shape
    width, units = w_query.shape[1], w_gate.shape[1]
    gather = functools.partial(lax.all_gather, axis_name="fsdp", tiled=True)
    if split:
        gains = (norm1_gain, norm2_gain)
        square = (w_query, w_key, w_value, w_out)
        wide = (w_gate.T, w_up.T, w_down)
    else:
        gains = (gather(norm1_gain), gather(norm2_gain))
        square = (gather(w_query), gather(w_key), gather(w_value), halves(gather(w_out, axis=1)))
        wide = (halves(gather(w_gate).T), halves(gather(w_up).T), halves(gather(w_down, axis=1)))
    (sums, late, query, pairs, attn, context, log_total, gain_rows, cosine, sine, down_grad, gate_grad, up_grad,
     *gathered) = front(
        split, tokens, first_values, cotangent, [gain.reshape(-1, 128) for gain in gains], square, wide, prefix)
    if split:
        square = tuple(gathered)
    wide_grads = (down_grad, gate_grad, up_grad)
    block_out, token_grad, half_value_grad, gain_grads, out_grad, key_grad, value_grad, query_grad, *ends = back(
        split, wide_grads if split else (), tokens, cotangent, sums, attn, late, gain_rows, square, query, pairs,
        context.reshape(query.shape), log_total, cosine, sine, prefix)
    half_value_grad = half_value_grad.reshape(seqs, rows, width)
    if split:
        arrays = (token_grad, block_out, half_value_grad, query_grad, key_grad, value_grad, out_grad, *ends)
        (token_grad, block_out, half_value_grad, query_grad, key_grad, value_grad, out_grad, down_grad, gate_grad,
         up_grad, gain_one_grad, gain_two_grad) = finish(arrays, (f32, bf16) + (f32,) * 8, gain_grads)
        over_rows = lambda grad: grad.reshape(-1, grad.shape[-1])
        over_columns = over_rows
        over_turned = lambda grad: over_rows(grad).T
        gain_one_grad, gain_two_grad = gain_one_grad[0], gain_two_grad[0]
    else:
        half_value_grad = half_value_grad.astype(f32)
        total = lambda grad, axis: lax.psum(
            lax.psum_scatter(grad, "fsdp", scatter_dimension=axis, tiled=True), "ctx").astype(f32)
        over_rows = lambda grad: total(jnp.swapaxes(grad, 0, 1).reshape(-1, grad.shape[-1]), 0)
        over_columns = lambda grad: total(
            jnp.transpose(grad, (0, 2, 1, 3)).reshape(2 * grad.shape[2], -1), 1)
        over_turned = lambda grad: over_columns(grad).T
        gain_one_grad, gain_two_grad = (total(gain_grads[:, n].reshape(-1), 0) for n in range(2))
    return (
        block_out,
        token_grad,
        half_value_grad,
        gain_one_grad,
        gain_two_grad,
        over_rows(query_grad),
        over_rows(key_grad),
        over_rows(value_grad),
        over_columns(out_grad),
        over_turned(gate_grad),
        over_turned(up_grad),
        over_columns(down_grad),
    )


def solution(mesh):
    return jax.shard_map(
        shards,
        mesh=mesh,
        in_specs=(
            P("fsdp", "ctx", None),
            P("fsdp", "ctx", "tp"),
            P("fsdp"),
            P("fsdp"),
            P("fsdp", "tp"),
            P("fsdp", "tp"),
            P("fsdp", "tp"),
            P("tp", "fsdp"),
            P("fsdp", "tp"),
            P("fsdp", "tp"),
            P("tp", "fsdp"),
            P("fsdp"),
            P("fsdp", "ctx", None),
        ),
        out_specs=(
            P("fsdp", "ctx", None),
            P("fsdp", "ctx", None),
            P("fsdp", "ctx", "tp"),
            P("fsdp"),
            P("fsdp"),
            P("fsdp", "tp"),
            P("fsdp", "tp"),
            P("fsdp", "tp"),
            P("tp", "fsdp"),
            P("fsdp", "tp"),
            P("fsdp", "tp"),
            P("tp", "fsdp"),
        ),
        check_vma=False,
    )
```

```python
import functools

import jax
import jax.numpy as jnp
from jax import lax
from jax.experimental import pallas as pl
from jax.experimental.pallas import tpu as pltpu
from jax.sharding import PartitionSpec as P

HEAD_DIM = 64
epsilon = 1e-06
rope_base = 10000.0
masked_score = -1e30
MESH = pl.DeviceIdType.MESH
bf16 = jnp.bfloat16
f32 = jnp.float32


def dot(a, b):
    return jnp.dot(a, b, preferred_element_type=f32)


def dot_nt(a, b):
    return lax.dot_general(a, b, (((1,), (1,)), ((), ())), preferred_element_type=f32)


def unit_norm(values):
    return values * lax.rsqrt(jnp.mean(values * values, axis=-1, keepdims=True) + epsilon)


def low_half(shape):
    return lax.rem(lax.broadcasted_iota(jnp.int32, shape, 1), HEAD_DIM) < HEAD_DIM // 2


class Sum:
    lag = 2

    def __init__(self, place, part, inward, across, sems, done):
        self.pair = near(place)
        self.middle = 3 - place
        self.inner = (place == 1) | (place == 2)
        self.outer = (place == 0) | (place == 3)
        self.part, self.inward, self.across, self.done = part, inward, across, done
        self.send_one, self.recv_one, self.send_two, self.recv_two = sems

    def copy_in(self, i):
        return remote(
            self.part.at[i], self.inward.at[i], self.send_one.at[i], self.recv_one.at[i], {"tp": self.pair})

    def copy_across(self, i):
        return remote(
            self.part.at[i], self.across.at[i], self.send_two.at[i], self.recv_two.at[i], {"tp": self.middle})

    def copy_out(self, i):
        return remote(
            self.part.at[i], self.inward.at[i], self.send_one.at[i], self.recv_one.at[i], {"tp": self.pair})

    def fill(self, first, piece, values):
        chunk, size = self.part.shape[1], values.shape[1]
        for k in range(values.shape[0] // chunk):
            self.part[first + k, :, piece * size : (piece + 1) * size] = values[
                k * chunk : (k + 1) * chunk].astype(bf16)

    def offer(self, first, count):
        @pl.when(self.outer)
        def _():
            @pl.loop(0, count)
            def _(k):
                self.copy_in(first + k).start()

    def take_in(self, i):
        self.copy_in(i).wait_recv()
        self.part[i] = (self.part[i].astype(f32) + self.inward[i].astype(f32)).astype(bf16)
        self.copy_across(i).start()

    def finish(self, i):
        self.copy_across(i).wait()
        self.part[i] = (self.part[i].astype(f32) + self.across[i].astype(f32)).astype(bf16)
        self.copy_out(i).start()
        self.done(i)

    def steps(self, first, count):
        @pl.when(self.inner)
        def _():
            @pl.loop(first, first + count)
            def _(i):
                self.take_in(i)

                @pl.when(i >= self.lag)
                def _():
                    self.finish(i - self.lag)

    def settled(self, first, count):
        @pl.when(self.outer)
        def _():
            @pl.loop(first, first + count)
            def _(i):
                self.copy_out(i).wait_recv()
                self.copy_in(i).wait_send()
                self.part[i] = self.inward[i]
                self.done(i)

    def close(self, count):
        @pl.when(self.inner)
        def _():
            for n in range(self.lag):
                self.finish(count - self.lag + n)

            @pl.loop(0, count)
            def _(i):
                self.copy_out(i).wait_send()


def near(place):
    return place + 1 - 2 * lax.rem(place, 2)


def greet(peers):
    barrier = pltpu.get_barrier_semaphore()
    for peer in peers:
        pl.semaphore_signal(barrier, inc=1, device_id=peer, device_id_type=MESH)
    pl.semaphore_wait(barrier, len(peers))


def block_place(ring, j):
    return jnp.where(
        j == 0, ring, jnp.where(j == 1, near(ring), jnp.where(j == 2, lax.rem(ring + 2, 4), 3 - ring)))


def line_peers(place):
    return [{"tp": near(place)}, {"tp": 3 - place}]


def ring_peers(ring):
    return [{"ctx": near(ring)}, {"ctx": lax.rem(ring + 2, 4)}]


def remote(source, target, send, recv, device):
    return pltpu.make_async_remote_copy(
        src_ref=source, dst_ref=target, send_sem=send, recv_sem=recv,
        device_id=device, device_id_type=MESH)


class Passing:
    def __init__(self, place, spot, sems, own=None):
        self.place, self.spot, self.own = place, spot, own
        self.send, self.recv = sems

    def move(self, piece, item, way, source=None):
        here = self.spot(piece, item)
        return remote(
            here if source is None else source, here, self.send.at[item, way, piece], self.recv.at[item, piece],
            {"tp": self.place + 1 - 2 * way})

    def begin(self, item):
        source = None if self.own is None else self.own(item)

        @pl.when(self.place < 3)
        def _():
            self.move(self.place, item, 0, source).start()

        @pl.when(self.place > 0)
        def _():
            self.move(self.place, item, 1, source).start()

    def step(self, item, distance):
        @pl.when(self.place >= distance)
        def _():
            piece = self.place - distance
            self.move(piece, item, 0).wait_recv()

            @pl.when(self.place < 3)
            def _():
                self.move(piece, item, 0).start()

        @pl.when(self.place + distance <= 3)
        def _():
            piece = self.place + distance
            self.move(piece, item, 1).wait_recv()

            @pl.when(self.place > 0)
            def _():
                self.move(piece, item, 1).start()

    def settle(self, items):
        for item in range(items):
            @pl.loop(0, 4)
            def _(piece, item=item):
                @pl.when((self.place < 3) & (piece <= self.place))
                def _():
                    self.move(piece, item, 0).wait_send()

                @pl.when((self.place > 0) & (piece >= self.place))
                def _():
                    self.move(piece, item, 1).wait_send()


def rows_at(start, size):
    return pl.ds(pl.multiple_of(start, size), size)


class Fold:
    def __init__(self, side, ring, refs, sems, saved):
        self.side, self.half = side, lax.rem(ring, 2)
        self.grad, self.one, self.two, self.three, self.final = refs
        self.send, self.recv, self.save = sems
        self.mate, self.peer, self.other = (
            {"ctx": near(ring)}, {"ctx": lax.rem(ring + 2, 4)}, {"fsdp": 1 - side})
        self.saved = saved
        self.began = set()

    def mine(self):
        return self.grad if self.one is None else self.grad.at[self.half, self.side]

    def copy(self, n):
        source, target, device = (
            lambda: (self.grad.at[1 - self.half], self.one, self.mate),
            lambda: (self.grad.at[self.half, 1 - self.side], self.two, self.other),
            lambda: (self.mine(), self.three, self.peer),
            lambda: (self.final.at[self.half], self.final.at[self.half], self.mate),
        )[n]()
        return remote(source, target, self.send.at[n], self.recv.at[n], device)

    def begin(self, n):
        self.began.add(n)
        self.copy(n).start()

    def first(self):
        self.begin(0)

    def second(self):
        self.copy(0).wait_recv()
        for side in range(2):
            self.grad[self.half, side] = (
                self.grad[self.half, side].astype(f32) + self.one[side].astype(f32)).astype(bf16)
        self.begin(1)

    def join(self):
        self.copy(1).wait_recv()
        mine = self.mine()
        mine[...] = (mine[...].astype(f32) + self.two[...].astype(f32)).astype(bf16)

    def quarter(self):
        self.join()
        self.saving().start()

    def resume(self):
        self.begin(2)

    def third(self):
        self.join()
        self.resume()

    def fourth(self):
        self.copy(2).wait_recv()
        self.final[self.half] = (self.mine()[...].astype(f32) + self.three[...].astype(f32)).astype(bf16)
        self.begin(3)

    def saving(self):
        return pltpu.make_async_copy(self.mine() if self.final is None else self.final, self.saved, self.save)

    def last(self):
        self.copy(3).wait_recv()
        self.saving().start()

    def settle(self):
        for n in sorted(self.began):
            self.copy(n).wait_send()
        self.saving().wait()


class Whole:
    def __init__(self, grad, sems, saved):
        self.copy = lambda: pltpu.make_async_copy(grad, saved, sems[2])

    def first(self):
        self.copy().start()

    def second(self):
        pass

    third = fourth = last = quarter = second

    def settle(self):
        self.copy().wait()


def fold_shapes(shapes, split, kinds):
    scratch = []
    for r, c in shapes:
        sizes = ((2, 2, r, c), (2, r, c), (r, c), (r, c), (2, r, c))
        if not split:
            kinds = (0,)
        elif 0 not in kinds:
            scratch.append(pltpu.VMEM((r, c), bf16))
        scratch += [pltpu.VMEM(sizes[kind], bf16) for kind in kinds]
    n = len(shapes)
    dma = pltpu.SemaphoreType.DMA
    scratch += [dma((n, 4)), dma((n, 4)), dma((n,))]
    ends = (2, 2) if not split else (2,) if 4 in kinds else ()
    return scratch, [jax.ShapeDtypeStruct(ends + (r, c), bf16) for r, c in shapes]


def make_folds(split, side, ring, scratch, saved, kinds):
    send, recv, save = scratch[-3:]
    folds, grads = [], []
    per = 1 if not split else len(kinds) + (0 not in kinds)
    for n, target in enumerate(saved):
        own = list(scratch[n * per : (n + 1) * per])
        sems = (send.at[n], recv.at[n], save.at[n])
        grads.append(own[0])
        if split:
            held = dict(zip(kinds if 0 in kinds else (0,) + kinds, own))
            folds.append(Fold(side, ring, [held.get(kind) for kind in range(5)], sems, target))
        else:
            folds.append(Whole(own[0], sems, target))
    return folds, grads


def turn(values, cosine, sine, sign=1.0):
    pieces = []
    half = HEAD_DIM // 2
    sine = sine * sign
    for at in range(0, values.shape[1], 128):
        piece = values[:, at : at + 128]
        swapped = jnp.where(
            low_half(piece.shape), pltpu.roll(piece, 128 - half, 1), pltpu.roll(piece, half, 1))
        pieces.append(piece * cosine + swapped * sine)
    return jnp.concatenate(pieces, axis=1)


def spread(target, values_t, start, rows):
    owner = lax.broadcasted_iota(jnp.int32, values_t.shape, 0) // HEAD_DIM
    for h in range(values_t.shape[0] // HEAD_DIM):
        target[h // 2, :, rows_at(h % 2 * rows + start, values_t.shape[1])] = jnp.where(
            owner == h, values_t, 0.0).astype(bf16)


def flat_row(folded):
    return jnp.concatenate([folded[n : n + 1, :].astype(f32) for n in range(folded.shape[0])], axis=1)


def gain_row(gains, which):
    return jnp.concatenate([gains[0, which : which + 1, :], gains[1, which : which + 1, :]], axis=1)


def front_kernel(split, *refs):
    place, ring, side = lax.axis_index("tp"), lax.axis_index("ctx"), lax.axis_index("fsdp")
    (tok, fv, cot_hbm, g1, g2, wq_in, wk_in, wv_in, wo_in, wg_in, wu_in, wd_in), refs = refs[:12], refs[12:]
    (prefix, sum_hbm, late_hbm, q_out, kv_hbm, attn_hbm, ctx_hbm, lse_out, gains, cosine, sine), refs = (
        refs[:11], refs[11:])
    saved, refs = refs[:3], refs[3:]
    if split:
        (wq_hbm, wk_hbm, wv_hbm, wo_hbm), refs = refs[:4], refs[4:]
        (wq, wk, wv, w_send, w_recv, w_save, g_sems, o_send, o_recv), refs = refs[:9], refs[9:]
    else:
        wq, wk, wv = wq_in, wk_in, wv_in
    (normed_s, kv, qtm, vt, acct, maxes, totals, part, inward, across,
     kv_send, kv_recv, kv_save, send_one, recv_one, send_two, recv_two, save,
     wg, wu, wd, loads, cot, inner_t, gg_t, ug_t, late, late_save, wo_all, ctx_all, attn,
     p_send, p_recv, c_send, c_recv, c_save, a_save), refs = refs[:37], refs[37:]
    (fold_d, fold_g, fold_u), grads = make_folds(split, side, ring, refs, saved, (0, 1, 2))
    seqs, rows, width = q_out.shape
    heads = width // HEAD_DIM
    tile = 256
    chunk, dim = part.shape[1:]
    per_seq = rows // chunk
    per_tile = tile // chunk
    middle = dim // 2
    units = wg_in.shape[-2]
    mate, peer = ring_peers(ring)
    half = lax.rem(ring, 2)
    for full in (wg, wu, wd):
        for piece in range(2):
            full[piece, units:] = jnp.zeros((full.shape[1] - units, full.shape[2]), bf16)
    own_loads = [pltpu.make_async_copy(cot_hbm, cot, loads.at[6])]
    for n, (source, full) in enumerate(((wg_in, wg), (wu_in, wu), (wd_in, wd))):
        if split:
            own_loads.append(pltpu.make_async_copy(source, full.at[side, 0:units], loads.at[n]))
        else:
            for piece in range(2):
                own_loads.append(pltpu.make_async_copy(
                    source.at[piece], full.at[piece, 0:units], loads.at[2 * n + piece]))
    greet(line_peers(place) + ring_peers(ring) + ([{"fsdp": 1 - side}] if split else []))

    if split:
        other = {"fsdp": 1 - side}
        for n, gain in enumerate((g1, g2)):
            gains[side, n : n + 1, :] = flat_row(gain)
        move_gains = remote(gains.at[side], gains.at[side], g_sems.at[0], g_sems.at[1], other)
        move_gains.start()

        def spot(full, owner, part_at, size):
            if full is wo_all:
                return full.at[place, owner, rows_at(part_at * size, size)]
            if full.shape[0] == 2:
                return full.at[owner, rows_at(part_at * size, size)]
            return full.at[rows_at((2 * owner + part_at) * size, size)]

        table = (
            (wk_in, wk, spot), (wv_in, wv, spot), (wq_in, wq, spot), (wo_in, wo_all, spot),
            (wg_in, wg, spot), (wu_in, wu, spot), (wd_in, wd, spot))

        def cross(n):
            own, full, where = table[n]
            size = own.shape[0] // 2
            return remote(own.at[rows_at(half * size, size)], where(full, side, half, size),
                          w_send.at[n, 0], w_recv.at[n, 0], other)

        def onto_mate(n):
            own, full, where = table[n]
            here = where(full, 1 - side, half, own.shape[0] // 2)
            return remote(here, here, w_send.at[n, 1], w_recv.at[n, 1], mate)

        def hand_on(n):
            cross(n).wait_recv()
            onto_mate(n).start()

        saves = tuple(
            pltpu.make_async_copy(full, target, w_save.at[n])
            for n, (full, target) in enumerate(((wk, wk_hbm), (wv, wv_hbm), (wq, wq_hbm), (wo_all.at[place], wo_hbm))))
        for n in range(3):
            cross(n).start()
        for own, full, _ in table[:3]:
            full[rows_at(side * own.shape[0], own.shape[0]), :] = own[...]
        wo_all[place, side] = wo_in[...]
        part_o = wo_in.shape[0] // 2
        item_side = lambda item: side if item == 0 else 1 - side
        pass_o = Passing(
            place, lambda piece, item: wo_all.at[piece, item_side(item), rows_at(half * part_o, part_o)],
            (p_send, p_recv),
            lambda item: wo_in.at[rows_at(half * part_o, part_o)] if item == 0 else None)
        pass_o.begin(0)

        def share_o(n):
            here = wo_all.at[lax.rem(place + n + 1, 4), :, rows_at(half * part_o, part_o)]
            return remote(here, here, o_send.at[n], o_recv.at[n], mate)
        remote(gains.at[side], gains.at[side], g_sems.at[0], g_sems.at[1], other).wait()
    else:
        size = gains.shape[2]
        for piece in range(2):
            for n, gain in enumerate((g1, g2)):
                gains[piece, n : n + 1, :] = flat_row(gain)[:, piece * size : (piece + 1) * size]
        wo_all[place] = wo_in[...]
        pass_o = Passing(place, lambda piece, item: wo_all.at[piece, item], (p_send, p_recv))
        pass_o.begin(0)
        pass_o.begin(1)

    for load in own_loads:
        load.start()

    def pass_block(s, which, source, target, device, slot):
        return remote(
            kv.at[s, source, which], kv.at[s, target, which], kv_send.at[s, which, slot],
            kv_recv.at[s, which, target], device)

    to_mate = lambda s, which: pass_block(s, which, 0, 1, mate, 0)
    to_peer = lambda s, which: pass_block(s, which, 0, 2, peer, 1)
    onward = lambda s, which: pass_block(s, which, 2, 3, mate, 2)
    gain_one = gain_row(gains, 0)
    fine = 16
    coarse_at = (ring * rows + fine * lax.broadcasted_iota(jnp.int32, (rows // fine, 128), 0)).astype(f32)
    fine_at = lax.broadcasted_iota(jnp.int32, (fine, 128), 0).astype(f32)
    step = lax.rem(lax.broadcasted_iota(jnp.int32, (1, 128), 1), HEAD_DIM // 2)
    frequency = jnp.ones((1, 128), f32)
    for bit in range(5):
        ratio = rope_base ** (-(2**bit) / (HEAD_DIM // 2))
        frequency = frequency * jnp.where(lax.rem(step // 2**bit, 2) == 1, ratio, 1.0)
    turns = [at * frequency for at in (coarse_at, fine_at)]
    (cos_a, sin_a), (cos_b, sin_b) = ((jnp.cos(x), jnp.sin(x)) for x in turns)
    cos_a, sin_a = cos_a[:, None, :], sin_a[:, None, :]
    cos_b, sin_b = cos_b[None], sin_b[None]
    cosine[...] = (cos_a * cos_b - sin_a * sin_b).reshape(rows, 128)
    sine[...] = (sin_a * cos_b + cos_a * sin_b).reshape(rows, 128) * jnp.where(
        low_half((rows, 128)), -1.0, 1.0)

    per_seq_tiles = rows // tile
    tiles = seqs * per_seq_tiles

    def tile_at(t):
        return t // per_seq_tiles, rows_at(lax.rem(t, per_seq_tiles) * tile, tile)

    @pl.loop(0, tiles)
    def _(t):
        s, at = tile_at(t)
        normed_s[s, at, :] = (unit_norm(tok[s, at, :].astype(f32)) * gain_one).astype(bf16)

    def keys(s):
        @pl.loop(0, per_seq_tiles)
        def _(t):
            at = rows_at(t * tile, tile)
            k = dot(normed_s[s, at, :], wk[...])
            kv[s, 0, 0, at, :] = turn(k, cosine[at, :], sine[at, :]).astype(bf16)

        to_peer(s, 0).start()
        to_mate(s, 0).start()

    def values(s):
        @pl.loop(0, per_seq_tiles)
        def _(t):
            at = rows_at(t * tile, tile)
            v = dot(normed_s[s, at, :], wv[...])
            kv[s, 0, 1, at, :] = (0.5 * v + 0.5 * fv[s, at, :].astype(f32)).astype(bf16)

        to_peer(s, 1).start()
        to_mate(s, 1).start()

    if split:
        hand_on(0)
        onto_mate(0).wait_recv()
    keys(0)
    if split:
        hand_on(1)
        cross(3).start()
        onto_mate(1).wait_recv()
    values(0)
    if split:
        hand_on(2)
    for s in range(1, seqs):
        keys(s)
        values(s)
    if split:
        onto_mate(2).wait_recv()

    @pl.loop(0, tiles)
    def _(t):
        s, at = tile_at(t)
        q = dot(normed_s[s, at, :], wq[...])
        q = turn(q, cosine[at, :], sine[at, :]) * HEAD_DIM ** (-0.5)
        q_out[s, at, :] = q.astype(bf16)
        spread(qtm.at[s], jnp.transpose(q), lax.rem(t, per_seq_tiles) * tile, rows)

    pass_o.step(0, 1)
    if split:
        hand_on(3)
        pass_o.begin(1)
        for n in range(4, 7):
            cross(n).start()

    def saving(i):
        return pltpu.make_async_copy(part.at[i], sum_hbm.at[i], save.at[i])

    sums = Sum(
        place, part, inward, across, (send_one, recv_one, send_two, recv_two), lambda i: saving(i).start())
    passing = Passing(place, lambda piece, item: ctx_all.at[piece, item], (c_send, c_recv))

    def saving_context(s):
        mine = pl.ds(s * per_seq_tiles, per_seq_tiles)
        return pltpu.make_async_copy(ctx_all.at[place, mine], ctx_hbm.at[mine], c_save.at[s])

    def saving_kv(s):
        return pltpu.make_async_copy(kv.at[s], kv_hbm.at[s], kv_save.at[s])

    @pl.loop(0, seqs)
    def _(s):
        maxes[...] = jnp.full_like(maxes, masked_score)
        totals[...] = jnp.zeros_like(totals)
        acct[...] = jnp.zeros_like(acct)

        @pl.loop(0, 4)
        def _(j):
            @pl.when(j == 1)
            def _():
                for which in range(2):
                    to_mate(s, which).wait_recv()

                @pl.when(s > 0)
                def _():
                    pass_o.step(1, 2)

            @pl.when(j == 2)
            def _():
                for which in range(2):
                    to_peer(s, which).wait_recv()
                    onward(s, which).start()

                @pl.when(s == 0)
                def _():
                    pass_o.step(0, 2)
                    pass_o.step(1, 1)

            @pl.when(j == 3)
            def _():
                for which in range(2):
                    onward(s, which).wait_recv()

                @pl.when(s > 0)
                def _():
                    pass_o.step(0, 3)
                    pass_o.step(1, 3)
                    if split:
                        for n in range(3):
                            share_o(n).start()
                        hand_on(6)

            vt[...] = jnp.transpose(kv[s, j, 1])
            key_pos = block_place(ring, j) * rows + lax.broadcasted_iota(jnp.int32, (rows, 1), 0)
            query_pos = ring * rows + lax.rem(lax.broadcasted_iota(jnp.int32, (1, 2 * rows), 1), rows)
            limit = jnp.maximum(query_pos + 1, prefix[s])

            @pl.loop(0, heads // 2)
            def _(h):
                scores = jnp.where(key_pos < limit, dot(kv[s, j, 0], qtm[s, h]), masked_score)
                old = maxes[h]
                new = jnp.maximum(old, jnp.max(scores, axis=0, keepdims=True))
                weights = jnp.exp(scores - new)
                fade = jnp.exp(old - new)
                maxes[h] = new
                totals[h] = totals[h] * fade + jnp.sum(weights, axis=0, keepdims=True)
                low = weights.astype(bf16)
                for n in range(2):
                    of_head = rows_at((2 * h + n) * HEAD_DIM, HEAD_DIM)
                    lanes = slice(n * rows, (n + 1) * rows)
                    acct[of_head, :] = acct[of_head, :] * fade[:, lanes] + dot(vt[of_head, :], low[:, lanes])
                at_step = j * (heads // 2) + h

                n = jnp.where(at_step == 7, 3, at_step // 2 - 1)

                @pl.when((s > 0) & (at_step > 1) & ((at_step == 7) | (lax.rem(at_step, 2) == 0)))
                def _():
                    passing.step((s - 1) * per_seq_tiles + lax.rem(n, per_seq_tiles), 1 + n // per_seq_tiles)

        for h in range(heads):
            if h % 2 == 0:
                lse_out[s, h // 2 : h // 2 + 1, :] = maxes[h // 2] + jnp.log(totals[h // 2])
            of_head = slice(h * HEAD_DIM, (h + 1) * HEAD_DIM)
            acct[of_head, :] = acct[of_head, :] / totals[h // 2][:, h % 2 * rows : (h % 2 + 1) * rows]
        for t in range(per_seq_tiles):
            ctx_all[place, s * per_seq_tiles + t] = jnp.transpose(acct[:, t * tile : (t + 1) * tile]).astype(bf16)
            passing.begin(s * per_seq_tiles + t)
        saving_context(s).start()
        saving_kv(s).start()

        @pl.when(s == 0)
        def _():
            if split:
                onto_mate(3).wait_recv()
                for copy in saves:
                    copy.start()
                hand_on(4)
                hand_on(5)

    if split:
        for n in range(3):
            share_o(n).wait_recv()
    if split:
        for n in range(4, 7):
            onto_mate(n).wait_recv()
    for load in own_loads:
        load.wait()
    lines = seqs * per_seq
    early = lines
    count = part.shape[0]
    gain_two = gain_row(gains, 1)

    def saving_attn(t):
        mine = pl.ds(t * per_tile, per_tile)
        return pltpu.make_async_copy(attn.at[mine], attn_hbm.at[mine], a_save.at[t])

    def across_both(left, full):
        return dot_nt(left[:, :middle], full[0]) + dot_nt(left[:, middle:], full[1])

    def saving_late(t):
        mine = pl.ds((t - 1) * per_tile, per_tile)
        return pltpu.make_async_copy(late.at[mine], late_hbm.at[mine], late_save.at[t - 1])

    stepped = [0]

    def act(*plan):
        for what in plan:
            if what == "sum":
                sums.steps(stepped[0], 1)
                stepped[0] += 1
            else:
                passing.step(*what)

    plans = {
        (0, 0): [(0, 3)], (0, 1): [(1, 3)], (0, 2): [(2, 1)], (0, 3): [],
        (1, 0): [], (1, 1): [(3, 1)], (1, 2): [], (1, 3): ["sum"],
        (2, 0): [(2, 2), "sum", (3, 2), "sum", (2, 3)], (2, 1): ["sum"], (2, 2): [], (2, 3): ["sum"],
        (3, 0): [(3, 3)], (3, 1): ["sum"], (3, 2): ["sum"], (3, 3): ["sum"],
    }
    for t in range(tiles):
        s, at = t // per_seq_tiles, slice(t % per_seq_tiles * tile, (t % per_seq_tiles + 1) * tile)
        flat = slice(t * tile, (t + 1) * tile)
        mine = t * per_tile
        act(*plans[t, 0])
        context = jnp.concatenate([ctx_all[p, t] for p in range(4)], axis=1)
        attended = [
            dot(context, jnp.concatenate([wo_all[p, piece] for p in range(4)], axis=0)) for piece in range(2)]
        for piece in range(2):
            for k in range(per_tile):
                attn[mine + k, :, piece * middle : (piece + 1) * middle] = attended[piece][
                    k * chunk : (k + 1) * chunk].astype(bf16)
        saving_attn(t).start()
        hidden = tok[s, at, :].astype(f32) + jnp.concatenate(attended, axis=1)
        normed = (unit_norm(hidden) * gain_two).astype(bf16)
        normed_s[s, at, :] = normed
        gate = across_both(normed, wg)
        up = across_both(normed, wu)
        sigmoid = jax.nn.sigmoid(gate)
        swish = gate * sigmoid
        inner = (swish * up).astype(bf16)
        inner_t[:, flat] = jnp.transpose(inner)
        inner_grad = across_both(cot[s, at, :], wd)
        gate_grad = (inner_grad * up * sigmoid * (1.0 + gate * (1.0 - sigmoid))).astype(bf16)
        up_grad = (inner_grad * swish).astype(bf16)
        act(*plans[t, 1])
        for piece in range(2):
            sums.fill(mine, piece, dot(gate_grad, wg[piece]) + dot(up_grad, wu[piece]))
        sums.offer(mine, per_tile)
        act(*plans[t, 2])
        feeds = [dot(inner, wd[piece]) for piece in range(2)]

        if t == 0:
            for piece in range(2):
                sums.fill(early, piece, feeds[piece])
        else:
            for piece in range(2):
                for k in range(per_tile):
                    late[mine - per_tile + k, :, piece * middle : (piece + 1) * middle] = feeds[piece][
                        k * chunk : (k + 1) * chunk].astype(bf16)
            saving_late(t).start()

        gg_t[:, flat] = jnp.transpose(gate_grad)
        ug_t[:, flat] = jnp.transpose(up_grad)
        act(*plans[t, 3])

    sums.offer(early, count - early)
    deep = units // 2

    def weight_grad(n, left_t, right):
        for h in range(2):
            for y in range(2):
                total = jnp.zeros((deep, middle), f32)
                for s in range(seqs):
                    total = total + dot(
                        left_t[h * deep : (h + 1) * deep, s * rows : (s + 1) * rows],
                        right[s, :, y * middle : (y + 1) * middle])
                grads[n][h, y] = total.astype(bf16)

    begun = stepped[0]
    weight_grad(0, inner_t, cot)
    fold_d.first()
    sums.steps(begun, 1)
    weight_grad(1, gg_t, normed_s)
    fold_g.first()
    fold_d.second()
    sums.steps(begun + 1, 1)
    weight_grad(2, ug_t, normed_s)
    fold_u.first()
    fold_g.second()
    sums.steps(begun + 2, 1)
    fold_u.second()
    sums.steps(begun + 3, 3)
    fold_d.quarter()
    sums.steps(begun + 6, 3)
    fold_g.quarter()
    sums.steps(begun + 9, count - begun - 9)
    fold_u.quarter()
    sums.settled(0, count)
    sums.close(count)
    for fold in (fold_d, fold_g, fold_u):
        fold.settle()
    for t in range(1, tiles):
        saving_late(t).wait()
    for s in range(seqs):
        for which in range(2):
            to_mate(s, which).wait_send()
            to_peer(s, which).wait_send()
            onward(s, which).wait_send()
        saving_kv(s).wait()
        saving_context(s).wait()
    for t in range(tiles):
        saving_attn(t).wait()
    pass_o.settle(2)
    passing.settle(tiles)

    @pl.loop(0, count)
    def _(i):
        saving(i).wait()

    if split:
        for n in range(7):
            cross(n).wait_send()
            onto_mate(n).wait_send()
        for n in range(3):
            share_o(n).wait_send()
        for copy in saves:
            copy.wait()


def limits(ident, megabytes=60):
    return pltpu.CompilerParams(
        collective_id=ident, has_side_effects=True, vmem_limit_bytes=megabytes * 1024 * 1024)


def front(split, tok, fv, cot, gains, square, wide, prefix):
    seqs, rows, dim = tok.shape
    width, units = square[0].shape[1], wide[0].shape[-2]
    heads = width // HEAD_DIM
    chunk, tile = 64, 256
    tokens = seqs * rows
    count = tokens // chunk + tile // chunk
    after = (tokens - tile) // chunk
    padded = -(-units // 256) * 256
    vmem = pl.BlockSpec(memory_space=pltpu.VMEM)
    anyw = pl.BlockSpec(memory_space=pl.ANY)
    dma = pltpu.SemaphoreType.DMA
    lines = pltpu.VMEM((count, chunk, dim), bf16)
    shape = jax.ShapeDtypeStruct
    full = [(dim, width)] * 3 + [(2, width, dim // 2)]
    fold_scratch, fold_outs = fold_shapes([(units // 2, dim // 2)] * 3, split, (0, 1, 2))
    outs = [
        shape((count, chunk, dim), bf16), shape((after, chunk, dim), bf16), shape((seqs, rows, width), bf16),
        shape((seqs, 4, 2, rows, width), bf16), shape((tokens // chunk, chunk, dim), bf16),
        shape((tokens // tile, tile, width), bf16),
        shape((seqs, heads // 2, 2 * rows), f32), shape((2, 8, dim // 2), f32),
        shape((rows, 128), f32), shape((rows, 128), f32)] + fold_outs
    out_specs = [anyw, anyw, vmem, anyw, anyw, anyw, vmem, vmem, vmem, vmem] + [anyw] * 3
    scratch = []
    if split:
        outs += [shape(size, bf16) for size in full]
        out_specs += [anyw] * 4
        scratch = [pltpu.VMEM(size, bf16) for size in full[:3]] + [
            dma((7, 2)), dma((7, 2)), dma((4,)), dma((2,)), dma((3,)), dma((3,))]
    scratch += [
        pltpu.VMEM((seqs, rows, dim), bf16),
        pltpu.VMEM((seqs, 4, 2, rows, width), bf16),
        pltpu.VMEM((seqs, heads // 2, width, 2 * rows), bf16),
        pltpu.VMEM((width, rows), bf16),
        pltpu.VMEM((width, rows), f32),
        pltpu.VMEM((heads // 2, 1, 2 * rows), f32),
        pltpu.VMEM((heads // 2, 1, 2 * rows), f32),
        lines, lines, lines,
        dma((seqs, 2, 3)), dma((seqs, 2, 4)), dma((seqs,)),
        dma((count,)), dma((count,)), dma((count,)), dma((count,)), dma((count,)),
        pltpu.VMEM((2, padded, dim // 2), bf16),
        pltpu.VMEM((2, padded, dim // 2), bf16),
        pltpu.VMEM((2, padded, dim // 2), bf16),
        dma((7,)),
        pltpu.VMEM((seqs, rows, dim), bf16),
        pltpu.VMEM((padded, tokens), bf16),
        pltpu.VMEM((padded, tokens), bf16),
        pltpu.VMEM((padded, tokens), bf16),
        pltpu.VMEM((after, chunk, dim), bf16),
        dma((tokens // tile,)),
        pltpu.VMEM((4, 2, width, dim // 2), bf16),
        pltpu.VMEM((4, tokens // tile, tile, width), bf16),
        pltpu.VMEM((tokens // chunk, chunk, dim), bf16),
        dma((2, 2, 4)), dma((2, 4)), dma((tokens // tile, 2, 4)), dma((tokens // tile, 4)),
        dma((seqs,)), dma((tokens // tile,)),
    ] + fold_scratch
    return pl.pallas_call(
        functools.partial(front_kernel, split),
        name="front",
        out_shape=outs,
        in_specs=[vmem] * 2 + [anyw] + [vmem] * 6 + [anyw] * 3 + [pl.BlockSpec(memory_space=pltpu.SMEM)],
        out_specs=out_specs,
        scratch_shapes=scratch,
        compiler_params=limits(0, 63),
        cost_estimate=pl.CostEstimate(flops=22 * 10**9, bytes_accessed=2 * 10**7, transcendentals=10**7),
    )(tok, fv, cot, *gains, *square, *wide, prefix)


def back_kernel(split, *refs):
    place, ring, side = lax.axis_index("tp"), lax.axis_index("ctx"), lax.axis_index("fsdp")
    quarters, refs = (refs[:3], refs[3:]) if split else ((), refs)
    loaded, refs = refs[:12], refs[12:]
    (gain_in, lse, cosine, sine, prefix, block_hbm, token_hbm, fv_hbm, gain_out), saved, refs = (
        refs[:9], refs[9:13], refs[13:])
    ends_saved, refs = (refs[:3], refs[3:]) if split else ((), refs)
    (tok, cot, wq, wk, wv, wo, q, kv, ctx, attn, mixed, early), refs = refs[:12], refs[12:]
    (hid, dwo_sum, qtm, qm, otm, om, kt, delta, dqt, dk, dv, give, take, proj, normed_t,
     part, inward, across, gain_part, gain_all,
     kv_send, kv_recv, send_one, recv_one, send_two, recv_two, save, gain_send, gain_recv, loads, fv_save), refs = (
        refs[:31], refs[31:])
    ends_scratch, refs = (refs[:12], refs[12:]) if split else ((), refs)
    (fold_o, fold_k, fold_v, fold_q), (dwo, dwk, dwv, dwq) = make_folds(split, side, ring, refs, saved, (0, 1, 2, 3, 4))
    ends, ends_mine = make_folds(split, side, ring, ends_scratch, ends_saved, (3, 4)) if split else ((), ())
    late_hbm, sum_hbm, attn_hbm, tok_hbm, cot_hbm, wq_hbm, wk_hbm, wv_hbm, wo_hbm, q_hbm, kv_hbm, ctx_hbm = loaded
    seqs, rows, dim = tok.shape
    width = wq.shape[1]
    heads = width // HEAD_DIM
    chunk = part.shape[1]
    per_seq = rows // chunk
    tile = 256
    per_tile = tile // chunk
    middle = dim // 2
    lines = seqs * per_seq
    count = 2 * lines - per_tile
    head_start = per_seq + 3
    rest = 2 * per_seq - per_tile - head_start
    rest_start = head_start + per_seq
    own_start = (head_start, rest_start + rest)
    mate, peer = ring_peers(ring)
    others = [(dy, dc) for dy in range(2) for dc in range(4) if dy or dc]
    group = [{"fsdp": lax.rem(side + dy, 2), "ctx": lax.rem(ring + dc, 4)} for dy, dc in others]

    copies = {}

    def load(name, source, target, start=True):
        copies[name] = pltpu.make_async_copy(source, target, loads.at[len(copies)])
        if start:
            copies[name].start()

    def ready(*names):
        for name in names:
            copies[name].wait()

    load("late", late_hbm.at[0:head_start], part.at[0:head_start])
    later = []
    for s in range(seqs):
        mine = slice(s * per_seq, (s + 1) * per_seq)
        for name, source, target in (
            ("tok", tok_hbm.at[s], tok.at[s]), ("attn", attn_hbm.at[mine], attn.at[mine]),
            ("cot", cot_hbm.at[s], cot), ("mixed", sum_hbm.at[mine], mixed),
            ("q", q_hbm.at[s], q.at[s]), ("ctx", ctx_hbm.at[s], ctx.at[s]), ("kv", kv_hbm.at[s], kv),
        ):
            now = s == 0 and name != "kv"
            load(f"{name}{s}", source, target, now)
            if not now and (s == 0 or name not in ("cot", "mixed", "kv")):
                later.append(f"{name}{s}")
        if s == 0:
            load("wo", wo_hbm, wo)
    for name, source, target in (
        [(f"quarter{n}", quarter, ends_mine[n]) for n, quarter in enumerate(quarters)] + [
            ("rest", late_hbm.at[head_start : head_start + rest], part.at[rest_start : rest_start + rest]),
            ("early", sum_hbm.at[lines : lines + per_tile], early),
            ("wq", wq_hbm, wq), ("wk", wk_hbm, wk), ("wv", wv_hbm, wv)]
    ):
        load(name, source, target, False)
        later.append(name)
    greet(line_peers(place) + (group if split else ring_peers(ring)))
    gain_one, gain_two = gain_row(gain_in, 0), gain_row(gain_in, 1)
    gain_part[...] = jnp.zeros_like(gain_part)

    def chunk_at(n):
        return n // per_seq, rows_at(lax.rem(n, per_seq) * chunk, chunk)

    def saving_block(i, n):
        s, own = chunk_at(n)
        return pltpu.make_async_copy(across.at[i], block_hbm.at[s, own], save.at[i])

    def saving_early(n):
        return pltpu.make_async_copy(early.at[n], block_hbm.at[0, n * chunk : (n + 1) * chunk], save.at[count + n])

    def saving_token(i, n):
        s, own = chunk_at(n)
        return pltpu.make_async_copy(across.at[i], token_hbm.at[s, own], save.at[i])

    def add_gain(which, value):
        for piece in range(2):
            gain_part[piece, which : which + 1, :] += value[:, piece * middle : (piece + 1) * middle]

    is_block = lambda i: (i < head_start) | ((i >= rest_start) & (i < own_start[1]))
    block_of = lambda i: per_tile + jnp.where(i < head_start, i, i - per_seq)
    token_of = lambda i: jnp.where(i < rest_start, i - head_start, i - own_start[1] + per_seq)

    def done(i):
        @pl.when(is_block(i))
        def _():
            n = block_of(i)
            s, own = chunk_at(n)
            across[i] = (
                tok[s, own, :].astype(f32) + attn[n].astype(f32) + part[i].astype(f32)).astype(bf16)
            saving_block(i, n).start()

        @pl.when(jnp.logical_not(is_block(i)))
        def _():
            n = token_of(i)
            s, own = chunk_at(n)
            values, upstream = tok[s, own, :].astype(f32), part[i].astype(f32)
            factor = lax.rsqrt(jnp.mean(values * values, axis=-1, keepdims=True) + epsilon)
            scaled = upstream * gain_one
            add_gain(0, jnp.sum(upstream * values * factor, axis=0, keepdims=True))
            across[i] = (hid[s, own, :] + factor * scaled - values * factor**3 * jnp.mean(
                scaled * values, axis=-1, keepdims=True)).astype(bf16)
            saving_token(i, n).start()

    sums = Sum(place, part, inward, across, (send_one, recv_one, send_two, recv_two), done)

    def move(s, source, target, device):
        return remote(give.at[source], take.at[s, target], kv_send.at[source], kv_recv.at[s, target], device)

    far_to_mate = lambda s: move(s, 2, 0, mate)
    peer_back = lambda s: move(s, 1, 1, peer)
    near_to_mate = lambda s: move(s, 0, 2, mate)
    ready("late")
    sums.offer(0, head_start)
    for name in later:
        copies[name].start()

    def hidden_stage(s):
        @pl.loop(0, rows // tile)
        def _(t):
            at = rows_at(t * tile, tile)
            first = s * per_seq + t * per_tile
            join = lambda ref: jnp.concatenate([ref[first + k] for k in range(per_tile)], axis=0).astype(f32)
            token = tok[s, at, :].astype(f32)
            values = token + join(attn)
            upstream = jnp.concatenate(
                [mixed[t * per_tile + k] for k in range(per_tile)], axis=0).astype(f32)
            factor = lax.rsqrt(jnp.mean(values * values, axis=-1, keepdims=True) + epsilon)
            scaled = upstream * gain_two
            add_gain(1, jnp.sum(upstream * values * factor, axis=0, keepdims=True))
            hid_now = cot[at, :].astype(f32) + factor * scaled - values * factor**3 * jnp.mean(
                scaled * values, axis=-1, keepdims=True)
            hid[s, at, :] = hid_now
            low = hid_now.astype(bf16)
            dwo_sum[...] += dot(jnp.transpose(ctx[s, at, :]), low)
            left, right = low[:, :middle], low[:, middle:]
            grad = dot_nt(left, wo[0]) + dot_nt(right, wo[1])
            lane_owner = lax.broadcasted_iota(jnp.int32, grad.shape, 1) // HEAD_DIM
            q_now = q[s, at, :].astype(f32)
            grad_t = jnp.transpose(grad)
            q_t = jnp.transpose(q_now)
            product = jnp.transpose(grad.astype(bf16).astype(f32) * ctx[s, at, :].astype(f32))
            for h in range(heads):
                low_rows = rows_at(h % 2 * rows + t * tile, tile)
                om[h // 2, low_rows, :] = jnp.where(lane_owner == h, grad, 0.0).astype(bf16)
                qm[h // 2, low_rows, :] = jnp.where(lane_owner == h, q_now, 0.0).astype(bf16)
                delta[h // 2, :, low_rows] = jnp.sum(
                    product[h * HEAD_DIM : (h + 1) * HEAD_DIM], axis=0, keepdims=True)
            spread(otm, grad_t, t * tile, rows)
            spread(qtm, q_t, t * tile, rows)
            normed = (unit_norm(token) * gain_one).astype(bf16)
            normed_t[:, rows_at(s * rows + t * tile, tile)] = jnp.transpose(normed)

    def back_block(s, j, tick):
        kt[...] = jnp.transpose(kv[j, 0])
        key_pos = block_place(ring, j) * rows + lax.broadcasted_iota(jnp.int32, (rows, 1), 0)
        query_pos = ring * rows + lax.rem(lax.broadcasted_iota(jnp.int32, (1, 2 * rows), 1), rows)
        limit = jnp.maximum(query_pos + 1, prefix[s])
        dk[...] = jnp.zeros_like(dk)
        dv[...] = jnp.zeros_like(dv)

        @pl.loop(0, heads // 2)
        def _(h):
            scores = dot(kv[j, 0], qtm[h])
            probs = jnp.where(key_pos < limit, jnp.exp(scores - lse[s, pl.ds(h, 1), :]), 0.0)
            dprobs = dot(kv[j, 1], otm[h])
            dv[...] += dot(probs.astype(bf16), om[h])
            dscores = (probs * (dprobs - delta[h])).astype(bf16)
            dk[...] += dot(dscores, qm[h])
            for n in range(2):
                of_head = rows_at((2 * h + n) * HEAD_DIM, HEAD_DIM)
                dqt[of_head, :] += dot(kt[of_head, :], dscores[:, n * rows : (n + 1) * rows])
            tick(h)

    def finalize(s):
        near_to_mate(s).wait_recv()
        peer_back(s).wait_recv()
        @pl.loop(0, rows // tile)
        def _(t):
            at = rows_at(t * tile, tile)
            flat = rows_at(s * rows + t * tile, tile)
            co, si = cosine[at, :], sine[at, :]
            grad_v = 0.5 * (dv[at, :] + take[s, 2, 1, at, :].astype(f32) + take[s, 1, 1, at, :].astype(f32))
            grad_k = dk[at, :] + take[s, 2, 0, at, :].astype(f32) + take[s, 1, 0, at, :].astype(f32)
            grad_q = jnp.transpose(dqt[:, at]) * HEAD_DIM ** (-0.5)
            proj[0, flat, :] = turn(grad_q, co, si, -1.0).astype(bf16)
            proj[1, flat, :] = turn(grad_k, co, si, -1.0).astype(bf16)
            proj[2, flat, :] = grad_v.astype(bf16)
            i = jnp.where(s == 0, own_start[0], own_start[1]) + t * per_tile
            for piece in range(2):
                cut = slice(piece * middle, (piece + 1) * middle)
                sums.fill(i, piece, dot_nt(proj[0, flat, :], wq[cut, :]) + dot_nt(
                    proj[1, flat, :], wk[cut, :]) + dot_nt(proj[2, flat, :], wv[cut, :]))
            sums.offer(i, per_tile)

        @pl.when(s == 0)
        def _():
            sums.offer(rest_start, rest)

    ready("wo")
    dwo_sum[...] = jnp.zeros_like(dwo_sum)
    if split:
        ready("quarter0")
        ends[0].resume()

    def start_at(phase, *names):
        for wanted in range(1, seqs):
            @pl.when(phase == wanted - 1)
            def _():
                for name in names:
                    copies[f"{name}{wanted}"].start()

    def at_phase(phase, wanted, names):
        @pl.when(phase == wanted)
        def _():
            ready(*names)

    plan = [(1, m, m) for m in range(7)] + [(2, m, 10 + line) for line, m in enumerate((0, 1, 3, 4, 6, 7))]

    @pl.loop(0, seqs + 1)
    def _(phase):
        s = jnp.maximum(phase - 1, 0)
        follows = phase > 1

        @pl.when(phase > 0)
        def _():
            for wanted in range(seqs):
                at_phase(phase, wanted + 1, [f"kv{wanted}"])
            for wanted in range(1, seqs):
                at_phase(phase, 1, [f"tok{wanted}", f"attn{wanted}"])
            dqt[...] = jnp.zeros_like(dqt)

            @pl.loop(0, 4)
            def _(n):
                def tick(h):
                    chosen = -1
                    for at_phase, at_step, line in plan:
                        chosen = jnp.where((phase == at_phase) & (2 * n + h == at_step), line, chosen)

                    @pl.when(chosen >= 0)
                    def _():
                        sums.steps(chosen, 1)

                back_block(s, 3 - n, tick)

                @pl.when(n == 0)
                def _():
                    @pl.when(follows)
                    def _():
                        far_to_mate(s - 1).wait_send()
                        fold_o.second()

                    give[2, 0] = dk[...].astype(bf16)
                    give[2, 1] = dv[...].astype(bf16)
                    far_to_mate(s).start()

                @pl.when(n == 1)
                def _():
                    far_to_mate(s).wait_recv()

                    @pl.when(follows)
                    def _():
                        peer_back(s - 1).wait_send()

                    give[1, 0] = (dk[...] + take[s, 0, 0].astype(f32)).astype(bf16)
                    give[1, 1] = (dv[...] + take[s, 0, 1].astype(f32)).astype(bf16)
                    peer_back(s).start()

                @pl.when(n == 2)
                def _():
                    @pl.when(follows)
                    def _():
                        near_to_mate(s - 1).wait_send()
                        fold_o.third()

                    give[0, 0] = dk[...].astype(bf16)
                    give[0, 1] = dv[...].astype(bf16)
                    near_to_mate(s).start()

            start_at(phase - 1, "kv")

        @pl.when(phase < seqs)
        def _():
            for wanted in range(seqs):
                names = ("tok", "attn") * (wanted == 0) + ("cot", "mixed", "q", "ctx")
                at_phase(phase, wanted, [f"{name}{wanted}" for name in names])
            hidden_stage(phase)
            start_at(phase, "cot", "mixed")

            @pl.when(phase == 1)
            def _():
                sums.steps(7, 1)

        @pl.when(phase > 0)
        def _():
            at_phase(phase, 1, ["wq", "wk", "wv", "rest"])
            sums.steps(jnp.where(phase == 1, 8, 16), 1)
            finalize(s)
            sums.steps(jnp.where(phase == 1, 9, 17), 1)

        @pl.when(phase == seqs - 1)
        def _():
            deep = dwo.shape[2]
            for h in range(2):
                for y in range(2):
                    dwo[h, y] = dwo_sum[h * deep : (h + 1) * deep, y * middle : (y + 1) * middle].astype(bf16)
            fold_o.first()
            if split:
                ends[0].fourth()
                ready("quarter1")
                ends[1].resume()

    begun = 18
    fv_copy = pltpu.make_async_copy(proj.at[2], fv_hbm, fv_save)
    fv_copy.start()
    if split:
        ends[1].fourth()
        ready("quarter2")
        ends[2].resume()
        ends[0].last()
    share = dwq.shape[2]

    def square_grad(target, which):
        @pl.loop(0, 4)
        def _(k):
            h, y = k // 2, lax.rem(k, 2)
            target[h, y] = dot(normed_t[rows_at((2 * y + h) * share, share), :], proj[which]).astype(bf16)

    ready("early")
    for n in range(per_tile):
        own = slice(n * chunk, (n + 1) * chunk)
        early[n] = (tok[0, own, :].astype(f32) + attn[n].astype(f32) + early[n].astype(f32)).astype(bf16)
        saving_early(n).start()
    square_grad(dwk, 1)
    fold_k.first()
    sums.steps(begun, 1)
    square_grad(dwv, 2)
    fold_v.first()
    fold_k.second()
    sums.steps(begun + 1, 1)
    square_grad(dwq, 0)
    fold_q.first()
    fold_v.second()
    sums.steps(begun + 2, 1)
    fold_q.second()
    fold_o.fourth()
    sums.steps(begun + 3, 1)
    fold_k.third()
    sums.steps(begun + 4, 1)
    fold_v.third()
    sums.steps(begun + 5, 1)
    fold_q.third()
    fold_k.fourth()
    sums.steps(begun + 6, 1)
    fold_v.fourth()
    sums.steps(begun + 7, 1)
    fold_q.fourth()
    for fold in (fold_o, fold_k, fold_v) + tuple(ends[1:2]):
        fold.last()
    if split:
        ends[2].fourth()
    sums.steps(begun + 8, count - begun - 8)
    for fold in (fold_q,) + tuple(ends[2:]):
        fold.last()
    sums.settled(0, count)
    sums.close(count)
    if split:
        me = 4 * side + ring
        gain_all[me] = gain_part[side]

        def share_gain(n):
            dy, dc = others[n]
            y = lax.rem(side + dy, 2)
            return remote(gain_part.at[y], gain_all.at[me], gain_send.at[n], gain_recv.at[n], group[n])

        for n in range(7):
            share_gain(n).start()
        for n in range(7):
            share_gain(n).wait()
        total = gain_all[0]
        for n in range(1, 8):
            total = total + gain_all[n]
        gain_out[...] = total
    else:
        gain_out[...] = gain_part[...]
    for fold in (fold_o, fold_k, fold_v, fold_q) + tuple(ends):
        fold.settle()
    fv_copy.wait()
    for copy in (far_to_mate, peer_back, near_to_mate):
        copy(seqs - 1).wait_send()

    for n in range(per_tile):
        saving_early(n).wait()

    @pl.loop(0, count)
    def _(i):
        @pl.when(is_block(i))
        def _():
            saving_block(i, block_of(i)).wait()

        @pl.when(jnp.logical_not(is_block(i)))
        def _():
            saving_token(i, token_of(i)).wait()


def back(split, quarters, tok, cot, sums, attn, late, gains, square, q, kv, ctx, lse, cosine, sine, prefix):
    seqs, rows, dim = tok.shape
    width = q.shape[2]
    heads = width // HEAD_DIM
    _, chunk, _ = sums.shape
    tokens = seqs * rows
    early = 256 // chunk
    count = 2 * tokens // chunk - early
    vmem = pl.BlockSpec(memory_space=pltpu.VMEM)
    anyw = pl.BlockSpec(memory_space=pl.ANY)
    dma = pltpu.SemaphoreType.DMA
    lines = pltpu.VMEM((count, chunk, dim), bf16)
    half_lines = pltpu.VMEM((tokens // chunk, chunk, dim), bf16)
    wide = pltpu.VMEM((heads // 2, 2 * rows, width), bf16)
    tall = pltpu.VMEM((heads // 2, width, 2 * rows), bf16)
    shape = jax.ShapeDtypeStruct
    fold_scratch, fold_outs = fold_shapes(
        [(width // 2, dim // 2)] + [(dim // 4, width)] * 3, split, (0, 1, 2, 3, 4))
    ends_scratch, ends_outs = fold_shapes([x.shape for x in quarters], True, (3, 4)) if split else ([], [])
    loaded = (tok, cot) + tuple(square) + (q, kv, ctx)
    held = [tok.shape, cot.shape[1:]] + [x.shape for x in square] + [q.shape, kv.shape[1:], ctx.shape]
    return pl.pallas_call(
        functools.partial(back_kernel, split),
        name="back",
        out_shape=[
            shape((seqs, rows, dim), bf16), shape((seqs, rows, dim), bf16), shape((tokens, width), bf16),
            shape((8, dim // 2) if split else (2, 8, dim // 2), f32)] + fold_outs + ends_outs,
        in_specs=[anyw] * (len(quarters) + 12) + [vmem] * 4 + [pl.BlockSpec(memory_space=pltpu.SMEM)],
        out_specs=[anyw, anyw, anyw, vmem] + [anyw] * (4 + len(quarters)),
        scratch_shapes=[pltpu.VMEM(x, bf16) for x in held] + [
            half_lines, pltpu.VMEM((rows // chunk, chunk, dim), bf16), pltpu.VMEM((early, chunk, dim), bf16),
            pltpu.VMEM((seqs, rows, dim), f32),
            pltpu.VMEM((width, dim), f32),
            tall, wide, tall, wide,
            pltpu.VMEM((width, rows), bf16),
            pltpu.VMEM((heads // 2, 1, 2 * rows), f32),
            pltpu.VMEM((width, rows), f32),
            pltpu.VMEM((rows, width), f32),
            pltpu.VMEM((rows, width), f32),
            pltpu.VMEM((3, 2, rows, width), bf16),
            pltpu.VMEM((seqs, 3, 2, rows, width), bf16),
            pltpu.VMEM((3, tokens, width), bf16),
            pltpu.VMEM((dim, tokens), bf16),
            lines, lines, lines,
            pltpu.VMEM((2, 8, dim // 2), f32),
            pltpu.VMEM((8, 8, dim // 2), f32),
            dma((3,)), dma((seqs, 3)),
            dma((count,)), dma((count,)), dma((count,)), dma((count,)), dma((count + early,)),
            dma((7,)), dma((7,)), dma((8 * seqs + 11,)), dma(()),
        ] + ends_scratch + fold_scratch,
        compiler_params=limits(2, 62),
        cost_estimate=pl.CostEstimate(flops=30 * 10**9, bytes_accessed=10**7, transcendentals=10**7),
    )(*quarters, late, sums, attn, *loaded, gains, lse, cosine, sine, prefix)


def finish_kernel(parts, *refs):
    n = len(parts)
    sources, gain_in, refs = refs[:n], refs[n], refs[n + 1 :]
    targets, gain_one, gain_two, refs = refs[:n], refs[n], refs[n + 1], refs[n + 2 :]
    held, wide, (loads, saves) = refs[:n], refs[n : 2 * n], refs[2 * n :]
    loading, saving = [], []
    for k, count in enumerate(parts):
        size = sources[k].shape[0] // count
        for piece in range(count):
            at = slice(piece * size, (piece + 1) * size)
            place = len(loading)
            loading.append(pltpu.make_async_copy(sources[k].at[at], held[k].at[at], loads.at[place]))
            plain = sources[k].dtype == targets[k].dtype
            saving.append((k, at, plain, pltpu.make_async_copy(
                (held if plain else wide)[k].at[at], targets[k].at[at], saves.at[place])))
    for load in loading:
        load.start()
    gain_one[...] = gain_in[0:1, :]
    gain_two[...] = gain_in[1:2, :]
    for load, (k, at, plain, save) in zip(loading, saving):
        load.wait()
        if not plain:
            wide[k][at] = held[k][at].astype(f32)
        save.start()
    for *_, save in saving:
        save.wait()


def finish(arrays, types, gain_rows):
    parts = [x.shape[0] if x.size > 300000 else 1 for x in arrays]
    vmem = pl.BlockSpec(memory_space=pltpu.VMEM)
    anyw = pl.BlockSpec(memory_space=pl.ANY)
    dma = pltpu.SemaphoreType.DMA
    shape = jax.ShapeDtypeStruct
    row = shape((1, gain_rows.shape[1]), f32)
    return pl.pallas_call(
        functools.partial(finish_kernel, parts),
        name="finish",
        out_shape=[shape(x.shape, t) for x, t in zip(arrays, types)] + [row, row],
        in_specs=[anyw] * len(arrays) + [vmem],
        out_specs=[anyw] * len(arrays) + [vmem, vmem],
        scratch_shapes=[pltpu.VMEM(x.shape, x.dtype) for x in arrays] + [
            pltpu.VMEM((8, 128) if x.dtype == t else x.shape, f32) for x, t in zip(arrays, types)] + [
            dma((sum(parts),)), dma((sum(parts),))],
        compiler_params=pltpu.CompilerParams(vmem_limit_bytes=60 * 1024 * 1024),
        cost_estimate=pl.CostEstimate(flops=10**6, bytes_accessed=25 * 10**6, transcendentals=0),
    )(*arrays, gain_rows)


def halves(weight):
    rows, columns = weight.shape
    return jnp.swapaxes(weight.reshape(rows, 2, columns // 2), 0, 1)


def shards(
    tokens, first_values, norm1_gain, norm2_gain, w_query, w_key, w_value, w_out, w_gate, w_up, w_down,
    prefix, cotangent,
):
    split = lax.axis_size("fsdp") == 2
    seqs, rows, dim = tokens.shape
    width, units = w_query.shape[1], w_gate.shape[1]
    gather = functools.partial(lax.all_gather, axis_name="fsdp", tiled=True)
    if split:
        gains = (norm1_gain, norm2_gain)
        square = (w_query, w_key, w_value, w_out)
        wide = (w_gate.T, w_up.T, w_down)
    else:
        gains = (gather(norm1_gain), gather(norm2_gain))
        square = (gather(w_query), gather(w_key), gather(w_value), halves(gather(w_out, axis=1)))
        wide = (halves(gather(w_gate).T), halves(gather(w_up).T), halves(gather(w_down, axis=1)))
    (sums, late, query, pairs, attn, context, log_total, gain_rows, cosine, sine, down_grad, gate_grad, up_grad,
     *gathered) = front(
        split, tokens, first_values, cotangent, [gain.reshape(-1, 128) for gain in gains], square, wide, prefix)
    if split:
        square = tuple(gathered)
    wide_grads = (down_grad, gate_grad, up_grad)
    block_out, token_grad, half_value_grad, gain_grads, out_grad, key_grad, value_grad, query_grad, *ends = back(
        split, wide_grads if split else (), tokens, cotangent, sums, attn, late, gain_rows, square, query, pairs,
        context.reshape(query.shape), log_total, cosine, sine, prefix)
    half_value_grad = half_value_grad.reshape(seqs, rows, width)
    if split:
        cut = lambda x: x.reshape(8, -1, dim)
        arrays = (cut(token_grad), cut(block_out), half_value_grad, query_grad, key_grad, value_grad, out_grad, *ends)
        (token_grad, block_out, half_value_grad, query_grad, key_grad, value_grad, out_grad, down_grad, gate_grad,
         up_grad, gain_one_grad, gain_two_grad) = finish(arrays, (f32, bf16) + (f32,) * 8, gain_grads)
        token_grad, block_out = token_grad.reshape(tokens.shape), block_out.reshape(tokens.shape)
        over_rows = lambda grad: grad.reshape(-1, grad.shape[-1])
        over_columns = over_rows
        over_turned = lambda grad: over_rows(grad).T
        gain_one_grad, gain_two_grad = gain_one_grad[0], gain_two_grad[0]
    else:
        half_value_grad, token_grad = half_value_grad.astype(f32), token_grad.astype(f32)
        total = lambda grad, axis: lax.psum(
            lax.psum_scatter(grad, "fsdp", scatter_dimension=axis, tiled=True), "ctx").astype(f32)
        over_rows = lambda grad: total(jnp.swapaxes(grad, 0, 1).reshape(-1, grad.shape[-1]), 0)
        over_columns = lambda grad: total(
            jnp.transpose(grad, (0, 2, 1, 3)).reshape(2 * grad.shape[2], -1), 1)
        over_turned = lambda grad: over_columns(grad).T
        gain_one_grad, gain_two_grad = (total(gain_grads[:, n].reshape(-1), 0) for n in range(2))
    return (
        block_out,
        token_grad,
        half_value_grad,
        gain_one_grad,
        gain_two_grad,
        over_rows(query_grad),
        over_rows(key_grad),
        over_rows(value_grad),
        over_columns(out_grad),
        over_turned(gate_grad),
        over_turned(up_grad),
        over_columns(down_grad),
    )


def solution(mesh):
    return jax.shard_map(
        shards,
        mesh=mesh,
        in_specs=(
            P("fsdp", "ctx", None),
            P("fsdp", "ctx", "tp"),
            P("fsdp"),
            P("fsdp"),
            P("fsdp", "tp"),
            P("fsdp", "tp"),
            P("fsdp", "tp"),
            P("tp", "fsdp"),
            P("fsdp", "tp"),
            P("fsdp", "tp"),
            P("tp", "fsdp"),
            P("fsdp"),
            P("fsdp", "ctx", None),
        ),
        out_specs=(
            P("fsdp", "ctx", None),
            P("fsdp", "ctx", None),
            P("fsdp", "ctx", "tp"),
            P("fsdp"),
            P("fsdp"),
            P("fsdp", "tp"),
            P("fsdp", "tp"),
            P("fsdp", "tp"),
            P("tp", "fsdp"),
            P("fsdp", "tp"),
            P("fsdp", "tp"),
            P("tp", "fsdp"),
        ),
        check_vma=False,
    )
```

```python
import functools

import jax
import jax.numpy as jnp
from jax import lax
from jax.experimental import pallas as pl
from jax.experimental.pallas import tpu as pltpu
from jax.sharding import PartitionSpec as P

HEAD_DIM = 64
epsilon = 1e-06
rope_base = 10000.0
masked_score = -1e30
MESH = pl.DeviceIdType.MESH
bf16 = jnp.bfloat16
f32 = jnp.float32


def dot(a, b):
    return jnp.dot(a, b, preferred_element_type=f32)


def dot_nt(a, b):
    return lax.dot_general(a, b, (((1,), (1,)), ((), ())), preferred_element_type=f32)


def unit_norm(values):
    return values * lax.rsqrt(jnp.mean(values * values, axis=-1, keepdims=True) + epsilon)


def low_half(shape):
    return lax.rem(lax.broadcasted_iota(jnp.int32, shape, 1), HEAD_DIM) < HEAD_DIM // 2


class Sum:
    lag = 2

    def __init__(self, place, part, inward, across, sems, done):
        self.pair = near(place)
        self.middle = 3 - place
        self.inner = (place == 1) | (place == 2)
        self.outer = (place == 0) | (place == 3)
        self.part, self.inward, self.across, self.done = part, inward, across, done
        self.send_one, self.recv_one, self.send_two, self.recv_two = sems

    def copy_in(self, i):
        return remote(
            self.part.at[i], self.inward.at[i], self.send_one.at[i], self.recv_one.at[i], {"tp": self.pair})

    def copy_across(self, i):
        return remote(
            self.part.at[i], self.across.at[i], self.send_two.at[i], self.recv_two.at[i], {"tp": self.middle})

    def copy_out(self, i):
        return remote(
            self.part.at[i], self.inward.at[i], self.send_one.at[i], self.recv_one.at[i], {"tp": self.pair})

    def fill(self, first, piece, values):
        chunk, size = self.part.shape[1], values.shape[1]
        for k in range(values.shape[0] // chunk):
            self.part[first + k, :, piece * size : (piece + 1) * size] = values[
                k * chunk : (k + 1) * chunk].astype(bf16)

    def offer(self, first, count):
        @pl.when(self.outer)
        def _():
            @pl.loop(0, count)
            def _(k):
                self.copy_in(first + k).start()

    def take_in(self, i):
        self.copy_in(i).wait_recv()
        self.part[i] = (self.part[i].astype(f32) + self.inward[i].astype(f32)).astype(bf16)
        self.copy_across(i).start()

    def finish(self, i):
        self.copy_across(i).wait()
        self.part[i] = (self.part[i].astype(f32) + self.across[i].astype(f32)).astype(bf16)
        self.copy_out(i).start()
        self.done(i)

    def steps(self, first, count):
        @pl.when(self.inner)
        def _():
            @pl.loop(first, first + count)
            def _(i):
                self.take_in(i)

                @pl.when(i >= self.lag)
                def _():
                    self.finish(i - self.lag)

    def settled(self, first, count):
        @pl.when(self.outer)
        def _():
            @pl.loop(first, first + count)
            def _(i):
                self.copy_out(i).wait_recv()
                self.copy_in(i).wait_send()
                self.part[i] = self.inward[i]
                self.done(i)

    def close(self, count):
        @pl.when(self.inner)
        def _():
            for n in range(self.lag):
                self.finish(count - self.lag + n)

            @pl.loop(0, count)
            def _(i):
                self.copy_out(i).wait_send()


def near(place):
    return place + 1 - 2 * lax.rem(place, 2)


def greet(peers):
    barrier = pltpu.get_barrier_semaphore()
    for peer in peers:
        pl.semaphore_signal(barrier, inc=1, device_id=peer, device_id_type=MESH)
    pl.semaphore_wait(barrier, len(peers))


def block_place(ring, j):
    return jnp.where(
        j == 0, ring, jnp.where(j == 1, near(ring), jnp.where(j == 2, lax.rem(ring + 2, 4), 3 - ring)))


def line_peers(place):
    return [{"tp": near(place)}, {"tp": 3 - place}]


def ring_peers(ring):
    return [{"ctx": near(ring)}, {"ctx": lax.rem(ring + 2, 4)}]


def remote(source, target, send, recv, device):
    return pltpu.make_async_remote_copy(
        src_ref=source, dst_ref=target, send_sem=send, recv_sem=recv,
        device_id=device, device_id_type=MESH)


class Passing:
    def __init__(self, place, spot, sems, own=None):
        self.place, self.spot, self.own = place, spot, own
        self.send, self.recv = sems

    def move(self, piece, item, way, source=None):
        here = self.spot(piece, item)
        return remote(
            here if source is None else source, here, self.send.at[item, way, piece], self.recv.at[item, piece],
            {"tp": self.place + 1 - 2 * way})

    def begin(self, item):
        source = None if self.own is None else self.own(item)

        @pl.when(self.place < 3)
        def _():
            self.move(self.place, item, 0, source).start()

        @pl.when(self.place > 0)
        def _():
            self.move(self.place, item, 1, source).start()

    def step(self, item, distance):
        @pl.when(self.place >= distance)
        def _():
            piece = self.place - distance
            self.move(piece, item, 0).wait_recv()

            @pl.when(self.place < 3)
            def _():
                self.move(piece, item, 0).start()

        @pl.when(self.place + distance <= 3)
        def _():
            piece = self.place + distance
            self.move(piece, item, 1).wait_recv()

            @pl.when(self.place > 0)
            def _():
                self.move(piece, item, 1).start()

    def settle(self, items):
        for item in range(items):
            @pl.loop(0, 4)
            def _(piece, item=item):
                @pl.when((self.place < 3) & (piece <= self.place))
                def _():
                    self.move(piece, item, 0).wait_send()

                @pl.when((self.place > 0) & (piece >= self.place))
                def _():
                    self.move(piece, item, 1).wait_send()


def rows_at(start, size):
    return pl.ds(pl.multiple_of(start, size), size)


class Fold:
    def __init__(self, side, ring, refs, sems, saved):
        self.side, self.half = side, lax.rem(ring, 2)
        self.grad, self.one, self.two, self.three, self.final = refs
        self.send, self.recv, self.save = sems
        self.mate, self.peer, self.other = (
            {"ctx": near(ring)}, {"ctx": lax.rem(ring + 2, 4)}, {"fsdp": 1 - side})
        self.saved = saved
        self.began = set()

    def mine(self):
        return self.grad if self.one is None else self.grad.at[self.half, self.side]

    def copy(self, n):
        source, target, device = (
            lambda: (self.grad.at[1 - self.half], self.one, self.mate),
            lambda: (self.grad.at[self.half, 1 - self.side], self.two, self.other),
            lambda: (self.mine(), self.three, self.peer),
            lambda: (self.final.at[self.half], self.final.at[self.half], self.mate),
        )[n]()
        return remote(source, target, self.send.at[n], self.recv.at[n], device)

    def begin(self, n):
        self.began.add(n)
        self.copy(n).start()

    def first(self):
        self.begin(0)

    def second(self):
        self.copy(0).wait_recv()
        for side in range(2):
            self.grad[self.half, side] = (
                self.grad[self.half, side].astype(f32) + self.one[side].astype(f32)).astype(bf16)
        self.begin(1)

    def join(self):
        self.copy(1).wait_recv()
        mine = self.mine()
        mine[...] = (mine[...].astype(f32) + self.two[...].astype(f32)).astype(bf16)

    def quarter(self):
        self.join()
        self.saving().start()

    def resume(self):
        self.begin(2)

    def third(self):
        self.join()
        self.resume()

    def fourth(self):
        self.copy(2).wait_recv()
        self.final[self.half] = (self.mine()[...].astype(f32) + self.three[...].astype(f32)).astype(bf16)
        self.begin(3)

    def saving(self):
        return pltpu.make_async_copy(self.mine() if self.final is None else self.final, self.saved, self.save)

    def last(self):
        self.copy(3).wait_recv()
        self.saving().start()

    def settle(self):
        for n in sorted(self.began):
            self.copy(n).wait_send()
        self.saving().wait()


class Whole:
    def __init__(self, grad, sems, saved):
        self.copy = lambda: pltpu.make_async_copy(grad, saved, sems[2])

    def first(self):
        self.copy().start()

    def second(self):
        pass

    third = fourth = last = quarter = second

    def settle(self):
        self.copy().wait()


def fold_shapes(shapes, split, kinds):
    scratch = []
    for r, c in shapes:
        sizes = ((2, 2, r, c), (2, r, c), (r, c), (r, c), (2, r, c))
        if not split:
            kinds = (0,)
        elif 0 not in kinds:
            scratch.append(pltpu.VMEM((r, c), bf16))
        scratch += [pltpu.VMEM(sizes[kind], bf16) for kind in kinds]
    n = len(shapes)
    dma = pltpu.SemaphoreType.DMA
    scratch += [dma((n, 4)), dma((n, 4)), dma((n,))]
    ends = (2, 2) if not split else (2,) if 4 in kinds else ()
    return scratch, [jax.ShapeDtypeStruct(ends + (r, c), bf16) for r, c in shapes]


def make_folds(split, side, ring, scratch, saved, kinds):
    send, recv, save = scratch[-3:]
    folds, grads = [], []
    per = 1 if not split else len(kinds) + (0 not in kinds)
    for n, target in enumerate(saved):
        own = list(scratch[n * per : (n + 1) * per])
        sems = (send.at[n], recv.at[n], save.at[n])
        grads.append(own[0])
        if split:
            held = dict(zip(kinds if 0 in kinds else (0,) + kinds, own))
            folds.append(Fold(side, ring, [held.get(kind) for kind in range(5)], sems, target))
        else:
            folds.append(Whole(own[0], sems, target))
    return folds, grads


def turn(values, cosine, sine, sign=1.0):
    pieces = []
    half = HEAD_DIM // 2
    sine = sine * sign
    for at in range(0, values.shape[1], 128):
        piece = values[:, at : at + 128]
        swapped = jnp.where(
            low_half(piece.shape), pltpu.roll(piece, 128 - half, 1), pltpu.roll(piece, half, 1))
        pieces.append(piece * cosine + swapped * sine)
    return jnp.concatenate(pieces, axis=1)


def spread(target, values_t, start, rows):
    owner = lax.broadcasted_iota(jnp.int32, values_t.shape, 0) // HEAD_DIM
    for h in range(values_t.shape[0] // HEAD_DIM):
        target[h // 2, :, rows_at(h % 2 * rows + start, values_t.shape[1])] = jnp.where(
            owner == h, values_t, 0.0).astype(bf16)


def flat_row(folded):
    return jnp.concatenate([folded[n : n + 1, :].astype(f32) for n in range(folded.shape[0])], axis=1)


def gain_row(gains, which):
    return jnp.concatenate([gains[0, which : which + 1, :], gains[1, which : which + 1, :]], axis=1)


def front_kernel(split, *refs):
    place, ring, side = lax.axis_index("tp"), lax.axis_index("ctx"), lax.axis_index("fsdp")
    (tok, fv, cot_hbm, g1, g2, wq_in, wk_in, wv_in, wo_in, wg_in, wu_in, wd_in), refs = refs[:12], refs[12:]
    (prefix, sum_hbm, late_hbm, q_out, kv_hbm, attn_hbm, ctx_hbm, lse_out, gains, cosine, sine), refs = (
        refs[:11], refs[11:])
    saved, refs = refs[:3], refs[3:]
    if split:
        (wq_hbm, wk_hbm, wv_hbm, wo_hbm), refs = refs[:4], refs[4:]
        (wq, wk, wv, w_send, w_recv, w_save, g_sems, o_send, o_recv), refs = refs[:9], refs[9:]
    else:
        wq, wk, wv = wq_in, wk_in, wv_in
    (normed_s, kv, qtm, vt, acct, maxes, totals, part, inward, across,
     kv_send, kv_recv, kv_save, send_one, recv_one, send_two, recv_two, save,
     wg, wu, wd, loads, cot, inner_t, gg_t, ug_t, late, late_save, wo_all, ctx_all, attn,
     p_send, p_recv, c_send, c_recv, c_save, a_save), refs = refs[:37], refs[37:]
    (fold_d, fold_g, fold_u), grads = make_folds(split, side, ring, refs, saved, (0, 1, 2))
    seqs, rows, width = q_out.shape
    heads = width // HEAD_DIM
    tile = 256
    chunk, dim = part.shape[1:]
    per_seq = rows // chunk
    per_tile = tile // chunk
    middle = dim // 2
    units = wg_in.shape[-2]
    mate, peer = ring_peers(ring)
    half = lax.rem(ring, 2)
    for full in (wg, wu, wd):
        for piece in range(2):
            full[piece, units:] = jnp.zeros((full.shape[1] - units, full.shape[2]), bf16)
    own_loads = [pltpu.make_async_copy(cot_hbm, cot, loads.at[6])]
    for n, (source, full) in enumerate(((wg_in, wg), (wu_in, wu), (wd_in, wd))):
        if split:
            own_loads.append(pltpu.make_async_copy(source, full.at[side, 0:units], loads.at[n]))
        else:
            for piece in range(2):
                own_loads.append(pltpu.make_async_copy(
                    source.at[piece], full.at[piece, 0:units], loads.at[2 * n + piece]))
    greet(line_peers(place) + ring_peers(ring) + ([{"fsdp": 1 - side}] if split else []))

    if split:
        other = {"fsdp": 1 - side}
        for n, gain in enumerate((g1, g2)):
            gains[side, n : n + 1, :] = flat_row(gain)
        move_gains = remote(gains.at[side], gains.at[side], g_sems.at[0], g_sems.at[1], other)
        move_gains.start()

        def spot(full, owner, part_at, size):
            if full is wo_all:
                return full.at[place, owner, rows_at(part_at * size, size)]
            if full.shape[0] == 2:
                return full.at[owner, rows_at(part_at * size, size)]
            return full.at[rows_at((2 * owner + part_at) * size, size)]

        table = (
            (wk_in, wk, spot), (wv_in, wv, spot), (wq_in, wq, spot), (wo_in, wo_all, spot),
            (wg_in, wg, spot), (wu_in, wu, spot), (wd_in, wd, spot))

        def cross(n):
            own, full, where = table[n]
            size = own.shape[0] // 2
            return remote(own.at[rows_at(half * size, size)], where(full, side, half, size),
                          w_send.at[n, 0], w_recv.at[n, 0], other)

        def onto_mate(n):
            own, full, where = table[n]
            here = where(full, 1 - side, half, own.shape[0] // 2)
            return remote(here, here, w_send.at[n, 1], w_recv.at[n, 1], mate)

        def hand_on(n):
            cross(n).wait_recv()
            onto_mate(n).start()

        saves = tuple(
            pltpu.make_async_copy(full, target, w_save.at[n])
            for n, (full, target) in enumerate(((wk, wk_hbm), (wv, wv_hbm), (wq, wq_hbm), (wo_all.at[place], wo_hbm))))
        for n in range(3):
            cross(n).start()
        for own, full, _ in table[:3]:
            full[rows_at(side * own.shape[0], own.shape[0]), :] = own[...]
        wo_all[place, side] = wo_in[...]
        part_o = wo_in.shape[0] // 2
        item_side = lambda item: side if item == 0 else 1 - side
        pass_o = Passing(
            place, lambda piece, item: wo_all.at[piece, item_side(item), rows_at(half * part_o, part_o)],
            (p_send, p_recv),
            lambda item: wo_in.at[rows_at(half * part_o, part_o)] if item == 0 else None)
        pass_o.begin(0)

        def share_o(n):
            here = wo_all.at[lax.rem(place + n + 1, 4), :, rows_at(half * part_o, part_o)]
            return remote(here, here, o_send.at[n], o_recv.at[n], mate)
        remote(gains.at[side], gains.at[side], g_sems.at[0], g_sems.at[1], other).wait()
    else:
        size = gains.shape[2]
        for piece in range(2):
            for n, gain in enumerate((g1, g2)):
                gains[piece, n : n + 1, :] = flat_row(gain)[:, piece * size : (piece + 1) * size]
        wo_all[place] = wo_in[...]
        pass_o = Passing(place, lambda piece, item: wo_all.at[piece, item], (p_send, p_recv))
        pass_o.begin(0)
        pass_o.begin(1)

    for load in own_loads:
        load.start()

    def pass_block(s, which, source, target, device, slot):
        return remote(
            kv.at[s, source, which], kv.at[s, target, which], kv_send.at[s, which, slot],
            kv_recv.at[s, which, target], device)

    to_mate = lambda s, which: pass_block(s, which, 0, 1, mate, 0)
    to_peer = lambda s, which: pass_block(s, which, 0, 2, peer, 1)
    onward = lambda s, which: pass_block(s, which, 2, 3, mate, 2)
    gain_one = gain_row(gains, 0)
    fine = 16
    coarse_at = (ring * rows + fine * lax.broadcasted_iota(jnp.int32, (rows // fine, 128), 0)).astype(f32)
    fine_at = lax.broadcasted_iota(jnp.int32, (fine, 128), 0).astype(f32)
    step = lax.rem(lax.broadcasted_iota(jnp.int32, (1, 128), 1), HEAD_DIM // 2)
    frequency = jnp.ones((1, 128), f32)
    for bit in range(5):
        ratio = rope_base ** (-(2**bit) / (HEAD_DIM // 2))
        frequency = frequency * jnp.where(lax.rem(step // 2**bit, 2) == 1, ratio, 1.0)
    turns = [at * frequency for at in (coarse_at, fine_at)]
    (cos_a, sin_a), (cos_b, sin_b) = ((jnp.cos(x), jnp.sin(x)) for x in turns)
    cos_a, sin_a = cos_a[:, None, :], sin_a[:, None, :]
    cos_b, sin_b = cos_b[None], sin_b[None]
    cosine[...] = (cos_a * cos_b - sin_a * sin_b).reshape(rows, 128)
    sine[...] = (sin_a * cos_b + cos_a * sin_b).reshape(rows, 128) * jnp.where(
        low_half((rows, 128)), -1.0, 1.0)

    per_seq_tiles = rows // tile
    tiles = seqs * per_seq_tiles

    def tile_at(t):
        return t // per_seq_tiles, rows_at(lax.rem(t, per_seq_tiles) * tile, tile)

    @pl.loop(0, tiles)
    def _(t):
        s, at = tile_at(t)
        normed_s[s, at, :] = (unit_norm(tok[s, at, :].astype(f32)) * gain_one).astype(bf16)

    def keys(s):
        @pl.loop(0, per_seq_tiles)
        def _(t):
            at = rows_at(t * tile, tile)
            k = dot(normed_s[s, at, :], wk[...])
            kv[s, 0, 0, at, :] = turn(k, cosine[at, :], sine[at, :]).astype(bf16)

        to_peer(s, 0).start()
        to_mate(s, 0).start()

    def values(s):
        @pl.loop(0, per_seq_tiles)
        def _(t):
            at = rows_at(t * tile, tile)
            v = dot(normed_s[s, at, :], wv[...])
            kv[s, 0, 1, at, :] = (0.5 * v + 0.5 * fv[s, at, :].astype(f32)).astype(bf16)

        to_peer(s, 1).start()
        to_mate(s, 1).start()

    if split:
        hand_on(0)
        onto_mate(0).wait_recv()
    keys(0)
    if split:
        hand_on(1)
        cross(3).start()
        onto_mate(1).wait_recv()
    values(0)
    if split:
        hand_on(2)
    for s in range(1, seqs):
        keys(s)
        values(s)
    if split:
        onto_mate(2).wait_recv()

    @pl.loop(0, tiles)
    def _(t):
        s, at = tile_at(t)
        q = dot(normed_s[s, at, :], wq[...])
        q = turn(q, cosine[at, :], sine[at, :]) * HEAD_DIM ** (-0.5)
        q_out[s, at, :] = q.astype(bf16)
        spread(qtm.at[s], jnp.transpose(q), lax.rem(t, per_seq_tiles) * tile, rows)

    pass_o.step(0, 1)
    if split:
        hand_on(3)
        pass_o.begin(1)
        for n in range(4, 7):
            cross(n).start()

    def saving(i):
        return pltpu.make_async_copy(part.at[i], sum_hbm.at[i], save.at[i])

    sums = Sum(
        place, part, inward, across, (send_one, recv_one, send_two, recv_two), lambda i: saving(i).start())
    passing = Passing(place, lambda piece, item: ctx_all.at[piece, item], (c_send, c_recv))

    def saving_context(s):
        mine = pl.ds(s * per_seq_tiles, per_seq_tiles)
        return pltpu.make_async_copy(ctx_all.at[place, mine], ctx_hbm.at[mine], c_save.at[s])

    def saving_kv(s):
        return pltpu.make_async_copy(kv.at[s], kv_hbm.at[s], kv_save.at[s])

    @pl.loop(0, seqs)
    def _(s):
        maxes[...] = jnp.full_like(maxes, masked_score)
        totals[...] = jnp.zeros_like(totals)
        acct[...] = jnp.zeros_like(acct)

        @pl.loop(0, 4)
        def _(j):
            @pl.when(j == 1)
            def _():
                for which in range(2):
                    to_mate(s, which).wait_recv()

                @pl.when(s > 0)
                def _():
                    pass_o.step(1, 2)

            @pl.when(j == 2)
            def _():
                for which in range(2):
                    to_peer(s, which).wait_recv()
                    onward(s, which).start()

                @pl.when(s == 0)
                def _():
                    pass_o.step(0, 2)
                    pass_o.step(1, 1)

            @pl.when(j == 3)
            def _():
                for which in range(2):
                    onward(s, which).wait_recv()

                @pl.when(s > 0)
                def _():
                    pass_o.step(0, 3)
                    pass_o.step(1, 3)
                    if split:
                        for n in range(3):
                            share_o(n).start()
                        hand_on(6)

            vt[...] = jnp.transpose(kv[s, j, 1])
            key_pos = block_place(ring, j) * rows + lax.broadcasted_iota(jnp.int32, (rows, 1), 0)
            query_pos = ring * rows + lax.rem(lax.broadcasted_iota(jnp.int32, (1, 2 * rows), 1), rows)
            limit = jnp.maximum(query_pos + 1, prefix[s])

            @pl.loop(0, heads // 2)
            def _(h):
                scores = jnp.where(key_pos < limit, dot(kv[s, j, 0], qtm[s, h]), masked_score)
                old = maxes[h]
                new = jnp.maximum(old, jnp.max(scores, axis=0, keepdims=True))
                weights = jnp.exp(scores - new)
                fade = jnp.exp(old - new)
                maxes[h] = new
                totals[h] = totals[h] * fade + jnp.sum(weights, axis=0, keepdims=True)
                low = weights.astype(bf16)
                for n in range(2):
                    of_head = rows_at((2 * h + n) * HEAD_DIM, HEAD_DIM)
                    lanes = slice(n * rows, (n + 1) * rows)
                    acct[of_head, :] = acct[of_head, :] * fade[:, lanes] + dot(vt[of_head, :], low[:, lanes])
                at_step = j * (heads // 2) + h

                n = jnp.where(at_step == 7, 3, at_step // 2 - 1)

                @pl.when((s > 0) & (at_step > 1) & ((at_step == 7) | (lax.rem(at_step, 2) == 0)))
                def _():
                    passing.step((s - 1) * per_seq_tiles + lax.rem(n, per_seq_tiles), 1 + n // per_seq_tiles)

        for h in range(heads):
            if h % 2 == 0:
                lse_out[s, h // 2 : h // 2 + 1, :] = maxes[h // 2] + jnp.log(totals[h // 2])
            of_head = slice(h * HEAD_DIM, (h + 1) * HEAD_DIM)
            acct[of_head, :] = acct[of_head, :] / totals[h // 2][:, h % 2 * rows : (h % 2 + 1) * rows]
        for t in range(per_seq_tiles):
            ctx_all[place, s * per_seq_tiles + t] = jnp.transpose(acct[:, t * tile : (t + 1) * tile]).astype(bf16)
            passing.begin(s * per_seq_tiles + t)
        saving_context(s).start()
        saving_kv(s).start()

        @pl.when(s == 0)
        def _():
            if split:
                onto_mate(3).wait_recv()
                for copy in saves:
                    copy.start()
                hand_on(4)
                hand_on(5)

    if split:
        for n in range(3):
            share_o(n).wait_recv()
    if split:
        for n in range(4, 7):
            onto_mate(n).wait_recv()
    for load in own_loads:
        load.wait()
    lines = seqs * per_seq
    early = lines
    count = part.shape[0]
    gain_two = gain_row(gains, 1)

    def saving_attn(t):
        mine = pl.ds(t * per_tile, per_tile)
        return pltpu.make_async_copy(attn.at[mine], attn_hbm.at[mine], a_save.at[t])

    def across_both(left, full):
        return dot_nt(left[:, :middle], full[0]) + dot_nt(left[:, middle:], full[1])

    def saving_late(t):
        mine = pl.ds((t - 1) * per_tile, per_tile)
        return pltpu.make_async_copy(late.at[mine], late_hbm.at[mine], late_save.at[t - 1])

    stepped = [0]

    def act(*plan):
        for what in plan:
            if what == "sum":
                sums.steps(stepped[0], 1)
                stepped[0] += 1
            else:
                passing.step(*what)

    plans = {
        (0, 0): [(0, 3)], (0, 1): [(1, 3)], (0, 2): [(2, 1)], (0, 3): [],
        (1, 0): [], (1, 1): [(3, 1)], (1, 2): [], (1, 3): ["sum"],
        (2, 0): [(2, 2), "sum", (3, 2), "sum", (2, 3)], (2, 1): ["sum"], (2, 2): [], (2, 3): ["sum"],
        (3, 0): [(3, 3)], (3, 1): ["sum"], (3, 2): ["sum"], (3, 3): ["sum"],
    }
    for t in range(tiles):
        s, at = t // per_seq_tiles, slice(t % per_seq_tiles * tile, (t % per_seq_tiles + 1) * tile)
        flat = slice(t * tile, (t + 1) * tile)
        mine = t * per_tile
        act(*plans[t, 0])
        context = jnp.concatenate([ctx_all[p, t] for p in range(4)], axis=1)
        attended = [
            dot(context, jnp.concatenate([wo_all[p, piece] for p in range(4)], axis=0)) for piece in range(2)]
        for piece in range(2):
            for k in range(per_tile):
                attn[mine + k, :, piece * middle : (piece + 1) * middle] = attended[piece][
                    k * chunk : (k + 1) * chunk].astype(bf16)
        saving_attn(t).start()
        hidden = tok[s, at, :].astype(f32) + jnp.concatenate(attended, axis=1)
        normed = (unit_norm(hidden) * gain_two).astype(bf16)
        normed_s[s, at, :] = normed
        gate = across_both(normed, wg)
        up = across_both(normed, wu)
        sigmoid = jax.nn.sigmoid(gate)
        swish = gate * sigmoid
        inner = (swish * up).astype(bf16)
        inner_t[:, flat] = jnp.transpose(inner)
        inner_grad = across_both(cot[s, at, :], wd)
        gate_grad = (inner_grad * up * sigmoid * (1.0 + gate * (1.0 - sigmoid))).astype(bf16)
        up_grad = (inner_grad * swish).astype(bf16)
        act(*plans[t, 1])
        for piece in range(2):
            sums.fill(mine, piece, dot(gate_grad, wg[piece]) + dot(up_grad, wu[piece]))
        sums.offer(mine, per_tile)
        act(*plans[t, 2])
        feeds = [dot(inner, wd[piece]) for piece in range(2)]

        if t == 0:
            for piece in range(2):
                sums.fill(early, piece, feeds[piece])
        else:
            for piece in range(2):
                for k in range(per_tile):
                    late[mine - per_tile + k, :, piece * middle : (piece + 1) * middle] = feeds[piece][
                        k * chunk : (k + 1) * chunk].astype(bf16)
            saving_late(t).start()

        gg_t[:, flat] = jnp.transpose(gate_grad)
        ug_t[:, flat] = jnp.transpose(up_grad)
        act(*plans[t, 3])

    sums.offer(early, count - early)
    deep = units // 2

    def weight_grad(n, left_t, right):
        for h in range(2):
            for y in range(2):
                total = jnp.zeros((deep, middle), f32)
                for s in range(seqs):
                    total = total + dot(
                        left_t[h * deep : (h + 1) * deep, s * rows : (s + 1) * rows],
                        right[s, :, y * middle : (y + 1) * middle])
                grads[n][h, y] = total.astype(bf16)

    begun = stepped[0]
    weight_grad(0, inner_t, cot)
    fold_d.first()
    sums.steps(begun, 1)
    weight_grad(1, gg_t, normed_s)
    fold_g.first()
    fold_d.second()
    sums.steps(begun + 1, 1)
    weight_grad(2, ug_t, normed_s)
    fold_u.first()
    fold_g.second()
    sums.steps(begun + 2, 1)
    fold_u.second()
    sums.steps(begun + 3, 3)
    fold_d.quarter()
    sums.steps(begun + 6, 3)
    fold_g.quarter()
    sums.steps(begun + 9, count - begun - 9)
    fold_u.quarter()
    sums.settled(0, count)
    sums.close(count)
    for fold in (fold_d, fold_g, fold_u):
        fold.settle()
    for t in range(1, tiles):
        saving_late(t).wait()
    for s in range(seqs):
        for which in range(2):
            to_mate(s, which).wait_send()
            to_peer(s, which).wait_send()
            onward(s, which).wait_send()
        saving_kv(s).wait()
        saving_context(s).wait()
    for t in range(tiles):
        saving_attn(t).wait()
    pass_o.settle(2)
    passing.settle(tiles)

    @pl.loop(0, count)
    def _(i):
        saving(i).wait()

    if split:
        for n in range(7):
            cross(n).wait_send()
            onto_mate(n).wait_send()
        for n in range(3):
            share_o(n).wait_send()
        for copy in saves:
            copy.wait()


def limits(ident, megabytes=60):
    return pltpu.CompilerParams(
        collective_id=ident, has_side_effects=True, vmem_limit_bytes=megabytes * 1024 * 1024)


def front(split, tok, fv, cot, gains, square, wide, prefix):
    seqs, rows, dim = tok.shape
    width, units = square[0].shape[1], wide[0].shape[-2]
    heads = width // HEAD_DIM
    chunk, tile = 64, 256
    tokens = seqs * rows
    count = tokens // chunk + tile // chunk
    after = (tokens - tile) // chunk
    padded = -(-units // 256) * 256
    vmem = pl.BlockSpec(memory_space=pltpu.VMEM)
    anyw = pl.BlockSpec(memory_space=pl.ANY)
    dma = pltpu.SemaphoreType.DMA
    lines = pltpu.VMEM((count, chunk, dim), bf16)
    shape = jax.ShapeDtypeStruct
    full = [(dim, width)] * 3 + [(2, width, dim // 2)]
    fold_scratch, fold_outs = fold_shapes([(units // 2, dim // 2)] * 3, split, (0, 1, 2))
    outs = [
        shape((count, chunk, dim), bf16), shape((after, chunk, dim), bf16), shape((seqs, rows, width), bf16),
        shape((seqs, 4, 2, rows, width), bf16), shape((tokens // chunk, chunk, dim), bf16),
        shape((tokens // tile, tile, width), bf16),
        shape((seqs, heads // 2, 2 * rows), f32), shape((2, 8, dim // 2), f32),
        shape((rows, 128), f32), shape((rows, 128), f32)] + fold_outs
    out_specs = [anyw, anyw, vmem, anyw, anyw, anyw, vmem, vmem, vmem, vmem] + [anyw] * 3
    scratch = []
    if split:
        outs += [shape(size, bf16) for size in full]
        out_specs += [anyw] * 4
        scratch = [pltpu.VMEM(size, bf16) for size in full[:3]] + [
            dma((7, 2)), dma((7, 2)), dma((4,)), dma((2,)), dma((3,)), dma((3,))]
    scratch += [
        pltpu.VMEM((seqs, rows, dim), bf16),
        pltpu.VMEM((seqs, 4, 2, rows, width), bf16),
        pltpu.VMEM((seqs, heads // 2, width, 2 * rows), bf16),
        pltpu.VMEM((width, rows), bf16),
        pltpu.VMEM((width, rows), f32),
        pltpu.VMEM((heads // 2, 1, 2 * rows), f32),
        pltpu.VMEM((heads // 2, 1, 2 * rows), f32),
        lines, lines, lines,
        dma((seqs, 2, 3)), dma((seqs, 2, 4)), dma((seqs,)),
        dma((count,)), dma((count,)), dma((count,)), dma((count,)), dma((count,)),
        pltpu.VMEM((2, padded, dim // 2), bf16),
        pltpu.VMEM((2, padded, dim // 2), bf16),
        pltpu.VMEM((2, padded, dim // 2), bf16),
        dma((7,)),
        pltpu.VMEM((seqs, rows, dim), bf16),
        pltpu.VMEM((padded, tokens), bf16),
        pltpu.VMEM((padded, tokens), bf16),
        pltpu.VMEM((padded, tokens), bf16),
        pltpu.VMEM((after, chunk, dim), bf16),
        dma((tokens // tile,)),
        pltpu.VMEM((4, 2, width, dim // 2), bf16),
        pltpu.VMEM((4, tokens // tile, tile, width), bf16),
        pltpu.VMEM((tokens // chunk, chunk, dim), bf16),
        dma((2, 2, 4)), dma((2, 4)), dma((tokens // tile, 2, 4)), dma((tokens // tile, 4)),
        dma((seqs,)), dma((tokens // tile,)),
    ] + fold_scratch
    return pl.pallas_call(
        functools.partial(front_kernel, split),
        name="front",
        out_shape=outs,
        in_specs=[vmem] * 2 + [anyw] + [vmem] * 6 + [anyw] * 3 + [pl.BlockSpec(memory_space=pltpu.SMEM)],
        out_specs=out_specs,
        scratch_shapes=scratch,
        compiler_params=limits(0, 63),
        cost_estimate=pl.CostEstimate(flops=22 * 10**9, bytes_accessed=2 * 10**7, transcendentals=10**7),
    )(tok, fv, cot, *gains, *square, *wide, prefix)


def back_kernel(split, *refs):
    place, ring, side = lax.axis_index("tp"), lax.axis_index("ctx"), lax.axis_index("fsdp")
    quarters, refs = (refs[:3], refs[3:]) if split else ((), refs)
    loaded, refs = refs[:12], refs[12:]
    (gain_in, lse, cosine, sine, prefix, block_hbm, token_hbm, fv_hbm, gain_out), saved, refs = (
        refs[:9], refs[9:13], refs[13:])
    ends_saved, refs = (refs[:3], refs[3:]) if split else ((), refs)
    (tok, cot, wq, wk, wv, wo, q, kv, ctx, attn, mixed, early), refs = refs[:12], refs[12:]
    (hid, dwo_sum, qtm, qm, otm, om, kt, delta, dqt, dk, dv, give, take, proj, normed_t,
     part, inward, across, gain_part, gain_all,
     kv_send, kv_recv, send_one, recv_one, send_two, recv_two, save, gain_send, gain_recv, loads, fv_save), refs = (
        refs[:31], refs[31:])
    ends_scratch, refs = (refs[:12], refs[12:]) if split else ((), refs)
    (fold_o, fold_k, fold_v, fold_q), (dwo, dwk, dwv, dwq) = make_folds(split, side, ring, refs, saved, (0, 1, 2, 3, 4))
    ends, ends_mine = make_folds(split, side, ring, ends_scratch, ends_saved, (3, 4)) if split else ((), ())
    late_hbm, sum_hbm, attn_hbm, tok_hbm, cot_hbm, wq_hbm, wk_hbm, wv_hbm, wo_hbm, q_hbm, kv_hbm, ctx_hbm = loaded
    seqs, rows, dim = tok.shape
    width = wq.shape[1]
    heads = width // HEAD_DIM
    chunk = part.shape[1]
    per_seq = rows // chunk
    tile = 256
    per_tile = tile // chunk
    middle = dim // 2
    lines = seqs * per_seq
    count = 2 * lines - per_tile
    head_start = per_seq + 3
    rest = 2 * per_seq - per_tile - head_start
    rest_start = head_start + per_seq
    own_start = (head_start, rest_start + rest)
    mate, peer = ring_peers(ring)
    others = [(dy, dc) for dy in range(2) for dc in range(4) if dy or dc]
    group = [{"fsdp": lax.rem(side + dy, 2), "ctx": lax.rem(ring + dc, 4)} for dy, dc in others]

    copies = {}

    def load(name, source, target, start=True):
        copies[name] = pltpu.make_async_copy(source, target, loads.at[len(copies)])
        if start:
            copies[name].start()

    def ready(*names):
        for name in names:
            copies[name].wait()

    load("late", late_hbm.at[0:head_start], part.at[0:head_start])
    later = []
    for s in range(seqs):
        mine = slice(s * per_seq, (s + 1) * per_seq)
        for name, source, target in (
            ("tok", tok_hbm.at[s], tok.at[s]), ("attn", attn_hbm.at[mine], attn.at[mine]),
            ("cot", cot_hbm.at[s], cot), ("mixed", sum_hbm.at[mine], mixed),
            ("q", q_hbm.at[s], q.at[s]), ("ctx", ctx_hbm.at[s], ctx.at[s]), ("kv", kv_hbm.at[s], kv),
        ):
            now = s == 0 and name != "kv"
            load(f"{name}{s}", source, target, now)
            if not now and (s == 0 or name not in ("cot", "mixed", "kv")):
                later.append(f"{name}{s}")
        if s == 0:
            load("wo", wo_hbm, wo)
    for name, source, target in (
        [(f"quarter{n}", quarter, ends_mine[n]) for n, quarter in enumerate(quarters)] + [
            ("rest", late_hbm.at[head_start : head_start + rest], part.at[rest_start : rest_start + rest]),
            ("early", sum_hbm.at[lines : lines + per_tile], early),
            ("wq", wq_hbm, wq), ("wk", wk_hbm, wk), ("wv", wv_hbm, wv)]
    ):
        load(name, source, target, False)
        later.append(name)
    greet(line_peers(place) + (group if split else ring_peers(ring)))
    gain_one, gain_two = gain_row(gain_in, 0), gain_row(gain_in, 1)
    gain_part[...] = jnp.zeros_like(gain_part)

    def chunk_at(n):
        return n // per_seq, rows_at(lax.rem(n, per_seq) * chunk, chunk)

    def saving_block(i, n):
        s, own = chunk_at(n)
        return pltpu.make_async_copy(across.at[i], block_hbm.at[s, own], save.at[i])

    def saving_early(n):
        return pltpu.make_async_copy(early.at[n], block_hbm.at[0, n * chunk : (n + 1) * chunk], save.at[count + n])

    def saving_token(i, n):
        s, own = chunk_at(n)
        return pltpu.make_async_copy(across.at[i], token_hbm.at[s, own], save.at[i])

    def add_gain(which, value):
        for piece in range(2):
            gain_part[piece, which : which + 1, :] += value[:, piece * middle : (piece + 1) * middle]

    is_block = lambda i: (i < head_start) | ((i >= rest_start) & (i < own_start[1]))
    block_of = lambda i: per_tile + jnp.where(i < head_start, i, i - per_seq)
    token_of = lambda i: jnp.where(i < rest_start, i - head_start, i - own_start[1] + per_seq)

    def done(i):
        @pl.when(is_block(i))
        def _():
            n = block_of(i)
            s, own = chunk_at(n)
            across[i] = (
                tok[s, own, :].astype(f32) + attn[n].astype(f32) + part[i].astype(f32)).astype(bf16)
            saving_block(i, n).start()

        @pl.when(jnp.logical_not(is_block(i)))
        def _():
            n = token_of(i)
            s, own = chunk_at(n)
            values, upstream = tok[s, own, :].astype(f32), part[i].astype(f32)
            factor = lax.rsqrt(jnp.mean(values * values, axis=-1, keepdims=True) + epsilon)
            scaled = upstream * gain_one
            add_gain(0, jnp.sum(upstream * values * factor, axis=0, keepdims=True))
            across[i] = (hid[s, own, :] + factor * scaled - values * factor**3 * jnp.mean(
                scaled * values, axis=-1, keepdims=True)).astype(bf16)
            saving_token(i, n).start()

    sums = Sum(place, part, inward, across, (send_one, recv_one, send_two, recv_two), done)

    def move(s, source, target, device):
        return remote(give.at[source], take.at[s, target], kv_send.at[source], kv_recv.at[s, target], device)

    far_to_mate = lambda s: move(s, 2, 0, mate)
    peer_back = lambda s: move(s, 1, 1, peer)
    near_to_mate = lambda s: move(s, 0, 2, mate)
    ready("late")
    sums.offer(0, head_start)
    for name in later:
        copies[name].start()

    def hidden_stage(s):
        @pl.loop(0, rows // tile)
        def _(t):
            at = rows_at(t * tile, tile)
            first = s * per_seq + t * per_tile
            join = lambda ref: jnp.concatenate([ref[first + k] for k in range(per_tile)], axis=0).astype(f32)
            token = tok[s, at, :].astype(f32)
            values = token + join(attn)
            upstream = jnp.concatenate(
                [mixed[t * per_tile + k] for k in range(per_tile)], axis=0).astype(f32)
            factor = lax.rsqrt(jnp.mean(values * values, axis=-1, keepdims=True) + epsilon)
            scaled = upstream * gain_two
            add_gain(1, jnp.sum(upstream * values * factor, axis=0, keepdims=True))
            hid_now = cot[at, :].astype(f32) + factor * scaled - values * factor**3 * jnp.mean(
                scaled * values, axis=-1, keepdims=True)
            hid[s, at, :] = hid_now
            low = hid_now.astype(bf16)
            dwo_sum[...] += dot(jnp.transpose(ctx[s, at, :]), low)
            left, right = low[:, :middle], low[:, middle:]
            grad = dot_nt(left, wo[0]) + dot_nt(right, wo[1])
            lane_owner = lax.broadcasted_iota(jnp.int32, grad.shape, 1) // HEAD_DIM
            q_now = q[s, at, :].astype(f32)
            grad_t = jnp.transpose(grad)
            q_t = jnp.transpose(q_now)
            product = jnp.transpose(grad.astype(bf16).astype(f32) * ctx[s, at, :].astype(f32))
            for h in range(heads):
                low_rows = rows_at(h % 2 * rows + t * tile, tile)
                om[h // 2, low_rows, :] = jnp.where(lane_owner == h, grad, 0.0).astype(bf16)
                qm[h // 2, low_rows, :] = jnp.where(lane_owner == h, q_now, 0.0).astype(bf16)
                delta[h // 2, :, low_rows] = jnp.sum(
                    product[h * HEAD_DIM : (h + 1) * HEAD_DIM], axis=0, keepdims=True)
            spread(otm, grad_t, t * tile, rows)
            spread(qtm, q_t, t * tile, rows)
            normed = (unit_norm(token) * gain_one).astype(bf16)
            normed_t[:, rows_at(s * rows + t * tile, tile)] = jnp.transpose(normed)

    def back_block(s, j, tick):
        kt[...] = jnp.transpose(kv[j, 0])
        key_pos = block_place(ring, j) * rows + lax.broadcasted_iota(jnp.int32, (rows, 1), 0)
        query_pos = ring * rows + lax.rem(lax.broadcasted_iota(jnp.int32, (1, 2 * rows), 1), rows)
        limit = jnp.maximum(query_pos + 1, prefix[s])
        dk[...] = jnp.zeros_like(dk)
        dv[...] = jnp.zeros_like(dv)

        def per_pair(h):
            scores = dot(kv[j, 0], qtm[h])
            probs = jnp.where(key_pos < limit, jnp.exp(scores - lse[s, pl.ds(h, 1), :]), 0.0)
            dprobs = dot(kv[j, 1], otm[h])
            dv[...] += dot(probs.astype(bf16), om[h])
            dscores = (probs * (dprobs - delta[h])).astype(bf16)
            dk[...] += dot(dscores, qm[h])
            for n in range(2):
                of_head = rows_at((2 * h + n) * HEAD_DIM, HEAD_DIM)
                dqt[of_head, :] += dot(kt[of_head, :], dscores[:, n * rows : (n + 1) * rows])
            tick(h)

        for h in range(heads // 2):
            per_pair(h)

    def finalize(s):
        near_to_mate(s).wait_recv()
        peer_back(s).wait_recv()
        @pl.loop(0, rows // tile)
        def _(t):
            at = rows_at(t * tile, tile)
            flat = rows_at(s * rows + t * tile, tile)
            co, si = cosine[at, :], sine[at, :]
            grad_v = 0.5 * (dv[at, :] + take[s, 2, 1, at, :].astype(f32) + take[s, 1, 1, at, :].astype(f32))
            grad_k = dk[at, :] + take[s, 2, 0, at, :].astype(f32) + take[s, 1, 0, at, :].astype(f32)
            grad_q = jnp.transpose(dqt[:, at]) * HEAD_DIM ** (-0.5)
            proj[0, flat, :] = turn(grad_q, co, si, -1.0).astype(bf16)
            proj[1, flat, :] = turn(grad_k, co, si, -1.0).astype(bf16)
            proj[2, flat, :] = grad_v.astype(bf16)
            i = jnp.where(s == 0, own_start[0], own_start[1]) + t * per_tile
            for piece in range(2):
                cut = slice(piece * middle, (piece + 1) * middle)
                sums.fill(i, piece, dot_nt(proj[0, flat, :], wq[cut, :]) + dot_nt(
                    proj[1, flat, :], wk[cut, :]) + dot_nt(proj[2, flat, :], wv[cut, :]))
            sums.offer(i, per_tile)

        @pl.when(s == 0)
        def _():
            sums.offer(rest_start, rest)

    ready("wo")
    dwo_sum[...] = jnp.zeros_like(dwo_sum)
    if split:
        ready("quarter0")
        ends[0].resume()

    def start_at(phase, *names):
        for wanted in range(1, seqs):
            @pl.when(phase == wanted - 1)
            def _():
                for name in names:
                    copies[f"{name}{wanted}"].start()

    def at_phase(phase, wanted, names):
        @pl.when(phase == wanted)
        def _():
            ready(*names)

    plan = [(1, m, m) for m in range(7)] + [(2, m, 10 + line) for line, m in enumerate((0, 1, 3, 4, 6, 7))]

    @pl.loop(0, seqs + 1)
    def _(phase):
        s = jnp.maximum(phase - 1, 0)
        follows = phase > 1

        @pl.when(phase > 0)
        def _():
            for wanted in range(seqs):
                at_phase(phase, wanted + 1, [f"kv{wanted}"])
            for wanted in range(1, seqs):
                at_phase(phase, 1, [f"tok{wanted}", f"attn{wanted}"])
            dqt[...] = jnp.zeros_like(dqt)

            @pl.loop(0, 4)
            def _(n):
                def tick(h):
                    chosen = -1
                    for at_phase, at_step, line in plan:
                        chosen = jnp.where((phase == at_phase) & (2 * n + h == at_step), line, chosen)

                    @pl.when(chosen >= 0)
                    def _():
                        sums.steps(chosen, 1)

                back_block(s, 3 - n, tick)

                @pl.when(n == 0)
                def _():
                    @pl.when(follows)
                    def _():
                        far_to_mate(s - 1).wait_send()
                        fold_o.second()

                    give[2, 0] = dk[...].astype(bf16)
                    give[2, 1] = dv[...].astype(bf16)
                    far_to_mate(s).start()

                @pl.when(n == 1)
                def _():
                    far_to_mate(s).wait_recv()

                    @pl.when(follows)
                    def _():
                        peer_back(s - 1).wait_send()

                    give[1, 0] = (dk[...] + take[s, 0, 0].astype(f32)).astype(bf16)
                    give[1, 1] = (dv[...] + take[s, 0, 1].astype(f32)).astype(bf16)
                    peer_back(s).start()

                @pl.when(n == 2)
                def _():
                    @pl.when(follows)
                    def _():
                        near_to_mate(s - 1).wait_send()
                        fold_o.third()

                    give[0, 0] = dk[...].astype(bf16)
                    give[0, 1] = dv[...].astype(bf16)
                    near_to_mate(s).start()

            start_at(phase - 1, "kv")

        @pl.when(phase < seqs)
        def _():
            for wanted in range(seqs):
                names = ("tok", "attn") * (wanted == 0) + ("cot", "mixed", "q", "ctx")
                at_phase(phase, wanted, [f"{name}{wanted}" for name in names])
            hidden_stage(phase)
            start_at(phase, "cot", "mixed")

            @pl.when(phase == 1)
            def _():
                sums.steps(7, 1)

        @pl.when(phase > 0)
        def _():
            at_phase(phase, 1, ["wq", "wk", "wv", "rest"])
            sums.steps(jnp.where(phase == 1, 8, 16), 1)
            finalize(s)
            sums.steps(jnp.where(phase == 1, 9, 17), 1)

        @pl.when(phase == seqs - 1)
        def _():
            deep = dwo.shape[2]
            for h in range(2):
                for y in range(2):
                    dwo[h, y] = dwo_sum[h * deep : (h + 1) * deep, y * middle : (y + 1) * middle].astype(bf16)
            fold_o.first()
            if split:
                ends[0].fourth()
                ready("quarter1")
                ends[1].resume()

    begun = 18
    fv_copy = pltpu.make_async_copy(proj.at[2], fv_hbm, fv_save)
    fv_copy.start()
    if split:
        ends[1].fourth()
        ready("quarter2")
        ends[2].resume()
        ends[0].last()
    share = dwq.shape[2]

    def square_grad(target, which):
        @pl.loop(0, 4)
        def _(k):
            h, y = k // 2, lax.rem(k, 2)
            target[h, y] = dot(normed_t[rows_at((2 * y + h) * share, share), :], proj[which]).astype(bf16)

    ready("early")
    for n in range(per_tile):
        own = slice(n * chunk, (n + 1) * chunk)
        early[n] = (tok[0, own, :].astype(f32) + attn[n].astype(f32) + early[n].astype(f32)).astype(bf16)
        saving_early(n).start()
    square_grad(dwk, 1)
    fold_k.first()
    sums.steps(begun, 1)
    square_grad(dwv, 2)
    fold_v.first()
    fold_k.second()
    sums.steps(begun + 1, 1)
    square_grad(dwq, 0)
    fold_q.first()
    fold_v.second()
    sums.steps(begun + 2, 1)
    fold_q.second()
    fold_o.fourth()
    sums.steps(begun + 3, 1)
    fold_k.third()
    sums.steps(begun + 4, 1)
    fold_v.third()
    sums.steps(begun + 5, 1)
    fold_q.third()
    fold_k.fourth()
    sums.steps(begun + 6, 1)
    fold_v.fourth()
    sums.steps(begun + 7, 1)
    fold_q.fourth()
    for fold in (fold_o, fold_k, fold_v) + tuple(ends[1:2]):
        fold.last()
    if split:
        ends[2].fourth()
    sums.steps(begun + 8, count - begun - 8)
    for fold in (fold_q,) + tuple(ends[2:]):
        fold.last()
    sums.settled(0, count)
    sums.close(count)
    if split:
        me = 4 * side + ring
        gain_all[me] = gain_part[side]

        def share_gain(n):
            dy, dc = others[n]
            y = lax.rem(side + dy, 2)
            return remote(gain_part.at[y], gain_all.at[me], gain_send.at[n], gain_recv.at[n], group[n])

        for n in range(7):
            share_gain(n).start()
        for n in range(7):
            share_gain(n).wait()
        total = gain_all[0]
        for n in range(1, 8):
            total = total + gain_all[n]
        gain_out[...] = total
    else:
        gain_out[...] = gain_part[...]
    for fold in (fold_o, fold_k, fold_v, fold_q) + tuple(ends):
        fold.settle()
    fv_copy.wait()
    for copy in (far_to_mate, peer_back, near_to_mate):
        copy(seqs - 1).wait_send()

    for n in range(per_tile):
        saving_early(n).wait()

    @pl.loop(0, count)
    def _(i):
        @pl.when(is_block(i))
        def _():
            saving_block(i, block_of(i)).wait()

        @pl.when(jnp.logical_not(is_block(i)))
        def _():
            saving_token(i, token_of(i)).wait()


def back(split, quarters, tok, cot, sums, attn, late, gains, square, q, kv, ctx, lse, cosine, sine, prefix):
    seqs, rows, dim = tok.shape
    width = q.shape[2]
    heads = width // HEAD_DIM
    _, chunk, _ = sums.shape
    tokens = seqs * rows
    early = 256 // chunk
    count = 2 * tokens // chunk - early
    vmem = pl.BlockSpec(memory_space=pltpu.VMEM)
    anyw = pl.BlockSpec(memory_space=pl.ANY)
    dma = pltpu.SemaphoreType.DMA
    lines = pltpu.VMEM((count, chunk, dim), bf16)
    half_lines = pltpu.VMEM((tokens // chunk, chunk, dim), bf16)
    wide = pltpu.VMEM((heads // 2, 2 * rows, width), bf16)
    tall = pltpu.VMEM((heads // 2, width, 2 * rows), bf16)
    shape = jax.ShapeDtypeStruct
    fold_scratch, fold_outs = fold_shapes(
        [(width // 2, dim // 2)] + [(dim // 4, width)] * 3, split, (0, 1, 2, 3, 4))
    ends_scratch, ends_outs = fold_shapes([x.shape for x in quarters], True, (3, 4)) if split else ([], [])
    loaded = (tok, cot) + tuple(square) + (q, kv, ctx)
    held = [tok.shape, cot.shape[1:]] + [x.shape for x in square] + [q.shape, kv.shape[1:], ctx.shape]
    return pl.pallas_call(
        functools.partial(back_kernel, split),
        name="back",
        out_shape=[
            shape((seqs, rows, dim), bf16), shape((seqs, rows, dim), bf16), shape((tokens, width), bf16),
            shape((8, dim // 2) if split else (2, 8, dim // 2), f32)] + fold_outs + ends_outs,
        in_specs=[anyw] * (len(quarters) + 12) + [vmem] * 4 + [pl.BlockSpec(memory_space=pltpu.SMEM)],
        out_specs=[anyw, anyw, anyw, vmem] + [anyw] * (4 + len(quarters)),
        scratch_shapes=[pltpu.VMEM(x, bf16) for x in held] + [
            half_lines, pltpu.VMEM((rows // chunk, chunk, dim), bf16), pltpu.VMEM((early, chunk, dim), bf16),
            pltpu.VMEM((seqs, rows, dim), f32),
            pltpu.VMEM((width, dim), f32),
            tall, wide, tall, wide,
            pltpu.VMEM((width, rows), bf16),
            pltpu.VMEM((heads // 2, 1, 2 * rows), f32),
            pltpu.VMEM((width, rows), f32),
            pltpu.VMEM((rows, width), f32),
            pltpu.VMEM((rows, width), f32),
            pltpu.VMEM((3, 2, rows, width), bf16),
            pltpu.VMEM((seqs, 3, 2, rows, width), bf16),
            pltpu.VMEM((3, tokens, width), bf16),
            pltpu.VMEM((dim, tokens), bf16),
            lines, lines, lines,
            pltpu.VMEM((2, 8, dim // 2), f32),
            pltpu.VMEM((8, 8, dim // 2), f32),
            dma((3,)), dma((seqs, 3)),
            dma((count,)), dma((count,)), dma((count,)), dma((count,)), dma((count + early,)),
            dma((7,)), dma((7,)), dma((8 * seqs + 11,)), dma(()),
        ] + ends_scratch + fold_scratch,
        compiler_params=limits(2, 62),
        cost_estimate=pl.CostEstimate(flops=30 * 10**9, bytes_accessed=10**7, transcendentals=10**7),
    )(*quarters, late, sums, attn, *loaded, gains, lse, cosine, sine, prefix)


def finish_kernel(parts, *refs):
    n = len(parts)
    sources, gain_in, refs = refs[:n], refs[n], refs[n + 1 :]
    targets, gain_one, gain_two, refs = refs[:n], refs[n], refs[n + 1], refs[n + 2 :]
    held, wide, (loads, saves) = refs[:n], refs[n : 2 * n], refs[2 * n :]
    loading, saving = [], []
    for k, count in enumerate(parts):
        size = sources[k].shape[0] // count
        for piece in range(count):
            at = slice(piece * size, (piece + 1) * size)
            place = len(loading)
            loading.append(pltpu.make_async_copy(sources[k].at[at], held[k].at[at], loads.at[place]))
            plain = sources[k].dtype == targets[k].dtype
            saving.append((k, at, plain, pltpu.make_async_copy(
                (held if plain else wide)[k].at[at], targets[k].at[at], saves.at[place])))
    for load in loading:
        load.start()
    gain_one[...] = gain_in[0:1, :]
    gain_two[...] = gain_in[1:2, :]
    for load, (k, at, plain, save) in zip(loading, saving):
        load.wait()
        if not plain:
            wide[k][at] = held[k][at].astype(f32)
        save.start()
    for *_, save in saving:
        save.wait()


def finish(arrays, types, gain_rows):
    parts = [x.shape[0] if x.size > 300000 else 1 for x in arrays]
    vmem = pl.BlockSpec(memory_space=pltpu.VMEM)
    anyw = pl.BlockSpec(memory_space=pl.ANY)
    dma = pltpu.SemaphoreType.DMA
    shape = jax.ShapeDtypeStruct
    row = shape((1, gain_rows.shape[1]), f32)
    return pl.pallas_call(
        functools.partial(finish_kernel, parts),
        name="finish",
        out_shape=[shape(x.shape, t) for x, t in zip(arrays, types)] + [row, row],
        in_specs=[anyw] * len(arrays) + [vmem],
        out_specs=[anyw] * len(arrays) + [vmem, vmem],
        scratch_shapes=[pltpu.VMEM(x.shape, x.dtype) for x in arrays] + [
            pltpu.VMEM((8, 128) if x.dtype == t else x.shape, f32) for x, t in zip(arrays, types)] + [
            dma((sum(parts),)), dma((sum(parts),))],
        compiler_params=pltpu.CompilerParams(vmem_limit_bytes=60 * 1024 * 1024),
        cost_estimate=pl.CostEstimate(flops=10**6, bytes_accessed=25 * 10**6, transcendentals=0),
    )(*arrays, gain_rows)


def halves(weight):
    rows, columns = weight.shape
    return jnp.swapaxes(weight.reshape(rows, 2, columns // 2), 0, 1)


def shards(
    tokens, first_values, norm1_gain, norm2_gain, w_query, w_key, w_value, w_out, w_gate, w_up, w_down,
    prefix, cotangent,
):
    split = lax.axis_size("fsdp") == 2
    seqs, rows, dim = tokens.shape
    width, units = w_query.shape[1], w_gate.shape[1]
    gather = functools.partial(lax.all_gather, axis_name="fsdp", tiled=True)
    if split:
        gains = (norm1_gain, norm2_gain)
        square = (w_query, w_key, w_value, w_out)
        wide = (w_gate.T, w_up.T, w_down)
    else:
        gains = (gather(norm1_gain), gather(norm2_gain))
        square = (gather(w_query), gather(w_key), gather(w_value), halves(gather(w_out, axis=1)))
        wide = (halves(gather(w_gate).T), halves(gather(w_up).T), halves(gather(w_down, axis=1)))
    (sums, late, query, pairs, attn, context, log_total, gain_rows, cosine, sine, down_grad, gate_grad, up_grad,
     *gathered) = front(
        split, tokens, first_values, cotangent, [gain.reshape(-1, 128) for gain in gains], square, wide, prefix)
    if split:
        square = tuple(gathered)
    wide_grads = (down_grad, gate_grad, up_grad)
    block_out, token_grad, half_value_grad, gain_grads, out_grad, key_grad, value_grad, query_grad, *ends = back(
        split, wide_grads if split else (), tokens, cotangent, sums, attn, late, gain_rows, square, query, pairs,
        context.reshape(query.shape), log_total, cosine, sine, prefix)
    half_value_grad = half_value_grad.reshape(seqs, rows, width)
    if split:
        cut = lambda x: x.reshape(8, -1, dim)
        arrays = (cut(token_grad), cut(block_out), half_value_grad, query_grad, key_grad, value_grad, out_grad, *ends)
        (token_grad, block_out, half_value_grad, query_grad, key_grad, value_grad, out_grad, down_grad, gate_grad,
         up_grad, gain_one_grad, gain_two_grad) = finish(arrays, (f32, bf16) + (f32,) * 8, gain_grads)
        token_grad, block_out = token_grad.reshape(tokens.shape), block_out.reshape(tokens.shape)
        over_rows = lambda grad: grad.reshape(-1, grad.shape[-1])
        over_columns = over_rows
        over_turned = lambda grad: over_rows(grad).T
        gain_one_grad, gain_two_grad = gain_one_grad[0], gain_two_grad[0]
    else:
        half_value_grad, token_grad = half_value_grad.astype(f32), token_grad.astype(f32)
        total = lambda grad, axis: lax.psum(
            lax.psum_scatter(grad, "fsdp", scatter_dimension=axis, tiled=True), "ctx").astype(f32)
        over_rows = lambda grad: total(jnp.swapaxes(grad, 0, 1).reshape(-1, grad.shape[-1]), 0)
        over_columns = lambda grad: total(
            jnp.transpose(grad, (0, 2, 1, 3)).reshape(2 * grad.shape[2], -1), 1)
        over_turned = lambda grad: over_columns(grad).T
        gain_one_grad, gain_two_grad = (total(gain_grads[:, n].reshape(-1), 0) for n in range(2))
    return (
        block_out,
        token_grad,
        half_value_grad,
        gain_one_grad,
        gain_two_grad,
        over_rows(query_grad),
        over_rows(key_grad),
        over_rows(value_grad),
        over_columns(out_grad),
        over_turned(gate_grad),
        over_turned(up_grad),
        over_columns(down_grad),
    )


def solution(mesh):
    return jax.shard_map(
        shards,
        mesh=mesh,
        in_specs=(
            P("fsdp", "ctx", None),
            P("fsdp", "ctx", "tp"),
            P("fsdp"),
            P("fsdp"),
            P("fsdp", "tp"),
            P("fsdp", "tp"),
            P("fsdp", "tp"),
            P("tp", "fsdp"),
            P("fsdp", "tp"),
            P("fsdp", "tp"),
            P("tp", "fsdp"),
            P("fsdp"),
            P("fsdp", "ctx", None),
        ),
        out_specs=(
            P("fsdp", "ctx", None),
            P("fsdp", "ctx", None),
            P("fsdp", "ctx", "tp"),
            P("fsdp"),
            P("fsdp"),
            P("fsdp", "tp"),
            P("fsdp", "tp"),
            P("fsdp", "tp"),
            P("tp", "fsdp"),
            P("fsdp", "tp"),
            P("fsdp", "tp"),
            P("tp", "fsdp"),
        ),
        check_vma=False,
    )
```
